32 devices in a mesh: groups: 2 (over y), seq: 4 (over z), tensor: 2 (over x), sub: 2 (over core).
Axes of the slice: x: 2, y: 2, z: 4, core: 2. Of those that a mesh axis runs over, the one named last changes fastest.
Arguments:
- features: bfloat16 [3072, 3, 8192], P(('groups', 'seq'), None, ('tensor', 'sub')), parts along dimension 0, may hold values from -6 to 6
- short_filter: float32 [7, 8192], P(None, ('tensor', 'sub')), may hold values from -5 to 5
- medium_filter: float32 [128, 8192], P(None, ('tensor', 'sub')), may hold values from -1.25 to 1.25
- skip_gain: float32 [8192], P(('tensor', 'sub')), may hold values from 0.5 to 1.5
- attn_query: bfloat16 [3072, 8192], P(('groups', 'seq'), ('tensor', 'sub')), parts along dimension 0, may hold values from -100 to 100
- attn_key: bfloat16 [3072, 8192], P(('groups', 'seq'), ('tensor', 'sub')), parts along dimension 0, may hold values from -5 to 5
- attn_value: bfloat16 [3072, 8192], P(('groups', 'seq'), ('tensor', 'sub')), parts along dimension 0, may hold values from -6 to 6
- lengths: int32 [8], P('groups'), parts along dimension 0, may hold values from 1 to 768, 1536 in all
Outputs:
- hyena_out: bfloat16 [3072, 8192], P(('groups', 'seq'), ('tensor', 'sub')), parts along dimension 0
- attn_out: bfloat16 [3072, 8192], P(('groups', 'seq'), ('tensor', 'sub')), parts along dimension 0
The draws below stay inside these ranges and needn't reach their ends.
There are 2 independent parts, one for each index of `groups`. The reference program is written for one: setup_inputs(seed, part) draws one part's arguments, and reference() takes and returns one part's arrays. A program takes and returns all parts, laid end to end along the dimension named above; an argument that names none is the same for every part. Nothing has to cross between parts.
Inputs may be any that keep to these rules, and one draw needn't show every extreme that they name: 4 documents packed end to end in order; their lengths sum to 1536 and the longest is exactly 768 tokens.
All inputs are finite; a program needn't handle non-finite values.
Results may differ from the reference program's by a relative error of at most 0.0051.
Values may be sent and summed in bfloat16 or wider, within the bound.
A program may use at most 192 MiB of HBM per device.

```python
import math
import jax
import jax.numpy as jnp
import numpy as np
from jax import lax

D = 8192
HEADS = 64
HD = 128
SHORT = 7
MEDIUM = 128
DOCS = 4
TOKENS = 1536
MOST = 768


def attention_pair(key):
    base_key = jax.random.fold_in(key, 31)
    query_seed, key_seed = jax.random.split(base_key, 2)
    array_shape = (TOKENS, HEADS * HD)
    key_rows = jnp.clip(jax.random.normal(key_seed, array_shape, jnp.float32), -5.0, 5.0)
    query_rows = jnp.clip(jax.random.normal(query_seed, array_shape, jnp.float32), -5.0, 5.0)
    return (query_rows, key_rows)


def draw_attn_query(key, part):
    return attention_pair(key)[0].astype(jnp.bfloat16)


def draw_attn_key(key, part):
    return attention_pair(key)[1].astype(jnp.bfloat16)


def levels(rng, extent, cuts, smallest, top_value):
    loudness = 1.0
    for position, shards_of in cuts:
        heights = jax.random.uniform(jax.random.fold_in(jax.random.fold_in(rng, 6), position), (shards_of,), jnp.float32, smallest / len(cuts), top_value / len(cuts))
        loudness = loudness * jnp.repeat(jnp.exp(heights), extent[position] // shards_of).reshape((-1,) + (1,) * (len(extent) - 1 - position))
    return loudness


def split_up(amount, total, most, slope):
    loads = [(1 << 20) // math.isqrt(rank ** slope) + 1 for rank in range(2, amount + 1)]
    rest, counts = total - most - (amount - 1), [1] * (amount - 1)
    while rest > 0:
        movable = [i for i in range(amount - 1) if counts[i] < most]
        mass, remaining = sum([loads[i] for i in movable]), rest
        for i in movable:
            more = min(most - counts[i], max(1, remaining * loads[i] // mass), rest)
            counts[i] = counts[i] + more
            rest = rest - more
    return np.array([most] + counts)


def uneven_parts(stream_key, amount, total, reach, skew):
    if amount == 2:
        one = jax.random.randint(stream_key, (), max(1, total - reach), min(reach, total - 1) + 1)
        return jnp.stack([one, total - one])
    tallies = jnp.asarray(split_up(amount, total, reach, skew), jnp.int32)
    couples = (amount - 1) // 2
    source_of, receiver = tallies[1:1 + 2 * couples:2], tallies[2:2 + 2 * couples:2]
    margin = jnp.minimum(source_of - 1, reach - receiver)
    passed = jax.random.randint(jax.random.fold_in(stream_key, 1), (couples,), 0, 1 << 20) % (margin + 1)
    tallies = tallies.at[1:1 + 2 * couples:2].set(source_of - passed).at[2:2 + 2 * couples:2].set(receiver + passed)
    return tallies[jax.random.permutation(jax.random.fold_in(stream_key, 2), amount)]


def noise(rng, dims, width, reach, cuts=(), kind=jnp.bfloat16):
    drawn = width * jax.random.normal(rng, dims, jnp.float32)
    if cuts:
        drawn = drawn * levels(rng, dims, cuts, -0.22, 0.18)
    return jnp.clip(drawn, -reach, reach).astype(kind)


def setup_inputs(seed: int = 0, part: int = 0) -> dict:
    seeds = jax.random.split(jax.random.key(seed), 9)
    part_splits = jax.random.split(jax.random.fold_in(seeds[8], part), 9)
    return {
        "features": noise(part_splits[0], (TOKENS, 3, D), 1.0, 6.0, ((0, 4), (2, 4))),
        "short_filter": noise(seeds[1], (SHORT, D), 0.35, 5.0, ((1, 4),), jnp.float32),
        "medium_filter": noise(seeds[2], (MEDIUM, D), 0.09, 1.25, ((1, 4),), jnp.float32),
        "skip_gain": jnp.clip(0.5 + 1.0 * jax.random.uniform(seeds[3], (D,), jnp.float32) ** levels(seeds[3], (D,), ((0, 4),), -0.2, 0.2), 0.5, 1.5),
        "attn_query": draw_attn_query(jax.random.fold_in(jax.random.fold_in(seeds[8], part), 71), part),
        "attn_key": draw_attn_key(jax.random.fold_in(jax.random.fold_in(seeds[8], part), 71), part),
        "attn_value": noise(part_splits[6], (TOKENS, HEADS * HD), 1.0, 6.0, ((0, 4), (1, 4))),
        "lengths": uneven_parts(part_splits[7], DOCS, TOKENS, MOST, 2).astype(jnp.int32),
    }


def doc_of(positions, lengths):
    doc_ends = jnp.cumsum(lengths, dtype=jnp.int32)
    return jnp.sum((positions[:, None] >= doc_ends[None, :]).astype(jnp.int32), axis=1, dtype=jnp.int32)


def reference(features, short_filter, medium_filter, skip_gain, attn_query, attn_key, attn_value, lengths):
    positions = jnp.arange(TOKENS, dtype=jnp.int32)
    docs = doc_of(positions, lengths)
    queries = features[:, 0].astype(jnp.float32)
    gated = (features[:, 1].astype(jnp.float32) * features[:, 2].astype(jnp.float32)).astype(jnp.bfloat16)
    gated = lax.optimization_barrier(gated)
    padded = jnp.concatenate((jnp.zeros((MEDIUM - 1, D), jnp.bfloat16), gated), axis=0)
    pad_docs = jnp.concatenate((jnp.full((MEDIUM - 1,), -1, jnp.int32), docs), axis=0)

    def tap_term(tap_index, filter_bank):
        first_row = (jnp.int32(MEDIUM - 1) - tap_index).astype(jnp.int32)
        window = lax.dynamic_slice_in_dim(padded, first_row, TOKENS, 0).astype(jnp.float32)
        window_docs = lax.dynamic_slice_in_dim(pad_docs, first_row, TOKENS, 0)
        keep_mask = (window_docs == docs).astype(jnp.float32)[:, None]
        taps = lax.dynamic_index_in_dim(filter_bank, tap_index, 0, keepdims=False)
        return taps[None, :] * window * keep_mask

    short_sum = jnp.zeros((TOKENS, D), jnp.float32)
    for tap_index in range(SHORT):
        short_sum = short_sum + tap_term(jnp.int32(tap_index), short_filter)
    medium_sum = lax.fori_loop(0, MEDIUM, lambda tap_index, partial_value: partial_value + tap_term(jnp.asarray(tap_index).astype(jnp.int32), medium_filter), jnp.zeros((TOKENS, D), jnp.float32))
    hyena_out = (queries * (short_sum + medium_sum + skip_gain[None, :] * gated.astype(jnp.float32))).astype(jnp.bfloat16)

    allowed = (positions[None, :] <= positions[:, None]) & (docs[None, :] == docs[:, None])
    score_scale = HD ** -0.5
    query_heads = attn_query.reshape(TOKENS, HEADS, HD).transpose(1, 0, 2)
    key_heads = attn_key.reshape(TOKENS, HEADS, HD).transpose(1, 0, 2)
    value_heads = attn_value.reshape(TOKENS, HEADS, HD).transpose(1, 0, 2)

    def one_head(operands):
        head_q, head_k, head_v = operands
        scores = jnp.dot(head_q, head_k.T, preferred_element_type=jnp.float32) * score_scale
        top_score = jnp.max(jnp.where(allowed, scores, -jnp.inf), axis=1)
        weights = jnp.where(allowed, jnp.exp(scores - top_score[:, None]), 0.0)
        total = jnp.sum(weights, axis=1)
        mixed = jnp.dot(weights.astype(jnp.bfloat16), head_v, preferred_element_type=jnp.float32)
        return (mixed / total[:, None]).astype(jnp.bfloat16)

    head_out = lax.map(one_head, (query_heads, key_heads, value_heads))
    attn_out = head_out.transpose(1, 0, 2).reshape(TOKENS, HEADS * HD)
    return (hyena_out, attn_out)
```

```python
import math

import jax
import jax.numpy as jnp
import numpy as np
from jax import lax
from jax.experimental import pallas as pl
from jax.experimental.pallas import tpu as pltpu
from jax.sharding import PartitionSpec as P

HD = 128


def passed_along(value, axis, by):
    length = lax.axis_size(axis)
    pairs = [(i, i + by) for i in range(length) if 0 <= i + by < length]
    return lax.ppermute(value, axis, pairs)


def doc_of(positions, lengths):
    doc_ends = jnp.cumsum(lengths, dtype=jnp.int32)
    return jnp.sum(
        (positions[:, None] >= doc_ends[None, :]).astype(jnp.int32), axis=1, dtype=jnp.int32
    )


def hyena_mix(features, short_filter, medium_filter, skip_gain, lengths):
    row_count = features.shape[0]
    medium_taps = medium_filter.shape[0]
    rim_rows = medium_taps - 1
    span_index = lax.axis_index("seq")
    queries = features[:, 0].astype(jnp.float32)
    gated = (features[:, 1].astype(jnp.float32) * features[:, 2].astype(jnp.float32)).astype(
        jnp.bfloat16
    )
    gated = lax.optimization_barrier(gated)
    carried = passed_along(gated[row_count - rim_rows :], "seq", 1)
    extended = jnp.concatenate((carried, gated), axis=0)
    ext_positions = (
        span_index * row_count - rim_rows + jnp.arange(row_count + rim_rows, dtype=jnp.int32)
    )
    ext_docs = doc_of(ext_positions, lengths)
    ext_live = ext_positions >= 0
    own_docs = ext_docs[rim_rows:]

    def tap_term(tap_index, filter_bank):
        first_row = rim_rows - tap_index
        window = lax.dynamic_slice_in_dim(extended, first_row, row_count, 0).astype(jnp.float32)
        same_doc = lax.dynamic_slice_in_dim(ext_docs, first_row, row_count, 0) == own_docs
        live_mask = lax.dynamic_slice_in_dim(ext_live, first_row, row_count, 0)
        keep_mask = (same_doc & live_mask).astype(jnp.float32)[:, None]
        taps = lax.dynamic_index_in_dim(filter_bank, tap_index, 0, keepdims=False)
        return taps[None, :] * window * keep_mask

    short_sum = jnp.zeros(gated.shape, jnp.float32)
    for tap_index in range(short_filter.shape[0]):
        short_sum = short_sum + tap_term(tap_index, short_filter)

    def tap_block(block_index, partial_value):
        for offset in range(8):
            partial_value = partial_value + tap_term(block_index * 8 + offset, medium_filter)
        return partial_value

    medium_sum = lax.fori_loop(0, medium_taps // 8, tap_block, jnp.zeros(gated.shape, jnp.float32))
    mixed = queries * (short_sum + medium_sum + skip_gain[None, :] * gated.astype(jnp.float32))
    return mixed.astype(jnp.bfloat16)


def attention_mix(attn_query, attn_key, attn_value, lengths):
    row_count, col_count = attn_query.shape
    heads_here = col_count // HD
    span_index = lax.axis_index("seq")
    query_positions = span_index * row_count + jnp.arange(row_count, dtype=jnp.int32)
    query_docs = doc_of(query_positions, lengths)
    query_heads = attn_query.reshape(row_count, heads_here, HD)
    score_scale = HD ** (-0.5)
    last_query = query_positions[row_count - 1]
    first_query_doc = query_docs[0]

    def absorb(state_now, key_block, value_block, first_row):
        key_count = key_block.shape[0]
        last_key = first_row + key_count - 1
        last_key_doc = doc_of(jnp.reshape(last_key, (1,)), lengths)[0]
        masked_out = (first_row > last_query) | (last_key < 0) | (last_key_doc < first_query_doc)

        def compute(state_in):
            running_max, running_total, running_sum = state_in
            key_heads = key_block.reshape(key_count, heads_here, HD)
            value_heads = value_block.reshape(key_count, heads_here, HD)
            scores = (
                jnp.einsum(
                    "rhd,nhd->hrn", query_heads, key_heads, preferred_element_type=jnp.float32
                )
                * score_scale
            )
            key_positions = first_row + jnp.arange(key_count, dtype=jnp.int32)
            key_docs = doc_of(key_positions, lengths)
            allowed = (
                (key_positions[None, :] <= query_positions[:, None])
                & (key_docs[None, :] == query_docs[:, None])
                & (key_positions >= 0)[None, :]
            )
            masked = jnp.where(allowed[None], scores, -1e30)
            new_max = jnp.maximum(running_max, jnp.max(masked, axis=2))
            rescale = jnp.exp(running_max - new_max)
            weights = jnp.where(allowed[None], jnp.exp(scores - new_max[:, :, None]), 0.0)
            new_total = running_total * rescale + jnp.sum(weights, axis=2)
            product = jnp.einsum(
                "hrn,nhd->hrd",
                weights.astype(jnp.bfloat16),
                value_heads,
                preferred_element_type=jnp.float32,
            )
            new_sum = running_sum * rescale[:, :, None] + product
            return (new_max, new_total, new_sum)

        def keep_state(state_in):
            return state_in

        return lax.cond(masked_out, keep_state, compute, state_now)

    def fold_keys(state_now, pieces, first_row):
        key_all, value_all = pieces
        key_count = key_all.shape[0]
        block_rows = math.gcd(key_count, 1536)
        if block_rows == key_count:
            return absorb(state_now, key_all, value_all, first_row)
        block_total = key_count // block_rows
        key_blocks = key_all.reshape(block_total, block_rows, col_count)
        value_blocks = value_all.reshape(block_total, block_rows, col_count)

        def scan_step(state_inner, block_items):
            key_block, value_block, block_index = block_items
            return (
                absorb(state_inner, key_block, value_block, first_row + block_index * block_rows),
                None,
            )

        state_now, unused = lax.scan(
            scan_step,
            state_now,
            (key_blocks, value_blocks, jnp.arange(block_total, dtype=jnp.int32)),
        )
        return state_now

    initial = (
        jnp.full((heads_here, row_count), -1e30, jnp.float32),
        jnp.zeros((heads_here, row_count), jnp.float32),
        jnp.zeros((heads_here, row_count, HD), jnp.float32),
    )
    state_now = fold_keys(
        initial,
        (
            lax.all_gather(attn_key, "seq", axis=0, tiled=True),
            lax.all_gather(attn_value, "seq", axis=0, tiled=True),
        ),
        jnp.int32(0),
    )
    running_max, running_total, running_sum = state_now
    result = running_sum / running_total[:, :, None]
    return result.transpose(1, 0, 2).reshape(row_count, col_count).astype(jnp.bfloat16)


LOG2E = 1.4426950408889634
LN2 = 0.6931471805599453
SCALE2 = HD**-0.5 * LOG2E
NEG = -1e30
STAT_ROWS = 16


def hyena_kernel(row_count, taps, lens_ref, feat_ref, rim_ref, filt_ref, fwd_ref, inv_ref, out_ref,
                 ext_ref, sum_ref):
    base = lens_ref[lens_ref.shape[0] - 1]
    ext_ref[:taps, :] = rim_ref[...]
    ext_ref[taps:, :] = (
        feat_ref[1].astype(jnp.float32) * feat_ref[2].astype(jnp.float32)
    ).astype(jnp.bfloat16)

    def dot(x, y):
        return jnp.dot(x, y, preferred_element_type=jnp.float32)

    filt = filt_ref[...]
    filt_hi = filt.astype(jnp.bfloat16)
    filt_lo = (filt - filt_hi.astype(jnp.float32)).astype(jnp.bfloat16)
    spec = (
        dot(fwd_ref[0, :, :taps], filt_hi)
        + dot(fwd_ref[1, :, :taps], filt_hi)
        + dot(fwd_ref[0, :, :taps], filt_lo)
    )
    spec_r, spec_i = spec[:taps], spec[taps:]
    win_iota = lax.broadcasted_iota(jnp.int32, (2 * taps, 1), 0)
    out_iota = lax.broadcasted_iota(jnp.int32, (taps, 1), 0)
    for block in range(row_count // taps):
        r0 = block * taps
        start = jnp.int32(0)
        for doc in range(lens_ref.shape[0] - 1):
            end = start + lens_ref[doc]
            first, last = start - base, end - base

            @pl.when((last > r0) & (first < r0 + taps) & (first < last))
            def _(first=first):
                window = ext_ref[r0 : r0 + 2 * taps, :]
                window = jnp.where(win_iota + (r0 - taps) >= first, window, jnp.zeros_like(window))
                wave = dot(fwd_ref[0], window) + dot(fwd_ref[1], window)
                wave_r, wave_i = wave[:taps], wave[taps:]
                prod = jnp.concatenate(
                    (
                        (wave_r * spec_r - wave_i * spec_i).astype(jnp.bfloat16),
                        (wave_r * spec_i + wave_i * spec_r).astype(jnp.bfloat16),
                    ),
                    axis=0,
                )
                sums = dot(inv_ref[0], prod) + dot(inv_ref[1], prod)
                sum_ref[...] = jnp.where(out_iota + r0 >= first, sums, sum_ref[...])

            start = end
        out_ref[r0 : r0 + taps, :] = (
            feat_ref[0, r0 : r0 + taps, :].astype(jnp.float32) * sum_ref[...]
        ).astype(out_ref.dtype)


def split_two(matrix):
    high = matrix.astype(jnp.bfloat16)
    low = (matrix - high.astype(np.float64)).astype(jnp.bfloat16)
    return np.stack((high, low))


def hyena_fast(features, short_filter, medium_filter, skip_gain, lengths):
    row_count, _, cols = features.shape
    taps = medium_filter.shape[0]
    span_index = lax.axis_index("seq")
    streams = features.transpose(1, 0, 2)
    tail = streams[:, row_count - taps :]
    gated_tail = (tail[1].astype(jnp.float32) * tail[2].astype(jnp.float32)).astype(jnp.bfloat16)
    carried = passed_along(gated_tail, "seq", 1)
    head = jnp.concatenate((short_filter[:1] + skip_gain[None, :], short_filter[1:]), axis=0)
    filt = medium_filter + jnp.pad(head, ((0, taps - head.shape[0]), (0, 0)))
    angle = np.pi / (2 * taps) * np.outer(2 * np.arange(taps) + 1, np.arange(2 * taps))
    fwd = split_two(np.concatenate((np.cos(angle), -np.sin(angle)), axis=0))
    inv = split_two(
        np.concatenate((np.cos(angle), -np.sin(angle)), axis=0).T[taps:] / taps
    )
    scalars = jnp.concatenate((lengths, jnp.reshape(span_index * row_count, (1,)).astype(jnp.int32)))
    width = math.gcd(cols, 512)
    return pl.pallas_call(
        lambda *refs: hyena_kernel(row_count, taps, *refs),
        grid=(cols // width,),
        out_shape=jax.ShapeDtypeStruct((row_count, cols), jnp.bfloat16),
        in_specs=[
            pl.BlockSpec(memory_space=pltpu.SMEM),
            pl.BlockSpec((3, row_count, width), lambda i: (0, 0, i)),
            pl.BlockSpec((taps, width), lambda i: (0, i)),
            pl.BlockSpec((taps, width), lambda i: (0, i)),
            pl.BlockSpec(fwd.shape, lambda i: (0, 0, 0)),
            pl.BlockSpec(inv.shape, lambda i: (0, 0, 0)),
        ],
        out_specs=pl.BlockSpec((row_count, width), lambda i: (0, i)),
        scratch_shapes=[
            pltpu.VMEM((row_count + taps, width), jnp.bfloat16),
            pltpu.VMEM((taps, width), jnp.float32),
        ],
        compiler_params=pltpu.CompilerParams(vmem_limit_bytes=32 * 2**20),
        cost_estimate=pl.CostEstimate(
            flops=2 * 9 * 2 * taps * taps * 3 * cols, bytes_accessed=8 * 2**20, transcendentals=0
        ),
        name="hyena",
    )(scalars, streams, carried, filt, fwd, inv)


def doc_start(pos, lens_ref):
    start = jnp.zeros_like(pos)
    end = jnp.int32(0)
    for doc in range(lens_ref.shape[0] - 1):
        end = end + lens_ref[doc]
        start = jnp.where(pos >= end, end, start)
    return start


def attend(query_ref, keys, values, biases, emit):
    rows = query_ref.shape[0]
    step = 128
    ones = jnp.ones((rows, 128), jnp.bfloat16)
    vals = [jnp.concatenate((v[...], ones), axis=1) for v in values]
    for r in range(0, rows, step):
        q = query_ref[r : r + step, :]
        scores = [
            lax.dot_general(q, k[...], (((1,), (1,)), ((), ())),
                            preferred_element_type=jnp.float32) + b[r : r + step, :]
            for k, b in zip(keys, biases)
        ]
        top = jnp.max(scores[0], axis=1, keepdims=True)
        for s in scores[1:]:
            top = jnp.maximum(top, jnp.max(s, axis=1, keepdims=True))
        acc = None
        for s, v in zip(scores, vals):
            w = jnp.exp2((s - top) * SCALE2).astype(jnp.bfloat16)
            part = jnp.dot(w, v, preferred_element_type=jnp.float32)
            acc = part if acc is None else acc + part
        total = acc[:, 128:]
        emit(r, acc[:, :128] / total, top * SCALE2 + jnp.log2(total))


def needs(lens_ref, base, rows, ahead, back):
    q_first = base + ahead * rows
    start = jnp.int32(0)
    end = jnp.int32(0)
    for doc in range(lens_ref.shape[0] - 1):
        end = end + lens_ref[doc]
        start = jnp.where(q_first >= end, end, start)
    return start < base + (1 - back) * rows


def fill_bias(lens_ref, base, rows, ref, ahead, back):
    qpos = base + ahead * rows + lax.broadcasted_iota(jnp.int32, (rows, 1), 0)
    starts = doc_start(qpos, lens_ref)
    kpos = base - back * rows + lax.broadcasted_iota(jnp.int32, (1, rows), 1)
    ref[...] = jnp.where((kpos <= qpos) & (kpos >= starts), 0.0, NEG).astype(jnp.float32)


def near_kernel(rows, lens_ref, q_ref, k_ref, v_ref, k1_ref, v1_ref, k2_ref, v2_ref, all_ref, o_ref,
                b0, b1, b2):
    span = lens_ref[lens_ref.shape[0] - 1]
    base = span * rows
    one = (span >= 1) & needs(lens_ref, base, rows, 0, 1)
    two = (span >= 2) & needs(lens_ref, base, rows, 0, 2)

    @pl.when(pl.program_id(0) == 0)
    def _():
        fill_bias(lens_ref, base, rows, b0, 0, 0)
        pl.when(one)(lambda: fill_bias(lens_ref, base, rows, b1, 0, 1))
        pl.when(two)(lambda: fill_bias(lens_ref, base, rows, b2, 0, 2))

    def emit(r, out, lse):
        o_ref[r : r + 128, :] = out.astype(jnp.bfloat16)

    pl.when(two)(
        lambda: attend(q_ref, (k_ref, k1_ref, k2_ref), (v_ref, v1_ref, v2_ref), (b0, b1, b2), emit)
    )
    pl.when(one & jnp.logical_not(two))(
        lambda: attend(q_ref, (k_ref, k1_ref), (v_ref, v1_ref), (b0, b1), emit)
    )
    pl.when(jnp.logical_not(one))(lambda: attend(q_ref, (k_ref,), (v_ref,), (b0,), emit))


def attn_kernel(rows, lens_ref, q_ref, qa_ref, qb_ref, kp_ref, vp_ref, k_ref, v_ref,
                o_ref, lse_ref, oa_ref, ob_ref, b00, b10, b01, b11, b02):
    span = lens_ref[lens_ref.shape[0] - 1]
    base = span * rows

    def reads(ahead, back):
        return needs(lens_ref, base, rows, ahead, back)

    own_prev = (span == 1) & reads(0, 1)
    a_here = ((span == 1) | (span == 2)) & reads(1, 0)
    a_prev = (span == 1) & reads(1, 1)
    b_here = (span == 1) & reads(2, 0)

    @pl.when(pl.program_id(0) == 0)
    def _():
        lse_ref[...] = jnp.zeros_like(lse_ref)

        def fill(ref, ahead, back):
            fill_bias(lens_ref, base, rows, ref, ahead, back)

        fill(b00, 0, 0)
        pl.when(own_prev)(lambda: fill(b01, 0, 1))
        pl.when(a_here)(lambda: fill(b10, 1, 0))
        pl.when(a_prev)(lambda: fill(b11, 1, 1))
        pl.when(b_here)(lambda: fill(b02, 2, 0))

    step = 128
    head_lane = lax.broadcasted_iota(jnp.int32, (step, 128), 1) == pl.program_id(0)

    def emit_own(r, out, lse):
        o_ref[r : r + step, :] = out.astype(jnp.bfloat16)
        lse_ref[r : r + step, :] = jnp.where(head_lane, lse, lse_ref[r : r + step, :])

    eye = lax.broadcasted_iota(jnp.int32, (128, 128), 0) == lax.broadcasted_iota(
        jnp.int32, (128, 128), 1
    )
    stat_iota = lax.broadcasted_iota(jnp.int32, (STAT_ROWS, 128), 0)

    def emit_to(ref):
        stats = [jnp.zeros((STAT_ROWS, 128), jnp.float32)]

        def emit(r, out, lse):
            ref[r : r + step, :] = out.astype(jnp.bfloat16)
            rest = jnp.sum(jnp.where(eye, lse, 0.0), axis=0, keepdims=True)
            for piece in range(3):
                high = rest.astype(jnp.bfloat16).astype(jnp.float32)
                stats[0] = jnp.where(stat_iota == piece * (rows // step) + r // step, high, stats[0])
                rest = rest - high
            if r + step == rows:
                ref[rows:, :] = stats[0].astype(jnp.bfloat16)

        return emit

    def empty(ref):
        ref[:rows, :] = jnp.zeros((rows, 128), jnp.bfloat16)
        ref[rows:, :] = jnp.where(stat_iota < rows // step, NEG, 0.0).astype(jnp.bfloat16)

    pl.when(own_prev)(lambda: attend(q_ref, (kp_ref, k_ref), (vp_ref, v_ref), (b01, b00), emit_own))
    pl.when(jnp.logical_not(own_prev))(lambda: attend(q_ref, (k_ref,), (v_ref,), (b00,), emit_own))
    pl.when(a_prev)(
        lambda: attend(qa_ref, (kp_ref, k_ref), (vp_ref, v_ref), (b11, b10), emit_to(oa_ref))
    )
    pl.when(a_here & jnp.logical_not(a_prev))(
        lambda: attend(qa_ref, (k_ref,), (v_ref,), (b10,), emit_to(oa_ref))
    )
    pl.when(jnp.logical_not(a_here))(lambda: empty(oa_ref))
    pl.when(b_here)(lambda: attend(qb_ref, (k_ref,), (v_ref,), (b02,), emit_to(ob_ref)))
    pl.when(jnp.logical_not(b_here))(lambda: empty(ob_ref))


def merge_kernel(rows, lens_ref, o_ref, lse_ref, ra_ref, rb_ref, all_ref, out_ref):
    span = lens_ref[lens_ref.shape[0] - 1]
    step = 128
    eye = lax.broadcasted_iota(jnp.int32, (128, 128), 0) == lax.broadcasted_iota(
        jnp.int32, (128, 128), 1
    )

    @pl.when(span < 2)
    def _():
        out_ref[...] = o_ref[...]

    @pl.when(span >= 2)
    def _():
        blocks = rows // step
        head_lane = lax.broadcasted_iota(jnp.int32, (step, 128), 1) == pl.program_id(0)
        stat_a = ra_ref[rows:, :].astype(jnp.float32)
        stat_b = rb_ref[rows:, :].astype(jnp.float32)

        def column(stats, i):
            row = (stats[i : i + 1] + stats[blocks + i : blocks + i + 1]) + stats[
                2 * blocks + i : 2 * blocks + i + 1
            ]
            return jnp.sum(jnp.where(eye, row, 0.0), axis=1, keepdims=True)

        for i in range(blocks):
            r = i * step
            own = jnp.sum(jnp.where(head_lane, lse_ref[r : r + step, :], 0.0), axis=1, keepdims=True)
            lse_a = column(stat_a, i)
            lse_b = jnp.where(span == 3, column(stat_b, i), NEG)
            top = jnp.maximum(own, jnp.maximum(lse_a, lse_b))
            w0 = jnp.exp2(own - top)
            w1 = jnp.exp2(lse_a - top)
            w2 = jnp.exp2(lse_b - top)
            total = (
                o_ref[r : r + step, :].astype(jnp.float32) * w0
                + ra_ref[r : r + step, :].astype(jnp.float32) * w1
                + rb_ref[r : r + step, :].astype(jnp.float32) * w2
            )
            out_ref[r : r + step, :] = (total / (w0 + w1 + w2)).astype(jnp.bfloat16)


def attention_fast(attn_query, attn_key, attn_value, lengths, hyena_out):
    rows, cols = attn_query.shape
    span_index = lax.axis_index("seq")
    scalars = jnp.concatenate((lengths, jnp.reshape(span_index, (1,)).astype(jnp.int32)))
    all_heads = cols // HD
    heads = all_heads * 3 // 8
    near = all_heads - 2 * heads
    width = heads * HD
    smem = pl.BlockSpec(memory_space=pltpu.SMEM)
    block = pl.BlockSpec((rows, HD), lambda h: (0, h))
    tall = pl.BlockSpec((rows + STAT_ROWS, HD), lambda h: (0, h))
    packed = pl.BlockSpec((rows, 128), lambda h: (0, 0))

    def at(offset):
        return pl.BlockSpec((rows, HD), lambda h: (0, offset + h))

    def pair(lo, hi):
        return jnp.concatenate((attn_key[:, lo:hi], attn_value[:, lo:hi]), axis=1)

    sent = []
    for c in range(2):
        qc = attn_query[:, c * width : (c + 1) * width]
        qa = lax.ppermute(qc, "seq", [(2, 1), (3, 2)])
        qb = lax.ppermute(qc, "seq", [(3, 1)])
        kv = pair(c * width, (c + 1) * width)
        sent.append((qa, qb, lax.ppermute(kv, "seq", [(0, 1)])))
    kv = pair(2 * width, cols)
    kv1 = lax.ppermute(kv, "seq", [(0, 1), (1, 2), (2, 3)])
    kv2 = lax.ppermute(kv, "seq", [(0, 2), (1, 3)])
    scalars, hyena_out = lax.optimization_barrier((scalars, hyena_out))
    outs = []
    for c in range(2):
        qa, qb, kvp = sent[c]
        whole = at(c * heads)
        own, lse, oa, ob = pl.pallas_call(
            lambda *refs: attn_kernel(rows, *refs),
            grid=(heads,),
            out_shape=(
                jax.ShapeDtypeStruct((rows, width), jnp.bfloat16),
                jax.ShapeDtypeStruct((rows, 128), jnp.float32),
                jax.ShapeDtypeStruct((rows + STAT_ROWS, width), jnp.bfloat16),
                jax.ShapeDtypeStruct((rows + STAT_ROWS, width), jnp.bfloat16),
            ),
            in_specs=[smem, whole, block, block, block, at(heads), whole, whole],
            out_specs=(block, packed, tall, tall),
            scratch_shapes=[pltpu.VMEM((rows, rows), jnp.float32)] * 5,
            compiler_params=pltpu.CompilerParams(vmem_limit_bytes=32 * 2**20),
            cost_estimate=pl.CostEstimate(
                flops=heads * 5 * rows * rows * HD * 4 * 2,
                bytes_accessed=8 * 2**20,
                transcendentals=heads * 5 * rows * rows,
            ),
            name="attend",
        )(scalars, attn_query, qa, qb, kvp, kvp, attn_key, attn_value)
        ra = lax.ppermute(oa, "seq", [(1, 2), (2, 3)])
        rb = lax.ppermute(ob, "seq", [(1, 3)])
        outs.append((own, lse, ra, rb))
        scalars, _ = lax.optimization_barrier((scalars, own))
    anywhere = pl.BlockSpec(memory_space=pl.ANY)
    whole_out = jax.ShapeDtypeStruct((rows, cols), jnp.bfloat16)
    mine = at(2 * heads)
    result = pl.pallas_call(
        lambda *refs: near_kernel(rows, *refs[:8], None, *refs[8:]),
        grid=(near,),
        out_shape=whole_out,
        in_specs=[smem, mine, mine, mine, block, at(near), block, at(near)],
        out_specs=mine,
        scratch_shapes=[pltpu.VMEM((rows, rows), jnp.float32)] * 3,
        compiler_params=pltpu.CompilerParams(vmem_limit_bytes=32 * 2**20),
        cost_estimate=pl.CostEstimate(
            flops=near * 3 * rows * rows * HD * 4 * 2,
            bytes_accessed=4 * 2**20,
            transcendentals=near * 3 * rows * rows,
        ),
        name="near",
    )(scalars, attn_query, attn_key, attn_value, kv1, kv1, kv2, kv2)
    for c in range(2):
        own, lse, ra, rb = outs[c]
        result = pl.pallas_call(
            lambda *refs: merge_kernel(rows, *refs),
            grid=(heads,),
            out_shape=whole_out,
            in_specs=[smem, block, packed, tall, tall, anywhere],
            out_specs=at(c * heads),
            input_output_aliases={5: 0},
            cost_estimate=pl.CostEstimate(
                flops=rows * width * 16, bytes_accessed=4 * 2**20, transcendentals=0
            ),
            name="merge",
        )(scalars, own, lse, ra, rb, result)
    return hyena_out, result


MESH_ID = pl.DeviceIdType.MESH
FAR = 1 << 20
CHUNK = 256


def start_at(pos, lens_ref):
    start = jnp.int32(0)
    end = jnp.int32(0)
    for doc in range(lens_ref.shape[0] - 1):
        end = end + lens_ref[doc]
        start = jnp.where(pos >= end, end, start)
    return start


def fused_kernel(
    rows, cols, lens_ref, feat_hbm, q_hbm, k_hbm, v_hbm, short_ref, med_ref, skip_ref, fwd_ref, inv_ref,
    hy_hbm, at_hbm,
    feat, qv, kv, vv, ext, halo, up_rx, st_rx, q_near, q_far, up_tx, st_tx,
    b_own, b_own_l, b_near, b_near_l, b_far, spec, fix, hy_v, at_v,
    load_sem, hy_sem, at_sem, halo_sem, near_tx, near_rx, far_tx, far_rx, up_tx_sem, up_rx_sem,
    st_tx_sem, st_rx_sem,
):
    f32, bf16 = jnp.float32, jnp.bfloat16
    heads = cols // HD
    part = rows // 3
    span = lax.axis_index("seq")
    base = span * rows
    has_left, has_right = span > 0, span < 3
    has_far, sends_far = span < 2, span > 1

    def load(index, src, dst):
        copy = pltpu.make_async_copy(src, dst, load_sem.at[index])
        copy.start()
        return copy

    tail_load = load(0, feat_hbm.at[1:3, 2 * part :, :], feat.at[1:3, 2 * part :, :])
    front_load = load(1, feat_hbm.at[1:3, : 2 * part, :], feat.at[1:3, : 2 * part, :])
    mix_load = load(2, feat_hbm.at[0], feat.at[0])
    k_load = load(3, k_hbm, kv)
    v_load = load(4, v_hbm, vv)
    q_load = load(5, q_hbm, qv)

    def lanes(h):
        return pl.ds(pl.multiple_of(h * HD, HD), HD)

    def remote(src, dst, tx, rx, to):
        return pltpu.make_async_remote_copy(
            src_ref=src, dst_ref=dst, send_sem=tx, recv_sem=rx, device_id={"seq": to},
            device_id_type=MESH_ID,
        )

    up_to = jnp.minimum(span + 1, 3)

    def near_copy(h):
        return remote(q_hbm.at[:, lanes(h)], q_near.at[h], near_tx.at[h], near_rx.at[h],
                      jnp.maximum(span - 1, 0))

    def far_copy(h):
        return remote(q_hbm.at[:part, lanes(h)], q_far.at[h], far_tx.at[h], far_rx.at[h],
                      jnp.maximum(span - 2, 0))

    def up_copy(h):
        return remote(up_tx.at[h], up_rx.at[h], up_tx_sem.at[h], up_rx_sem.at[h], up_to)

    def st_copy(h):
        return remote(st_tx.at[h], st_rx.at[h], st_tx_sem.at[h], st_rx_sem.at[h], up_to)

    halo_copy = remote(ext.at[rows : rows + part, :], halo, halo_sem.at[0], halo_sem.at[1], up_to)

    barrier = pltpu.get_barrier_semaphore()
    for away in (-2, -1, 1, 2):

        @pl.when((span + away >= 0) & (span + away < 4))
        def _(away=away):
            pl.semaphore_signal(barrier, inc=1, device_id={"seq": span + away}, device_id_type=MESH_ID)

    pl.semaphore_wait(barrier, jnp.where(has_left & has_right, 3, 2))

    def send_queries(h, carry):
        pl.when(has_left)(lambda: near_copy(h).start())
        pl.when(sends_far)(lambda: far_copy(h).start())
        return carry

    lax.fori_loop(0, heads, send_queries, 0)

    chunks = cols // CHUNK

    def chunk_cols(c):
        return pl.ds(pl.multiple_of(c * CHUNK, CHUNK), CHUNK)

    def gate(lo, hi, at):
        return (feat[1, lo:hi, at].astype(f32) * feat[2, lo:hi, at].astype(f32)).astype(bf16)

    tail_load.wait()

    def gate_tail(c, carry):
        at = chunk_cols(c)
        ext[rows : rows + part, at] = gate(2 * part, rows, at)
        ext[:part, at] = jnp.zeros((part, CHUNK), bf16)
        return carry

    lax.fori_loop(0, chunks, gate_tail, 0)
    pl.when(has_right)(lambda: halo_copy.start())

    @pl.when(jnp.logical_not(has_left))
    def _():
        def clear(h, carry):
            up_rx[h] = jnp.zeros((rows + part, HD), bf16)
            st_rx[h] = jnp.zeros((8, HD), f32)
            return carry

        lax.fori_loop(0, heads, clear, 0)

    left_q = has_left & (base - start_at(base, lens_ref) > 2 * part)
    right_q = has_right & (base + rows - start_at(base + rows, lens_ref) > 2 * part)
    fresh = has_far & right_q & (start_at(base + 2 * rows, lens_ref) < base + rows)
    slot_mine = (span > 1) & (base - rows - start_at(base, lens_ref) > 2 * part)

    def column_iota(first, count):
        return first + lax.broadcasted_iota(jnp.int32, (count, 1), 0)

    own_pos = column_iota(base, rows)
    near_pos = column_iota(base + rows, rows)
    far_pos = column_iota(base + 2 * rows, part)
    key_pos = base + lax.broadcasted_iota(jnp.int32, (1, rows), 1)
    left_pos = base - 2 * part + lax.broadcasted_iota(jnp.int32, (1, 2 * part), 1)
    no_keys = jnp.where(has_left & jnp.logical_not(left_q), 0, FAR)
    no_near = jnp.where(right_q, 0, FAR)
    no_far = jnp.where(fresh, 0, FAR)
    own_start = doc_start(own_pos, lens_ref)
    near_start = doc_start(near_pos, lens_ref) + no_near
    far_start = doc_start(far_pos, lens_ref) + no_far

    def bias(ok):
        return jnp.where(ok, 0.0, NEG).astype(f32)

    b_own[...] = bias((key_pos <= own_pos) & (key_pos >= own_start))
    b_own_l[...] = bias(left_pos >= own_start + no_keys)
    b_near[...] = bias(key_pos >= near_start)
    b_near_l[...] = bias(left_pos >= near_start + no_keys)
    b_far[...] = bias(key_pos >= far_start)

    def dot(x, y):
        return jnp.dot(x, y, preferred_element_type=f32)

    first_cut = jnp.int32(FAR)
    last_cut = jnp.int32(-1)
    end = jnp.int32(0)
    for doc in range(lens_ref.shape[0] - 1):
        end = end + lens_ref[doc]
        first_cut = jnp.where((end > base) & (end < first_cut), end, first_cut)
        last_cut = jnp.where((end < base + rows) & (end > last_cut), end, last_cut)
    cuts = []
    for cut in (first_cut, last_cut):
        valid = (cut > base) & (cut < base + rows)
        block = jnp.where(valid, lax.div(jnp.where(valid, cut - base, 0), part), 0)
        cuts.append((jnp.where(valid, cut, FAR), block))
    win_iota = lax.broadcasted_iota(jnp.int32, (2 * part, 1), 0)
    out_iota = lax.broadcasted_iota(jnp.int32, (part, 1), 0)

    def transform(window, first_pos, from_pos, spec_r, spec_i):
        window = jnp.where(win_iota + first_pos >= from_pos, window, jnp.zeros_like(window))
        return spread(window, spec_r, spec_i)

    def spread(window, spec_r, spec_i):
        wave = dot(fwd_ref[0], window)
        wave_r, wave_i = wave[:part], wave[part:]
        prod = jnp.concatenate(
            (
                (wave_r * spec_r - wave_i * spec_i).astype(bf16),
                (wave_r * spec_i + wave_i * spec_r).astype(bf16),
            ),
            axis=0,
        )
        return dot(inv_ref[0], prod)

    def finish(block, at, sums, fixes):
        for (cut, cut_block), fixed in zip(cuts, fixes):
            cut_from = jnp.where(cut_block == block, cut, FAR)
            sums = jnp.where(out_iota + (base + block * part) >= cut_from, fixed, sums)
        r0 = block * part
        hy_v[r0 : r0 + part, at] = (feat[0, r0 : r0 + part, at].astype(f32) * sums).astype(bf16)

    front_load.wait()
    mix_load.wait()

    def hyena_main(c, carry):
        at = chunk_cols(c)
        ext[part:rows, at] = gate(0, 2 * part, at)
        short = short_ref[:, at]
        head = jnp.concatenate(
            (short[:1] + skip_ref[:, at], short[1:], jnp.zeros((8 - short.shape[0], CHUNK), f32)), axis=0
        )
        filt = jnp.concatenate((med_ref[:8, at] + head, med_ref[8:, at]), axis=0)
        filt_hi = filt.astype(bf16)
        filt_lo = (filt - filt_hi.astype(f32)).astype(bf16)
        both = (
            dot(fwd_ref[0, :, :part], filt_hi)
            + dot(fwd_ref[1, :, :part], filt_hi)
            + dot(fwd_ref[0, :, :part], filt_lo)
        )
        spec[:, at] = both
        spec_r, spec_i = both[:part], both[part:]
        fixes = []
        for index, (cut, cut_block) in enumerate(cuts):
            window = jnp.zeros((2 * part, CHUNK), bf16)
            for block in range(3):
                r0 = block * part
                cut_from = jnp.where(cut_block == block, cut, FAR)
                window = jnp.where(
                    win_iota + (base + r0 - part) >= cut_from, ext[r0 : r0 + 2 * part, at], window
                )
            sums = spread(window, spec_r, spec_i)
            fix[index, :, at] = sums
            fixes.append(sums)
        for block in (1, 2):
            r0 = block * part
            sums = transform(
                ext[r0 : r0 + 2 * part, at], base + r0 - part, start_at(base + r0, lens_ref), spec_r, spec_i
            )
            finish(block, at, sums, fixes)
        return carry

    lax.fori_loop(0, chunks, hyena_main, 0)
    hy_late = pltpu.make_async_copy(hy_v.at[part:, :], hy_hbm.at[part:, :], hy_sem.at[0])
    hy_late.start()
    hy_first = pltpu.make_async_copy(hy_v.at[:part, :], hy_hbm.at[:part, :], hy_sem.at[1])

    def hyena_first():
        pl.when(has_left)(lambda: halo_copy.wait_recv())

        def one(c, carry):
            at = chunk_cols(c)
            window = jnp.concatenate((halo[:, at], ext[part : 2 * part, at]), axis=0)
            sums = transform(
                window, base - part, start_at(base, lens_ref), spec[:part, at], spec[part:, at]
            )
            finish(0, at, sums, [fix[i, :, at] for i in range(2)])
            return carry

        lax.fori_loop(0, chunks, one, 0)
        hy_first.start()

    k_load.wait()
    v_load.wait()
    q_load.wait()
    ones = jnp.ones((rows, HD), bf16)
    eye = lax.broadcasted_iota(jnp.int32, (part, HD), 0) == lax.broadcasted_iota(jnp.int32, (part, HD), 1)
    stat_iota = lax.broadcasted_iota(jnp.int32, (8, HD), 0)
    left_off = jnp.where(left_q, 0.0, NEG)
    slot_off = jnp.where(slot_mine, 0.0, NEG)

    def attend_to(q, keys, values, biases):
        scores = [
            lax.dot_general(q, k, (((1,), (1,)), ((), ())), preferred_element_type=f32) + b
            for k, b in zip(keys, biases)
        ]
        top = jnp.max(scores[0], axis=1, keepdims=True)
        for s in scores[1:]:
            top = jnp.maximum(top, jnp.max(s, axis=1, keepdims=True))
        acc = None
        for s, v in zip(scores, values):
            w = jnp.exp2((s - top) * SCALE2).astype(bf16)
            term = dot(w, v)
            acc = term if acc is None else acc + term
        return acc[:, :HD], acc[:, HD:], top * SCALE2

    def head_step(h, carry):
        at = lanes(h)
        pl.when(h == 3)(hyena_first)

        @pl.when(has_left)
        def _():
            up_copy(h).wait_recv()
            st_copy(h).wait_recv()

        k = kv[:, at]
        v = vv[:, at]
        k_left = up_rx[h, : 2 * part, :]
        v_ones = jnp.concatenate((v, ones), axis=1)
        v_left = jnp.concatenate((up_rx[h, 2 * part :, :], ones[: 2 * part]), axis=1)

        @pl.when(has_right)
        def _():
            near_copy(h).wait_recv()
            tails = (k[part : 2 * part], k[2 * part :], v[part : 2 * part], v[2 * part :])
            stats = jnp.zeros((8, HD), f32)

            def give(i, out):
                up_tx[h, i * part : (i + 1) * part, :] = jnp.where(
                    right_q, out, tails[i].astype(f32)
                ).astype(bf16)

            def to_row(lse):
                return jnp.sum(jnp.where(eye, lse, 0.0), axis=0, keepdims=True)

            for i in range(3):
                r0 = i * part
                acc, total, top = attend_to(
                    q_near[h, r0 : r0 + part, :],
                    (k, k_left),
                    (v_ones, v_left),
                    (b_near[r0 : r0 + part, :], b_near_l[r0 : r0 + part, :]),
                )
                give(i, acc / total)
                stats = jnp.where(stat_iota == i, to_row(top + jnp.log2(total)), stats)
            passed = up_rx[h, rows:, :].astype(f32)
            passed_stat = st_rx[h]

            @pl.when(has_far)
            def _():
                far_copy(h).wait_recv()
                acc, total, top = attend_to(q_far[h], (k,), (v_ones,), (b_far[...],))
                give(3, jnp.where(fresh, acc / total, passed))
                lse = to_row(top + jnp.log2(total))
                st_tx[h] = jnp.where(
                    stat_iota == 3, jnp.where(fresh, lse, passed_stat[3:4]), stats
                )

            @pl.when(jnp.logical_not(has_far))
            def _():
                give(3, passed)
                st_tx[h] = jnp.where(stat_iota == 3, passed_stat[3:4], stats)

            up_copy(h).start()
            st_copy(h).start()

        stats_in = st_rx[h]

        def column(i):
            return jnp.sum(jnp.where(eye, stats_in[i : i + 1], 0.0), axis=1, keepdims=True)

        for i in range(3):
            r0 = i * part
            r1 = r0 + part
            acc, total, top = attend_to(
                qv[r0:r1, at],
                (k[:r1], k_left),
                (v_ones[:r1], v_left),
                (b_own[r0:r1, :r1], b_own_l[r0:r1, :]),
            )
            lse = column(i) + left_off
            best = jnp.maximum(top, lse)
            if i == 0:
                slot_lse = column(3) + slot_off
                best = jnp.maximum(best, slot_lse)
            w0 = jnp.exp2(top - best)
            w1 = jnp.exp2(lse - best)
            mixed = acc * w0 + up_rx[h, r0:r1, :].astype(f32) * w1
            norm = total * w0 + w1
            if i == 0:
                w2 = jnp.exp2(slot_lse - best)
                mixed = mixed + up_rx[h, rows:, :].astype(f32) * w2
                norm = norm + w2
            at_v[r0:r1, at] = (mixed / norm).astype(bf16)
        pltpu.make_async_copy(at_v.at[:, at], at_hbm.at[:, at], at_sem.at[h]).start()
        return carry

    lax.fori_loop(0, heads, head_step, 0)

    def drain(h, carry):
        at = lanes(h)
        pltpu.make_async_copy(at_v.at[:, at], at_hbm.at[:, at], at_sem.at[h]).wait()

        @pl.when(has_right)
        def _():
            up_copy(h).wait_send()
            st_copy(h).wait_send()

        pl.when(has_left)(lambda: near_copy(h).wait_send())
        pl.when(sends_far)(lambda: far_copy(h).wait_send())
        return carry

    lax.fori_loop(0, heads, drain, 0)
    pl.when(has_right)(lambda: halo_copy.wait_send())
    hy_late.wait()
    hy_first.wait()


def fused(features, short_filter, medium_filter, skip_gain, attn_query, attn_key, attn_value, lengths):
    rows, cols = attn_query.shape
    part = rows // 3
    heads = cols // HD
    angle = np.pi / (2 * part) * np.outer(2 * np.arange(part) + 1, np.arange(2 * part))
    wave = np.concatenate((np.cos(angle), -np.sin(angle)), axis=0)
    fwd = split_two(wave)
    inv = split_two(wave.T[part:] / part)
    anywhere = pl.BlockSpec(memory_space=pl.ANY)
    vmem = pl.BlockSpec(memory_space=pltpu.VMEM)
    smem = pl.BlockSpec(memory_space=pltpu.SMEM)
    out = jax.ShapeDtypeStruct((rows, cols), jnp.bfloat16)

    def buf(*shape):
        return pltpu.VMEM(shape, jnp.bfloat16)

    def wide(*shape):
        return pltpu.VMEM(shape, jnp.float32)

    each = pltpu.SemaphoreType.DMA((heads,))
    return pl.pallas_call(
        lambda *refs: fused_kernel(rows, cols, *refs),
        out_shape=(out, out),
        in_specs=[smem] + [anywhere] * 4 + [vmem] * 5,
        out_specs=(anywhere, anywhere),
        scratch_shapes=[
            buf(3, rows, cols), buf(rows, cols), buf(rows, cols), buf(rows, cols),
            buf(rows + part, cols), buf(part, cols),
            buf(heads, rows + part, HD), wide(heads, 8, HD),
            buf(heads, rows, HD), buf(heads, part, HD),
            buf(heads, rows + part, HD), wide(heads, 8, HD),
            wide(rows, rows), wide(rows, 2 * part), wide(rows, rows), wide(rows, 2 * part),
            wide(part, rows),
            wide(2 * part, cols), wide(2, part, cols),
            buf(rows, cols), buf(rows, cols),
            pltpu.SemaphoreType.DMA((6,)), pltpu.SemaphoreType.DMA((2,)), each,
            pltpu.SemaphoreType.DMA((2,)),
        ] + [each] * 8,
        compiler_params=pltpu.CompilerParams(
            collective_id=0, has_side_effects=True, vmem_limit_bytes=48 * 2**20
        ),
        cost_estimate=pl.CostEstimate(
            flops=heads * 32 * part * part * HD * 4, bytes_accessed=16 * 2**20,
            transcendentals=heads * 32 * part * part,
        ),
        name="fused",
    )(
        lengths, features.transpose(1, 0, 2), attn_query, attn_key, attn_value,
        short_filter, medium_filter, skip_gain[None, :], fwd, inv,
    )


def local(
    features, short_filter, medium_filter, skip_gain, attn_query, attn_key, attn_value, lengths
):
    rows, cols = attn_query.shape
    spans = lax.axis_size("seq")
    taps = medium_filter.shape[0]
    if spans == 4 and rows == 3 * taps and taps == HD and cols % CHUNK == 0 and short_filter.shape[0] < 8:
        return fused(
            features, short_filter, medium_filter, skip_gain, attn_query, attn_key, attn_value, lengths
        )
    if cols % 128 == 0 and taps % 128 == 0 and rows % taps == 0:
        hyena = hyena_fast
    else:
        hyena = hyena_mix
    hyena_out = hyena(features, short_filter, medium_filter, skip_gain, lengths)
    if spans == 4 and rows % 128 == 0 and rows <= 640 and cols % (8 * HD) == 0:
        return attention_fast(attn_query, attn_key, attn_value, lengths, hyena_out)
    return (hyena_out, attention_mix(attn_query, attn_key, attn_value, lengths))


def solution(mesh):
    in_specs = (
        P(("groups", "seq"), None, ("tensor", "sub")),
        P(None, ("tensor", "sub")),
        P(None, ("tensor", "sub")),
        P(("tensor", "sub")),
        P(("groups", "seq"), ("tensor", "sub")),
        P(("groups", "seq"), ("tensor", "sub")),
        P(("groups", "seq"), ("tensor", "sub")),
        P("groups"),
    )
    out_specs = (P(("groups", "seq"), ("tensor", "sub")), P(("groups", "seq"), ("tensor", "sub")))
    return jax.shard_map(local, mesh=mesh, in_specs=in_specs, out_specs=out_specs, check_vma=False)
```

```python
import math

import jax
import jax.numpy as jnp
import numpy as np
from jax import lax
from jax.experimental import pallas as pl
from jax.experimental.pallas import tpu as pltpu
from jax.sharding import PartitionSpec as P

HD = 128


def passed_along(value, axis, by):
    length = lax.axis_size(axis)
    pairs = [(i, i + by) for i in range(length) if 0 <= i + by < length]
    return lax.ppermute(value, axis, pairs)


def doc_of(positions, lengths):
    doc_ends = jnp.cumsum(lengths, dtype=jnp.int32)
    return jnp.sum(
        (positions[:, None] >= doc_ends[None, :]).astype(jnp.int32), axis=1, dtype=jnp.int32
    )


def hyena_mix(features, short_filter, medium_filter, skip_gain, lengths):
    row_count = features.shape[0]
    medium_taps = medium_filter.shape[0]
    rim_rows = medium_taps - 1
    span_index = lax.axis_index("seq")
    queries = features[:, 0].astype(jnp.float32)
    gated = (features[:, 1].astype(jnp.float32) * features[:, 2].astype(jnp.float32)).astype(
        jnp.bfloat16
    )
    gated = lax.optimization_barrier(gated)
    carried = passed_along(gated[row_count - rim_rows :], "seq", 1)
    extended = jnp.concatenate((carried, gated), axis=0)
    ext_positions = (
        span_index * row_count - rim_rows + jnp.arange(row_count + rim_rows, dtype=jnp.int32)
    )
    ext_docs = doc_of(ext_positions, lengths)
    ext_live = ext_positions >= 0
    own_docs = ext_docs[rim_rows:]

    def tap_term(tap_index, filter_bank):
        first_row = rim_rows - tap_index
        window = lax.dynamic_slice_in_dim(extended, first_row, row_count, 0).astype(jnp.float32)
        same_doc = lax.dynamic_slice_in_dim(ext_docs, first_row, row_count, 0) == own_docs
        live_mask = lax.dynamic_slice_in_dim(ext_live, first_row, row_count, 0)
        keep_mask = (same_doc & live_mask).astype(jnp.float32)[:, None]
        taps = lax.dynamic_index_in_dim(filter_bank, tap_index, 0, keepdims=False)
        return taps[None, :] * window * keep_mask

    short_sum = jnp.zeros(gated.shape, jnp.float32)
    for tap_index in range(short_filter.shape[0]):
        short_sum = short_sum + tap_term(tap_index, short_filter)

    def tap_block(block_index, partial_value):
        for offset in range(8):
            partial_value = partial_value + tap_term(block_index * 8 + offset, medium_filter)
        return partial_value

    medium_sum = lax.fori_loop(0, medium_taps // 8, tap_block, jnp.zeros(gated.shape, jnp.float32))
    mixed = queries * (short_sum + medium_sum + skip_gain[None, :] * gated.astype(jnp.float32))
    return mixed.astype(jnp.bfloat16)


def attention_mix(attn_query, attn_key, attn_value, lengths):
    row_count, col_count = attn_query.shape
    heads_here = col_count // HD
    span_index = lax.axis_index("seq")
    query_positions = span_index * row_count + jnp.arange(row_count, dtype=jnp.int32)
    query_docs = doc_of(query_positions, lengths)
    query_heads = attn_query.reshape(row_count, heads_here, HD)
    score_scale = HD ** (-0.5)
    last_query = query_positions[row_count - 1]
    first_query_doc = query_docs[0]

    def absorb(state_now, key_block, value_block, first_row):
        key_count = key_block.shape[0]
        last_key = first_row + key_count - 1
        last_key_doc = doc_of(jnp.reshape(last_key, (1,)), lengths)[0]
        masked_out = (first_row > last_query) | (last_key < 0) | (last_key_doc < first_query_doc)

        def compute(state_in):
            running_max, running_total, running_sum = state_in
            key_heads = key_block.reshape(key_count, heads_here, HD)
            value_heads = value_block.reshape(key_count, heads_here, HD)
            scores = (
                jnp.einsum(
                    "rhd,nhd->hrn", query_heads, key_heads, preferred_element_type=jnp.float32
                )
                * score_scale
            )
            key_positions = first_row + jnp.arange(key_count, dtype=jnp.int32)
            key_docs = doc_of(key_positions, lengths)
            allowed = (
                (key_positions[None, :] <= query_positions[:, None])
                & (key_docs[None, :] == query_docs[:, None])
                & (key_positions >= 0)[None, :]
            )
            masked = jnp.where(allowed[None], scores, -1e30)
            new_max = jnp.maximum(running_max, jnp.max(masked, axis=2))
            rescale = jnp.exp(running_max - new_max)
            weights = jnp.where(allowed[None], jnp.exp(scores - new_max[:, :, None]), 0.0)
            new_total = running_total * rescale + jnp.sum(weights, axis=2)
            product = jnp.einsum(
                "hrn,nhd->hrd",
                weights.astype(jnp.bfloat16),
                value_heads,
                preferred_element_type=jnp.float32,
            )
            new_sum = running_sum * rescale[:, :, None] + product
            return (new_max, new_total, new_sum)

        def keep_state(state_in):
            return state_in

        return lax.cond(masked_out, keep_state, compute, state_now)

    def fold_keys(state_now, pieces, first_row):
        key_all, value_all = pieces
        key_count = key_all.shape[0]
        block_rows = math.gcd(key_count, 1536)
        if block_rows == key_count:
            return absorb(state_now, key_all, value_all, first_row)
        block_total = key_count // block_rows
        key_blocks = key_all.reshape(block_total, block_rows, col_count)
        value_blocks = value_all.reshape(block_total, block_rows, col_count)

        def scan_step(state_inner, block_items):
            key_block, value_block, block_index = block_items
            return (
                absorb(state_inner, key_block, value_block, first_row + block_index * block_rows),
                None,
            )

        state_now, unused = lax.scan(
            scan_step,
            state_now,
            (key_blocks, value_blocks, jnp.arange(block_total, dtype=jnp.int32)),
        )
        return state_now

    initial = (
        jnp.full((heads_here, row_count), -1e30, jnp.float32),
        jnp.zeros((heads_here, row_count), jnp.float32),
        jnp.zeros((heads_here, row_count, HD), jnp.float32),
    )
    state_now = fold_keys(
        initial,
        (
            lax.all_gather(attn_key, "seq", axis=0, tiled=True),
            lax.all_gather(attn_value, "seq", axis=0, tiled=True),
        ),
        jnp.int32(0),
    )
    running_max, running_total, running_sum = state_now
    result = running_sum / running_total[:, :, None]
    return result.transpose(1, 0, 2).reshape(row_count, col_count).astype(jnp.bfloat16)


LOG2E = 1.4426950408889634
LN2 = 0.6931471805599453
SCALE2 = HD**-0.5 * LOG2E
NEG = -1e30
STAT_ROWS = 16


def hyena_kernel(row_count, taps, lens_ref, feat_ref, rim_ref, filt_ref, fwd_ref, inv_ref, out_ref,
                 ext_ref, sum_ref):
    base = lens_ref[lens_ref.shape[0] - 1]
    ext_ref[:taps, :] = rim_ref[...]
    ext_ref[taps:, :] = (
        feat_ref[1].astype(jnp.float32) * feat_ref[2].astype(jnp.float32)
    ).astype(jnp.bfloat16)

    def dot(x, y):
        return jnp.dot(x, y, preferred_element_type=jnp.float32)

    filt = filt_ref[...]
    filt_hi = filt.astype(jnp.bfloat16)
    filt_lo = (filt - filt_hi.astype(jnp.float32)).astype(jnp.bfloat16)
    spec = (
        dot(fwd_ref[0, :, :taps], filt_hi)
        + dot(fwd_ref[1, :, :taps], filt_hi)
        + dot(fwd_ref[0, :, :taps], filt_lo)
    )
    spec_r, spec_i = spec[:taps], spec[taps:]
    win_iota = lax.broadcasted_iota(jnp.int32, (2 * taps, 1), 0)
    out_iota = lax.broadcasted_iota(jnp.int32, (taps, 1), 0)
    for block in range(row_count // taps):
        r0 = block * taps
        start = jnp.int32(0)
        for doc in range(lens_ref.shape[0] - 1):
            end = start + lens_ref[doc]
            first, last = start - base, end - base

            @pl.when((last > r0) & (first < r0 + taps) & (first < last))
            def _(first=first):
                window = ext_ref[r0 : r0 + 2 * taps, :]
                window = jnp.where(win_iota + (r0 - taps) >= first, window, jnp.zeros_like(window))
                wave = dot(fwd_ref[0], window) + dot(fwd_ref[1], window)
                wave_r, wave_i = wave[:taps], wave[taps:]
                prod = jnp.concatenate(
                    (
                        (wave_r * spec_r - wave_i * spec_i).astype(jnp.bfloat16),
                        (wave_r * spec_i + wave_i * spec_r).astype(jnp.bfloat16),
                    ),
                    axis=0,
                )
                sums = dot(inv_ref[0], prod) + dot(inv_ref[1], prod)
                sum_ref[...] = jnp.where(out_iota + r0 >= first, sums, sum_ref[...])

            start = end
        out_ref[r0 : r0 + taps, :] = (
            feat_ref[0, r0 : r0 + taps, :].astype(jnp.float32) * sum_ref[...]
        ).astype(out_ref.dtype)


def split_two(matrix):
    high = matrix.astype(jnp.bfloat16)
    low = (matrix - high.astype(np.float64)).astype(jnp.bfloat16)
    return np.stack((high, low))


def hyena_fast(features, short_filter, medium_filter, skip_gain, lengths):
    row_count, _, cols = features.shape
    taps = medium_filter.shape[0]
    span_index = lax.axis_index("seq")
    streams = features.transpose(1, 0, 2)
    tail = streams[:, row_count - taps :]
    gated_tail = (tail[1].astype(jnp.float32) * tail[2].astype(jnp.float32)).astype(jnp.bfloat16)
    carried = passed_along(gated_tail, "seq", 1)
    head = jnp.concatenate((short_filter[:1] + skip_gain[None, :], short_filter[1:]), axis=0)
    filt = medium_filter + jnp.pad(head, ((0, taps - head.shape[0]), (0, 0)))
    angle = np.pi / (2 * taps) * np.outer(2 * np.arange(taps) + 1, np.arange(2 * taps))
    fwd = split_two(np.concatenate((np.cos(angle), -np.sin(angle)), axis=0))
    inv = split_two(
        np.concatenate((np.cos(angle), -np.sin(angle)), axis=0).T[taps:] / taps
    )
    scalars = jnp.concatenate((lengths, jnp.reshape(span_index * row_count, (1,)).astype(jnp.int32)))
    width = math.gcd(cols, 512)
    return pl.pallas_call(
        lambda *refs: hyena_kernel(row_count, taps, *refs),
        grid=(cols // width,),
        out_shape=jax.ShapeDtypeStruct((row_count, cols), jnp.bfloat16),
        in_specs=[
            pl.BlockSpec(memory_space=pltpu.SMEM),
            pl.BlockSpec((3, row_count, width), lambda i: (0, 0, i)),
            pl.BlockSpec((taps, width), lambda i: (0, i)),
            pl.BlockSpec((taps, width), lambda i: (0, i)),
            pl.BlockSpec(fwd.shape, lambda i: (0, 0, 0)),
            pl.BlockSpec(inv.shape, lambda i: (0, 0, 0)),
        ],
        out_specs=pl.BlockSpec((row_count, width), lambda i: (0, i)),
        scratch_shapes=[
            pltpu.VMEM((row_count + taps, width), jnp.bfloat16),
            pltpu.VMEM((taps, width), jnp.float32),
        ],
        compiler_params=pltpu.CompilerParams(vmem_limit_bytes=32 * 2**20),
        cost_estimate=pl.CostEstimate(
            flops=2 * 9 * 2 * taps * taps * 3 * cols, bytes_accessed=8 * 2**20, transcendentals=0
        ),
        name="hyena",
    )(scalars, streams, carried, filt, fwd, inv)


def doc_start(pos, lens_ref):
    start = jnp.zeros_like(pos)
    end = jnp.int32(0)
    for doc in range(lens_ref.shape[0] - 1):
        end = end + lens_ref[doc]
        start = jnp.where(pos >= end, end, start)
    return start


def attend(query_ref, keys, values, biases, emit):
    rows = query_ref.shape[0]
    step = 128
    ones = jnp.ones((rows, 128), jnp.bfloat16)
    vals = [jnp.concatenate((v[...], ones), axis=1) for v in values]
    for r in range(0, rows, step):
        q = query_ref[r : r + step, :]
        scores = [
            lax.dot_general(q, k[...], (((1,), (1,)), ((), ())),
                            preferred_element_type=jnp.float32) + b[r : r + step, :]
            for k, b in zip(keys, biases)
        ]
        top = jnp.max(scores[0], axis=1, keepdims=True)
        for s in scores[1:]:
            top = jnp.maximum(top, jnp.max(s, axis=1, keepdims=True))
        acc = None
        for s, v in zip(scores, vals):
            w = jnp.exp2((s - top) * SCALE2).astype(jnp.bfloat16)
            part = jnp.dot(w, v, preferred_element_type=jnp.float32)
            acc = part if acc is None else acc + part
        total = acc[:, 128:]
        emit(r, acc[:, :128] / total, top * SCALE2 + jnp.log2(total))


def needs(lens_ref, base, rows, ahead, back):
    q_first = base + ahead * rows
    start = jnp.int32(0)
    end = jnp.int32(0)
    for doc in range(lens_ref.shape[0] - 1):
        end = end + lens_ref[doc]
        start = jnp.where(q_first >= end, end, start)
    return start < base + (1 - back) * rows


def fill_bias(lens_ref, base, rows, ref, ahead, back):
    qpos = base + ahead * rows + lax.broadcasted_iota(jnp.int32, (rows, 1), 0)
    starts = doc_start(qpos, lens_ref)
    kpos = base - back * rows + lax.broadcasted_iota(jnp.int32, (1, rows), 1)
    ref[...] = jnp.where((kpos <= qpos) & (kpos >= starts), 0.0, NEG).astype(jnp.float32)


def near_kernel(rows, lens_ref, q_ref, k_ref, v_ref, k1_ref, v1_ref, k2_ref, v2_ref, all_ref, o_ref,
                b0, b1, b2):
    span = lens_ref[lens_ref.shape[0] - 1]
    base = span * rows
    one = (span >= 1) & needs(lens_ref, base, rows, 0, 1)
    two = (span >= 2) & needs(lens_ref, base, rows, 0, 2)

    @pl.when(pl.program_id(0) == 0)
    def _():
        fill_bias(lens_ref, base, rows, b0, 0, 0)
        pl.when(one)(lambda: fill_bias(lens_ref, base, rows, b1, 0, 1))
        pl.when(two)(lambda: fill_bias(lens_ref, base, rows, b2, 0, 2))

    def emit(r, out, lse):
        o_ref[r : r + 128, :] = out.astype(jnp.bfloat16)

    pl.when(two)(
        lambda: attend(q_ref, (k_ref, k1_ref, k2_ref), (v_ref, v1_ref, v2_ref), (b0, b1, b2), emit)
    )
    pl.when(one & jnp.logical_not(two))(
        lambda: attend(q_ref, (k_ref, k1_ref), (v_ref, v1_ref), (b0, b1), emit)
    )
    pl.when(jnp.logical_not(one))(lambda: attend(q_ref, (k_ref,), (v_ref,), (b0,), emit))


def attn_kernel(rows, lens_ref, q_ref, qa_ref, qb_ref, kp_ref, vp_ref, k_ref, v_ref,
                o_ref, lse_ref, oa_ref, ob_ref, b00, b10, b01, b11, b02):
    span = lens_ref[lens_ref.shape[0] - 1]
    base = span * rows

    def reads(ahead, back):
        return needs(lens_ref, base, rows, ahead, back)

    own_prev = (span == 1) & reads(0, 1)
    a_here = ((span == 1) | (span == 2)) & reads(1, 0)
    a_prev = (span == 1) & reads(1, 1)
    b_here = (span == 1) & reads(2, 0)

    @pl.when(pl.program_id(0) == 0)
    def _():
        lse_ref[...] = jnp.zeros_like(lse_ref)

        def fill(ref, ahead, back):
            fill_bias(lens_ref, base, rows, ref, ahead, back)

        fill(b00, 0, 0)
        pl.when(own_prev)(lambda: fill(b01, 0, 1))
        pl.when(a_here)(lambda: fill(b10, 1, 0))
        pl.when(a_prev)(lambda: fill(b11, 1, 1))
        pl.when(b_here)(lambda: fill(b02, 2, 0))

    step = 128
    head_lane = lax.broadcasted_iota(jnp.int32, (step, 128), 1) == pl.program_id(0)

    def emit_own(r, out, lse):
        o_ref[r : r + step, :] = out.astype(jnp.bfloat16)
        lse_ref[r : r + step, :] = jnp.where(head_lane, lse, lse_ref[r : r + step, :])

    eye = lax.broadcasted_iota(jnp.int32, (128, 128), 0) == lax.broadcasted_iota(
        jnp.int32, (128, 128), 1
    )
    stat_iota = lax.broadcasted_iota(jnp.int32, (STAT_ROWS, 128), 0)

    def emit_to(ref):
        stats = [jnp.zeros((STAT_ROWS, 128), jnp.float32)]

        def emit(r, out, lse):
            ref[r : r + step, :] = out.astype(jnp.bfloat16)
            rest = jnp.sum(jnp.where(eye, lse, 0.0), axis=0, keepdims=True)
            for piece in range(3):
                high = rest.astype(jnp.bfloat16).astype(jnp.float32)
                stats[0] = jnp.where(stat_iota == piece * (rows // step) + r // step, high, stats[0])
                rest = rest - high
            if r + step == rows:
                ref[rows:, :] = stats[0].astype(jnp.bfloat16)

        return emit

    def empty(ref):
        ref[:rows, :] = jnp.zeros((rows, 128), jnp.bfloat16)
        ref[rows:, :] = jnp.where(stat_iota < rows // step, NEG, 0.0).astype(jnp.bfloat16)

    pl.when(own_prev)(lambda: attend(q_ref, (kp_ref, k_ref), (vp_ref, v_ref), (b01, b00), emit_own))
    pl.when(jnp.logical_not(own_prev))(lambda: attend(q_ref, (k_ref,), (v_ref,), (b00,), emit_own))
    pl.when(a_prev)(
        lambda: attend(qa_ref, (kp_ref, k_ref), (vp_ref, v_ref), (b11, b10), emit_to(oa_ref))
    )
    pl.when(a_here & jnp.logical_not(a_prev))(
        lambda: attend(qa_ref, (k_ref,), (v_ref,), (b10,), emit_to(oa_ref))
    )
    pl.when(jnp.logical_not(a_here))(lambda: empty(oa_ref))
    pl.when(b_here)(lambda: attend(qb_ref, (k_ref,), (v_ref,), (b02,), emit_to(ob_ref)))
    pl.when(jnp.logical_not(b_here))(lambda: empty(ob_ref))


def merge_kernel(rows, lens_ref, o_ref, lse_ref, ra_ref, rb_ref, all_ref, out_ref):
    span = lens_ref[lens_ref.shape[0] - 1]
    step = 128
    eye = lax.broadcasted_iota(jnp.int32, (128, 128), 0) == lax.broadcasted_iota(
        jnp.int32, (128, 128), 1
    )

    @pl.when(span < 2)
    def _():
        out_ref[...] = o_ref[...]

    @pl.when(span >= 2)
    def _():
        blocks = rows // step
        head_lane = lax.broadcasted_iota(jnp.int32, (step, 128), 1) == pl.program_id(0)
        stat_a = ra_ref[rows:, :].astype(jnp.float32)
        stat_b = rb_ref[rows:, :].astype(jnp.float32)

        def column(stats, i):
            row = (stats[i : i + 1] + stats[blocks + i : blocks + i + 1]) + stats[
                2 * blocks + i : 2 * blocks + i + 1
            ]
            return jnp.sum(jnp.where(eye, row, 0.0), axis=1, keepdims=True)

        for i in range(blocks):
            r = i * step
            own = jnp.sum(jnp.where(head_lane, lse_ref[r : r + step, :], 0.0), axis=1, keepdims=True)
            lse_a = column(stat_a, i)
            lse_b = jnp.where(span == 3, column(stat_b, i), NEG)
            top = jnp.maximum(own, jnp.maximum(lse_a, lse_b))
            w0 = jnp.exp2(own - top)
            w1 = jnp.exp2(lse_a - top)
            w2 = jnp.exp2(lse_b - top)
            total = (
                o_ref[r : r + step, :].astype(jnp.float32) * w0
                + ra_ref[r : r + step, :].astype(jnp.float32) * w1
                + rb_ref[r : r + step, :].astype(jnp.float32) * w2
            )
            out_ref[r : r + step, :] = (total / (w0 + w1 + w2)).astype(jnp.bfloat16)


def attention_fast(attn_query, attn_key, attn_value, lengths, hyena_out):
    rows, cols = attn_query.shape
    span_index = lax.axis_index("seq")
    scalars = jnp.concatenate((lengths, jnp.reshape(span_index, (1,)).astype(jnp.int32)))
    all_heads = cols // HD
    heads = all_heads * 3 // 8
    near = all_heads - 2 * heads
    width = heads * HD
    smem = pl.BlockSpec(memory_space=pltpu.SMEM)
    block = pl.BlockSpec((rows, HD), lambda h: (0, h))
    tall = pl.BlockSpec((rows + STAT_ROWS, HD), lambda h: (0, h))
    packed = pl.BlockSpec((rows, 128), lambda h: (0, 0))

    def at(offset):
        return pl.BlockSpec((rows, HD), lambda h: (0, offset + h))

    def pair(lo, hi):
        return jnp.concatenate((attn_key[:, lo:hi], attn_value[:, lo:hi]), axis=1)

    sent = []
    for c in range(2):
        qc = attn_query[:, c * width : (c + 1) * width]
        qa = lax.ppermute(qc, "seq", [(2, 1), (3, 2)])
        qb = lax.ppermute(qc, "seq", [(3, 1)])
        kv = pair(c * width, (c + 1) * width)
        sent.append((qa, qb, lax.ppermute(kv, "seq", [(0, 1)])))
    kv = pair(2 * width, cols)
    kv1 = lax.ppermute(kv, "seq", [(0, 1), (1, 2), (2, 3)])
    kv2 = lax.ppermute(kv, "seq", [(0, 2), (1, 3)])
    scalars, hyena_out = lax.optimization_barrier((scalars, hyena_out))
    outs = []
    for c in range(2):
        qa, qb, kvp = sent[c]
        whole = at(c * heads)
        own, lse, oa, ob = pl.pallas_call(
            lambda *refs: attn_kernel(rows, *refs),
            grid=(heads,),
            out_shape=(
                jax.ShapeDtypeStruct((rows, width), jnp.bfloat16),
                jax.ShapeDtypeStruct((rows, 128), jnp.float32),
                jax.ShapeDtypeStruct((rows + STAT_ROWS, width), jnp.bfloat16),
                jax.ShapeDtypeStruct((rows + STAT_ROWS, width), jnp.bfloat16),
            ),
            in_specs=[smem, whole, block, block, block, at(heads), whole, whole],
            out_specs=(block, packed, tall, tall),
            scratch_shapes=[pltpu.VMEM((rows, rows), jnp.float32)] * 5,
            compiler_params=pltpu.CompilerParams(vmem_limit_bytes=32 * 2**20),
            cost_estimate=pl.CostEstimate(
                flops=heads * 5 * rows * rows * HD * 4 * 2,
                bytes_accessed=8 * 2**20,
                transcendentals=heads * 5 * rows * rows,
            ),
            name="attend",
        )(scalars, attn_query, qa, qb, kvp, kvp, attn_key, attn_value)
        ra = lax.ppermute(oa, "seq", [(1, 2), (2, 3)])
        rb = lax.ppermute(ob, "seq", [(1, 3)])
        outs.append((own, lse, ra, rb))
        scalars, _ = lax.optimization_barrier((scalars, own))
    anywhere = pl.BlockSpec(memory_space=pl.ANY)
    whole_out = jax.ShapeDtypeStruct((rows, cols), jnp.bfloat16)
    mine = at(2 * heads)
    result = pl.pallas_call(
        lambda *refs: near_kernel(rows, *refs[:8], None, *refs[8:]),
        grid=(near,),
        out_shape=whole_out,
        in_specs=[smem, mine, mine, mine, block, at(near), block, at(near)],
        out_specs=mine,
        scratch_shapes=[pltpu.VMEM((rows, rows), jnp.float32)] * 3,
        compiler_params=pltpu.CompilerParams(vmem_limit_bytes=32 * 2**20),
        cost_estimate=pl.CostEstimate(
            flops=near * 3 * rows * rows * HD * 4 * 2,
            bytes_accessed=4 * 2**20,
            transcendentals=near * 3 * rows * rows,
        ),
        name="near",
    )(scalars, attn_query, attn_key, attn_value, kv1, kv1, kv2, kv2)
    for c in range(2):
        own, lse, ra, rb = outs[c]
        result = pl.pallas_call(
            lambda *refs: merge_kernel(rows, *refs),
            grid=(heads,),
            out_shape=whole_out,
            in_specs=[smem, block, packed, tall, tall, anywhere],
            out_specs=at(c * heads),
            input_output_aliases={5: 0},
            cost_estimate=pl.CostEstimate(
                flops=rows * width * 16, bytes_accessed=4 * 2**20, transcendentals=0
            ),
            name="merge",
        )(scalars, own, lse, ra, rb, result)
    return hyena_out, result


MESH_ID = pl.DeviceIdType.MESH
FAR = 1 << 20
CHUNK = 256


def start_at(pos, lens_ref):
    start = jnp.int32(0)
    end = jnp.int32(0)
    for doc in range(lens_ref.shape[0] - 1):
        end = end + lens_ref[doc]
        start = jnp.where(pos >= end, end, start)
    return start


def fused_kernel(
    rows, cols, lens_hbm, feat_hbm, q_hbm, k_hbm, v_hbm, short_hbm, med_hbm, skip_hbm, fwd_hbm, inv_hbm,
    hy_hbm, at_hbm,
    lens_ref, short_ref, med_ref, skip_ref, fwd_ref, inv_ref,
    feat, qv, kv, vv, ext, halo, up_rx, st_rx, q_near, q_far, up_tx, st_tx,
    b_own, b_own_l, b_near, b_near_l, b_far, spec, fix, hy_v, at_v,
    load_sem, hy_sem, at_sem, halo_sem, near_tx, near_rx, far_tx, far_rx, up_tx_sem, up_rx_sem,
    st_tx_sem, st_rx_sem,
):
    f32, bf16 = jnp.float32, jnp.bfloat16
    heads = cols // HD
    part = rows // 3
    span = lax.axis_index("seq")
    base = span * rows
    has_left, has_right = span > 0, span < 3
    has_far, sends_far = span < 2, span > 1

    def load(index, src, dst):
        copy = pltpu.make_async_copy(src, dst, load_sem.at[index])
        copy.start()
        return copy

    tail_load = load(0, feat_hbm.at[1:3, 2 * part :, :], feat.at[1:3, 2 * part :, :])
    front_load = load(1, feat_hbm.at[1:3, : 2 * part, :], feat.at[1:3, : 2 * part, :])
    lens_load = load(6, lens_hbm, lens_ref)
    filter_loads = [
        load(7, short_hbm, short_ref),
        load(8, med_hbm, med_ref),
        load(9, skip_hbm, skip_ref),
        load(10, fwd_hbm, fwd_ref),
        load(11, inv_hbm, inv_ref),
    ]
    mix_load = load(2, feat_hbm.at[0], feat.at[0])
    k_load = load(3, k_hbm, kv)
    v_load = load(4, v_hbm, vv)
    q_load = load(5, q_hbm, qv)

    def lanes(h):
        return pl.ds(pl.multiple_of(h * HD, HD), HD)

    def remote(src, dst, tx, rx, to):
        return pltpu.make_async_remote_copy(
            src_ref=src, dst_ref=dst, send_sem=tx, recv_sem=rx, device_id={"seq": to},
            device_id_type=MESH_ID,
        )

    up_to = jnp.minimum(span + 1, 3)

    def near_copy(h):
        return remote(q_hbm.at[:, lanes(h)], q_near.at[h], near_tx.at[h], near_rx.at[h],
                      jnp.maximum(span - 1, 0))

    def far_copy(h):
        return remote(q_hbm.at[:part, lanes(h)], q_far.at[h], far_tx.at[h], far_rx.at[h],
                      jnp.maximum(span - 2, 0))

    def up_copy(h):
        return remote(up_tx.at[h], up_rx.at[h], up_tx_sem.at[h], up_rx_sem.at[h], up_to)

    def st_copy(h):
        return remote(st_tx.at[h], st_rx.at[h], st_tx_sem.at[h], st_rx_sem.at[h], up_to)

    halo_copy = remote(ext.at[rows : rows + part, :], halo, halo_sem.at[0], halo_sem.at[1], up_to)

    barrier = pltpu.get_barrier_semaphore()
    for away in (-2, -1, 1, 2):

        @pl.when((span + away >= 0) & (span + away < 4))
        def _(away=away):
            pl.semaphore_signal(barrier, inc=1, device_id={"seq": span + away}, device_id_type=MESH_ID)

    pl.semaphore_wait(barrier, jnp.where(has_left & has_right, 3, 2))

    @pl.when(span == 2)
    def _():
        def send_far(h, carry):
            far_copy(h).start()
            return carry

        lax.fori_loop(0, heads, send_far, 0)

    def send_queries(h, carry):
        pl.when(has_left)(lambda: near_copy(h).start())
        pl.when(span == 3)(lambda: far_copy(h).start())
        return carry

    lax.fori_loop(0, heads, send_queries, 0)

    chunks = cols // CHUNK

    def chunk_cols(c):
        return pl.ds(pl.multiple_of(c * CHUNK, CHUNK), CHUNK)

    def gate(lo, hi, at):
        return (feat[1, lo:hi, at].astype(f32) * feat[2, lo:hi, at].astype(f32)).astype(bf16)

    tail_load.wait()

    def gate_tail(c, carry):
        at = chunk_cols(c)
        ext[rows : rows + part, at] = gate(2 * part, rows, at)
        ext[:part, at] = jnp.zeros((part, CHUNK), bf16)
        return carry

    lax.fori_loop(0, chunks, gate_tail, 0)
    pl.when(has_right)(lambda: halo_copy.start())

    @pl.when(jnp.logical_not(has_left))
    def _():
        def clear(h, carry):
            up_rx[h] = jnp.zeros((rows + part, HD), bf16)
            st_rx[h] = jnp.zeros((8, HD), f32)
            return carry

        lax.fori_loop(0, heads, clear, 0)

    lens_load.wait()
    left_q = has_left & (base - start_at(base, lens_ref) > 2 * part)
    right_q = has_right & (base + rows - start_at(base + rows, lens_ref) > 2 * part)
    fresh = has_far & right_q & (start_at(base + 2 * rows, lens_ref) < base + rows)
    slot_mine = (span > 1) & (base - rows - start_at(base, lens_ref) > 2 * part)

    def column_iota(first, count):
        return first + lax.broadcasted_iota(jnp.int32, (count, 1), 0)

    own_pos = column_iota(base, rows)
    near_pos = column_iota(base + rows, rows)
    far_pos = column_iota(base + 2 * rows, part)
    key_pos = base + lax.broadcasted_iota(jnp.int32, (1, rows), 1)
    left_pos = base - 2 * part + lax.broadcasted_iota(jnp.int32, (1, 2 * part), 1)
    no_keys = jnp.where(has_left & jnp.logical_not(left_q), 0, FAR)
    no_near = jnp.where(right_q, 0, FAR)
    no_far = jnp.where(fresh, 0, FAR)
    own_start = doc_start(own_pos, lens_ref)
    near_start = doc_start(near_pos, lens_ref) + no_near
    far_start = doc_start(far_pos, lens_ref) + no_far

    def bias(ok):
        return jnp.where(ok, 0.0, NEG).astype(f32)

    b_own[...] = bias((key_pos <= own_pos) & (key_pos >= own_start))
    b_own_l[...] = bias(left_pos >= own_start + no_keys)
    b_near[...] = bias(key_pos >= near_start)
    b_near_l[...] = bias(left_pos >= near_start + no_keys)
    b_far[...] = bias(key_pos >= far_start)

    def dot(x, y):
        return jnp.dot(x, y, preferred_element_type=f32)

    first_cut = jnp.int32(FAR)
    last_cut = jnp.int32(-1)
    end = jnp.int32(0)
    for doc in range(lens_ref.shape[0] - 1):
        end = end + lens_ref[doc]
        first_cut = jnp.where((end > base) & (end < first_cut), end, first_cut)
        last_cut = jnp.where((end < base + rows) & (end > last_cut), end, last_cut)
    cuts = []
    for cut in (first_cut, last_cut):
        valid = (cut > base) & (cut < base + rows)
        block = jnp.where(valid, lax.div(jnp.where(valid, cut - base, 0), part), 0)
        cuts.append((jnp.where(valid, cut, FAR), block))
    win_iota = lax.broadcasted_iota(jnp.int32, (2 * part, 1), 0)
    out_iota = lax.broadcasted_iota(jnp.int32, (part, 1), 0)

    def transform(window, first_pos, from_pos, spec_r, spec_i):
        window = jnp.where(win_iota + first_pos >= from_pos, window, jnp.zeros_like(window))
        return spread(window, spec_r, spec_i)

    def spread(window, spec_r, spec_i):
        wave = dot(fwd_ref[0], window)
        wave_r, wave_i = wave[:part], wave[part:]
        prod = jnp.concatenate(
            (
                (wave_r * spec_r - wave_i * spec_i).astype(bf16),
                (wave_r * spec_i + wave_i * spec_r).astype(bf16),
            ),
            axis=0,
        )
        return dot(inv_ref[0], prod)

    def finish(block, at, sums, fixes):
        for (cut, cut_block), fixed in zip(cuts, fixes):
            cut_from = jnp.where(cut_block == block, cut, FAR)
            sums = jnp.where(out_iota + (base + block * part) >= cut_from, fixed, sums)
        r0 = block * part
        hy_v[r0 : r0 + part, at] = (feat[0, r0 : r0 + part, at].astype(f32) * sums).astype(bf16)

    front_load.wait()
    mix_load.wait()
    for copy in filter_loads:
        copy.wait()

    def hyena_main(c, carry):
        at = chunk_cols(c)
        ext[part:rows, at] = gate(0, 2 * part, at)
        short = short_ref[:, at]
        head = jnp.concatenate(
            (short[:1] + skip_ref[:, at], short[1:], jnp.zeros((8 - short.shape[0], CHUNK), f32)), axis=0
        )
        filt = jnp.concatenate((med_ref[:8, at] + head, med_ref[8:, at]), axis=0)
        filt_hi = filt.astype(bf16)
        filt_lo = (filt - filt_hi.astype(f32)).astype(bf16)
        both = (
            dot(fwd_ref[0, :, :part], filt_hi)
            + dot(fwd_ref[1, :, :part], filt_hi)
            + dot(fwd_ref[0, :, :part], filt_lo)
        )
        spec[:, at] = both
        spec_r, spec_i = both[:part], both[part:]
        fixes = []
        for index, (cut, cut_block) in enumerate(cuts):
            window = jnp.zeros((2 * part, CHUNK), bf16)
            for block in range(3):
                r0 = block * part
                cut_from = jnp.where(cut_block == block, cut, FAR)
                window = jnp.where(
                    win_iota + (base + r0 - part) >= cut_from, ext[r0 : r0 + 2 * part, at], window
                )
            sums = spread(window, spec_r, spec_i)
            fix[index, :, at] = sums
            fixes.append(sums)
        for block in (1, 2):
            r0 = block * part
            sums = transform(
                ext[r0 : r0 + 2 * part, at], base + r0 - part, start_at(base + r0, lens_ref), spec_r, spec_i
            )
            finish(block, at, sums, fixes)
        return carry

    lax.fori_loop(0, chunks, hyena_main, 0)
    hy_late = pltpu.make_async_copy(hy_v.at[part:, :], hy_hbm.at[part:, :], hy_sem.at[0])
    hy_late.start()
    hy_first = pltpu.make_async_copy(hy_v.at[:part, :], hy_hbm.at[:part, :], hy_sem.at[1])

    def hyena_first():
        pl.when(has_left)(lambda: halo_copy.wait_recv())

        def one(c, carry):
            at = chunk_cols(c)
            window = jnp.concatenate((halo[:, at], ext[part : 2 * part, at]), axis=0)
            sums = transform(
                window, base - part, start_at(base, lens_ref), spec[:part, at], spec[part:, at]
            )
            finish(0, at, sums, [fix[i, :, at] for i in range(2)])
            return carry

        lax.fori_loop(0, chunks, one, 0)
        hy_first.start()

    k_load.wait()
    v_load.wait()
    q_load.wait()
    ones = jnp.ones((rows, HD), bf16)
    eye = lax.broadcasted_iota(jnp.int32, (part, HD), 0) == lax.broadcasted_iota(jnp.int32, (part, HD), 1)
    stat_iota = lax.broadcasted_iota(jnp.int32, (8, HD), 0)
    left_off = jnp.where(left_q, 0.0, NEG)
    slot_off = jnp.where(slot_mine, 0.0, NEG)

    def attend_to(q, keys, values, biases):
        scores = [
            lax.dot_general(q, k, (((1,), (1,)), ((), ())), preferred_element_type=f32) + b
            for k, b in zip(keys, biases)
        ]
        top = jnp.max(scores[0], axis=1, keepdims=True)
        for s in scores[1:]:
            top = jnp.maximum(top, jnp.max(s, axis=1, keepdims=True))
        acc = None
        for s, v in zip(scores, values):
            w = jnp.exp2((s - top) * SCALE2).astype(bf16)
            term = dot(w, v)
            acc = term if acc is None else acc + term
        return acc[:, :HD], acc[:, HD:], top * SCALE2

    def head_step(h, carry):
        at = lanes(h)
        pl.when(h == 3)(hyena_first)

        @pl.when(has_left)
        def _():
            up_copy(h).wait_recv()
            st_copy(h).wait_recv()

        k = kv[:, at]
        v = vv[:, at]
        k_left = up_rx[h, : 2 * part, :]
        v_ones = jnp.concatenate((v, ones), axis=1)
        v_left = jnp.concatenate((up_rx[h, 2 * part :, :], ones[: 2 * part]), axis=1)

        @pl.when(has_right)
        def _():
            near_copy(h).wait_recv()
            tails = (k[part : 2 * part], k[2 * part :], v[part : 2 * part], v[2 * part :])
            stats = jnp.zeros((8, HD), f32)

            def give(i, out):
                up_tx[h, i * part : (i + 1) * part, :] = jnp.where(
                    right_q, out, tails[i].astype(f32)
                ).astype(bf16)

            def to_row(lse):
                return jnp.sum(jnp.where(eye, lse, 0.0), axis=0, keepdims=True)

            for i in range(3):
                r0 = i * part
                acc, total, top = attend_to(
                    q_near[h, r0 : r0 + part, :],
                    (k, k_left),
                    (v_ones, v_left),
                    (b_near[r0 : r0 + part, :], b_near_l[r0 : r0 + part, :]),
                )
                give(i, acc / total)
                stats = jnp.where(stat_iota == i, to_row(top + jnp.log2(total)), stats)
            passed = up_rx[h, rows:, :].astype(f32)
            passed_stat = st_rx[h]

            @pl.when(has_far)
            def _():
                far_copy(h).wait_recv()
                acc, total, top = attend_to(q_far[h], (k,), (v_ones,), (b_far[...],))
                give(3, jnp.where(fresh, acc / total, passed))
                lse = to_row(top + jnp.log2(total))
                st_tx[h] = jnp.where(
                    stat_iota == 3, jnp.where(fresh, lse, passed_stat[3:4]), stats
                )

            @pl.when(jnp.logical_not(has_far))
            def _():
                give(3, passed)
                st_tx[h] = jnp.where(stat_iota == 3, passed_stat[3:4], stats)

            up_copy(h).start()
            st_copy(h).start()

        stats_in = st_rx[h]

        def column(i):
            return jnp.sum(jnp.where(eye, stats_in[i : i + 1], 0.0), axis=1, keepdims=True)

        for i in range(3):
            r0 = i * part
            r1 = r0 + part
            acc, total, top = attend_to(
                qv[r0:r1, at],
                (k[:r1], k_left),
                (v_ones[:r1], v_left),
                (b_own[r0:r1, :r1], b_own_l[r0:r1, :]),
            )
            lse = column(i) + left_off
            best = jnp.maximum(top, lse)
            if i == 0:
                slot_lse = column(3) + slot_off
                best = jnp.maximum(best, slot_lse)
            w0 = jnp.exp2(top - best)
            w1 = jnp.exp2(lse - best)
            mixed = acc * w0 + up_rx[h, r0:r1, :].astype(f32) * w1
            norm = total * w0 + w1
            if i == 0:
                w2 = jnp.exp2(slot_lse - best)
                mixed = mixed + up_rx[h, rows:, :].astype(f32) * w2
                norm = norm + w2
            at_v[r0:r1, at] = (mixed / norm).astype(bf16)
        pltpu.make_async_copy(at_v.at[:, at], at_hbm.at[:, at], at_sem.at[h]).start()
        return carry

    lax.fori_loop(0, heads, head_step, 0)

    def drain(h, carry):
        at = lanes(h)
        pltpu.make_async_copy(at_v.at[:, at], at_hbm.at[:, at], at_sem.at[h]).wait()

        @pl.when(has_right)
        def _():
            up_copy(h).wait_send()
            st_copy(h).wait_send()

        pl.when(has_left)(lambda: near_copy(h).wait_send())
        pl.when(sends_far)(lambda: far_copy(h).wait_send())
        return carry

    lax.fori_loop(0, heads, drain, 0)
    pl.when(has_right)(lambda: halo_copy.wait_send())
    hy_late.wait()
    hy_first.wait()


def fused(features, short_filter, medium_filter, skip_gain, attn_query, attn_key, attn_value, lengths):
    rows, cols = attn_query.shape
    part = rows // 3
    heads = cols // HD
    angle = np.pi / (2 * part) * np.outer(2 * np.arange(part) + 1, np.arange(2 * part))
    wave = np.concatenate((np.cos(angle), -np.sin(angle)), axis=0)
    fwd = split_two(wave)
    inv = split_two(wave.T[part:] / part)
    anywhere = pl.BlockSpec(memory_space=pl.ANY)
    out = jax.ShapeDtypeStruct((rows, cols), jnp.bfloat16)

    def buf(*shape):
        return pltpu.VMEM(shape, jnp.bfloat16)

    def wide(*shape):
        return pltpu.VMEM(shape, jnp.float32)

    each = pltpu.SemaphoreType.DMA((heads,))
    return pl.pallas_call(
        lambda *refs: fused_kernel(rows, cols, *refs),
        out_shape=(out, out),
        in_specs=[pl.BlockSpec(memory_space=pltpu.HBM)] * 10,
        out_specs=(anywhere, anywhere),
        scratch_shapes=[
            pltpu.SMEM(lengths.shape, jnp.int32), wide(*short_filter.shape), wide(part, cols), wide(1, cols),
            buf(*fwd.shape), buf(*inv.shape),
            buf(3, rows, cols), buf(rows, cols), buf(rows, cols), buf(rows, cols),
            buf(rows + part, cols), buf(part, cols),
            buf(heads, rows + part, HD), wide(heads, 8, HD),
            buf(heads, rows, HD), buf(heads, part, HD),
            buf(heads, rows + part, HD), wide(heads, 8, HD),
            wide(rows, rows), wide(rows, 2 * part), wide(rows, rows), wide(rows, 2 * part),
            wide(part, rows),
            wide(2 * part, cols), wide(2, part, cols),
            buf(rows, cols), buf(rows, cols),
            pltpu.SemaphoreType.DMA((12,)), pltpu.SemaphoreType.DMA((2,)), each,
            pltpu.SemaphoreType.DMA((2,)),
        ] + [each] * 8,
        compiler_params=pltpu.CompilerParams(
            collective_id=0, has_side_effects=True, vmem_limit_bytes=60 * 2**20
        ),
        cost_estimate=pl.CostEstimate(
            flops=heads * 32 * part * part * HD * 4, bytes_accessed=16 * 2**20,
            transcendentals=heads * 32 * part * part,
        ),
        name="fused",
    )(
        lengths, features.transpose(1, 0, 2), attn_query, attn_key, attn_value,
        short_filter, medium_filter, skip_gain[None, :], fwd, inv,
    )


def local(
    features, short_filter, medium_filter, skip_gain, attn_query, attn_key, attn_value, lengths
):
    rows, cols = attn_query.shape
    spans = lax.axis_size("seq")
    taps = medium_filter.shape[0]
    if spans == 4 and rows == 3 * taps and taps == HD and cols % CHUNK == 0 and short_filter.shape[0] < 8:
        return fused(
            features, short_filter, medium_filter, skip_gain, attn_query, attn_key, attn_value, lengths
        )
    if cols % 128 == 0 and taps % 128 == 0 and rows % taps == 0:
        hyena = hyena_fast
    else:
        hyena = hyena_mix
    hyena_out = hyena(features, short_filter, medium_filter, skip_gain, lengths)
    if spans == 4 and rows % 128 == 0 and rows <= 640 and cols % (8 * HD) == 0:
        return attention_fast(attn_query, attn_key, attn_value, lengths, hyena_out)
    return (hyena_out, attention_mix(attn_query, attn_key, attn_value, lengths))


def solution(mesh):
    in_specs = (
        P(("groups", "seq"), None, ("tensor", "sub")),
        P(None, ("tensor", "sub")),
        P(None, ("tensor", "sub")),
        P(("tensor", "sub")),
        P(("groups", "seq"), ("tensor", "sub")),
        P(("groups", "seq"), ("tensor", "sub")),
        P(("groups", "seq"), ("tensor", "sub")),
        P("groups"),
    )
    out_specs = (P(("groups", "seq"), ("tensor", "sub")), P(("groups", "seq"), ("tensor", "sub")))
    return jax.shard_map(local, mesh=mesh, in_specs=in_specs, out_specs=out_specs, check_vma=False)
```

```python
import math

import jax
import jax.numpy as jnp
import numpy as np
from jax import lax
from jax.experimental import pallas as pl
from jax.experimental.pallas import tpu as pltpu
from jax.sharding import PartitionSpec as P

HD = 128


def passed_along(value, axis, by):
    length = lax.axis_size(axis)
    pairs = [(i, i + by) for i in range(length) if 0 <= i + by < length]
    return lax.ppermute(value, axis, pairs)


def doc_of(positions, lengths):
    doc_ends = jnp.cumsum(lengths, dtype=jnp.int32)
    return jnp.sum(
        (positions[:, None] >= doc_ends[None, :]).astype(jnp.int32), axis=1, dtype=jnp.int32
    )


def hyena_mix(features, short_filter, medium_filter, skip_gain, lengths):
    row_count = features.shape[0]
    medium_taps = medium_filter.shape[0]
    rim_rows = medium_taps - 1
    span_index = lax.axis_index("seq")
    queries = features[:, 0].astype(jnp.float32)
    gated = (features[:, 1].astype(jnp.float32) * features[:, 2].astype(jnp.float32)).astype(
        jnp.bfloat16
    )
    gated = lax.optimization_barrier(gated)
    carried = passed_along(gated[row_count - rim_rows :], "seq", 1)
    extended = jnp.concatenate((carried, gated), axis=0)
    ext_positions = (
        span_index * row_count - rim_rows + jnp.arange(row_count + rim_rows, dtype=jnp.int32)
    )
    ext_docs = doc_of(ext_positions, lengths)
    ext_live = ext_positions >= 0
    own_docs = ext_docs[rim_rows:]

    def tap_term(tap_index, filter_bank):
        first_row = rim_rows - tap_index
        window = lax.dynamic_slice_in_dim(extended, first_row, row_count, 0).astype(jnp.float32)
        same_doc = lax.dynamic_slice_in_dim(ext_docs, first_row, row_count, 0) == own_docs
        live_mask = lax.dynamic_slice_in_dim(ext_live, first_row, row_count, 0)
        keep_mask = (same_doc & live_mask).astype(jnp.float32)[:, None]
        taps = lax.dynamic_index_in_dim(filter_bank, tap_index, 0, keepdims=False)
        return taps[None, :] * window * keep_mask

    short_sum = jnp.zeros(gated.shape, jnp.float32)
    for tap_index in range(short_filter.shape[0]):
        short_sum = short_sum + tap_term(tap_index, short_filter)

    def tap_block(block_index, partial_value):
        for offset in range(8):
            partial_value = partial_value + tap_term(block_index * 8 + offset, medium_filter)
        return partial_value

    medium_sum = lax.fori_loop(0, medium_taps // 8, tap_block, jnp.zeros(gated.shape, jnp.float32))
    mixed = queries * (short_sum + medium_sum + skip_gain[None, :] * gated.astype(jnp.float32))
    return mixed.astype(jnp.bfloat16)


def attention_mix(attn_query, attn_key, attn_value, lengths):
    row_count, col_count = attn_query.shape
    heads_here = col_count // HD
    span_index = lax.axis_index("seq")
    query_positions = span_index * row_count + jnp.arange(row_count, dtype=jnp.int32)
    query_docs = doc_of(query_positions, lengths)
    query_heads = attn_query.reshape(row_count, heads_here, HD)
    score_scale = HD ** (-0.5)
    last_query = query_positions[row_count - 1]
    first_query_doc = query_docs[0]

    def absorb(state_now, key_block, value_block, first_row):
        key_count = key_block.shape[0]
        last_key = first_row + key_count - 1
        last_key_doc = doc_of(jnp.reshape(last_key, (1,)), lengths)[0]
        masked_out = (first_row > last_query) | (last_key < 0) | (last_key_doc < first_query_doc)

        def compute(state_in):
            running_max, running_total, running_sum = state_in
            key_heads = key_block.reshape(key_count, heads_here, HD)
            value_heads = value_block.reshape(key_count, heads_here, HD)
            scores = (
                jnp.einsum(
                    "rhd,nhd->hrn", query_heads, key_heads, preferred_element_type=jnp.float32
                )
                * score_scale
            )
            key_positions = first_row + jnp.arange(key_count, dtype=jnp.int32)
            key_docs = doc_of(key_positions, lengths)
            allowed = (
                (key_positions[None, :] <= query_positions[:, None])
                & (key_docs[None, :] == query_docs[:, None])
                & (key_positions >= 0)[None, :]
            )
            masked = jnp.where(allowed[None], scores, -1e30)
            new_max = jnp.maximum(running_max, jnp.max(masked, axis=2))
            rescale = jnp.exp(running_max - new_max)
            weights = jnp.where(allowed[None], jnp.exp(scores - new_max[:, :, None]), 0.0)
            new_total = running_total * rescale + jnp.sum(weights, axis=2)
            product = jnp.einsum(
                "hrn,nhd->hrd",
                weights.astype(jnp.bfloat16),
                value_heads,
                preferred_element_type=jnp.float32,
            )
            new_sum = running_sum * rescale[:, :, None] + product
            return (new_max, new_total, new_sum)

        def keep_state(state_in):
            return state_in

        return lax.cond(masked_out, keep_state, compute, state_now)

    def fold_keys(state_now, pieces, first_row):
        key_all, value_all = pieces
        key_count = key_all.shape[0]
        block_rows = math.gcd(key_count, 1536)
        if block_rows == key_count:
            return absorb(state_now, key_all, value_all, first_row)
        block_total = key_count // block_rows
        key_blocks = key_all.reshape(block_total, block_rows, col_count)
        value_blocks = value_all.reshape(block_total, block_rows, col_count)

        def scan_step(state_inner, block_items):
            key_block, value_block, block_index = block_items
            return (
                absorb(state_inner, key_block, value_block, first_row + block_index * block_rows),
                None,
            )

        state_now, unused = lax.scan(
            scan_step,
            state_now,
            (key_blocks, value_blocks, jnp.arange(block_total, dtype=jnp.int32)),
        )
        return state_now

    initial = (
        jnp.full((heads_here, row_count), -1e30, jnp.float32),
        jnp.zeros((heads_here, row_count), jnp.float32),
        jnp.zeros((heads_here, row_count, HD), jnp.float32),
    )
    state_now = fold_keys(
        initial,
        (
            lax.all_gather(attn_key, "seq", axis=0, tiled=True),
            lax.all_gather(attn_value, "seq", axis=0, tiled=True),
        ),
        jnp.int32(0),
    )
    running_max, running_total, running_sum = state_now
    result = running_sum / running_total[:, :, None]
    return result.transpose(1, 0, 2).reshape(row_count, col_count).astype(jnp.bfloat16)


LOG2E = 1.4426950408889634
LN2 = 0.6931471805599453
SCALE2 = HD**-0.5 * LOG2E
NEG = -1e30
STAT_ROWS = 16


def hyena_kernel(row_count, taps, lens_ref, feat_ref, rim_ref, filt_ref, fwd_ref, inv_ref, out_ref,
                 ext_ref, sum_ref):
    base = lens_ref[lens_ref.shape[0] - 1]
    ext_ref[:taps, :] = rim_ref[...]
    ext_ref[taps:, :] = (
        feat_ref[1].astype(jnp.float32) * feat_ref[2].astype(jnp.float32)
    ).astype(jnp.bfloat16)

    def dot(x, y):
        return jnp.dot(x, y, preferred_element_type=jnp.float32)

    filt = filt_ref[...]
    filt_hi = filt.astype(jnp.bfloat16)
    filt_lo = (filt - filt_hi.astype(jnp.float32)).astype(jnp.bfloat16)
    spec = (
        dot(fwd_ref[0, :, :taps], filt_hi)
        + dot(fwd_ref[1, :, :taps], filt_hi)
        + dot(fwd_ref[0, :, :taps], filt_lo)
    )
    spec_r, spec_i = spec[:taps], spec[taps:]
    win_iota = lax.broadcasted_iota(jnp.int32, (2 * taps, 1), 0)
    out_iota = lax.broadcasted_iota(jnp.int32, (taps, 1), 0)
    for block in range(row_count // taps):
        r0 = block * taps
        start = jnp.int32(0)
        for doc in range(lens_ref.shape[0] - 1):
            end = start + lens_ref[doc]
            first, last = start - base, end - base

            @pl.when((last > r0) & (first < r0 + taps) & (first < last))
            def _(first=first):
                window = ext_ref[r0 : r0 + 2 * taps, :]
                window = jnp.where(win_iota + (r0 - taps) >= first, window, jnp.zeros_like(window))
                wave = dot(fwd_ref[0], window) + dot(fwd_ref[1], window)
                wave_r, wave_i = wave[:taps], wave[taps:]
                prod = jnp.concatenate(
                    (
                        (wave_r * spec_r - wave_i * spec_i).astype(jnp.bfloat16),
                        (wave_r * spec_i + wave_i * spec_r).astype(jnp.bfloat16),
                    ),
                    axis=0,
                )
                sums = dot(inv_ref[0], prod) + dot(inv_ref[1], prod)
                sum_ref[...] = jnp.where(out_iota + r0 >= first, sums, sum_ref[...])

            start = end
        out_ref[r0 : r0 + taps, :] = (
            feat_ref[0, r0 : r0 + taps, :].astype(jnp.float32) * sum_ref[...]
        ).astype(out_ref.dtype)


def split_two(matrix):
    high = matrix.astype(jnp.bfloat16)
    low = (matrix - high.astype(np.float64)).astype(jnp.bfloat16)
    return np.stack((high, low))


def hyena_fast(features, short_filter, medium_filter, skip_gain, lengths):
    row_count, _, cols = features.shape
    taps = medium_filter.shape[0]
    span_index = lax.axis_index("seq")
    streams = features.transpose(1, 0, 2)
    tail = streams[:, row_count - taps :]
    gated_tail = (tail[1].astype(jnp.float32) * tail[2].astype(jnp.float32)).astype(jnp.bfloat16)
    carried = passed_along(gated_tail, "seq", 1)
    head = jnp.concatenate((short_filter[:1] + skip_gain[None, :], short_filter[1:]), axis=0)
    filt = medium_filter + jnp.pad(head, ((0, taps - head.shape[0]), (0, 0)))
    angle = np.pi / (2 * taps) * np.outer(2 * np.arange(taps) + 1, np.arange(2 * taps))
    fwd = split_two(np.concatenate((np.cos(angle), -np.sin(angle)), axis=0))
    inv = split_two(
        np.concatenate((np.cos(angle), -np.sin(angle)), axis=0).T[taps:] / taps
    )
    scalars = jnp.concatenate((lengths, jnp.reshape(span_index * row_count, (1,)).astype(jnp.int32)))
    width = math.gcd(cols, 512)
    return pl.pallas_call(
        lambda *refs: hyena_kernel(row_count, taps, *refs),
        grid=(cols // width,),
        out_shape=jax.ShapeDtypeStruct((row_count, cols), jnp.bfloat16),
        in_specs=[
            pl.BlockSpec(memory_space=pltpu.SMEM),
            pl.BlockSpec((3, row_count, width), lambda i: (0, 0, i)),
            pl.BlockSpec((taps, width), lambda i: (0, i)),
            pl.BlockSpec((taps, width), lambda i: (0, i)),
            pl.BlockSpec(fwd.shape, lambda i: (0, 0, 0)),
            pl.BlockSpec(inv.shape, lambda i: (0, 0, 0)),
        ],
        out_specs=pl.BlockSpec((row_count, width), lambda i: (0, i)),
        scratch_shapes=[
            pltpu.VMEM((row_count + taps, width), jnp.bfloat16),
            pltpu.VMEM((taps, width), jnp.float32),
        ],
        compiler_params=pltpu.CompilerParams(vmem_limit_bytes=32 * 2**20),
        cost_estimate=pl.CostEstimate(
            flops=2 * 9 * 2 * taps * taps * 3 * cols, bytes_accessed=8 * 2**20, transcendentals=0
        ),
        name="hyena",
    )(scalars, streams, carried, filt, fwd, inv)


def doc_start(pos, lens_ref):
    start = jnp.zeros_like(pos)
    end = jnp.int32(0)
    for doc in range(lens_ref.shape[0] - 1):
        end = end + lens_ref[doc]
        start = jnp.where(pos >= end, end, start)
    return start


def attend(query_ref, keys, values, biases, emit):
    rows = query_ref.shape[0]
    step = 128
    ones = jnp.ones((rows, 128), jnp.bfloat16)
    vals = [jnp.concatenate((v[...], ones), axis=1) for v in values]
    for r in range(0, rows, step):
        q = query_ref[r : r + step, :]
        scores = [
            lax.dot_general(q, k[...], (((1,), (1,)), ((), ())),
                            preferred_element_type=jnp.float32) + b[r : r + step, :]
            for k, b in zip(keys, biases)
        ]
        top = jnp.max(scores[0], axis=1, keepdims=True)
        for s in scores[1:]:
            top = jnp.maximum(top, jnp.max(s, axis=1, keepdims=True))
        acc = None
        for s, v in zip(scores, vals):
            w = jnp.exp2((s - top) * SCALE2).astype(jnp.bfloat16)
            part = jnp.dot(w, v, preferred_element_type=jnp.float32)
            acc = part if acc is None else acc + part
        total = acc[:, 128:]
        emit(r, acc[:, :128] / total, top * SCALE2 + jnp.log2(total))


def needs(lens_ref, base, rows, ahead, back):
    q_first = base + ahead * rows
    start = jnp.int32(0)
    end = jnp.int32(0)
    for doc in range(lens_ref.shape[0] - 1):
        end = end + lens_ref[doc]
        start = jnp.where(q_first >= end, end, start)
    return start < base + (1 - back) * rows


def fill_bias(lens_ref, base, rows, ref, ahead, back):
    qpos = base + ahead * rows + lax.broadcasted_iota(jnp.int32, (rows, 1), 0)
    starts = doc_start(qpos, lens_ref)
    kpos = base - back * rows + lax.broadcasted_iota(jnp.int32, (1, rows), 1)
    ref[...] = jnp.where((kpos <= qpos) & (kpos >= starts), 0.0, NEG).astype(jnp.float32)


def near_kernel(rows, lens_ref, q_ref, k_ref, v_ref, k1_ref, v1_ref, k2_ref, v2_ref, all_ref, o_ref,
                b0, b1, b2):
    span = lens_ref[lens_ref.shape[0] - 1]
    base = span * rows
    one = (span >= 1) & needs(lens_ref, base, rows, 0, 1)
    two = (span >= 2) & needs(lens_ref, base, rows, 0, 2)

    @pl.when(pl.program_id(0) == 0)
    def _():
        fill_bias(lens_ref, base, rows, b0, 0, 0)
        pl.when(one)(lambda: fill_bias(lens_ref, base, rows, b1, 0, 1))
        pl.when(two)(lambda: fill_bias(lens_ref, base, rows, b2, 0, 2))

    def emit(r, out, lse):
        o_ref[r : r + 128, :] = out.astype(jnp.bfloat16)

    pl.when(two)(
        lambda: attend(q_ref, (k_ref, k1_ref, k2_ref), (v_ref, v1_ref, v2_ref), (b0, b1, b2), emit)
    )
    pl.when(one & jnp.logical_not(two))(
        lambda: attend(q_ref, (k_ref, k1_ref), (v_ref, v1_ref), (b0, b1), emit)
    )
    pl.when(jnp.logical_not(one))(lambda: attend(q_ref, (k_ref,), (v_ref,), (b0,), emit))


def attn_kernel(rows, lens_ref, q_ref, qa_ref, qb_ref, kp_ref, vp_ref, k_ref, v_ref,
                o_ref, lse_ref, oa_ref, ob_ref, b00, b10, b01, b11, b02):
    span = lens_ref[lens_ref.shape[0] - 1]
    base = span * rows

    def reads(ahead, back):
        return needs(lens_ref, base, rows, ahead, back)

    own_prev = (span == 1) & reads(0, 1)
    a_here = ((span == 1) | (span == 2)) & reads(1, 0)
    a_prev = (span == 1) & reads(1, 1)
    b_here = (span == 1) & reads(2, 0)

    @pl.when(pl.program_id(0) == 0)
    def _():
        lse_ref[...] = jnp.zeros_like(lse_ref)

        def fill(ref, ahead, back):
            fill_bias(lens_ref, base, rows, ref, ahead, back)

        fill(b00, 0, 0)
        pl.when(own_prev)(lambda: fill(b01, 0, 1))
        pl.when(a_here)(lambda: fill(b10, 1, 0))
        pl.when(a_prev)(lambda: fill(b11, 1, 1))
        pl.when(b_here)(lambda: fill(b02, 2, 0))

    step = 128
    head_lane = lax.broadcasted_iota(jnp.int32, (step, 128), 1) == pl.program_id(0)

    def emit_own(r, out, lse):
        o_ref[r : r + step, :] = out.astype(jnp.bfloat16)
        lse_ref[r : r + step, :] = jnp.where(head_lane, lse, lse_ref[r : r + step, :])

    eye = lax.broadcasted_iota(jnp.int32, (128, 128), 0) == lax.broadcasted_iota(
        jnp.int32, (128, 128), 1
    )
    stat_iota = lax.broadcasted_iota(jnp.int32, (STAT_ROWS, 128), 0)

    def emit_to(ref):
        stats = [jnp.zeros((STAT_ROWS, 128), jnp.float32)]

        def emit(r, out, lse):
            ref[r : r + step, :] = out.astype(jnp.bfloat16)
            rest = jnp.sum(jnp.where(eye, lse, 0.0), axis=0, keepdims=True)
            for piece in range(3):
                high = rest.astype(jnp.bfloat16).astype(jnp.float32)
                stats[0] = jnp.where(stat_iota == piece * (rows // step) + r // step, high, stats[0])
                rest = rest - high
            if r + step == rows:
                ref[rows:, :] = stats[0].astype(jnp.bfloat16)

        return emit

    def empty(ref):
        ref[:rows, :] = jnp.zeros((rows, 128), jnp.bfloat16)
        ref[rows:, :] = jnp.where(stat_iota < rows // step, NEG, 0.0).astype(jnp.bfloat16)

    pl.when(own_prev)(lambda: attend(q_ref, (kp_ref, k_ref), (vp_ref, v_ref), (b01, b00), emit_own))
    pl.when(jnp.logical_not(own_prev))(lambda: attend(q_ref, (k_ref,), (v_ref,), (b00,), emit_own))
    pl.when(a_prev)(
        lambda: attend(qa_ref, (kp_ref, k_ref), (vp_ref, v_ref), (b11, b10), emit_to(oa_ref))
    )
    pl.when(a_here & jnp.logical_not(a_prev))(
        lambda: attend(qa_ref, (k_ref,), (v_ref,), (b10,), emit_to(oa_ref))
    )
    pl.when(jnp.logical_not(a_here))(lambda: empty(oa_ref))
    pl.when(b_here)(lambda: attend(qb_ref, (k_ref,), (v_ref,), (b02,), emit_to(ob_ref)))
    pl.when(jnp.logical_not(b_here))(lambda: empty(ob_ref))


def merge_kernel(rows, lens_ref, o_ref, lse_ref, ra_ref, rb_ref, all_ref, out_ref):
    span = lens_ref[lens_ref.shape[0] - 1]
    step = 128
    eye = lax.broadcasted_iota(jnp.int32, (128, 128), 0) == lax.broadcasted_iota(
        jnp.int32, (128, 128), 1
    )

    @pl.when(span < 2)
    def _():
        out_ref[...] = o_ref[...]

    @pl.when(span >= 2)
    def _():
        blocks = rows // step
        head_lane = lax.broadcasted_iota(jnp.int32, (step, 128), 1) == pl.program_id(0)
        stat_a = ra_ref[rows:, :].astype(jnp.float32)
        stat_b = rb_ref[rows:, :].astype(jnp.float32)

        def column(stats, i):
            row = (stats[i : i + 1] + stats[blocks + i : blocks + i + 1]) + stats[
                2 * blocks + i : 2 * blocks + i + 1
            ]
            return jnp.sum(jnp.where(eye, row, 0.0), axis=1, keepdims=True)

        for i in range(blocks):
            r = i * step
            own = jnp.sum(jnp.where(head_lane, lse_ref[r : r + step, :], 0.0), axis=1, keepdims=True)
            lse_a = column(stat_a, i)
            lse_b = jnp.where(span == 3, column(stat_b, i), NEG)
            top = jnp.maximum(own, jnp.maximum(lse_a, lse_b))
            w0 = jnp.exp2(own - top)
            w1 = jnp.exp2(lse_a - top)
            w2 = jnp.exp2(lse_b - top)
            total = (
                o_ref[r : r + step, :].astype(jnp.float32) * w0
                + ra_ref[r : r + step, :].astype(jnp.float32) * w1
                + rb_ref[r : r + step, :].astype(jnp.float32) * w2
            )
            out_ref[r : r + step, :] = (total / (w0 + w1 + w2)).astype(jnp.bfloat16)


def attention_fast(attn_query, attn_key, attn_value, lengths, hyena_out):
    rows, cols = attn_query.shape
    span_index = lax.axis_index("seq")
    scalars = jnp.concatenate((lengths, jnp.reshape(span_index, (1,)).astype(jnp.int32)))
    all_heads = cols // HD
    heads = all_heads * 3 // 8
    near = all_heads - 2 * heads
    width = heads * HD
    smem = pl.BlockSpec(memory_space=pltpu.SMEM)
    block = pl.BlockSpec((rows, HD), lambda h: (0, h))
    tall = pl.BlockSpec((rows + STAT_ROWS, HD), lambda h: (0, h))
    packed = pl.BlockSpec((rows, 128), lambda h: (0, 0))

    def at(offset):
        return pl.BlockSpec((rows, HD), lambda h: (0, offset + h))

    def pair(lo, hi):
        return jnp.concatenate((attn_key[:, lo:hi], attn_value[:, lo:hi]), axis=1)

    sent = []
    for c in range(2):
        qc = attn_query[:, c * width : (c + 1) * width]
        qa = lax.ppermute(qc, "seq", [(2, 1), (3, 2)])
        qb = lax.ppermute(qc, "seq", [(3, 1)])
        kv = pair(c * width, (c + 1) * width)
        sent.append((qa, qb, lax.ppermute(kv, "seq", [(0, 1)])))
    kv = pair(2 * width, cols)
    kv1 = lax.ppermute(kv, "seq", [(0, 1), (1, 2), (2, 3)])
    kv2 = lax.ppermute(kv, "seq", [(0, 2), (1, 3)])
    scalars, hyena_out = lax.optimization_barrier((scalars, hyena_out))
    outs = []
    for c in range(2):
        qa, qb, kvp = sent[c]
        whole = at(c * heads)
        own, lse, oa, ob = pl.pallas_call(
            lambda *refs: attn_kernel(rows, *refs),
            grid=(heads,),
            out_shape=(
                jax.ShapeDtypeStruct((rows, width), jnp.bfloat16),
                jax.ShapeDtypeStruct((rows, 128), jnp.float32),
                jax.ShapeDtypeStruct((rows + STAT_ROWS, width), jnp.bfloat16),
                jax.ShapeDtypeStruct((rows + STAT_ROWS, width), jnp.bfloat16),
            ),
            in_specs=[smem, whole, block, block, block, at(heads), whole, whole],
            out_specs=(block, packed, tall, tall),
            scratch_shapes=[pltpu.VMEM((rows, rows), jnp.float32)] * 5,
            compiler_params=pltpu.CompilerParams(vmem_limit_bytes=32 * 2**20),
            cost_estimate=pl.CostEstimate(
                flops=heads * 5 * rows * rows * HD * 4 * 2,
                bytes_accessed=8 * 2**20,
                transcendentals=heads * 5 * rows * rows,
            ),
            name="attend",
        )(scalars, attn_query, qa, qb, kvp, kvp, attn_key, attn_value)
        ra = lax.ppermute(oa, "seq", [(1, 2), (2, 3)])
        rb = lax.ppermute(ob, "seq", [(1, 3)])
        outs.append((own, lse, ra, rb))
        scalars, _ = lax.optimization_barrier((scalars, own))
    anywhere = pl.BlockSpec(memory_space=pl.ANY)
    whole_out = jax.ShapeDtypeStruct((rows, cols), jnp.bfloat16)
    mine = at(2 * heads)
    result = pl.pallas_call(
        lambda *refs: near_kernel(rows, *refs[:8], None, *refs[8:]),
        grid=(near,),
        out_shape=whole_out,
        in_specs=[smem, mine, mine, mine, block, at(near), block, at(near)],
        out_specs=mine,
        scratch_shapes=[pltpu.VMEM((rows, rows), jnp.float32)] * 3,
        compiler_params=pltpu.CompilerParams(vmem_limit_bytes=32 * 2**20),
        cost_estimate=pl.CostEstimate(
            flops=near * 3 * rows * rows * HD * 4 * 2,
            bytes_accessed=4 * 2**20,
            transcendentals=near * 3 * rows * rows,
        ),
        name="near",
    )(scalars, attn_query, attn_key, attn_value, kv1, kv1, kv2, kv2)
    for c in range(2):
        own, lse, ra, rb = outs[c]
        result = pl.pallas_call(
            lambda *refs: merge_kernel(rows, *refs),
            grid=(heads,),
            out_shape=whole_out,
            in_specs=[smem, block, packed, tall, tall, anywhere],
            out_specs=at(c * heads),
            input_output_aliases={5: 0},
            cost_estimate=pl.CostEstimate(
                flops=rows * width * 16, bytes_accessed=4 * 2**20, transcendentals=0
            ),
            name="merge",
        )(scalars, own, lse, ra, rb, result)
    return hyena_out, result


MESH_ID = pl.DeviceIdType.MESH
FAR = 1 << 20
CHUNK = 256


def start_at(pos, lens_ref):
    start = jnp.int32(0)
    end = jnp.int32(0)
    for doc in range(lens_ref.shape[0] - 1):
        end = end + lens_ref[doc]
        start = jnp.where(pos >= end, end, start)
    return start


def fused_kernel(
    rows, cols, lens_hbm, feat_hbm, q_hbm, k_hbm, v_hbm, short_hbm, med_hbm, skip_hbm, fwd_hbm, inv_hbm,
    hy_hbm, at_hbm,
    lens_ref, short_ref, med_ref, skip_ref, fwd_ref, inv_ref,
    feat, qv, kv, vv, ext, halo, up_rx, st_rx, q_near, q_far, up_tx, st_tx,
    b_own, b_own_l, b_near, b_near_l, b_far, spec, fix, hy_v, at_v,
    load_sem, hy_sem, at_sem, halo_sem, near_tx, near_rx, far_tx, far_rx, up_tx_sem, up_rx_sem,
    st_tx_sem, st_rx_sem,
):
    f32, bf16 = jnp.float32, jnp.bfloat16
    heads = cols // HD
    part = rows // 3
    span = lax.axis_index("seq")
    base = span * rows
    has_left, has_right = span > 0, span < 3
    has_far, sends_far = span < 2, span > 1

    def load(index, src, dst):
        copy = pltpu.make_async_copy(src, dst, load_sem.at[index])
        copy.start()
        return copy

    tail_load = load(0, feat_hbm.at[1:3, 2 * part :, :], feat.at[1:3, 2 * part :, :])
    lens_load = load(6, lens_hbm, lens_ref)
    k_load = load(3, k_hbm, kv)
    v_load = load(4, v_hbm, vv)
    q_load = load(5, q_hbm, qv)
    filter_loads = [
        load(7, short_hbm, short_ref),
        load(8, med_hbm, med_ref),
        load(9, skip_hbm, skip_ref),
        load(10, fwd_hbm, fwd_ref),
        load(11, inv_hbm, inv_ref),
    ]
    front_load = load(1, feat_hbm.at[1:3, : 2 * part, :], feat.at[1:3, : 2 * part, :])
    mix_load = load(2, feat_hbm.at[0], feat.at[0])

    def lanes(h):
        return pl.ds(pl.multiple_of(h * HD, HD), HD)

    def remote(src, dst, tx, rx, to):
        return pltpu.make_async_remote_copy(
            src_ref=src, dst_ref=dst, send_sem=tx, recv_sem=rx, device_id={"seq": to},
            device_id_type=MESH_ID,
        )

    up_to = jnp.minimum(span + 1, 3)

    def near_copy(h):
        return remote(q_hbm.at[:, lanes(h)], q_near.at[h], near_tx.at[h], near_rx.at[h],
                      jnp.maximum(span - 1, 0))

    def far_copy(h):
        return remote(q_hbm.at[:part, lanes(h)], q_far.at[h], far_tx.at[h], far_rx.at[h],
                      jnp.maximum(span - 2, 0))

    def up_copy(h):
        return remote(up_tx.at[h], up_rx.at[h], up_tx_sem.at[h], up_rx_sem.at[h], up_to)

    def st_copy(h):
        return remote(st_tx.at[h], st_rx.at[h], st_tx_sem.at[h], st_rx_sem.at[h], up_to)

    halo_copy = remote(ext.at[rows : rows + part, :], halo, halo_sem.at[0], halo_sem.at[1], up_to)

    barrier = pltpu.get_barrier_semaphore()
    for away in (-2, -1, 1, 2):

        @pl.when((span + away >= 0) & (span + away < 4))
        def _(away=away):
            pl.semaphore_signal(barrier, inc=1, device_id={"seq": span + away}, device_id_type=MESH_ID)

    pl.semaphore_wait(barrier, jnp.where(has_left & has_right, 3, 2))

    @pl.when(span == 2)
    def _():
        def send_far(h, carry):
            far_copy(h).start()
            return carry

        lax.fori_loop(0, heads, send_far, 0)

    def send_queries(h, carry):
        pl.when(has_left)(lambda: near_copy(h).start())
        pl.when(span == 3)(lambda: far_copy(h).start())
        return carry

    lax.fori_loop(0, heads, send_queries, 0)

    chunks = cols // CHUNK

    def chunk_cols(c):
        return pl.ds(pl.multiple_of(c * CHUNK, CHUNK), CHUNK)

    def gate(lo, hi, at):
        return (feat[1, lo:hi, at].astype(f32) * feat[2, lo:hi, at].astype(f32)).astype(bf16)

    tail_load.wait()

    def gate_tail(c, carry):
        at = chunk_cols(c)
        ext[rows : rows + part, at] = gate(2 * part, rows, at)
        ext[:part, at] = jnp.zeros((part, CHUNK), bf16)
        return carry

    lax.fori_loop(0, chunks, gate_tail, 0)
    pl.when(has_left & has_right)(lambda: halo_copy.start())

    @pl.when(jnp.logical_not(has_left))
    def _():
        def clear(h, carry):
            up_rx[h] = jnp.zeros((rows + part, HD), bf16)
            st_rx[h] = jnp.zeros((8, HD), f32)
            return carry

        lax.fori_loop(0, heads, clear, 0)

    @pl.when(span == 2)
    def _():
        def clear(h, carry):
            q_far[h] = jnp.zeros((part, HD), bf16)
            return carry

        lax.fori_loop(0, heads, clear, 0)

    lens_load.wait()
    left_q = has_left & (base - start_at(base, lens_ref) > 2 * part)
    right_q = has_right & (base + rows - start_at(base + rows, lens_ref) > 2 * part)
    fresh = has_far & right_q & (start_at(base + 2 * rows, lens_ref) < base + rows)
    slot_mine = (span > 1) & (base - rows - start_at(base, lens_ref) > 2 * part)

    def column_iota(first, count):
        return first + lax.broadcasted_iota(jnp.int32, (count, 1), 0)

    own_pos = column_iota(base, rows)
    near_pos = column_iota(base + rows, rows)
    far_pos = column_iota(base + 2 * rows, part)
    key_pos = base + lax.broadcasted_iota(jnp.int32, (1, rows), 1)
    left_pos = base - 2 * part + lax.broadcasted_iota(jnp.int32, (1, 2 * part), 1)
    no_keys = jnp.where(has_left & jnp.logical_not(left_q), 0, FAR)
    no_near = jnp.where(right_q, 0, FAR)
    no_far = jnp.where(fresh, 0, FAR)
    own_start = doc_start(own_pos, lens_ref)
    near_start = doc_start(near_pos, lens_ref) + no_near
    far_start = doc_start(far_pos, lens_ref) + no_far

    def bias(ok):
        return jnp.where(ok, 0.0, NEG).astype(f32)

    b_own[...] = bias((key_pos <= own_pos) & (key_pos >= own_start))
    b_own_l[...] = bias(left_pos >= own_start + no_keys)
    b_near[...] = bias(key_pos >= near_start)
    b_near_l[...] = bias(left_pos >= near_start + no_keys)
    b_far[...] = bias(key_pos >= far_start)

    def dot(x, y):
        return jnp.dot(x, y, preferred_element_type=f32)

    first_cut = jnp.int32(FAR)
    last_cut = jnp.int32(-1)
    end = jnp.int32(0)
    for doc in range(lens_ref.shape[0] - 1):
        end = end + lens_ref[doc]
        first_cut = jnp.where((end > base) & (end < first_cut), end, first_cut)
        last_cut = jnp.where((end < base + rows) & (end > last_cut), end, last_cut)
    cuts = []
    for cut in (first_cut, last_cut):
        valid = (cut > base) & (cut < base + rows)
        block = jnp.where(valid, lax.div(jnp.where(valid, cut - base, 0), part), 0)
        cuts.append((jnp.where(valid, cut, FAR), block))
    win_iota = lax.broadcasted_iota(jnp.int32, (2 * part, 1), 0)
    out_iota = lax.broadcasted_iota(jnp.int32, (part, 1), 0)

    def transform(window, first_pos, from_pos, spec_r, spec_i):
        window = jnp.where(win_iota + first_pos >= from_pos, window, jnp.zeros_like(window))
        return spread(window, spec_r, spec_i)

    def spread(window, spec_r, spec_i):
        wave = dot(fwd_ref[0], window)
        wave_r, wave_i = wave[:part], wave[part:]
        prod = jnp.concatenate(
            (
                (wave_r * spec_r - wave_i * spec_i).astype(bf16),
                (wave_r * spec_i + wave_i * spec_r).astype(bf16),
            ),
            axis=0,
        )
        return dot(inv_ref[0], prod)

    def finish(block, at, sums, fixes):
        for (cut, cut_block), fixed in zip(cuts, fixes):
            cut_from = jnp.where(cut_block == block, cut, FAR)
            sums = jnp.where(out_iota + (base + block * part) >= cut_from, fixed, sums)
        r0 = block * part
        hy_v[r0 : r0 + part, at] = (feat[0, r0 : r0 + part, at].astype(f32) * sums).astype(bf16)

    def hyena_loads():
        front_load.wait()
        mix_load.wait()
        for copy in filter_loads:
            copy.wait()

    def hyena_main(c, carry):
        at = chunk_cols(c)
        ext[part:rows, at] = gate(0, 2 * part, at)
        short = short_ref[:, at]
        head = jnp.concatenate(
            (short[:1] + skip_ref[:, at], short[1:], jnp.zeros((8 - short.shape[0], CHUNK), f32)), axis=0
        )
        filt = jnp.concatenate((med_ref[:8, at] + head, med_ref[8:, at]), axis=0)
        filt_hi = filt.astype(bf16)
        filt_lo = (filt - filt_hi.astype(f32)).astype(bf16)
        both = (
            dot(fwd_ref[0, :, :part], filt_hi)
            + dot(fwd_ref[1, :, :part], filt_hi)
            + dot(fwd_ref[0, :, :part], filt_lo)
        )
        spec[:, at] = both
        spec_r, spec_i = both[:part], both[part:]
        fixes = []
        for index, (cut, cut_block) in enumerate(cuts):
            window = jnp.zeros((2 * part, CHUNK), bf16)
            for block in range(3):
                r0 = block * part
                cut_from = jnp.where(cut_block == block, cut, FAR)
                window = jnp.where(
                    win_iota + (base + r0 - part) >= cut_from, ext[r0 : r0 + 2 * part, at], window
                )
            sums = spread(window, spec_r, spec_i)
            fix[index, :, at] = sums
            fixes.append(sums)
        for block in (1, 2):
            r0 = block * part
            sums = transform(
                ext[r0 : r0 + 2 * part, at], base + r0 - part, start_at(base + r0, lens_ref), spec_r, spec_i
            )
            finish(block, at, sums, fixes)
        return carry

    hy_late = pltpu.make_async_copy(hy_v.at[part:, :], hy_hbm.at[part:, :], hy_sem.at[0])
    hy_first = pltpu.make_async_copy(hy_v.at[:part, :], hy_hbm.at[:part, :], hy_sem.at[1])

    def hyena_first():
        pl.when(has_left)(lambda: halo_copy.wait_recv())

        def one(c, carry):
            at = chunk_cols(c)
            window = jnp.concatenate((halo[:, at], ext[part : 2 * part, at]), axis=0)
            sums = transform(
                window, base - part, start_at(base, lens_ref), spec[:part, at], spec[part:, at]
            )
            finish(0, at, sums, [fix[i, :, at] for i in range(2)])
            return carry

        lax.fori_loop(0, chunks, one, 0)
        hy_first.start()

    @pl.when(has_left)
    def _():
        hyena_loads()
        lax.fori_loop(0, chunks, hyena_main, 0)
        hy_late.start()
        pl.when(sends_far)(hyena_first)

    k_load.wait()
    v_load.wait()
    q_load.wait()
    ones = jnp.ones((rows, HD), bf16)
    eye = lax.broadcasted_iota(jnp.int32, (part, HD), 0) == lax.broadcasted_iota(jnp.int32, (part, HD), 1)
    stat_iota = lax.broadcasted_iota(jnp.int32, (8, HD), 0)
    left_off = jnp.where(left_q, 0.0, NEG)
    slot_off = jnp.where(slot_mine, 0.0, NEG)

    def attend_to(q, keys, values, biases):
        scores = [
            lax.dot_general(q, k, (((1,), (1,)), ((), ())), preferred_element_type=f32) + b
            for k, b in zip(keys, biases)
        ]
        top = jnp.max(scores[0], axis=1, keepdims=True)
        for s in scores[1:]:
            top = jnp.maximum(top, jnp.max(s, axis=1, keepdims=True))
        acc = None
        for s, v in zip(scores, values):
            w = jnp.exp2((s - top) * SCALE2).astype(bf16)
            term = dot(w, v)
            acc = term if acc is None else acc + term
        return acc[:, :HD], acc[:, HD:], top * SCALE2

    spread_from = min(4, heads - chunks - 1)

    def head_step(h, carry):
        at = lanes(h)

        @pl.when(jnp.logical_not(has_left))
        def _():
            pl.when(h == spread_from)(hyena_loads)

            @pl.when((h >= spread_from) & (h < spread_from + chunks))
            def _():
                hyena_main(h - spread_from, 0)

            @pl.when(h == spread_from + chunks)
            def _():
                hy_late.start()
                hyena_first()

        @pl.when(has_left)
        def _():
            up_copy(h).wait_recv()
            st_copy(h).wait_recv()

        k = kv[:, at]
        v = vv[:, at]
        k_left = up_rx[h, : 2 * part, :]
        v_ones = jnp.concatenate((v, ones), axis=1)
        v_left = jnp.concatenate((up_rx[h, 2 * part :, :], ones[: 2 * part]), axis=1)

        @pl.when(has_right)
        def _():
            near_copy(h).wait_recv()
            pl.when(has_far)(lambda: far_copy(h).wait_recv())
            tails = (k[part : 2 * part], k[2 * part :], v[part : 2 * part], v[2 * part :])
            stats = jnp.zeros((8, HD), f32)

            def give(i, out):
                up_tx[h, i * part : (i + 1) * part, :] = jnp.where(
                    right_q, out, tails[i].astype(f32)
                ).astype(bf16)

            def to_row(lse):
                return jnp.sum(jnp.where(eye, lse, 0.0), axis=0, keepdims=True)

            for i in range(3):
                r0 = i * part
                acc, total, top = attend_to(
                    q_near[h, r0 : r0 + part, :],
                    (k, k_left),
                    (v_ones, v_left),
                    (b_near[r0 : r0 + part, :], b_near_l[r0 : r0 + part, :]),
                )
                give(i, acc / total)
                stats = jnp.where(stat_iota == i, to_row(top + jnp.log2(total)), stats)
            passed = up_rx[h, rows:, :].astype(f32)
            passed_stat = st_rx[h]

            acc, total, top = attend_to(q_far[h], (k,), (v_ones,), (b_far[...],))
            give(3, jnp.where(fresh, acc / total, passed))
            lse = to_row(top + jnp.log2(total))
            st_tx[h] = jnp.where(stat_iota == 3, jnp.where(fresh, lse, passed_stat[3:4]), stats)
            up_copy(h).start()
            st_copy(h).start()

        stats_in = st_rx[h]

        def column(i):
            return jnp.sum(jnp.where(eye, stats_in[i : i + 1], 0.0), axis=1, keepdims=True)

        for i in range(3):
            r0 = i * part
            r1 = r0 + part
            acc, total, top = attend_to(
                qv[r0:r1, at],
                (k[:r1], k_left),
                (v_ones[:r1], v_left),
                (b_own[r0:r1, :r1], b_own_l[r0:r1, :]),
            )
            lse = column(i) + left_off
            best = jnp.maximum(top, lse)
            if i == 0:
                slot_lse = column(3) + slot_off
                best = jnp.maximum(best, slot_lse)
            w0 = jnp.exp2(top - best)
            w1 = jnp.exp2(lse - best)
            mixed = acc * w0 + up_rx[h, r0:r1, :].astype(f32) * w1
            norm = total * w0 + w1
            if i == 0:
                w2 = jnp.exp2(slot_lse - best)
                mixed = mixed + up_rx[h, rows:, :].astype(f32) * w2
                norm = norm + w2
            at_v[r0:r1, at] = (mixed / norm).astype(bf16)
        pltpu.make_async_copy(at_v.at[:, at], at_hbm.at[:, at], at_sem.at[h]).start()
        return carry

    lax.fori_loop(0, heads, head_step, 0)
    pl.when(jnp.logical_not(has_left))(lambda: halo_copy.start())
    pl.when(span == 1)(hyena_first)

    def drain(h, carry):
        at = lanes(h)
        pltpu.make_async_copy(at_v.at[:, at], at_hbm.at[:, at], at_sem.at[h]).wait()

        @pl.when(has_right)
        def _():
            up_copy(h).wait_send()
            st_copy(h).wait_send()

        pl.when(has_left)(lambda: near_copy(h).wait_send())
        pl.when(sends_far)(lambda: far_copy(h).wait_send())
        return carry

    lax.fori_loop(0, heads, drain, 0)
    pl.when(has_right)(lambda: halo_copy.wait_send())
    hy_late.wait()
    hy_first.wait()


def land_kernel(hy_src, at_src, hy_dst, at_dst):
    hy_dst[...] = hy_src[...]
    at_dst[...] = at_src[...]


def fused(features, short_filter, medium_filter, skip_gain, attn_query, attn_key, attn_value, lengths):
    rows, cols = attn_query.shape
    part = rows // 3
    heads = cols // HD
    angle = np.pi / (2 * part) * np.outer(2 * np.arange(part) + 1, np.arange(2 * part))
    wave = np.concatenate((np.cos(angle), -np.sin(angle)), axis=0)
    fwd = split_two(wave)
    inv = split_two(wave.T[part:] / part)
    anywhere = pl.BlockSpec(memory_space=pl.ANY)
    out = jax.ShapeDtypeStruct((rows, cols), jnp.bfloat16)

    def buf(*shape):
        return pltpu.VMEM(shape, jnp.bfloat16)

    def wide(*shape):
        return pltpu.VMEM(shape, jnp.float32)

    each = pltpu.SemaphoreType.DMA((heads,))
    made = pl.pallas_call(
        lambda *refs: fused_kernel(rows, cols, *refs),
        out_shape=(out, out),
        in_specs=[pl.BlockSpec(memory_space=pltpu.HBM)] * 10,
        out_specs=(anywhere, anywhere),
        scratch_shapes=[
            pltpu.SMEM(lengths.shape, jnp.int32), wide(*short_filter.shape), wide(part, cols), wide(1, cols),
            buf(*fwd.shape), buf(*inv.shape),
            buf(3, rows, cols), buf(rows, cols), buf(rows, cols), buf(rows, cols),
            buf(rows + part, cols), buf(part, cols),
            buf(heads, rows + part, HD), wide(heads, 8, HD),
            buf(heads, rows, HD), buf(heads, part, HD),
            buf(heads, rows + part, HD), wide(heads, 8, HD),
            wide(rows, rows), wide(rows, 2 * part), wide(rows, rows), wide(rows, 2 * part),
            wide(part, rows),
            wide(2 * part, cols), wide(2, part, cols),
            buf(rows, cols), buf(rows, cols),
            pltpu.SemaphoreType.DMA((12,)), pltpu.SemaphoreType.DMA((2,)), each,
            pltpu.SemaphoreType.DMA((2,)),
        ] + [each] * 8,
        compiler_params=pltpu.CompilerParams(
            collective_id=0, has_side_effects=True, vmem_limit_bytes=60 * 2**20
        ),
        cost_estimate=pl.CostEstimate(
            flops=heads * 32 * part * part * HD * 4, bytes_accessed=16 * 2**20,
            transcendentals=heads * 32 * part * part,
        ),
        name="fused",
    )(
        lengths, features.transpose(1, 0, 2), attn_query, attn_key, attn_value,
        short_filter, medium_filter, skip_gain[None, :], fwd, inv,
    )
    block = pl.BlockSpec((rows, cols // 2), lambda i: (0, i))
    return pl.pallas_call(
        land_kernel,
        grid=(2,),
        out_shape=(out, out),
        in_specs=[block, block],
        out_specs=(block, block),
        compiler_params=pltpu.CompilerParams(vmem_limit_bytes=60 * 2**20),
        cost_estimate=pl.CostEstimate(flops=0, bytes_accessed=8 * rows * cols, transcendentals=0),
        name="land",
    )(*made)


def local(
    features, short_filter, medium_filter, skip_gain, attn_query, attn_key, attn_value, lengths
):
    rows, cols = attn_query.shape
    spans = lax.axis_size("seq")
    taps = medium_filter.shape[0]
    if spans == 4 and rows == 3 * taps and taps == HD and cols % CHUNK == 0 and short_filter.shape[0] < 8:
        return fused(
            features, short_filter, medium_filter, skip_gain, attn_query, attn_key, attn_value, lengths
        )
    if cols % 128 == 0 and taps % 128 == 0 and rows % taps == 0:
        hyena = hyena_fast
    else:
        hyena = hyena_mix
    hyena_out = hyena(features, short_filter, medium_filter, skip_gain, lengths)
    if spans == 4 and rows % 128 == 0 and rows <= 640 and cols % (8 * HD) == 0:
        return attention_fast(attn_query, attn_key, attn_value, lengths, hyena_out)
    return (hyena_out, attention_mix(attn_query, attn_key, attn_value, lengths))


def solution(mesh):
    in_specs = (
        P(("groups", "seq"), None, ("tensor", "sub")),
        P(None, ("tensor", "sub")),
        P(None, ("tensor", "sub")),
        P(("tensor", "sub")),
        P(("groups", "seq"), ("tensor", "sub")),
        P(("groups", "seq"), ("tensor", "sub")),
        P(("groups", "seq"), ("tensor", "sub")),
        P("groups"),
    )
    out_specs = (P(("groups", "seq"), ("tensor", "sub")), P(("groups", "seq"), ("tensor", "sub")))
    return jax.shard_map(local, mesh=mesh, in_specs=in_specs, out_specs=out_specs, check_vma=False)
```

```python
import math

import jax
import jax.numpy as jnp
import numpy as np
from jax import lax
from jax.experimental import pallas as pl
from jax.experimental.pallas import tpu as pltpu
from jax.sharding import PartitionSpec as P

HD = 128


def passed_along(value, axis, by):
    length = lax.axis_size(axis)
    pairs = [(i, i + by) for i in range(length) if 0 <= i + by < length]
    return lax.ppermute(value, axis, pairs)


def doc_of(positions, lengths):
    doc_ends = jnp.cumsum(lengths, dtype=jnp.int32)
    return jnp.sum(
        (positions[:, None] >= doc_ends[None, :]).astype(jnp.int32), axis=1, dtype=jnp.int32
    )


def hyena_mix(features, short_filter, medium_filter, skip_gain, lengths):
    row_count = features.shape[0]
    medium_taps = medium_filter.shape[0]
    rim_rows = medium_taps - 1
    span_index = lax.axis_index("seq")
    queries = features[:, 0].astype(jnp.float32)
    gated = (features[:, 1].astype(jnp.float32) * features[:, 2].astype(jnp.float32)).astype(
        jnp.bfloat16
    )
    gated = lax.optimization_barrier(gated)
    carried = passed_along(gated[row_count - rim_rows :], "seq", 1)
    extended = jnp.concatenate((carried, gated), axis=0)
    ext_positions = (
        span_index * row_count - rim_rows + jnp.arange(row_count + rim_rows, dtype=jnp.int32)
    )
    ext_docs = doc_of(ext_positions, lengths)
    ext_live = ext_positions >= 0
    own_docs = ext_docs[rim_rows:]

    def tap_term(tap_index, filter_bank):
        first_row = rim_rows - tap_index
        window = lax.dynamic_slice_in_dim(extended, first_row, row_count, 0).astype(jnp.float32)
        same_doc = lax.dynamic_slice_in_dim(ext_docs, first_row, row_count, 0) == own_docs
        live_mask = lax.dynamic_slice_in_dim(ext_live, first_row, row_count, 0)
        keep_mask = (same_doc & live_mask).astype(jnp.float32)[:, None]
        taps = lax.dynamic_index_in_dim(filter_bank, tap_index, 0, keepdims=False)
        return taps[None, :] * window * keep_mask

    short_sum = jnp.zeros(gated.shape, jnp.float32)
    for tap_index in range(short_filter.shape[0]):
        short_sum = short_sum + tap_term(tap_index, short_filter)

    def tap_block(block_index, partial_value):
        for offset in range(8):
            partial_value = partial_value + tap_term(block_index * 8 + offset, medium_filter)
        return partial_value

    medium_sum = lax.fori_loop(0, medium_taps // 8, tap_block, jnp.zeros(gated.shape, jnp.float32))
    mixed = queries * (short_sum + medium_sum + skip_gain[None, :] * gated.astype(jnp.float32))
    return mixed.astype(jnp.bfloat16)


def attention_mix(attn_query, attn_key, attn_value, lengths):
    row_count, col_count = attn_query.shape
    heads_here = col_count // HD
    span_index = lax.axis_index("seq")
    query_positions = span_index * row_count + jnp.arange(row_count, dtype=jnp.int32)
    query_docs = doc_of(query_positions, lengths)
    query_heads = attn_query.reshape(row_count, heads_here, HD)
    score_scale = HD ** (-0.5)
    last_query = query_positions[row_count - 1]
    first_query_doc = query_docs[0]

    def absorb(state_now, key_block, value_block, first_row):
        key_count = key_block.shape[0]
        last_key = first_row + key_count - 1
        last_key_doc = doc_of(jnp.reshape(last_key, (1,)), lengths)[0]
        masked_out = (first_row > last_query) | (last_key < 0) | (last_key_doc < first_query_doc)

        def compute(state_in):
            running_max, running_total, running_sum = state_in
            key_heads = key_block.reshape(key_count, heads_here, HD)
            value_heads = value_block.reshape(key_count, heads_here, HD)
            scores = (
                jnp.einsum(
                    "rhd,nhd->hrn", query_heads, key_heads, preferred_element_type=jnp.float32
                )
                * score_scale
            )
            key_positions = first_row + jnp.arange(key_count, dtype=jnp.int32)
            key_docs = doc_of(key_positions, lengths)
            allowed = (
                (key_positions[None, :] <= query_positions[:, None])
                & (key_docs[None, :] == query_docs[:, None])
                & (key_positions >= 0)[None, :]
            )
            masked = jnp.where(allowed[None], scores, -1e30)
            new_max = jnp.maximum(running_max, jnp.max(masked, axis=2))
            rescale = jnp.exp(running_max - new_max)
            weights = jnp.where(allowed[None], jnp.exp(scores - new_max[:, :, None]), 0.0)
            new_total = running_total * rescale + jnp.sum(weights, axis=2)
            product = jnp.einsum(
                "hrn,nhd->hrd",
                weights.astype(jnp.bfloat16),
                value_heads,
                preferred_element_type=jnp.float32,
            )
            new_sum = running_sum * rescale[:, :, None] + product
            return (new_max, new_total, new_sum)

        def keep_state(state_in):
            return state_in

        return lax.cond(masked_out, keep_state, compute, state_now)

    def fold_keys(state_now, pieces, first_row):
        key_all, value_all = pieces
        key_count = key_all.shape[0]
        block_rows = math.gcd(key_count, 1536)
        if block_rows == key_count:
            return absorb(state_now, key_all, value_all, first_row)
        block_total = key_count // block_rows
        key_blocks = key_all.reshape(block_total, block_rows, col_count)
        value_blocks = value_all.reshape(block_total, block_rows, col_count)

        def scan_step(state_inner, block_items):
            key_block, value_block, block_index = block_items
            return (
                absorb(state_inner, key_block, value_block, first_row + block_index * block_rows),
                None,
            )

        state_now, unused = lax.scan(
            scan_step,
            state_now,
            (key_blocks, value_blocks, jnp.arange(block_total, dtype=jnp.int32)),
        )
        return state_now

    initial = (
        jnp.full((heads_here, row_count), -1e30, jnp.float32),
        jnp.zeros((heads_here, row_count), jnp.float32),
        jnp.zeros((heads_here, row_count, HD), jnp.float32),
    )
    state_now = fold_keys(
        initial,
        (
            lax.all_gather(attn_key, "seq", axis=0, tiled=True),
            lax.all_gather(attn_value, "seq", axis=0, tiled=True),
        ),
        jnp.int32(0),
    )
    running_max, running_total, running_sum = state_now
    result = running_sum / running_total[:, :, None]
    return result.transpose(1, 0, 2).reshape(row_count, col_count).astype(jnp.bfloat16)


LOG2E = 1.4426950408889634
LN2 = 0.6931471805599453
SCALE2 = HD**-0.5 * LOG2E
NEG = -1e30
STAT_ROWS = 16


def hyena_kernel(row_count, taps, lens_ref, feat_ref, rim_ref, filt_ref, fwd_ref, inv_ref, out_ref,
                 ext_ref, sum_ref):
    base = lens_ref[lens_ref.shape[0] - 1]
    ext_ref[:taps, :] = rim_ref[...]
    ext_ref[taps:, :] = (
        feat_ref[1].astype(jnp.float32) * feat_ref[2].astype(jnp.float32)
    ).astype(jnp.bfloat16)

    def dot(x, y):
        return jnp.dot(x, y, preferred_element_type=jnp.float32)

    filt = filt_ref[...]
    filt_hi = filt.astype(jnp.bfloat16)
    filt_lo = (filt - filt_hi.astype(jnp.float32)).astype(jnp.bfloat16)
    spec = (
        dot(fwd_ref[0, :, :taps], filt_hi)
        + dot(fwd_ref[1, :, :taps], filt_hi)
        + dot(fwd_ref[0, :, :taps], filt_lo)
    )
    spec_r, spec_i = spec[:taps], spec[taps:]
    win_iota = lax.broadcasted_iota(jnp.int32, (2 * taps, 1), 0)
    out_iota = lax.broadcasted_iota(jnp.int32, (taps, 1), 0)
    for block in range(row_count // taps):
        r0 = block * taps
        start = jnp.int32(0)
        for doc in range(lens_ref.shape[0] - 1):
            end = start + lens_ref[doc]
            first, last = start - base, end - base

            @pl.when((last > r0) & (first < r0 + taps) & (first < last))
            def _(first=first):
                window = ext_ref[r0 : r0 + 2 * taps, :]
                window = jnp.where(win_iota + (r0 - taps) >= first, window, jnp.zeros_like(window))
                wave = dot(fwd_ref[0], window) + dot(fwd_ref[1], window)
                wave_r, wave_i = wave[:taps], wave[taps:]
                prod = jnp.concatenate(
                    (
                        (wave_r * spec_r - wave_i * spec_i).astype(jnp.bfloat16),
                        (wave_r * spec_i + wave_i * spec_r).astype(jnp.bfloat16),
                    ),
                    axis=0,
                )
                sums = dot(inv_ref[0], prod) + dot(inv_ref[1], prod)
                sum_ref[...] = jnp.where(out_iota + r0 >= first, sums, sum_ref[...])

            start = end
        out_ref[r0 : r0 + taps, :] = (
            feat_ref[0, r0 : r0 + taps, :].astype(jnp.float32) * sum_ref[...]
        ).astype(out_ref.dtype)


def split_two(matrix):
    high = matrix.astype(jnp.bfloat16)
    low = (matrix - high.astype(np.float64)).astype(jnp.bfloat16)
    return np.stack((high, low))


def hyena_fast(features, short_filter, medium_filter, skip_gain, lengths):
    row_count, _, cols = features.shape
    taps = medium_filter.shape[0]
    span_index = lax.axis_index("seq")
    streams = features.transpose(1, 0, 2)
    tail = streams[:, row_count - taps :]
    gated_tail = (tail[1].astype(jnp.float32) * tail[2].astype(jnp.float32)).astype(jnp.bfloat16)
    carried = passed_along(gated_tail, "seq", 1)
    head = jnp.concatenate((short_filter[:1] + skip_gain[None, :], short_filter[1:]), axis=0)
    filt = medium_filter + jnp.pad(head, ((0, taps - head.shape[0]), (0, 0)))
    angle = np.pi / (2 * taps) * np.outer(2 * np.arange(taps) + 1, np.arange(2 * taps))
    fwd = split_two(np.concatenate((np.cos(angle), -np.sin(angle)), axis=0))
    inv = split_two(
        np.concatenate((np.cos(angle), -np.sin(angle)), axis=0).T[taps:] / taps
    )
    scalars = jnp.concatenate((lengths, jnp.reshape(span_index * row_count, (1,)).astype(jnp.int32)))
    width = math.gcd(cols, 512)
    return pl.pallas_call(
        lambda *refs: hyena_kernel(row_count, taps, *refs),
        grid=(cols // width,),
        out_shape=jax.ShapeDtypeStruct((row_count, cols), jnp.bfloat16),
        in_specs=[
            pl.BlockSpec(memory_space=pltpu.SMEM),
            pl.BlockSpec((3, row_count, width), lambda i: (0, 0, i)),
            pl.BlockSpec((taps, width), lambda i: (0, i)),
            pl.BlockSpec((taps, width), lambda i: (0, i)),
            pl.BlockSpec(fwd.shape, lambda i: (0, 0, 0)),
            pl.BlockSpec(inv.shape, lambda i: (0, 0, 0)),
        ],
        out_specs=pl.BlockSpec((row_count, width), lambda i: (0, i)),
        scratch_shapes=[
            pltpu.VMEM((row_count + taps, width), jnp.bfloat16),
            pltpu.VMEM((taps, width), jnp.float32),
        ],
        compiler_params=pltpu.CompilerParams(vmem_limit_bytes=32 * 2**20),
        cost_estimate=pl.CostEstimate(
            flops=2 * 9 * 2 * taps * taps * 3 * cols, bytes_accessed=8 * 2**20, transcendentals=0
        ),
        name="hyena",
    )(scalars, streams, carried, filt, fwd, inv)


def doc_start(pos, lens_ref):
    start = jnp.zeros_like(pos)
    end = jnp.int32(0)
    for doc in range(lens_ref.shape[0] - 1):
        end = end + lens_ref[doc]
        start = jnp.where(pos >= end, end, start)
    return start


def attend(query_ref, keys, values, biases, emit):
    rows = query_ref.shape[0]
    step = 128
    ones = jnp.ones((rows, 128), jnp.bfloat16)
    vals = [jnp.concatenate((v[...], ones), axis=1) for v in values]
    for r in range(0, rows, step):
        q = query_ref[r : r + step, :]
        scores = [
            lax.dot_general(q, k[...], (((1,), (1,)), ((), ())),
                            preferred_element_type=jnp.float32) + b[r : r + step, :]
            for k, b in zip(keys, biases)
        ]
        top = jnp.max(scores[0], axis=1, keepdims=True)
        for s in scores[1:]:
            top = jnp.maximum(top, jnp.max(s, axis=1, keepdims=True))
        acc = None
        for s, v in zip(scores, vals):
            w = jnp.exp2((s - top) * SCALE2).astype(jnp.bfloat16)
            part = jnp.dot(w, v, preferred_element_type=jnp.float32)
            acc = part if acc is None else acc + part
        total = acc[:, 128:]
        emit(r, acc[:, :128] / total, top * SCALE2 + jnp.log2(total))


def needs(lens_ref, base, rows, ahead, back):
    q_first = base + ahead * rows
    start = jnp.int32(0)
    end = jnp.int32(0)
    for doc in range(lens_ref.shape[0] - 1):
        end = end + lens_ref[doc]
        start = jnp.where(q_first >= end, end, start)
    return start < base + (1 - back) * rows


def fill_bias(lens_ref, base, rows, ref, ahead, back):
    qpos = base + ahead * rows + lax.broadcasted_iota(jnp.int32, (rows, 1), 0)
    starts = doc_start(qpos, lens_ref)
    kpos = base - back * rows + lax.broadcasted_iota(jnp.int32, (1, rows), 1)
    ref[...] = jnp.where((kpos <= qpos) & (kpos >= starts), 0.0, NEG).astype(jnp.float32)


def near_kernel(rows, lens_ref, q_ref, k_ref, v_ref, k1_ref, v1_ref, k2_ref, v2_ref, all_ref, o_ref,
                b0, b1, b2):
    span = lens_ref[lens_ref.shape[0] - 1]
    base = span * rows
    one = (span >= 1) & needs(lens_ref, base, rows, 0, 1)
    two = (span >= 2) & needs(lens_ref, base, rows, 0, 2)

    @pl.when(pl.program_id(0) == 0)
    def _():
        fill_bias(lens_ref, base, rows, b0, 0, 0)
        pl.when(one)(lambda: fill_bias(lens_ref, base, rows, b1, 0, 1))
        pl.when(two)(lambda: fill_bias(lens_ref, base, rows, b2, 0, 2))

    def emit(r, out, lse):
        o_ref[r : r + 128, :] = out.astype(jnp.bfloat16)

    pl.when(two)(
        lambda: attend(q_ref, (k_ref, k1_ref, k2_ref), (v_ref, v1_ref, v2_ref), (b0, b1, b2), emit)
    )
    pl.when(one & jnp.logical_not(two))(
        lambda: attend(q_ref, (k_ref, k1_ref), (v_ref, v1_ref), (b0, b1), emit)
    )
    pl.when(jnp.logical_not(one))(lambda: attend(q_ref, (k_ref,), (v_ref,), (b0,), emit))


def attn_kernel(rows, lens_ref, q_ref, qa_ref, qb_ref, kp_ref, vp_ref, k_ref, v_ref,
                o_ref, lse_ref, oa_ref, ob_ref, b00, b10, b01, b11, b02):
    span = lens_ref[lens_ref.shape[0] - 1]
    base = span * rows

    def reads(ahead, back):
        return needs(lens_ref, base, rows, ahead, back)

    own_prev = (span == 1) & reads(0, 1)
    a_here = ((span == 1) | (span == 2)) & reads(1, 0)
    a_prev = (span == 1) & reads(1, 1)
    b_here = (span == 1) & reads(2, 0)

    @pl.when(pl.program_id(0) == 0)
    def _():
        lse_ref[...] = jnp.zeros_like(lse_ref)

        def fill(ref, ahead, back):
            fill_bias(lens_ref, base, rows, ref, ahead, back)

        fill(b00, 0, 0)
        pl.when(own_prev)(lambda: fill(b01, 0, 1))
        pl.when(a_here)(lambda: fill(b10, 1, 0))
        pl.when(a_prev)(lambda: fill(b11, 1, 1))
        pl.when(b_here)(lambda: fill(b02, 2, 0))

    step = 128
    head_lane = lax.broadcasted_iota(jnp.int32, (step, 128), 1) == pl.program_id(0)

    def emit_own(r, out, lse):
        o_ref[r : r + step, :] = out.astype(jnp.bfloat16)
        lse_ref[r : r + step, :] = jnp.where(head_lane, lse, lse_ref[r : r + step, :])

    eye = lax.broadcasted_iota(jnp.int32, (128, 128), 0) == lax.broadcasted_iota(
        jnp.int32, (128, 128), 1
    )
    stat_iota = lax.broadcasted_iota(jnp.int32, (STAT_ROWS, 128), 0)

    def emit_to(ref):
        stats = [jnp.zeros((STAT_ROWS, 128), jnp.float32)]

        def emit(r, out, lse):
            ref[r : r + step, :] = out.astype(jnp.bfloat16)
            rest = jnp.sum(jnp.where(eye, lse, 0.0), axis=0, keepdims=True)
            for piece in range(3):
                high = rest.astype(jnp.bfloat16).astype(jnp.float32)
                stats[0] = jnp.where(stat_iota == piece * (rows // step) + r // step, high, stats[0])
                rest = rest - high
            if r + step == rows:
                ref[rows:, :] = stats[0].astype(jnp.bfloat16)

        return emit

    def empty(ref):
        ref[:rows, :] = jnp.zeros((rows, 128), jnp.bfloat16)
        ref[rows:, :] = jnp.where(stat_iota < rows // step, NEG, 0.0).astype(jnp.bfloat16)

    pl.when(own_prev)(lambda: attend(q_ref, (kp_ref, k_ref), (vp_ref, v_ref), (b01, b00), emit_own))
    pl.when(jnp.logical_not(own_prev))(lambda: attend(q_ref, (k_ref,), (v_ref,), (b00,), emit_own))
    pl.when(a_prev)(
        lambda: attend(qa_ref, (kp_ref, k_ref), (vp_ref, v_ref), (b11, b10), emit_to(oa_ref))
    )
    pl.when(a_here & jnp.logical_not(a_prev))(
        lambda: attend(qa_ref, (k_ref,), (v_ref,), (b10,), emit_to(oa_ref))
    )
    pl.when(jnp.logical_not(a_here))(lambda: empty(oa_ref))
    pl.when(b_here)(lambda: attend(qb_ref, (k_ref,), (v_ref,), (b02,), emit_to(ob_ref)))
    pl.when(jnp.logical_not(b_here))(lambda: empty(ob_ref))


def merge_kernel(rows, lens_ref, o_ref, lse_ref, ra_ref, rb_ref, all_ref, out_ref):
    span = lens_ref[lens_ref.shape[0] - 1]
    step = 128
    eye = lax.broadcasted_iota(jnp.int32, (128, 128), 0) == lax.broadcasted_iota(
        jnp.int32, (128, 128), 1
    )

    @pl.when(span < 2)
    def _():
        out_ref[...] = o_ref[...]

    @pl.when(span >= 2)
    def _():
        blocks = rows // step
        head_lane = lax.broadcasted_iota(jnp.int32, (step, 128), 1) == pl.program_id(0)
        stat_a = ra_ref[rows:, :].astype(jnp.float32)
        stat_b = rb_ref[rows:, :].astype(jnp.float32)

        def column(stats, i):
            row = (stats[i : i + 1] + stats[blocks + i : blocks + i + 1]) + stats[
                2 * blocks + i : 2 * blocks + i + 1
            ]
            return jnp.sum(jnp.where(eye, row, 0.0), axis=1, keepdims=True)

        for i in range(blocks):
            r = i * step
            own = jnp.sum(jnp.where(head_lane, lse_ref[r : r + step, :], 0.0), axis=1, keepdims=True)
            lse_a = column(stat_a, i)
            lse_b = jnp.where(span == 3, column(stat_b, i), NEG)
            top = jnp.maximum(own, jnp.maximum(lse_a, lse_b))
            w0 = jnp.exp2(own - top)
            w1 = jnp.exp2(lse_a - top)
            w2 = jnp.exp2(lse_b - top)
            total = (
                o_ref[r : r + step, :].astype(jnp.float32) * w0
                + ra_ref[r : r + step, :].astype(jnp.float32) * w1
                + rb_ref[r : r + step, :].astype(jnp.float32) * w2
            )
            out_ref[r : r + step, :] = (total / (w0 + w1 + w2)).astype(jnp.bfloat16)


def attention_fast(attn_query, attn_key, attn_value, lengths, hyena_out):
    rows, cols = attn_query.shape
    span_index = lax.axis_index("seq")
    scalars = jnp.concatenate((lengths, jnp.reshape(span_index, (1,)).astype(jnp.int32)))
    all_heads = cols // HD
    heads = all_heads * 3 // 8
    near = all_heads - 2 * heads
    width = heads * HD
    smem = pl.BlockSpec(memory_space=pltpu.SMEM)
    block = pl.BlockSpec((rows, HD), lambda h: (0, h))
    tall = pl.BlockSpec((rows + STAT_ROWS, HD), lambda h: (0, h))
    packed = pl.BlockSpec((rows, 128), lambda h: (0, 0))

    def at(offset):
        return pl.BlockSpec((rows, HD), lambda h: (0, offset + h))

    def pair(lo, hi):
        return jnp.concatenate((attn_key[:, lo:hi], attn_value[:, lo:hi]), axis=1)

    sent = []
    for c in range(2):
        qc = attn_query[:, c * width : (c + 1) * width]
        qa = lax.ppermute(qc, "seq", [(2, 1), (3, 2)])
        qb = lax.ppermute(qc, "seq", [(3, 1)])
        kv = pair(c * width, (c + 1) * width)
        sent.append((qa, qb, lax.ppermute(kv, "seq", [(0, 1)])))
    kv = pair(2 * width, cols)
    kv1 = lax.ppermute(kv, "seq", [(0, 1), (1, 2), (2, 3)])
    kv2 = lax.ppermute(kv, "seq", [(0, 2), (1, 3)])
    scalars, hyena_out = lax.optimization_barrier((scalars, hyena_out))
    outs = []
    for c in range(2):
        qa, qb, kvp = sent[c]
        whole = at(c * heads)
        own, lse, oa, ob = pl.pallas_call(
            lambda *refs: attn_kernel(rows, *refs),
            grid=(heads,),
            out_shape=(
                jax.ShapeDtypeStruct((rows, width), jnp.bfloat16),
                jax.ShapeDtypeStruct((rows, 128), jnp.float32),
                jax.ShapeDtypeStruct((rows + STAT_ROWS, width), jnp.bfloat16),
                jax.ShapeDtypeStruct((rows + STAT_ROWS, width), jnp.bfloat16),
            ),
            in_specs=[smem, whole, block, block, block, at(heads), whole, whole],
            out_specs=(block, packed, tall, tall),
            scratch_shapes=[pltpu.VMEM((rows, rows), jnp.float32)] * 5,
            compiler_params=pltpu.CompilerParams(vmem_limit_bytes=32 * 2**20),
            cost_estimate=pl.CostEstimate(
                flops=heads * 5 * rows * rows * HD * 4 * 2,
                bytes_accessed=8 * 2**20,
                transcendentals=heads * 5 * rows * rows,
            ),
            name="attend",
        )(scalars, attn_query, qa, qb, kvp, kvp, attn_key, attn_value)
        ra = lax.ppermute(oa, "seq", [(1, 2), (2, 3)])
        rb = lax.ppermute(ob, "seq", [(1, 3)])
        outs.append((own, lse, ra, rb))
        scalars, _ = lax.optimization_barrier((scalars, own))
    anywhere = pl.BlockSpec(memory_space=pl.ANY)
    whole_out = jax.ShapeDtypeStruct((rows, cols), jnp.bfloat16)
    mine = at(2 * heads)
    result = pl.pallas_call(
        lambda *refs: near_kernel(rows, *refs[:8], None, *refs[8:]),
        grid=(near,),
        out_shape=whole_out,
        in_specs=[smem, mine, mine, mine, block, at(near), block, at(near)],
        out_specs=mine,
        scratch_shapes=[pltpu.VMEM((rows, rows), jnp.float32)] * 3,
        compiler_params=pltpu.CompilerParams(vmem_limit_bytes=32 * 2**20),
        cost_estimate=pl.CostEstimate(
            flops=near * 3 * rows * rows * HD * 4 * 2,
            bytes_accessed=4 * 2**20,
            transcendentals=near * 3 * rows * rows,
        ),
        name="near",
    )(scalars, attn_query, attn_key, attn_value, kv1, kv1, kv2, kv2)
    for c in range(2):
        own, lse, ra, rb = outs[c]
        result = pl.pallas_call(
            lambda *refs: merge_kernel(rows, *refs),
            grid=(heads,),
            out_shape=whole_out,
            in_specs=[smem, block, packed, tall, tall, anywhere],
            out_specs=at(c * heads),
            input_output_aliases={5: 0},
            cost_estimate=pl.CostEstimate(
                flops=rows * width * 16, bytes_accessed=4 * 2**20, transcendentals=0
            ),
            name="merge",
        )(scalars, own, lse, ra, rb, result)
    return hyena_out, result


MESH_ID = pl.DeviceIdType.MESH
FAR = 1 << 20
CHUNK = 256


def start_at(pos, lens_ref):
    start = jnp.int32(0)
    end = jnp.int32(0)
    for doc in range(lens_ref.shape[0] - 1):
        end = end + lens_ref[doc]
        start = jnp.where(pos >= end, end, start)
    return start


def fused_kernel(
    rows, cols, lens_hbm, feat_hbm, q_hbm, k_hbm, v_hbm, short_hbm, med_hbm, skip_hbm, fwd_hbm, inv_hbm,
    hy_hbm, at_hbm,
    lens_ref, short_ref, med_ref, skip_ref, fwd_ref, inv_ref,
    feat, qv, kv, vv, ext, halo, up_rx, st_rx, q_near, q_far, up_tx, st_tx,
    b_own, b_own_l, b_near, b_near_l, b_far, spec, fix, hy_v, at_v,
    load_sem, hy_sem, at_sem, halo_sem, near_tx, near_rx, far_tx, far_rx, up_tx_sem, up_rx_sem,
    st_tx_sem, st_rx_sem,
):
    f32, bf16 = jnp.float32, jnp.bfloat16
    heads = cols // HD
    part = rows // 3
    span = lax.axis_index("seq")
    base = span * rows
    has_left, has_right = span > 0, span < 3
    has_far, sends_far = span < 2, span > 1

    def load(index, src, dst):
        copy = pltpu.make_async_copy(src, dst, load_sem.at[index])
        copy.start()
        return copy

    tail_load = load(0, feat_hbm.at[1:3, 2 * part :, :], feat.at[1:3, 2 * part :, :])
    lens_load = load(6, lens_hbm, lens_ref)
    k_load = load(3, k_hbm, kv)
    v_load = load(4, v_hbm, vv)
    q_load = load(5, q_hbm, qv)
    filter_loads = [
        load(7, short_hbm, short_ref),
        load(8, med_hbm, med_ref),
        load(9, skip_hbm, skip_ref),
        load(10, fwd_hbm, fwd_ref),
        load(11, inv_hbm, inv_ref),
    ]
    front_load = load(1, feat_hbm.at[1:3, : 2 * part, :], feat.at[1:3, : 2 * part, :])
    mix_load = load(2, feat_hbm.at[0], feat.at[0])

    def lanes(h):
        return pl.ds(pl.multiple_of(h * HD, HD), HD)

    def remote(src, dst, tx, rx, to):
        return pltpu.make_async_remote_copy(
            src_ref=src, dst_ref=dst, send_sem=tx, recv_sem=rx, device_id={"seq": to},
            device_id_type=MESH_ID,
        )

    up_to = jnp.minimum(span + 1, 3)

    def near_copy(h):
        return remote(q_hbm.at[:, lanes(h)], q_near.at[h], near_tx.at[h], near_rx.at[h],
                      jnp.maximum(span - 1, 0))

    def far_copy(h):
        return remote(q_hbm.at[:part, lanes(h)], q_far.at[h], far_tx.at[h], far_rx.at[h],
                      jnp.maximum(span - 2, 0))

    def up_copy(h):
        return remote(up_tx.at[h], up_rx.at[h], up_tx_sem.at[h], up_rx_sem.at[h], up_to)

    def st_copy(h):
        return remote(st_tx.at[h], st_rx.at[h], st_tx_sem.at[h], st_rx_sem.at[h], up_to)

    def pass_copy(h):
        return remote(q_near.at[h, :part, :], q_far.at[h], far_tx.at[h], far_rx.at[h],
                      jnp.maximum(span - 1, 0))

    def pass_on(h):
        near_copy(h).wait_recv()
        pass_copy(h).start()
        pl.when(h + 2 < heads)(lambda: near_copy(h + 2).start())

    halo_copies = [
        remote(
            ext.at[rows : rows + part, i * cols // 2 : (i + 1) * cols // 2],
            halo.at[:, i * cols // 2 : (i + 1) * cols // 2],
            halo_sem.at[i], halo_sem.at[2 + i], up_to,
        )
        for i in range(2)
    ]

    barrier = pltpu.get_barrier_semaphore()
    for away in (-2, -1, 1, 2):

        @pl.when((span + away >= 0) & (span + away < 4))
        def _(away=away):
            pl.semaphore_signal(barrier, inc=1, device_id={"seq": span + away}, device_id_type=MESH_ID)

    pl.semaphore_wait(barrier, jnp.where(has_left & has_right, 3, 2))

    @pl.when(sends_far)
    def _():
        def send_queries(h, carry):
            near_copy(h).start()
            pl.when(span == 3)(lambda: far_copy(h).start())
            return carry

        lax.fori_loop(0, heads, send_queries, 0)

    @pl.when(span == 1)
    def _():
        near_copy(0).start()
        near_copy(1).start()

    chunks = cols // CHUNK

    def chunk_cols(c):
        return pl.ds(pl.multiple_of(c * CHUNK, CHUNK), CHUNK)

    def gate(lo, hi, at):
        return (feat[1, lo:hi, at].astype(f32) * feat[2, lo:hi, at].astype(f32)).astype(bf16)

    tail_load.wait()

    def gate_tail(c, carry):
        at = chunk_cols(c)
        ext[rows : rows + part, at] = gate(2 * part, rows, at)
        ext[:part, at] = jnp.zeros((part, CHUNK), bf16)
        return carry

    lax.fori_loop(0, chunks, gate_tail, 0)
    pl.when(has_right)(lambda: halo_copies[0].start())
    pl.when(has_left & has_right)(lambda: halo_copies[1].start())

    @pl.when(jnp.logical_not(has_left))
    def _():
        def clear(h, carry):
            up_rx[h] = jnp.zeros((rows + part, HD), bf16)
            st_rx[h] = jnp.zeros((8, HD), f32)
            return carry

        lax.fori_loop(0, heads, clear, 0)

    @pl.when(span == 2)
    def _():
        def clear(h, carry):
            q_far[h] = jnp.zeros((part, HD), bf16)
            return carry

        lax.fori_loop(0, heads, clear, 0)

    lens_load.wait()
    left_q = has_left & (base - start_at(base, lens_ref) > 2 * part)
    right_q = has_right & (base + rows - start_at(base + rows, lens_ref) > 2 * part)
    fresh = has_far & right_q & (start_at(base + 2 * rows, lens_ref) < base + rows)
    slot_mine = (span > 1) & (base - rows - start_at(base, lens_ref) > 2 * part)

    def column_iota(first, count):
        return first + lax.broadcasted_iota(jnp.int32, (count, 1), 0)

    own_pos = column_iota(base, rows)
    near_pos = column_iota(base + rows, rows)
    far_pos = column_iota(base + 2 * rows, part)
    key_pos = base + lax.broadcasted_iota(jnp.int32, (1, rows), 1)
    left_pos = base - 2 * part + lax.broadcasted_iota(jnp.int32, (1, 2 * part), 1)
    no_keys = jnp.where(has_left & jnp.logical_not(left_q), 0, FAR)
    no_near = jnp.where(right_q, 0, FAR)
    no_far = jnp.where(fresh, 0, FAR)
    own_start = doc_start(own_pos, lens_ref)
    near_start = doc_start(near_pos, lens_ref) + no_near
    far_start = doc_start(far_pos, lens_ref) + no_far

    def bias(ok):
        return jnp.where(ok, 0.0, NEG).astype(f32)

    b_own[...] = bias((key_pos <= own_pos) & (key_pos >= own_start))
    b_own_l[...] = bias(left_pos >= own_start + no_keys)
    b_near[...] = bias(key_pos >= near_start)
    b_near_l[...] = bias(left_pos >= near_start + no_keys)
    b_far[...] = bias(key_pos >= far_start)

    def dot(x, y):
        return jnp.dot(x, y, preferred_element_type=f32)

    first_cut = jnp.int32(FAR)
    last_cut = jnp.int32(-1)
    end = jnp.int32(0)
    for doc in range(lens_ref.shape[0] - 1):
        end = end + lens_ref[doc]
        first_cut = jnp.where((end > base) & (end < first_cut), end, first_cut)
        last_cut = jnp.where((end < base + rows) & (end > last_cut), end, last_cut)
    cuts = []
    for cut in (first_cut, last_cut):
        valid = (cut > base) & (cut < base + rows)
        block = jnp.where(valid, lax.div(jnp.where(valid, cut - base, 0), part), 0)
        cuts.append((jnp.where(valid, cut, FAR), block))
    win_iota = lax.broadcasted_iota(jnp.int32, (2 * part, 1), 0)
    out_iota = lax.broadcasted_iota(jnp.int32, (part, 1), 0)

    def transform(window, first_pos, from_pos, spec_r, spec_i):
        window = jnp.where(win_iota + first_pos >= from_pos, window, jnp.zeros_like(window))
        return spread(window, spec_r, spec_i)

    def spread(window, spec_r, spec_i):
        wave = dot(fwd_ref[0], window)
        wave_r, wave_i = wave[:part], wave[part:]
        prod = jnp.concatenate(
            (
                (wave_r * spec_r - wave_i * spec_i).astype(bf16),
                (wave_r * spec_i + wave_i * spec_r).astype(bf16),
            ),
            axis=0,
        )
        return dot(inv_ref[0], prod)

    def finish(block, at, sums, fixes):
        for (cut, cut_block), fixed in zip(cuts, fixes):
            cut_from = jnp.where(cut_block == block, cut, FAR)
            sums = jnp.where(out_iota + (base + block * part) >= cut_from, fixed, sums)
        r0 = block * part
        hy_v[r0 : r0 + part, at] = (feat[0, r0 : r0 + part, at].astype(f32) * sums).astype(bf16)

    def hyena_loads():
        front_load.wait()
        mix_load.wait()
        for copy in filter_loads:
            copy.wait()

    def hyena_main(c, carry):
        at = chunk_cols(c)
        ext[part:rows, at] = gate(0, 2 * part, at)
        short = short_ref[:, at]
        head = jnp.concatenate(
            (short[:1] + skip_ref[:, at], short[1:], jnp.zeros((8 - short.shape[0], CHUNK), f32)), axis=0
        )
        filt = jnp.concatenate((med_ref[:8, at] + head, med_ref[8:, at]), axis=0)
        filt_hi = filt.astype(bf16)
        filt_lo = (filt - filt_hi.astype(f32)).astype(bf16)
        both = (
            dot(fwd_ref[0, :, :part], filt_hi)
            + dot(fwd_ref[1, :, :part], filt_hi)
            + dot(fwd_ref[0, :, :part], filt_lo)
        )
        spec[:, at] = both
        spec_r, spec_i = both[:part], both[part:]
        fixes = []
        for index, (cut, cut_block) in enumerate(cuts):
            window = jnp.zeros((2 * part, CHUNK), bf16)
            for block in range(3):
                r0 = block * part
                cut_from = jnp.where(cut_block == block, cut, FAR)
                window = jnp.where(
                    win_iota + (base + r0 - part) >= cut_from, ext[r0 : r0 + 2 * part, at], window
                )
            sums = spread(window, spec_r, spec_i)
            fix[index, :, at] = sums
            fixes.append(sums)
        for block in (1, 2):
            r0 = block * part
            sums = transform(
                ext[r0 : r0 + 2 * part, at], base + r0 - part, start_at(base + r0, lens_ref), spec_r, spec_i
            )
            finish(block, at, sums, fixes)
        return carry

    hy_late = pltpu.make_async_copy(hy_v.at[part:, :], hy_hbm.at[part:, :], hy_sem.at[0])
    hy_first = pltpu.make_async_copy(hy_v.at[:part, :], hy_hbm.at[:part, :], hy_sem.at[1])

    def hyena_first():
        @pl.when(has_left)
        def _():
            for copy in halo_copies:
                copy.wait_recv()

        def one(c, carry):
            at = chunk_cols(c)
            window = jnp.concatenate((halo[:, at], ext[part : 2 * part, at]), axis=0)
            sums = transform(
                window, base - part, start_at(base, lens_ref), spec[:part, at], spec[part:, at]
            )
            finish(0, at, sums, [fix[i, :, at] for i in range(2)])
            return carry

        lax.fori_loop(0, chunks, one, 0)
        hy_first.start()

    @pl.when(has_left)
    def _():
        hyena_loads()

        def step(c, carry):
            for h, when in enumerate((0, 3, 5)):

                @pl.when((span == 1) & (c == min(when, chunks - 1)))
                def _(h=h):
                    pass_on(h)

            return hyena_main(c, carry)

        lax.fori_loop(0, chunks, step, 0)
        hy_late.start()
        pl.when(sends_far)(hyena_first)

    k_load.wait()
    v_load.wait()
    q_load.wait()
    ones = jnp.ones((rows, HD), bf16)
    eye = lax.broadcasted_iota(jnp.int32, (part, HD), 0) == lax.broadcasted_iota(jnp.int32, (part, HD), 1)
    stat_iota = lax.broadcasted_iota(jnp.int32, (8, HD), 0)
    left_off = jnp.where(left_q, 0.0, NEG)
    slot_off = jnp.where(slot_mine, 0.0, NEG)

    def attend_to(q, keys, values, biases):
        scores = [
            lax.dot_general(q, k, (((1,), (1,)), ((), ())), preferred_element_type=f32) + b
            for k, b in zip(keys, biases)
        ]
        top = jnp.max(scores[0], axis=1, keepdims=True)
        for s in scores[1:]:
            top = jnp.maximum(top, jnp.max(s, axis=1, keepdims=True))
        acc = None
        for s, v in zip(scores, values):
            w = jnp.exp2((s - top) * SCALE2).astype(bf16)
            term = dot(w, v)
            acc = term if acc is None else acc + term
        return acc[:, :HD], acc[:, HD:], top * SCALE2

    spread_from = min(4, heads - chunks - 1)

    def head_step(h, carry):
        at = lanes(h)

        @pl.when(jnp.logical_not(has_left))
        def _():
            pl.when(h == spread_from)(hyena_loads)

            @pl.when((h >= spread_from) & (h < spread_from + chunks))
            def _():
                hyena_main(h - spread_from, 0)

            @pl.when(h == spread_from + chunks)
            def _():
                hy_late.start()
                hyena_first()

        @pl.when(has_left)
        def _():
            up_copy(h).wait_recv()
            st_copy(h).wait_recv()

        k = kv[:, at]
        v = vv[:, at]
        k_left = up_rx[h, : 2 * part, :]
        v_ones = jnp.concatenate((v, ones), axis=1)
        v_left = jnp.concatenate((up_rx[h, 2 * part :, :], ones[: 2 * part]), axis=1)

        @pl.when(has_right)
        def _():
            pl.when(span != 1)(lambda: near_copy(h).wait_recv())
            pl.when(has_far)(lambda: far_copy(h).wait_recv())
            tails = (k[part : 2 * part], k[2 * part :], v[part : 2 * part], v[2 * part :])
            stats = jnp.zeros((8, HD), f32)

            def give(i, out):
                up_tx[h, i * part : (i + 1) * part, :] = jnp.where(
                    right_q, out, tails[i].astype(f32)
                ).astype(bf16)

            def to_row(lse):
                return jnp.sum(jnp.where(eye, lse, 0.0), axis=0, keepdims=True)

            for i in range(3):
                r0 = i * part
                acc, total, top = attend_to(
                    q_near[h, r0 : r0 + part, :],
                    (k, k_left),
                    (v_ones, v_left),
                    (b_near[r0 : r0 + part, :], b_near_l[r0 : r0 + part, :]),
                )
                give(i, acc / total)
                stats = jnp.where(stat_iota == i, to_row(top + jnp.log2(total)), stats)
            passed = up_rx[h, rows:, :].astype(f32)
            passed_stat = st_rx[h]

            acc, total, top = attend_to(q_far[h], (k,), (v_ones,), (b_far[...],))
            give(3, jnp.where(fresh, acc / total, passed))
            lse = to_row(top + jnp.log2(total))
            st_tx[h] = jnp.where(stat_iota == 3, jnp.where(fresh, lse, passed_stat[3:4]), stats)
            up_copy(h).start()
            st_copy(h).start()
            pl.when((span == 1) & (h + 3 < heads))(lambda: pass_on(h + 3))

        stats_in = st_rx[h]

        def column(i):
            return jnp.sum(jnp.where(eye, stats_in[i : i + 1], 0.0), axis=1, keepdims=True)

        for i in range(3):
            r0 = i * part
            r1 = r0 + part
            acc, total, top = attend_to(
                qv[r0:r1, at],
                (k[:r1], k_left),
                (v_ones[:r1], v_left),
                (b_own[r0:r1, :r1], b_own_l[r0:r1, :]),
            )
            lse = column(i) + left_off
            best = jnp.maximum(top, lse)
            if i == 0:
                slot_lse = column(3) + slot_off
                best = jnp.maximum(best, slot_lse)
            w0 = jnp.exp2(top - best)
            w1 = jnp.exp2(lse - best)
            mixed = acc * w0 + up_rx[h, r0:r1, :].astype(f32) * w1
            norm = total * w0 + w1
            if i == 0:
                w2 = jnp.exp2(slot_lse - best)
                mixed = mixed + up_rx[h, rows:, :].astype(f32) * w2
                norm = norm + w2
            at_v[r0:r1, at] = (mixed / norm).astype(bf16)
        pltpu.make_async_copy(at_v.at[:, at], at_hbm.at[:, at], at_sem.at[h]).start()
        return carry

    lax.fori_loop(0, heads, head_step, 0)
    pl.when(jnp.logical_not(has_left))(lambda: halo_copies[1].start())
    pl.when(span == 1)(hyena_first)

    def drain(h, carry):
        at = lanes(h)
        pltpu.make_async_copy(at_v.at[:, at], at_hbm.at[:, at], at_sem.at[h]).wait()

        @pl.when(has_right)
        def _():
            up_copy(h).wait_send()
            st_copy(h).wait_send()

        pl.when(has_left)(lambda: near_copy(h).wait_send())
        pl.when(span == 3)(lambda: far_copy(h).wait_send())
        pl.when(span == 1)(lambda: pass_copy(h).wait_send())
        return carry

    lax.fori_loop(0, heads, drain, 0)

    @pl.when(has_right)
    def _():
        for copy in halo_copies:
            copy.wait_send()

    hy_late.wait()
    hy_first.wait()


def land_kernel(hy_src, at_src, hy_dst, at_dst):
    hy_dst[...] = hy_src[...]
    at_dst[...] = at_src[...]


def fused(features, short_filter, medium_filter, skip_gain, attn_query, attn_key, attn_value, lengths):
    rows, cols = attn_query.shape
    part = rows // 3
    heads = cols // HD
    angle = np.pi / (2 * part) * np.outer(2 * np.arange(part) + 1, np.arange(2 * part))
    wave = np.concatenate((np.cos(angle), -np.sin(angle)), axis=0)
    fwd = split_two(wave)
    inv = split_two(wave.T[part:] / part)
    anywhere = pl.BlockSpec(memory_space=pl.ANY)
    out = jax.ShapeDtypeStruct((rows, cols), jnp.bfloat16)

    def buf(*shape):
        return pltpu.VMEM(shape, jnp.bfloat16)

    def wide(*shape):
        return pltpu.VMEM(shape, jnp.float32)

    each = pltpu.SemaphoreType.DMA((heads,))
    made = pl.pallas_call(
        lambda *refs: fused_kernel(rows, cols, *refs),
        out_shape=(out, out),
        in_specs=[pl.BlockSpec(memory_space=pltpu.HBM)] * 10,
        out_specs=(anywhere, anywhere),
        scratch_shapes=[
            pltpu.SMEM(lengths.shape, jnp.int32), wide(*short_filter.shape), wide(part, cols), wide(1, cols),
            buf(*fwd.shape), buf(*inv.shape),
            buf(3, rows, cols), buf(rows, cols), buf(rows, cols), buf(rows, cols),
            buf(rows + part, cols), buf(part, cols),
            buf(heads, rows + part, HD), wide(heads, 8, HD),
            buf(heads, rows, HD), buf(heads, part, HD),
            buf(heads, rows + part, HD), wide(heads, 8, HD),
            wide(rows, rows), wide(rows, 2 * part), wide(rows, rows), wide(rows, 2 * part),
            wide(part, rows),
            wide(2 * part, cols), wide(2, part, cols),
            buf(rows, cols), buf(rows, cols),
            pltpu.SemaphoreType.DMA((12,)), pltpu.SemaphoreType.DMA((2,)), each,
            pltpu.SemaphoreType.DMA((4,)),
        ] + [each] * 8,
        compiler_params=pltpu.CompilerParams(
            collective_id=0, has_side_effects=True, vmem_limit_bytes=60 * 2**20
        ),
        cost_estimate=pl.CostEstimate(
            flops=heads * 32 * part * part * HD * 4, bytes_accessed=16 * 2**20,
            transcendentals=heads * 32 * part * part,
        ),
        name="fused",
    )(
        lengths, features.transpose(1, 0, 2), attn_query, attn_key, attn_value,
        short_filter, medium_filter, skip_gain[None, :], fwd, inv,
    )
    block = pl.BlockSpec((rows, cols // 2), lambda i: (0, i))
    return pl.pallas_call(
        land_kernel,
        grid=(2,),
        out_shape=(out, out),
        in_specs=[block, block],
        out_specs=(block, block),
        compiler_params=pltpu.CompilerParams(vmem_limit_bytes=60 * 2**20),
        cost_estimate=pl.CostEstimate(flops=0, bytes_accessed=8 * rows * cols, transcendentals=0),
        name="land",
    )(*made)


def local(
    features, short_filter, medium_filter, skip_gain, attn_query, attn_key, attn_value, lengths
):
    rows, cols = attn_query.shape
    spans = lax.axis_size("seq")
    taps = medium_filter.shape[0]
    if spans == 4 and rows == 3 * taps and taps == HD and cols % CHUNK == 0 and short_filter.shape[0] < 8:
        return fused(
            features, short_filter, medium_filter, skip_gain, attn_query, attn_key, attn_value, lengths
        )
    if cols % 128 == 0 and taps % 128 == 0 and rows % taps == 0:
        hyena = hyena_fast
    else:
        hyena = hyena_mix
    hyena_out = hyena(features, short_filter, medium_filter, skip_gain, lengths)
    if spans == 4 and rows % 128 == 0 and rows <= 640 and cols % (8 * HD) == 0:
        return attention_fast(attn_query, attn_key, attn_value, lengths, hyena_out)
    return (hyena_out, attention_mix(attn_query, attn_key, attn_value, lengths))


def solution(mesh):
    in_specs = (
        P(("groups", "seq"), None, ("tensor", "sub")),
        P(None, ("tensor", "sub")),
        P(None, ("tensor", "sub")),
        P(("tensor", "sub")),
        P(("groups", "seq"), ("tensor", "sub")),
        P(("groups", "seq"), ("tensor", "sub")),
        P(("groups", "seq"), ("tensor", "sub")),
        P("groups"),
    )
    out_specs = (P(("groups", "seq"), ("tensor", "sub")), P(("groups", "seq"), ("tensor", "sub")))
    return jax.shard_map(local, mesh=mesh, in_specs=in_specs, out_specs=out_specs, check_vma=False)
```

```python
import math

import jax
import jax.numpy as jnp
import numpy as np
from jax import lax
from jax.experimental import pallas as pl
from jax.experimental.pallas import tpu as pltpu
from jax.sharding import PartitionSpec as P

HD = 128


def passed_along(value, axis, by):
    length = lax.axis_size(axis)
    pairs = [(i, i + by) for i in range(length) if 0 <= i + by < length]
    return lax.ppermute(value, axis, pairs)


def doc_of(positions, lengths):
    doc_ends = jnp.cumsum(lengths, dtype=jnp.int32)
    return jnp.sum(
        (positions[:, None] >= doc_ends[None, :]).astype(jnp.int32), axis=1, dtype=jnp.int32
    )


def hyena_mix(features, short_filter, medium_filter, skip_gain, lengths):
    row_count = features.shape[0]
    medium_taps = medium_filter.shape[0]
    rim_rows = medium_taps - 1
    span_index = lax.axis_index("seq")
    queries = features[:, 0].astype(jnp.float32)
    gated = (features[:, 1].astype(jnp.float32) * features[:, 2].astype(jnp.float32)).astype(
        jnp.bfloat16
    )
    gated = lax.optimization_barrier(gated)
    carried = passed_along(gated[row_count - rim_rows :], "seq", 1)
    extended = jnp.concatenate((carried, gated), axis=0)
    ext_positions = (
        span_index * row_count - rim_rows + jnp.arange(row_count + rim_rows, dtype=jnp.int32)
    )
    ext_docs = doc_of(ext_positions, lengths)
    ext_live = ext_positions >= 0
    own_docs = ext_docs[rim_rows:]

    def tap_term(tap_index, filter_bank):
        first_row = rim_rows - tap_index
        window = lax.dynamic_slice_in_dim(extended, first_row, row_count, 0).astype(jnp.float32)
        same_doc = lax.dynamic_slice_in_dim(ext_docs, first_row, row_count, 0) == own_docs
        live_mask = lax.dynamic_slice_in_dim(ext_live, first_row, row_count, 0)
        keep_mask = (same_doc & live_mask).astype(jnp.float32)[:, None]
        taps = lax.dynamic_index_in_dim(filter_bank, tap_index, 0, keepdims=False)
        return taps[None, :] * window * keep_mask

    short_sum = jnp.zeros(gated.shape, jnp.float32)
    for tap_index in range(short_filter.shape[0]):
        short_sum = short_sum + tap_term(tap_index, short_filter)

    def tap_block(block_index, partial_value):
        for offset in range(8):
            partial_value = partial_value + tap_term(block_index * 8 + offset, medium_filter)
        return partial_value

    medium_sum = lax.fori_loop(0, medium_taps // 8, tap_block, jnp.zeros(gated.shape, jnp.float32))
    mixed = queries * (short_sum + medium_sum + skip_gain[None, :] * gated.astype(jnp.float32))
    return mixed.astype(jnp.bfloat16)


def attention_mix(attn_query, attn_key, attn_value, lengths):
    row_count, col_count = attn_query.shape
    heads_here = col_count // HD
    span_index = lax.axis_index("seq")
    query_positions = span_index * row_count + jnp.arange(row_count, dtype=jnp.int32)
    query_docs = doc_of(query_positions, lengths)
    query_heads = attn_query.reshape(row_count, heads_here, HD)
    score_scale = HD ** (-0.5)
    last_query = query_positions[row_count - 1]
    first_query_doc = query_docs[0]

    def absorb(state_now, key_block, value_block, first_row):
        key_count = key_block.shape[0]
        last_key = first_row + key_count - 1
        last_key_doc = doc_of(jnp.reshape(last_key, (1,)), lengths)[0]
        masked_out = (first_row > last_query) | (last_key < 0) | (last_key_doc < first_query_doc)

        def compute(state_in):
            running_max, running_total, running_sum = state_in
            key_heads = key_block.reshape(key_count, heads_here, HD)
            value_heads = value_block.reshape(key_count, heads_here, HD)
            scores = (
                jnp.einsum(
                    "rhd,nhd->hrn", query_heads, key_heads, preferred_element_type=jnp.float32
                )
                * score_scale
            )
            key_positions = first_row + jnp.arange(key_count, dtype=jnp.int32)
            key_docs = doc_of(key_positions, lengths)
            allowed = (
                (key_positions[None, :] <= query_positions[:, None])
                & (key_docs[None, :] == query_docs[:, None])
                & (key_positions >= 0)[None, :]
            )
            masked = jnp.where(allowed[None], scores, -1e30)
            new_max = jnp.maximum(running_max, jnp.max(masked, axis=2))
            rescale = jnp.exp(running_max - new_max)
            weights = jnp.where(allowed[None], jnp.exp(scores - new_max[:, :, None]), 0.0)
            new_total = running_total * rescale + jnp.sum(weights, axis=2)
            product = jnp.einsum(
                "hrn,nhd->hrd",
                weights.astype(jnp.bfloat16),
                value_heads,
                preferred_element_type=jnp.float32,
            )
            new_sum = running_sum * rescale[:, :, None] + product
            return (new_max, new_total, new_sum)

        def keep_state(state_in):
            return state_in

        return lax.cond(masked_out, keep_state, compute, state_now)

    def fold_keys(state_now, pieces, first_row):
        key_all, value_all = pieces
        key_count = key_all.shape[0]
        block_rows = math.gcd(key_count, 1536)
        if block_rows == key_count:
            return absorb(state_now, key_all, value_all, first_row)
        block_total = key_count // block_rows
        key_blocks = key_all.reshape(block_total, block_rows, col_count)
        value_blocks = value_all.reshape(block_total, block_rows, col_count)

        def scan_step(state_inner, block_items):
            key_block, value_block, block_index = block_items
            return (
                absorb(state_inner, key_block, value_block, first_row + block_index * block_rows),
                None,
            )

        state_now, unused = lax.scan(
            scan_step,
            state_now,
            (key_blocks, value_blocks, jnp.arange(block_total, dtype=jnp.int32)),
        )
        return state_now

    initial = (
        jnp.full((heads_here, row_count), -1e30, jnp.float32),
        jnp.zeros((heads_here, row_count), jnp.float32),
        jnp.zeros((heads_here, row_count, HD), jnp.float32),
    )
    state_now = fold_keys(
        initial,
        (
            lax.all_gather(attn_key, "seq", axis=0, tiled=True),
            lax.all_gather(attn_value, "seq", axis=0, tiled=True),
        ),
        jnp.int32(0),
    )
    running_max, running_total, running_sum = state_now
    result = running_sum / running_total[:, :, None]
    return result.transpose(1, 0, 2).reshape(row_count, col_count).astype(jnp.bfloat16)


LOG2E = 1.4426950408889634
LN2 = 0.6931471805599453
SCALE2 = HD**-0.5 * LOG2E
NEG = -1e30
STAT_ROWS = 16


def hyena_kernel(row_count, taps, lens_ref, feat_ref, rim_ref, filt_ref, fwd_ref, inv_ref, out_ref,
                 ext_ref, sum_ref):
    base = lens_ref[lens_ref.shape[0] - 1]
    ext_ref[:taps, :] = rim_ref[...]
    ext_ref[taps:, :] = (
        feat_ref[1].astype(jnp.float32) * feat_ref[2].astype(jnp.float32)
    ).astype(jnp.bfloat16)

    def dot(x, y):
        return jnp.dot(x, y, preferred_element_type=jnp.float32)

    filt = filt_ref[...]
    filt_hi = filt.astype(jnp.bfloat16)
    filt_lo = (filt - filt_hi.astype(jnp.float32)).astype(jnp.bfloat16)
    spec = (
        dot(fwd_ref[0, :, :taps], filt_hi)
        + dot(fwd_ref[1, :, :taps], filt_hi)
        + dot(fwd_ref[0, :, :taps], filt_lo)
    )
    spec_r, spec_i = spec[:taps], spec[taps:]
    win_iota = lax.broadcasted_iota(jnp.int32, (2 * taps, 1), 0)
    out_iota = lax.broadcasted_iota(jnp.int32, (taps, 1), 0)
    for block in range(row_count // taps):
        r0 = block * taps
        start = jnp.int32(0)
        for doc in range(lens_ref.shape[0] - 1):
            end = start + lens_ref[doc]
            first, last = start - base, end - base

            @pl.when((last > r0) & (first < r0 + taps) & (first < last))
            def _(first=first):
                window = ext_ref[r0 : r0 + 2 * taps, :]
                window = jnp.where(win_iota + (r0 - taps) >= first, window, jnp.zeros_like(window))
                wave = dot(fwd_ref[0], window) + dot(fwd_ref[1], window)
                wave_r, wave_i = wave[:taps], wave[taps:]
                prod = jnp.concatenate(
                    (
                        (wave_r * spec_r - wave_i * spec_i).astype(jnp.bfloat16),
                        (wave_r * spec_i + wave_i * spec_r).astype(jnp.bfloat16),
                    ),
                    axis=0,
                )
                sums = dot(inv_ref[0], prod) + dot(inv_ref[1], prod)
                sum_ref[...] = jnp.where(out_iota + r0 >= first, sums, sum_ref[...])

            start = end
        out_ref[r0 : r0 + taps, :] = (
            feat_ref[0, r0 : r0 + taps, :].astype(jnp.float32) * sum_ref[...]
        ).astype(out_ref.dtype)


def split_two(matrix):
    high = matrix.astype(jnp.bfloat16)
    low = (matrix - high.astype(np.float64)).astype(jnp.bfloat16)
    return np.stack((high, low))


def hyena_fast(features, short_filter, medium_filter, skip_gain, lengths):
    row_count, _, cols = features.shape
    taps = medium_filter.shape[0]
    span_index = lax.axis_index("seq")
    streams = features.transpose(1, 0, 2)
    tail = streams[:, row_count - taps :]
    gated_tail = (tail[1].astype(jnp.float32) * tail[2].astype(jnp.float32)).astype(jnp.bfloat16)
    carried = passed_along(gated_tail, "seq", 1)
    head = jnp.concatenate((short_filter[:1] + skip_gain[None, :], short_filter[1:]), axis=0)
    filt = medium_filter + jnp.pad(head, ((0, taps - head.shape[0]), (0, 0)))
    angle = np.pi / (2 * taps) * np.outer(2 * np.arange(taps) + 1, np.arange(2 * taps))
    fwd = split_two(np.concatenate((np.cos(angle), -np.sin(angle)), axis=0))
    inv = split_two(
        np.concatenate((np.cos(angle), -np.sin(angle)), axis=0).T[taps:] / taps
    )
    scalars = jnp.concatenate((lengths, jnp.reshape(span_index * row_count, (1,)).astype(jnp.int32)))
    width = math.gcd(cols, 512)
    return pl.pallas_call(
        lambda *refs: hyena_kernel(row_count, taps, *refs),
        grid=(cols // width,),
        out_shape=jax.ShapeDtypeStruct((row_count, cols), jnp.bfloat16),
        in_specs=[
            pl.BlockSpec(memory_space=pltpu.SMEM),
            pl.BlockSpec((3, row_count, width), lambda i: (0, 0, i)),
            pl.BlockSpec((taps, width), lambda i: (0, i)),
            pl.BlockSpec((taps, width), lambda i: (0, i)),
            pl.BlockSpec(fwd.shape, lambda i: (0, 0, 0)),
            pl.BlockSpec(inv.shape, lambda i: (0, 0, 0)),
        ],
        out_specs=pl.BlockSpec((row_count, width), lambda i: (0, i)),
        scratch_shapes=[
            pltpu.VMEM((row_count + taps, width), jnp.bfloat16),
            pltpu.VMEM((taps, width), jnp.float32),
        ],
        compiler_params=pltpu.CompilerParams(vmem_limit_bytes=32 * 2**20),
        cost_estimate=pl.CostEstimate(
            flops=2 * 9 * 2 * taps * taps * 3 * cols, bytes_accessed=8 * 2**20, transcendentals=0
        ),
        name="hyena",
    )(scalars, streams, carried, filt, fwd, inv)


def doc_start(pos, lens_ref):
    start = jnp.zeros_like(pos)
    end = jnp.int32(0)
    for doc in range(lens_ref.shape[0] - 1):
        end = end + lens_ref[doc]
        start = jnp.where(pos >= end, end, start)
    return start


def attend(query_ref, keys, values, biases, emit):
    rows = query_ref.shape[0]
    step = 128
    ones = jnp.ones((rows, 128), jnp.bfloat16)
    vals = [jnp.concatenate((v[...], ones), axis=1) for v in values]
    for r in range(0, rows, step):
        q = query_ref[r : r + step, :]
        scores = [
            lax.dot_general(q, k[...], (((1,), (1,)), ((), ())),
                            preferred_element_type=jnp.float32) + b[r : r + step, :]
            for k, b in zip(keys, biases)
        ]
        top = jnp.max(scores[0], axis=1, keepdims=True)
        for s in scores[1:]:
            top = jnp.maximum(top, jnp.max(s, axis=1, keepdims=True))
        acc = None
        for s, v in zip(scores, vals):
            w = jnp.exp2((s - top) * SCALE2).astype(jnp.bfloat16)
            part = jnp.dot(w, v, preferred_element_type=jnp.float32)
            acc = part if acc is None else acc + part
        total = acc[:, 128:]
        emit(r, acc[:, :128] / total, top * SCALE2 + jnp.log2(total))


def needs(lens_ref, base, rows, ahead, back):
    q_first = base + ahead * rows
    start = jnp.int32(0)
    end = jnp.int32(0)
    for doc in range(lens_ref.shape[0] - 1):
        end = end + lens_ref[doc]
        start = jnp.where(q_first >= end, end, start)
    return start < base + (1 - back) * rows


def fill_bias(lens_ref, base, rows, ref, ahead, back):
    qpos = base + ahead * rows + lax.broadcasted_iota(jnp.int32, (rows, 1), 0)
    starts = doc_start(qpos, lens_ref)
    kpos = base - back * rows + lax.broadcasted_iota(jnp.int32, (1, rows), 1)
    ref[...] = jnp.where((kpos <= qpos) & (kpos >= starts), 0.0, NEG).astype(jnp.float32)


def near_kernel(rows, lens_ref, q_ref, k_ref, v_ref, k1_ref, v1_ref, k2_ref, v2_ref, all_ref, o_ref,
                b0, b1, b2):
    span = lens_ref[lens_ref.shape[0] - 1]
    base = span * rows
    one = (span >= 1) & needs(lens_ref, base, rows, 0, 1)
    two = (span >= 2) & needs(lens_ref, base, rows, 0, 2)

    @pl.when(pl.program_id(0) == 0)
    def _():
        fill_bias(lens_ref, base, rows, b0, 0, 0)
        pl.when(one)(lambda: fill_bias(lens_ref, base, rows, b1, 0, 1))
        pl.when(two)(lambda: fill_bias(lens_ref, base, rows, b2, 0, 2))

    def emit(r, out, lse):
        o_ref[r : r + 128, :] = out.astype(jnp.bfloat16)

    pl.when(two)(
        lambda: attend(q_ref, (k_ref, k1_ref, k2_ref), (v_ref, v1_ref, v2_ref), (b0, b1, b2), emit)
    )
    pl.when(one & jnp.logical_not(two))(
        lambda: attend(q_ref, (k_ref, k1_ref), (v_ref, v1_ref), (b0, b1), emit)
    )
    pl.when(jnp.logical_not(one))(lambda: attend(q_ref, (k_ref,), (v_ref,), (b0,), emit))


def attn_kernel(rows, lens_ref, q_ref, qa_ref, qb_ref, kp_ref, vp_ref, k_ref, v_ref,
                o_ref, lse_ref, oa_ref, ob_ref, b00, b10, b01, b11, b02):
    span = lens_ref[lens_ref.shape[0] - 1]
    base = span * rows

    def reads(ahead, back):
        return needs(lens_ref, base, rows, ahead, back)

    own_prev = (span == 1) & reads(0, 1)
    a_here = ((span == 1) | (span == 2)) & reads(1, 0)
    a_prev = (span == 1) & reads(1, 1)
    b_here = (span == 1) & reads(2, 0)

    @pl.when(pl.program_id(0) == 0)
    def _():
        lse_ref[...] = jnp.zeros_like(lse_ref)

        def fill(ref, ahead, back):
            fill_bias(lens_ref, base, rows, ref, ahead, back)

        fill(b00, 0, 0)
        pl.when(own_prev)(lambda: fill(b01, 0, 1))
        pl.when(a_here)(lambda: fill(b10, 1, 0))
        pl.when(a_prev)(lambda: fill(b11, 1, 1))
        pl.when(b_here)(lambda: fill(b02, 2, 0))

    step = 128
    head_lane = lax.broadcasted_iota(jnp.int32, (step, 128), 1) == pl.program_id(0)

    def emit_own(r, out, lse):
        o_ref[r : r + step, :] = out.astype(jnp.bfloat16)
        lse_ref[r : r + step, :] = jnp.where(head_lane, lse, lse_ref[r : r + step, :])

    eye = lax.broadcasted_iota(jnp.int32, (128, 128), 0) == lax.broadcasted_iota(
        jnp.int32, (128, 128), 1
    )
    stat_iota = lax.broadcasted_iota(jnp.int32, (STAT_ROWS, 128), 0)

    def emit_to(ref):
        stats = [jnp.zeros((STAT_ROWS, 128), jnp.float32)]

        def emit(r, out, lse):
            ref[r : r + step, :] = out.astype(jnp.bfloat16)
            rest = jnp.sum(jnp.where(eye, lse, 0.0), axis=0, keepdims=True)
            for piece in range(3):
                high = rest.astype(jnp.bfloat16).astype(jnp.float32)
                stats[0] = jnp.where(stat_iota == piece * (rows // step) + r // step, high, stats[0])
                rest = rest - high
            if r + step == rows:
                ref[rows:, :] = stats[0].astype(jnp.bfloat16)

        return emit

    def empty(ref):
        ref[:rows, :] = jnp.zeros((rows, 128), jnp.bfloat16)
        ref[rows:, :] = jnp.where(stat_iota < rows // step, NEG, 0.0).astype(jnp.bfloat16)

    pl.when(own_prev)(lambda: attend(q_ref, (kp_ref, k_ref), (vp_ref, v_ref), (b01, b00), emit_own))
    pl.when(jnp.logical_not(own_prev))(lambda: attend(q_ref, (k_ref,), (v_ref,), (b00,), emit_own))
    pl.when(a_prev)(
        lambda: attend(qa_ref, (kp_ref, k_ref), (vp_ref, v_ref), (b11, b10), emit_to(oa_ref))
    )
    pl.when(a_here & jnp.logical_not(a_prev))(
        lambda: attend(qa_ref, (k_ref,), (v_ref,), (b10,), emit_to(oa_ref))
    )
    pl.when(jnp.logical_not(a_here))(lambda: empty(oa_ref))
    pl.when(b_here)(lambda: attend(qb_ref, (k_ref,), (v_ref,), (b02,), emit_to(ob_ref)))
    pl.when(jnp.logical_not(b_here))(lambda: empty(ob_ref))


def merge_kernel(rows, lens_ref, o_ref, lse_ref, ra_ref, rb_ref, all_ref, out_ref):
    span = lens_ref[lens_ref.shape[0] - 1]
    step = 128
    eye = lax.broadcasted_iota(jnp.int32, (128, 128), 0) == lax.broadcasted_iota(
        jnp.int32, (128, 128), 1
    )

    @pl.when(span < 2)
    def _():
        out_ref[...] = o_ref[...]

    @pl.when(span >= 2)
    def _():
        blocks = rows // step
        head_lane = lax.broadcasted_iota(jnp.int32, (step, 128), 1) == pl.program_id(0)
        stat_a = ra_ref[rows:, :].astype(jnp.float32)
        stat_b = rb_ref[rows:, :].astype(jnp.float32)

        def column(stats, i):
            row = (stats[i : i + 1] + stats[blocks + i : blocks + i + 1]) + stats[
                2 * blocks + i : 2 * blocks + i + 1
            ]
            return jnp.sum(jnp.where(eye, row, 0.0), axis=1, keepdims=True)

        for i in range(blocks):
            r = i * step
            own = jnp.sum(jnp.where(head_lane, lse_ref[r : r + step, :], 0.0), axis=1, keepdims=True)
            lse_a = column(stat_a, i)
            lse_b = jnp.where(span == 3, column(stat_b, i), NEG)
            top = jnp.maximum(own, jnp.maximum(lse_a, lse_b))
            w0 = jnp.exp2(own - top)
            w1 = jnp.exp2(lse_a - top)
            w2 = jnp.exp2(lse_b - top)
            total = (
                o_ref[r : r + step, :].astype(jnp.float32) * w0
                + ra_ref[r : r + step, :].astype(jnp.float32) * w1
                + rb_ref[r : r + step, :].astype(jnp.float32) * w2
            )
            out_ref[r : r + step, :] = (total / (w0 + w1 + w2)).astype(jnp.bfloat16)


def attention_fast(attn_query, attn_key, attn_value, lengths, hyena_out):
    rows, cols = attn_query.shape
    span_index = lax.axis_index("seq")
    scalars = jnp.concatenate((lengths, jnp.reshape(span_index, (1,)).astype(jnp.int32)))
    all_heads = cols // HD
    heads = all_heads * 3 // 8
    near = all_heads - 2 * heads
    width = heads * HD
    smem = pl.BlockSpec(memory_space=pltpu.SMEM)
    block = pl.BlockSpec((rows, HD), lambda h: (0, h))
    tall = pl.BlockSpec((rows + STAT_ROWS, HD), lambda h: (0, h))
    packed = pl.BlockSpec((rows, 128), lambda h: (0, 0))

    def at(offset):
        return pl.BlockSpec((rows, HD), lambda h: (0, offset + h))

    def pair(lo, hi):
        return jnp.concatenate((attn_key[:, lo:hi], attn_value[:, lo:hi]), axis=1)

    sent = []
    for c in range(2):
        qc = attn_query[:, c * width : (c + 1) * width]
        qa = lax.ppermute(qc, "seq", [(2, 1), (3, 2)])
        qb = lax.ppermute(qc, "seq", [(3, 1)])
        kv = pair(c * width, (c + 1) * width)
        sent.append((qa, qb, lax.ppermute(kv, "seq", [(0, 1)])))
    kv = pair(2 * width, cols)
    kv1 = lax.ppermute(kv, "seq", [(0, 1), (1, 2), (2, 3)])
    kv2 = lax.ppermute(kv, "seq", [(0, 2), (1, 3)])
    scalars, hyena_out = lax.optimization_barrier((scalars, hyena_out))
    outs = []
    for c in range(2):
        qa, qb, kvp = sent[c]
        whole = at(c * heads)
        own, lse, oa, ob = pl.pallas_call(
            lambda *refs: attn_kernel(rows, *refs),
            grid=(heads,),
            out_shape=(
                jax.ShapeDtypeStruct((rows, width), jnp.bfloat16),
                jax.ShapeDtypeStruct((rows, 128), jnp.float32),
                jax.ShapeDtypeStruct((rows + STAT_ROWS, width), jnp.bfloat16),
                jax.ShapeDtypeStruct((rows + STAT_ROWS, width), jnp.bfloat16),
            ),
            in_specs=[smem, whole, block, block, block, at(heads), whole, whole],
            out_specs=(block, packed, tall, tall),
            scratch_shapes=[pltpu.VMEM((rows, rows), jnp.float32)] * 5,
            compiler_params=pltpu.CompilerParams(vmem_limit_bytes=32 * 2**20),
            cost_estimate=pl.CostEstimate(
                flops=heads * 5 * rows * rows * HD * 4 * 2,
                bytes_accessed=8 * 2**20,
                transcendentals=heads * 5 * rows * rows,
            ),
            name="attend",
        )(scalars, attn_query, qa, qb, kvp, kvp, attn_key, attn_value)
        ra = lax.ppermute(oa, "seq", [(1, 2), (2, 3)])
        rb = lax.ppermute(ob, "seq", [(1, 3)])
        outs.append((own, lse, ra, rb))
        scalars, _ = lax.optimization_barrier((scalars, own))
    anywhere = pl.BlockSpec(memory_space=pl.ANY)
    whole_out = jax.ShapeDtypeStruct((rows, cols), jnp.bfloat16)
    mine = at(2 * heads)
    result = pl.pallas_call(
        lambda *refs: near_kernel(rows, *refs[:8], None, *refs[8:]),
        grid=(near,),
        out_shape=whole_out,
        in_specs=[smem, mine, mine, mine, block, at(near), block, at(near)],
        out_specs=mine,
        scratch_shapes=[pltpu.VMEM((rows, rows), jnp.float32)] * 3,
        compiler_params=pltpu.CompilerParams(vmem_limit_bytes=32 * 2**20),
        cost_estimate=pl.CostEstimate(
            flops=near * 3 * rows * rows * HD * 4 * 2,
            bytes_accessed=4 * 2**20,
            transcendentals=near * 3 * rows * rows,
        ),
        name="near",
    )(scalars, attn_query, attn_key, attn_value, kv1, kv1, kv2, kv2)
    for c in range(2):
        own, lse, ra, rb = outs[c]
        result = pl.pallas_call(
            lambda *refs: merge_kernel(rows, *refs),
            grid=(heads,),
            out_shape=whole_out,
            in_specs=[smem, block, packed, tall, tall, anywhere],
            out_specs=at(c * heads),
            input_output_aliases={5: 0},
            cost_estimate=pl.CostEstimate(
                flops=rows * width * 16, bytes_accessed=4 * 2**20, transcendentals=0
            ),
            name="merge",
        )(scalars, own, lse, ra, rb, result)
    return hyena_out, result


MESH_ID = pl.DeviceIdType.MESH
FAR = 1 << 20
CHUNK = 256
AHEAD = 4


def start_at(pos, lens_ref):
    start = jnp.int32(0)
    end = jnp.int32(0)
    for doc in range(lens_ref.shape[0] - 1):
        end = end + lens_ref[doc]
        start = jnp.where(pos >= end, end, start)
    return start


def fused_kernel(
    rows, cols, lens_hbm, feat_hbm, q_hbm, k_hbm, v_hbm, short_hbm, med_hbm, skip_hbm, fwd_hbm, inv_hbm,
    hy_hbm, at_hbm,
    lens_ref, short_ref, med_ref, skip_ref, fwd_ref, inv_ref,
    feat, qv, kv, vv, ext, halo, up_rx, st_rx, q_near, q_far, up_tx, st_tx,
    b_own, b_own_l, b_near, b_near_l, b_far, spec, fix, hy_v, at_v,
    load_sem, hy_sem, at_sem, halo_sem, near_tx, near_rx, far_tx, far_rx, up_tx_sem, up_rx_sem,
    st_tx_sem, st_rx_sem,
):
    f32, bf16 = jnp.float32, jnp.bfloat16
    heads = cols // HD
    part = rows // 3
    span = lax.axis_index("seq")
    base = span * rows
    has_left, has_right = span > 0, span < 3
    has_far, sends_far = span < 2, span > 1

    def load(index, src, dst):
        return pltpu.make_async_copy(src, dst, load_sem.at[index])

    tail_load = load(0, feat_hbm.at[1:3, 2 * part :, :], feat.at[1:3, 2 * part :, :])
    front_load = load(1, feat_hbm.at[1:3, : 2 * part, :], feat.at[1:3, : 2 * part, :])
    mix_load = load(2, feat_hbm.at[0], feat.at[0])
    k_load = load(3, k_hbm, kv)
    v_load = load(4, v_hbm, vv)
    q_load = load(5, q_hbm, qv)
    lens_load = load(6, lens_hbm, lens_ref)
    filter_loads = [
        load(7, short_hbm, short_ref),
        load(8, med_hbm, med_ref),
        load(9, skip_hbm, skip_ref),
        load(10, fwd_hbm, fwd_ref),
        load(11, inv_hbm, inv_ref),
    ]

    def start_all(copies):
        for copy in copies:
            copy.start()

    start_all([lens_load, tail_load])
    head_loads = [k_load, v_load, q_load]
    mix_loads = filter_loads + [front_load, mix_load]
    pl.when(has_left)(lambda: start_all(mix_loads + head_loads))
    pl.when(jnp.logical_not(has_left))(lambda: start_all(head_loads + mix_loads))

    def lanes(h):
        return pl.ds(pl.multiple_of(h * HD, HD), HD)

    def remote(src, dst, tx, rx, to):
        return pltpu.make_async_remote_copy(
            src_ref=src, dst_ref=dst, send_sem=tx, recv_sem=rx, device_id={"seq": to},
            device_id_type=MESH_ID,
        )

    up_to = jnp.minimum(span + 1, 3)

    def near_copy(h):
        return remote(q_hbm.at[:, lanes(h)], q_near.at[h], near_tx.at[h], near_rx.at[h],
                      jnp.maximum(span - 1, 0))

    def far_copy(h):
        return remote(q_hbm.at[:part, lanes(h)], q_far.at[h], far_tx.at[h], far_rx.at[h],
                      jnp.maximum(span - 2, 0))

    def up_copy(h):
        return remote(up_tx.at[h], up_rx.at[h], up_tx_sem.at[h], up_rx_sem.at[h], up_to)

    def st_copy(h):
        return remote(st_tx.at[h], st_rx.at[h], st_tx_sem.at[h], st_rx_sem.at[h], up_to)

    def pass_copy(h):
        return remote(q_near.at[h, :part, :], q_far.at[h], far_tx.at[h], far_rx.at[h],
                      jnp.maximum(span - 1, 0))

    def pass_on(h):
        near_copy(h).wait_recv()
        pass_copy(h).start()
        pl.when(h + 2 < heads)(lambda: near_copy(h + 2).start())

    halo_copies = [
        remote(
            ext.at[rows : rows + part, i * cols // 2 : (i + 1) * cols // 2],
            halo.at[:, i * cols // 2 : (i + 1) * cols // 2],
            halo_sem.at[i], halo_sem.at[2 + i], up_to,
        )
        for i in range(2)
    ]

    barrier = pltpu.get_barrier_semaphore()
    for away in (-2, -1, 1, 2):

        @pl.when((span + away >= 0) & (span + away < 4))
        def _(away=away):
            pl.semaphore_signal(barrier, inc=1, device_id={"seq": span + away}, device_id_type=MESH_ID)

    pl.semaphore_wait(barrier, jnp.where(has_left & has_right, 3, 2))

    @pl.when(sends_far)
    def _():
        def send_queries(h, carry):
            near_copy(h).start()
            pl.when(span == 3)(lambda: far_copy(h).start())
            return carry

        lax.fori_loop(0, heads, send_queries, 0)

    @pl.when(span == 1)
    def _():
        near_copy(0).start()
        near_copy(1).start()

    chunks = cols // CHUNK

    def chunk_cols(c):
        return pl.ds(pl.multiple_of(c * CHUNK, CHUNK), CHUNK)

    def gate(lo, hi, at):
        return (feat[1, lo:hi, at].astype(f32) * feat[2, lo:hi, at].astype(f32)).astype(bf16)

    tail_load.wait()

    def gate_tail(c, carry):
        at = chunk_cols(c)
        ext[rows : rows + part, at] = gate(2 * part, rows, at)
        ext[:part, at] = jnp.zeros((part, CHUNK), bf16)
        return carry

    lax.fori_loop(0, chunks, gate_tail, 0)
    pl.when(has_right)(lambda: halo_copies[0].start())
    pl.when(has_left & has_right)(lambda: halo_copies[1].start())

    @pl.when(jnp.logical_not(has_left))
    def _():
        def clear(h, carry):
            up_rx[h] = jnp.zeros((rows + part, HD), bf16)
            st_rx[h] = jnp.zeros((8, HD), f32)
            return carry

        lax.fori_loop(0, heads, clear, 0)

    @pl.when(span == 2)
    def _():
        def clear(h, carry):
            q_far[h] = jnp.zeros((part, HD), bf16)
            return carry

        lax.fori_loop(0, heads, clear, 0)

    lens_load.wait()
    left_q = has_left & (base - start_at(base, lens_ref) > 2 * part)
    right_q = has_right & (base + rows - start_at(base + rows, lens_ref) > 2 * part)
    fresh = has_far & right_q & (start_at(base + 2 * rows, lens_ref) < base + rows)
    slot_mine = (span > 1) & (base - rows - start_at(base, lens_ref) > 2 * part)

    def column_iota(first, count):
        return first + lax.broadcasted_iota(jnp.int32, (count, 1), 0)

    own_pos = column_iota(base, rows)
    near_pos = column_iota(base + rows, rows)
    far_pos = column_iota(base + 2 * rows, part)
    key_pos = base + lax.broadcasted_iota(jnp.int32, (1, rows), 1)
    left_pos = base - 2 * part + lax.broadcasted_iota(jnp.int32, (1, 2 * part), 1)
    no_keys = jnp.where(has_left & jnp.logical_not(left_q), 0, FAR)
    no_near = jnp.where(right_q, 0, FAR)
    no_far = jnp.where(fresh, 0, FAR)
    own_start = doc_start(own_pos, lens_ref)
    near_start = doc_start(near_pos, lens_ref) + no_near
    far_start = doc_start(far_pos, lens_ref) + no_far

    def bias(ok):
        return jnp.where(ok, 0.0, NEG).astype(f32)

    b_own[...] = bias((key_pos <= own_pos) & (key_pos >= own_start))
    b_own_l[...] = bias(left_pos >= own_start + no_keys)
    b_near[...] = bias(key_pos >= near_start)
    b_near_l[...] = bias(left_pos >= near_start + no_keys)
    b_far[...] = bias(key_pos >= far_start)

    def dot(x, y):
        return jnp.dot(x, y, preferred_element_type=f32)

    first_cut = jnp.int32(FAR)
    last_cut = jnp.int32(-1)
    end = jnp.int32(0)
    for doc in range(lens_ref.shape[0] - 1):
        end = end + lens_ref[doc]
        first_cut = jnp.where((end > base) & (end < first_cut), end, first_cut)
        last_cut = jnp.where((end < base + rows) & (end > last_cut), end, last_cut)
    cuts = []
    for cut in (first_cut, last_cut):
        valid = (cut > base) & (cut < base + rows)
        block = jnp.where(valid, lax.div(jnp.where(valid, cut - base, 0), part), 0)
        cuts.append((jnp.where(valid, cut, FAR), block))
    win_iota = lax.broadcasted_iota(jnp.int32, (2 * part, 1), 0)
    out_iota = lax.broadcasted_iota(jnp.int32, (part, 1), 0)

    def transform(window, first_pos, from_pos, spec_r, spec_i):
        window = jnp.where(win_iota + first_pos >= from_pos, window, jnp.zeros_like(window))
        return spread(window, spec_r, spec_i)

    def spread(window, spec_r, spec_i):
        wave = dot(fwd_ref[0], window)
        wave_r, wave_i = wave[:part], wave[part:]
        prod = jnp.concatenate(
            (
                (wave_r * spec_r - wave_i * spec_i).astype(bf16),
                (wave_r * spec_i + wave_i * spec_r).astype(bf16),
            ),
            axis=0,
        )
        return dot(inv_ref[0], prod)

    def finish(block, at, sums, fixes):
        for (cut, cut_block), fixed in zip(cuts, fixes):
            cut_from = jnp.where(cut_block == block, cut, FAR)
            sums = jnp.where(out_iota + (base + block * part) >= cut_from, fixed, sums)
        r0 = block * part
        hy_v[r0 : r0 + part, at] = (feat[0, r0 : r0 + part, at].astype(f32) * sums).astype(bf16)

    def hyena_loads():
        front_load.wait()
        mix_load.wait()
        for copy in filter_loads:
            copy.wait()

    def hyena_main(c, carry):
        at = chunk_cols(c)
        ext[part:rows, at] = gate(0, 2 * part, at)
        short = short_ref[:, at]
        head = jnp.concatenate(
            (short[:1] + skip_ref[:, at], short[1:], jnp.zeros((8 - short.shape[0], CHUNK), f32)), axis=0
        )
        filt = jnp.concatenate((med_ref[:8, at] + head, med_ref[8:, at]), axis=0)
        filt_hi = filt.astype(bf16)
        filt_lo = (filt - filt_hi.astype(f32)).astype(bf16)
        both = (
            dot(fwd_ref[0, :, :part], filt_hi)
            + dot(fwd_ref[1, :, :part], filt_hi)
            + dot(fwd_ref[0, :, :part], filt_lo)
        )
        spec[:, at] = both
        spec_r, spec_i = both[:part], both[part:]
        fixes = []
        for index, (cut, cut_block) in enumerate(cuts):
            window = jnp.zeros((2 * part, CHUNK), bf16)
            for block in range(3):
                r0 = block * part
                cut_from = jnp.where(cut_block == block, cut, FAR)
                window = jnp.where(
                    win_iota + (base + r0 - part) >= cut_from, ext[r0 : r0 + 2 * part, at], window
                )
            sums = spread(window, spec_r, spec_i)
            fix[index, :, at] = sums
            fixes.append(sums)
        for block in (1, 2):
            r0 = block * part
            sums = transform(
                ext[r0 : r0 + 2 * part, at], base + r0 - part, start_at(base + r0, lens_ref), spec_r, spec_i
            )
            finish(block, at, sums, fixes)
        return carry

    hy_late = pltpu.make_async_copy(hy_v.at[part:, :], hy_hbm.at[part:, :], hy_sem.at[0])
    hy_first = pltpu.make_async_copy(hy_v.at[:part, :], hy_hbm.at[:part, :], hy_sem.at[1])

    def hyena_first():
        @pl.when(has_left)
        def _():
            for copy in halo_copies:
                copy.wait_recv()

        def one(c, carry):
            at = chunk_cols(c)
            window = jnp.concatenate((halo[:, at], ext[part : 2 * part, at]), axis=0)
            sums = transform(
                window, base - part, start_at(base, lens_ref), spec[:part, at], spec[part:, at]
            )
            finish(0, at, sums, [fix[i, :, at] for i in range(2)])
            return carry

        lax.fori_loop(0, chunks, one, 0)
        hy_first.start()

    @pl.when(has_left)
    def _():
        pl.when(span == 1)(lambda: pass_on(0))
        hyena_loads()

        def step(c, carry):
            for h, when in ((1, 1), (2, 3), (3, 5), (4, 7), (5, 7))[: AHEAD - 1]:

                @pl.when((span == 1) & (c == min(when, chunks - 1)))
                def _(h=h):
                    pass_on(h)

            return hyena_main(c, carry)

        lax.fori_loop(0, chunks, step, 0)
        hy_late.start()
        pl.when(sends_far)(hyena_first)

    k_load.wait()
    v_load.wait()
    q_load.wait()
    ones = jnp.ones((rows, HD), bf16)
    eye = lax.broadcasted_iota(jnp.int32, (part, HD), 0) == lax.broadcasted_iota(jnp.int32, (part, HD), 1)
    stat_iota = lax.broadcasted_iota(jnp.int32, (8, HD), 0)
    left_off = jnp.where(left_q, 0.0, NEG)
    slot_off = jnp.where(slot_mine, 0.0, NEG)

    def attend_to(q, keys, values, biases):
        scores = [
            lax.dot_general(q, k, (((1,), (1,)), ((), ())), preferred_element_type=f32) + b
            for k, b in zip(keys, biases)
        ]
        top = jnp.max(scores[0], axis=1, keepdims=True)
        for s in scores[1:]:
            top = jnp.maximum(top, jnp.max(s, axis=1, keepdims=True))
        acc = None
        for s, v in zip(scores, values):
            w = jnp.exp2((s - top) * SCALE2).astype(bf16)
            term = dot(w, v)
            acc = term if acc is None else acc + term
        return acc[:, :HD], acc[:, HD:], top * SCALE2

    spread_from = min(4, heads - chunks - 1)

    def head_step(h, carry):
        at = lanes(h)

        @pl.when(jnp.logical_not(has_left))
        def _():
            pl.when(h == spread_from)(hyena_loads)

            @pl.when((h >= spread_from) & (h < spread_from + chunks))
            def _():
                hyena_main(h - spread_from, 0)

            @pl.when(h == spread_from + chunks)
            def _():
                hy_late.start()
                hyena_first()

        @pl.when(has_left)
        def _():
            up_copy(h).wait_recv()
            st_copy(h).wait_recv()

        k = kv[:, at]
        v = vv[:, at]
        k_left = up_rx[h, : 2 * part, :]
        v_ones = jnp.concatenate((v, ones), axis=1)
        v_left = jnp.concatenate((up_rx[h, 2 * part :, :], ones[: 2 * part]), axis=1)

        @pl.when(has_right)
        def _():
            pl.when(span != 1)(lambda: near_copy(h).wait_recv())
            pl.when(has_far)(lambda: far_copy(h).wait_recv())
            tails = (k[part : 2 * part], k[2 * part :], v[part : 2 * part], v[2 * part :])
            stats = jnp.zeros((8, HD), f32)

            def give(i, out):
                up_tx[h, i * part : (i + 1) * part, :] = jnp.where(
                    right_q, out, tails[i].astype(f32)
                ).astype(bf16)

            def to_row(lse):
                return jnp.sum(jnp.where(eye, lse, 0.0), axis=0, keepdims=True)

            for i in range(3):
                r0 = i * part
                acc, total, top = attend_to(
                    q_near[h, r0 : r0 + part, :],
                    (k, k_left),
                    (v_ones, v_left),
                    (b_near[r0 : r0 + part, :], b_near_l[r0 : r0 + part, :]),
                )
                give(i, acc / total)
                stats = jnp.where(stat_iota == i, to_row(top + jnp.log2(total)), stats)
            passed = up_rx[h, rows:, :].astype(f32)
            passed_stat = st_rx[h]

            acc, total, top = attend_to(q_far[h], (k,), (v_ones,), (b_far[...],))
            give(3, jnp.where(fresh, acc / total, passed))
            lse = to_row(top + jnp.log2(total))
            st_tx[h] = jnp.where(stat_iota == 3, jnp.where(fresh, lse, passed_stat[3:4]), stats)
            up_copy(h).start()
            st_copy(h).start()
            pl.when((span == 1) & (h + AHEAD < heads))(lambda: pass_on(h + AHEAD))

        stats_in = st_rx[h]

        def column(i):
            return jnp.sum(jnp.where(eye, stats_in[i : i + 1], 0.0), axis=1, keepdims=True)

        for i in range(3):
            r0 = i * part
            r1 = r0 + part
            acc, total, top = attend_to(
                qv[r0:r1, at],
                (k[:r1], k_left),
                (v_ones[:r1], v_left),
                (b_own[r0:r1, :r1], b_own_l[r0:r1, :]),
            )
            lse = column(i) + left_off
            best = jnp.maximum(top, lse)
            if i == 0:
                slot_lse = column(3) + slot_off
                best = jnp.maximum(best, slot_lse)
            w0 = jnp.exp2(top - best)
            w1 = jnp.exp2(lse - best)
            mixed = acc * w0 + up_rx[h, r0:r1, :].astype(f32) * w1
            norm = total * w0 + w1
            if i == 0:
                w2 = jnp.exp2(slot_lse - best)
                mixed = mixed + up_rx[h, rows:, :].astype(f32) * w2
                norm = norm + w2
            at_v[r0:r1, at] = (mixed / norm).astype(bf16)
        pltpu.make_async_copy(at_v.at[:, at], at_hbm.at[:, at], at_sem.at[h]).start()
        return carry

    lax.fori_loop(0, heads, head_step, 0)
    pl.when(jnp.logical_not(has_left))(lambda: halo_copies[1].start())
    pl.when(span == 1)(hyena_first)

    def drain(h, carry):
        at = lanes(h)
        pltpu.make_async_copy(at_v.at[:, at], at_hbm.at[:, at], at_sem.at[h]).wait()

        @pl.when(has_right)
        def _():
            up_copy(h).wait_send()
            st_copy(h).wait_send()

        pl.when(has_left)(lambda: near_copy(h).wait_send())
        pl.when(span == 3)(lambda: far_copy(h).wait_send())
        pl.when(span == 1)(lambda: pass_copy(h).wait_send())
        return carry

    lax.fori_loop(0, heads, drain, 0)

    @pl.when(has_right)
    def _():
        for copy in halo_copies:
            copy.wait_send()

    hy_late.wait()
    hy_first.wait()


def land_kernel(pieces, hy_src, at_src, hy_dst, at_dst, held, in_sem, out_sem):
    step = hy_src.shape[0] // pieces
    moves = []
    for array, (src, dst) in enumerate(((hy_src, hy_dst), (at_src, at_dst))):
        for i in range(pieces):
            rows = pl.ds(i * step, step)
            here = held.at[array, rows, :]
            index = array * pieces + i
            inward = pltpu.make_async_copy(src.at[rows, :], here, in_sem.at[index])
            moves.append((inward, pltpu.make_async_copy(here, dst.at[rows, :], out_sem.at[index])))
            inward.start()
    for inward, outward in moves:
        inward.wait()
        outward.start()
    for inward, outward in moves:
        outward.wait()


def fused(features, short_filter, medium_filter, skip_gain, attn_query, attn_key, attn_value, lengths):
    rows, cols = attn_query.shape
    part = rows // 3
    heads = cols // HD
    angle = np.pi / (2 * part) * np.outer(2 * np.arange(part) + 1, np.arange(2 * part))
    wave = np.concatenate((np.cos(angle), -np.sin(angle)), axis=0)
    fwd = split_two(wave)
    inv = split_two(wave.T[part:] / part)
    anywhere = pl.BlockSpec(memory_space=pl.ANY)
    out = jax.ShapeDtypeStruct((rows, cols), jnp.bfloat16)

    def buf(*shape):
        return pltpu.VMEM(shape, jnp.bfloat16)

    def wide(*shape):
        return pltpu.VMEM(shape, jnp.float32)

    each = pltpu.SemaphoreType.DMA((heads,))
    made = pl.pallas_call(
        lambda *refs: fused_kernel(rows, cols, *refs),
        out_shape=(out, out),
        in_specs=[pl.BlockSpec(memory_space=pltpu.HBM)] * 10,
        out_specs=(anywhere, anywhere),
        scratch_shapes=[
            pltpu.SMEM(lengths.shape, jnp.int32), wide(*short_filter.shape), wide(part, cols), wide(1, cols),
            buf(*fwd.shape), buf(*inv.shape),
            buf(3, rows, cols), buf(rows, cols), buf(rows, cols), buf(rows, cols),
            buf(rows + part, cols), buf(part, cols),
            buf(heads, rows + part, HD), wide(heads, 8, HD),
            buf(heads, rows, HD), buf(heads, part, HD),
            buf(heads, rows + part, HD), wide(heads, 8, HD),
            wide(rows, rows), wide(rows, 2 * part), wide(rows, rows), wide(rows, 2 * part),
            wide(part, rows),
            wide(2 * part, cols), wide(2, part, cols),
            buf(rows, cols), buf(rows, cols),
            pltpu.SemaphoreType.DMA((12,)), pltpu.SemaphoreType.DMA((2,)), each,
            pltpu.SemaphoreType.DMA((4,)),
        ] + [each] * 8,
        compiler_params=pltpu.CompilerParams(
            collective_id=0, has_side_effects=True, vmem_limit_bytes=60 * 2**20
        ),
        cost_estimate=pl.CostEstimate(
            flops=heads * 32 * part * part * HD * 4, bytes_accessed=16 * 2**20,
            transcendentals=heads * 32 * part * part,
        ),
        name="fused",
    )(
        lengths, features.transpose(1, 0, 2), attn_query, attn_key, attn_value,
        short_filter, medium_filter, skip_gain[None, :], fwd, inv,
    )
    pieces = 4
    return pl.pallas_call(
        lambda *refs: land_kernel(pieces, *refs),
        out_shape=(out, out),
        in_specs=[anywhere] * 2,
        out_specs=(anywhere, anywhere),
        scratch_shapes=[
            buf(2, rows, cols), pltpu.SemaphoreType.DMA((2 * pieces,)), pltpu.SemaphoreType.DMA((2 * pieces,))
        ],
        compiler_params=pltpu.CompilerParams(vmem_limit_bytes=60 * 2**20),
        cost_estimate=pl.CostEstimate(flops=0, bytes_accessed=8 * rows * cols, transcendentals=0),
        name="land",
    )(*made)


def local(
    features, short_filter, medium_filter, skip_gain, attn_query, attn_key, attn_value, lengths
):
    rows, cols = attn_query.shape
    spans = lax.axis_size("seq")
    taps = medium_filter.shape[0]
    if spans == 4 and rows == 3 * taps and taps == HD and cols % CHUNK == 0 and short_filter.shape[0] < 8:
        return fused(
            features, short_filter, medium_filter, skip_gain, attn_query, attn_key, attn_value, lengths
        )
    if cols % 128 == 0 and taps % 128 == 0 and rows % taps == 0:
        hyena = hyena_fast
    else:
        hyena = hyena_mix
    hyena_out = hyena(features, short_filter, medium_filter, skip_gain, lengths)
    if spans == 4 and rows % 128 == 0 and rows <= 640 and cols % (8 * HD) == 0:
        return attention_fast(attn_query, attn_key, attn_value, lengths, hyena_out)
    return (hyena_out, attention_mix(attn_query, attn_key, attn_value, lengths))


def solution(mesh):
    in_specs = (
        P(("groups", "seq"), None, ("tensor", "sub")),
        P(None, ("tensor", "sub")),
        P(None, ("tensor", "sub")),
        P(("tensor", "sub")),
        P(("groups", "seq"), ("tensor", "sub")),
        P(("groups", "seq"), ("tensor", "sub")),
        P(("groups", "seq"), ("tensor", "sub")),
        P("groups"),
    )
    out_specs = (P(("groups", "seq"), ("tensor", "sub")), P(("groups", "seq"), ("tensor", "sub")))
    return jax.shard_map(local, mesh=mesh, in_specs=in_specs, out_specs=out_specs, check_vma=False)
```

```python
import math

import jax
import jax.numpy as jnp
import numpy as np
from jax import lax
from jax.experimental import pallas as pl
from jax.experimental.pallas import tpu as pltpu
from jax.sharding import PartitionSpec as P

HD = 128


def passed_along(value, axis, by):
    length = lax.axis_size(axis)
    pairs = [(i, i + by) for i in range(length) if 0 <= i + by < length]
    return lax.ppermute(value, axis, pairs)


def doc_of(positions, lengths):
    doc_ends = jnp.cumsum(lengths, dtype=jnp.int32)
    return jnp.sum(
        (positions[:, None] >= doc_ends[None, :]).astype(jnp.int32), axis=1, dtype=jnp.int32
    )


def hyena_mix(features, short_filter, medium_filter, skip_gain, lengths):
    row_count = features.shape[0]
    medium_taps = medium_filter.shape[0]
    rim_rows = medium_taps - 1
    span_index = lax.axis_index("seq")
    queries = features[:, 0].astype(jnp.float32)
    gated = (features[:, 1].astype(jnp.float32) * features[:, 2].astype(jnp.float32)).astype(
        jnp.bfloat16
    )
    gated = lax.optimization_barrier(gated)
    carried = passed_along(gated[row_count - rim_rows :], "seq", 1)
    extended = jnp.concatenate((carried, gated), axis=0)
    ext_positions = (
        span_index * row_count - rim_rows + jnp.arange(row_count + rim_rows, dtype=jnp.int32)
    )
    ext_docs = doc_of(ext_positions, lengths)
    ext_live = ext_positions >= 0
    own_docs = ext_docs[rim_rows:]

    def tap_term(tap_index, filter_bank):
        first_row = rim_rows - tap_index
        window = lax.dynamic_slice_in_dim(extended, first_row, row_count, 0).astype(jnp.float32)
        same_doc = lax.dynamic_slice_in_dim(ext_docs, first_row, row_count, 0) == own_docs
        live_mask = lax.dynamic_slice_in_dim(ext_live, first_row, row_count, 0)
        keep_mask = (same_doc & live_mask).astype(jnp.float32)[:, None]
        taps = lax.dynamic_index_in_dim(filter_bank, tap_index, 0, keepdims=False)
        return taps[None, :] * window * keep_mask

    short_sum = jnp.zeros(gated.shape, jnp.float32)
    for tap_index in range(short_filter.shape[0]):
        short_sum = short_sum + tap_term(tap_index, short_filter)

    def tap_block(block_index, partial_value):
        for offset in range(8):
            partial_value = partial_value + tap_term(block_index * 8 + offset, medium_filter)
        return partial_value

    medium_sum = lax.fori_loop(0, medium_taps // 8, tap_block, jnp.zeros(gated.shape, jnp.float32))
    mixed = queries * (short_sum + medium_sum + skip_gain[None, :] * gated.astype(jnp.float32))
    return mixed.astype(jnp.bfloat16)


def attention_mix(attn_query, attn_key, attn_value, lengths):
    row_count, col_count = attn_query.shape
    heads_here = col_count // HD
    span_index = lax.axis_index("seq")
    query_positions = span_index * row_count + jnp.arange(row_count, dtype=jnp.int32)
    query_docs = doc_of(query_positions, lengths)
    query_heads = attn_query.reshape(row_count, heads_here, HD)
    score_scale = HD ** (-0.5)
    last_query = query_positions[row_count - 1]
    first_query_doc = query_docs[0]

    def absorb(state_now, key_block, value_block, first_row):
        key_count = key_block.shape[0]
        last_key = first_row + key_count - 1
        last_key_doc = doc_of(jnp.reshape(last_key, (1,)), lengths)[0]
        masked_out = (first_row > last_query) | (last_key < 0) | (last_key_doc < first_query_doc)

        def compute(state_in):
            running_max, running_total, running_sum = state_in
            key_heads = key_block.reshape(key_count, heads_here, HD)
            value_heads = value_block.reshape(key_count, heads_here, HD)
            scores = (
                jnp.einsum(
                    "rhd,nhd->hrn", query_heads, key_heads, preferred_element_type=jnp.float32
                )
                * score_scale
            )
            key_positions = first_row + jnp.arange(key_count, dtype=jnp.int32)
            key_docs = doc_of(key_positions, lengths)
            allowed = (
                (key_positions[None, :] <= query_positions[:, None])
                & (key_docs[None, :] == query_docs[:, None])
                & (key_positions >= 0)[None, :]
            )
            masked = jnp.where(allowed[None], scores, -1e30)
            new_max = jnp.maximum(running_max, jnp.max(masked, axis=2))
            rescale = jnp.exp(running_max - new_max)
            weights = jnp.where(allowed[None], jnp.exp(scores - new_max[:, :, None]), 0.0)
            new_total = running_total * rescale + jnp.sum(weights, axis=2)
            product = jnp.einsum(
                "hrn,nhd->hrd",
                weights.astype(jnp.bfloat16),
                value_heads,
                preferred_element_type=jnp.float32,
            )
            new_sum = running_sum * rescale[:, :, None] + product
            return (new_max, new_total, new_sum)

        def keep_state(state_in):
            return state_in

        return lax.cond(masked_out, keep_state, compute, state_now)

    def fold_keys(state_now, pieces, first_row):
        key_all, value_all = pieces
        key_count = key_all.shape[0]
        block_rows = math.gcd(key_count, 1536)
        if block_rows == key_count:
            return absorb(state_now, key_all, value_all, first_row)
        block_total = key_count // block_rows
        key_blocks = key_all.reshape(block_total, block_rows, col_count)
        value_blocks = value_all.reshape(block_total, block_rows, col_count)

        def scan_step(state_inner, block_items):
            key_block, value_block, block_index = block_items
            return (
                absorb(state_inner, key_block, value_block, first_row + block_index * block_rows),
                None,
            )

        state_now, unused = lax.scan(
            scan_step,
            state_now,
            (key_blocks, value_blocks, jnp.arange(block_total, dtype=jnp.int32)),
        )
        return state_now

    initial = (
        jnp.full((heads_here, row_count), -1e30, jnp.float32),
        jnp.zeros((heads_here, row_count), jnp.float32),
        jnp.zeros((heads_here, row_count, HD), jnp.float32),
    )
    state_now = fold_keys(
        initial,
        (
            lax.all_gather(attn_key, "seq", axis=0, tiled=True),
            lax.all_gather(attn_value, "seq", axis=0, tiled=True),
        ),
        jnp.int32(0),
    )
    running_max, running_total, running_sum = state_now
    result = running_sum / running_total[:, :, None]
    return result.transpose(1, 0, 2).reshape(row_count, col_count).astype(jnp.bfloat16)


LOG2E = 1.4426950408889634
LN2 = 0.6931471805599453
SCALE2 = HD**-0.5 * LOG2E
NEG = -1e30
STAT_ROWS = 16


def hyena_kernel(row_count, taps, lens_ref, feat_ref, rim_ref, filt_ref, fwd_ref, inv_ref, out_ref,
                 ext_ref, sum_ref):
    base = lens_ref[lens_ref.shape[0] - 1]
    ext_ref[:taps, :] = rim_ref[...]
    ext_ref[taps:, :] = (
        feat_ref[1].astype(jnp.float32) * feat_ref[2].astype(jnp.float32)
    ).astype(jnp.bfloat16)

    def dot(x, y):
        return jnp.dot(x, y, preferred_element_type=jnp.float32)

    filt = filt_ref[...]
    filt_hi = filt.astype(jnp.bfloat16)
    filt_lo = (filt - filt_hi.astype(jnp.float32)).astype(jnp.bfloat16)
    spec = (
        dot(fwd_ref[0, :, :taps], filt_hi)
        + dot(fwd_ref[1, :, :taps], filt_hi)
        + dot(fwd_ref[0, :, :taps], filt_lo)
    )
    spec_r, spec_i = spec[:taps], spec[taps:]
    win_iota = lax.broadcasted_iota(jnp.int32, (2 * taps, 1), 0)
    out_iota = lax.broadcasted_iota(jnp.int32, (taps, 1), 0)
    for block in range(row_count // taps):
        r0 = block * taps
        start = jnp.int32(0)
        for doc in range(lens_ref.shape[0] - 1):
            end = start + lens_ref[doc]
            first, last = start - base, end - base

            @pl.when((last > r0) & (first < r0 + taps) & (first < last))
            def _(first=first):
                window = ext_ref[r0 : r0 + 2 * taps, :]
                window = jnp.where(win_iota + (r0 - taps) >= first, window, jnp.zeros_like(window))
                wave = dot(fwd_ref[0], window) + dot(fwd_ref[1], window)
                wave_r, wave_i = wave[:taps], wave[taps:]
                prod = jnp.concatenate(
                    (
                        (wave_r * spec_r - wave_i * spec_i).astype(jnp.bfloat16),
                        (wave_r * spec_i + wave_i * spec_r).astype(jnp.bfloat16),
                    ),
                    axis=0,
                )
                sums = dot(inv_ref[0], prod) + dot(inv_ref[1], prod)
                sum_ref[...] = jnp.where(out_iota + r0 >= first, sums, sum_ref[...])

            start = end
        out_ref[r0 : r0 + taps, :] = (
            feat_ref[0, r0 : r0 + taps, :].astype(jnp.float32) * sum_ref[...]
        ).astype(out_ref.dtype)


def split_two(matrix):
    high = matrix.astype(jnp.bfloat16)
    low = (matrix - high.astype(np.float64)).astype(jnp.bfloat16)
    return np.stack((high, low))


def hyena_fast(features, short_filter, medium_filter, skip_gain, lengths):
    row_count, _, cols = features.shape
    taps = medium_filter.shape[0]
    span_index = lax.axis_index("seq")
    streams = features.transpose(1, 0, 2)
    tail = streams[:, row_count - taps :]
    gated_tail = (tail[1].astype(jnp.float32) * tail[2].astype(jnp.float32)).astype(jnp.bfloat16)
    carried = passed_along(gated_tail, "seq", 1)
    head = jnp.concatenate((short_filter[:1] + skip_gain[None, :], short_filter[1:]), axis=0)
    filt = medium_filter + jnp.pad(head, ((0, taps - head.shape[0]), (0, 0)))
    angle = np.pi / (2 * taps) * np.outer(2 * np.arange(taps) + 1, np.arange(2 * taps))
    fwd = split_two(np.concatenate((np.cos(angle), -np.sin(angle)), axis=0))
    inv = split_two(
        np.concatenate((np.cos(angle), -np.sin(angle)), axis=0).T[taps:] / taps
    )
    scalars = jnp.concatenate((lengths, jnp.reshape(span_index * row_count, (1,)).astype(jnp.int32)))
    width = math.gcd(cols, 512)
    return pl.pallas_call(
        lambda *refs: hyena_kernel(row_count, taps, *refs),
        grid=(cols // width,),
        out_shape=jax.ShapeDtypeStruct((row_count, cols), jnp.bfloat16),
        in_specs=[
            pl.BlockSpec(memory_space=pltpu.SMEM),
            pl.BlockSpec((3, row_count, width), lambda i: (0, 0, i)),
            pl.BlockSpec((taps, width), lambda i: (0, i)),
            pl.BlockSpec((taps, width), lambda i: (0, i)),
            pl.BlockSpec(fwd.shape, lambda i: (0, 0, 0)),
            pl.BlockSpec(inv.shape, lambda i: (0, 0, 0)),
        ],
        out_specs=pl.BlockSpec((row_count, width), lambda i: (0, i)),
        scratch_shapes=[
            pltpu.VMEM((row_count + taps, width), jnp.bfloat16),
            pltpu.VMEM((taps, width), jnp.float32),
        ],
        compiler_params=pltpu.CompilerParams(vmem_limit_bytes=32 * 2**20),
        cost_estimate=pl.CostEstimate(
            flops=2 * 9 * 2 * taps * taps * 3 * cols, bytes_accessed=8 * 2**20, transcendentals=0
        ),
        name="hyena",
    )(scalars, streams, carried, filt, fwd, inv)


def doc_start(pos, lens_ref):
    start = jnp.zeros_like(pos)
    end = jnp.int32(0)
    for doc in range(lens_ref.shape[0] - 1):
        end = end + lens_ref[doc]
        start = jnp.where(pos >= end, end, start)
    return start


def attend(query_ref, keys, values, biases, emit):
    rows = query_ref.shape[0]
    step = 128
    ones = jnp.ones((rows, 128), jnp.bfloat16)
    vals = [jnp.concatenate((v[...], ones), axis=1) for v in values]
    for r in range(0, rows, step):
        q = query_ref[r : r + step, :]
        scores = [
            lax.dot_general(q, k[...], (((1,), (1,)), ((), ())),
                            preferred_element_type=jnp.float32) + b[r : r + step, :]
            for k, b in zip(keys, biases)
        ]
        top = jnp.max(scores[0], axis=1, keepdims=True)
        for s in scores[1:]:
            top = jnp.maximum(top, jnp.max(s, axis=1, keepdims=True))
        acc = None
        for s, v in zip(scores, vals):
            w = jnp.exp2((s - top) * SCALE2).astype(jnp.bfloat16)
            part = jnp.dot(w, v, preferred_element_type=jnp.float32)
            acc = part if acc is None else acc + part
        total = acc[:, 128:]
        emit(r, acc[:, :128] / total, top * SCALE2 + jnp.log2(total))


def needs(lens_ref, base, rows, ahead, back):
    q_first = base + ahead * rows
    start = jnp.int32(0)
    end = jnp.int32(0)
    for doc in range(lens_ref.shape[0] - 1):
        end = end + lens_ref[doc]
        start = jnp.where(q_first >= end, end, start)
    return start < base + (1 - back) * rows


def fill_bias(lens_ref, base, rows, ref, ahead, back):
    qpos = base + ahead * rows + lax.broadcasted_iota(jnp.int32, (rows, 1), 0)
    starts = doc_start(qpos, lens_ref)
    kpos = base - back * rows + lax.broadcasted_iota(jnp.int32, (1, rows), 1)
    ref[...] = jnp.where((kpos <= qpos) & (kpos >= starts), 0.0, NEG).astype(jnp.float32)


def near_kernel(rows, lens_ref, q_ref, k_ref, v_ref, k1_ref, v1_ref, k2_ref, v2_ref, all_ref, o_ref,
                b0, b1, b2):
    span = lens_ref[lens_ref.shape[0] - 1]
    base = span * rows
    one = (span >= 1) & needs(lens_ref, base, rows, 0, 1)
    two = (span >= 2) & needs(lens_ref, base, rows, 0, 2)

    @pl.when(pl.program_id(0) == 0)
    def _():
        fill_bias(lens_ref, base, rows, b0, 0, 0)
        pl.when(one)(lambda: fill_bias(lens_ref, base, rows, b1, 0, 1))
        pl.when(two)(lambda: fill_bias(lens_ref, base, rows, b2, 0, 2))

    def emit(r, out, lse):
        o_ref[r : r + 128, :] = out.astype(jnp.bfloat16)

    pl.when(two)(
        lambda: attend(q_ref, (k_ref, k1_ref, k2_ref), (v_ref, v1_ref, v2_ref), (b0, b1, b2), emit)
    )
    pl.when(one & jnp.logical_not(two))(
        lambda: attend(q_ref, (k_ref, k1_ref), (v_ref, v1_ref), (b0, b1), emit)
    )
    pl.when(jnp.logical_not(one))(lambda: attend(q_ref, (k_ref,), (v_ref,), (b0,), emit))


def attn_kernel(rows, lens_ref, q_ref, qa_ref, qb_ref, kp_ref, vp_ref, k_ref, v_ref,
                o_ref, lse_ref, oa_ref, ob_ref, b00, b10, b01, b11, b02):
    span = lens_ref[lens_ref.shape[0] - 1]
    base = span * rows

    def reads(ahead, back):
        return needs(lens_ref, base, rows, ahead, back)

    own_prev = (span == 1) & reads(0, 1)
    a_here = ((span == 1) | (span == 2)) & reads(1, 0)
    a_prev = (span == 1) & reads(1, 1)
    b_here = (span == 1) & reads(2, 0)

    @pl.when(pl.program_id(0) == 0)
    def _():
        lse_ref[...] = jnp.zeros_like(lse_ref)

        def fill(ref, ahead, back):
            fill_bias(lens_ref, base, rows, ref, ahead, back)

        fill(b00, 0, 0)
        pl.when(own_prev)(lambda: fill(b01, 0, 1))
        pl.when(a_here)(lambda: fill(b10, 1, 0))
        pl.when(a_prev)(lambda: fill(b11, 1, 1))
        pl.when(b_here)(lambda: fill(b02, 2, 0))

    step = 128
    head_lane = lax.broadcasted_iota(jnp.int32, (step, 128), 1) == pl.program_id(0)

    def emit_own(r, out, lse):
        o_ref[r : r + step, :] = out.astype(jnp.bfloat16)
        lse_ref[r : r + step, :] = jnp.where(head_lane, lse, lse_ref[r : r + step, :])

    eye = lax.broadcasted_iota(jnp.int32, (128, 128), 0) == lax.broadcasted_iota(
        jnp.int32, (128, 128), 1
    )
    stat_iota = lax.broadcasted_iota(jnp.int32, (STAT_ROWS, 128), 0)

    def emit_to(ref):
        stats = [jnp.zeros((STAT_ROWS, 128), jnp.float32)]

        def emit(r, out, lse):
            ref[r : r + step, :] = out.astype(jnp.bfloat16)
            rest = jnp.sum(jnp.where(eye, lse, 0.0), axis=0, keepdims=True)
            for piece in range(3):
                high = rest.astype(jnp.bfloat16).astype(jnp.float32)
                stats[0] = jnp.where(stat_iota == piece * (rows // step) + r // step, high, stats[0])
                rest = rest - high
            if r + step == rows:
                ref[rows:, :] = stats[0].astype(jnp.bfloat16)

        return emit

    def empty(ref):
        ref[:rows, :] = jnp.zeros((rows, 128), jnp.bfloat16)
        ref[rows:, :] = jnp.where(stat_iota < rows // step, NEG, 0.0).astype(jnp.bfloat16)

    pl.when(own_prev)(lambda: attend(q_ref, (kp_ref, k_ref), (vp_ref, v_ref), (b01, b00), emit_own))
    pl.when(jnp.logical_not(own_prev))(lambda: attend(q_ref, (k_ref,), (v_ref,), (b00,), emit_own))
    pl.when(a_prev)(
        lambda: attend(qa_ref, (kp_ref, k_ref), (vp_ref, v_ref), (b11, b10), emit_to(oa_ref))
    )
    pl.when(a_here & jnp.logical_not(a_prev))(
        lambda: attend(qa_ref, (k_ref,), (v_ref,), (b10,), emit_to(oa_ref))
    )
    pl.when(jnp.logical_not(a_here))(lambda: empty(oa_ref))
    pl.when(b_here)(lambda: attend(qb_ref, (k_ref,), (v_ref,), (b02,), emit_to(ob_ref)))
    pl.when(jnp.logical_not(b_here))(lambda: empty(ob_ref))


def merge_kernel(rows, lens_ref, o_ref, lse_ref, ra_ref, rb_ref, all_ref, out_ref):
    span = lens_ref[lens_ref.shape[0] - 1]
    step = 128
    eye = lax.broadcasted_iota(jnp.int32, (128, 128), 0) == lax.broadcasted_iota(
        jnp.int32, (128, 128), 1
    )

    @pl.when(span < 2)
    def _():
        out_ref[...] = o_ref[...]

    @pl.when(span >= 2)
    def _():
        blocks = rows // step
        head_lane = lax.broadcasted_iota(jnp.int32, (step, 128), 1) == pl.program_id(0)
        stat_a = ra_ref[rows:, :].astype(jnp.float32)
        stat_b = rb_ref[rows:, :].astype(jnp.float32)

        def column(stats, i):
            row = (stats[i : i + 1] + stats[blocks + i : blocks + i + 1]) + stats[
                2 * blocks + i : 2 * blocks + i + 1
            ]
            return jnp.sum(jnp.where(eye, row, 0.0), axis=1, keepdims=True)

        for i in range(blocks):
            r = i * step
            own = jnp.sum(jnp.where(head_lane, lse_ref[r : r + step, :], 0.0), axis=1, keepdims=True)
            lse_a = column(stat_a, i)
            lse_b = jnp.where(span == 3, column(stat_b, i), NEG)
            top = jnp.maximum(own, jnp.maximum(lse_a, lse_b))
            w0 = jnp.exp2(own - top)
            w1 = jnp.exp2(lse_a - top)
            w2 = jnp.exp2(lse_b - top)
            total = (
                o_ref[r : r + step, :].astype(jnp.float32) * w0
                + ra_ref[r : r + step, :].astype(jnp.float32) * w1
                + rb_ref[r : r + step, :].astype(jnp.float32) * w2
            )
            out_ref[r : r + step, :] = (total / (w0 + w1 + w2)).astype(jnp.bfloat16)


def attention_fast(attn_query, attn_key, attn_value, lengths, hyena_out):
    rows, cols = attn_query.shape
    span_index = lax.axis_index("seq")
    scalars = jnp.concatenate((lengths, jnp.reshape(span_index, (1,)).astype(jnp.int32)))
    all_heads = cols // HD
    heads = all_heads * 3 // 8
    near = all_heads - 2 * heads
    width = heads * HD
    smem = pl.BlockSpec(memory_space=pltpu.SMEM)
    block = pl.BlockSpec((rows, HD), lambda h: (0, h))
    tall = pl.BlockSpec((rows + STAT_ROWS, HD), lambda h: (0, h))
    packed = pl.BlockSpec((rows, 128), lambda h: (0, 0))

    def at(offset):
        return pl.BlockSpec((rows, HD), lambda h: (0, offset + h))

    def pair(lo, hi):
        return jnp.concatenate((attn_key[:, lo:hi], attn_value[:, lo:hi]), axis=1)

    sent = []
    for c in range(2):
        qc = attn_query[:, c * width : (c + 1) * width]
        qa = lax.ppermute(qc, "seq", [(2, 1), (3, 2)])
        qb = lax.ppermute(qc, "seq", [(3, 1)])
        kv = pair(c * width, (c + 1) * width)
        sent.append((qa, qb, lax.ppermute(kv, "seq", [(0, 1)])))
    kv = pair(2 * width, cols)
    kv1 = lax.ppermute(kv, "seq", [(0, 1), (1, 2), (2, 3)])
    kv2 = lax.ppermute(kv, "seq", [(0, 2), (1, 3)])
    scalars, hyena_out = lax.optimization_barrier((scalars, hyena_out))
    outs = []
    for c in range(2):
        qa, qb, kvp = sent[c]
        whole = at(c * heads)
        own, lse, oa, ob = pl.pallas_call(
            lambda *refs: attn_kernel(rows, *refs),
            grid=(heads,),
            out_shape=(
                jax.ShapeDtypeStruct((rows, width), jnp.bfloat16),
                jax.ShapeDtypeStruct((rows, 128), jnp.float32),
                jax.ShapeDtypeStruct((rows + STAT_ROWS, width), jnp.bfloat16),
                jax.ShapeDtypeStruct((rows + STAT_ROWS, width), jnp.bfloat16),
            ),
            in_specs=[smem, whole, block, block, block, at(heads), whole, whole],
            out_specs=(block, packed, tall, tall),
            scratch_shapes=[pltpu.VMEM((rows, rows), jnp.float32)] * 5,
            compiler_params=pltpu.CompilerParams(vmem_limit_bytes=32 * 2**20),
            cost_estimate=pl.CostEstimate(
                flops=heads * 5 * rows * rows * HD * 4 * 2,
                bytes_accessed=8 * 2**20,
                transcendentals=heads * 5 * rows * rows,
            ),
            name="attend",
        )(scalars, attn_query, qa, qb, kvp, kvp, attn_key, attn_value)
        ra = lax.ppermute(oa, "seq", [(1, 2), (2, 3)])
        rb = lax.ppermute(ob, "seq", [(1, 3)])
        outs.append((own, lse, ra, rb))
        scalars, _ = lax.optimization_barrier((scalars, own))
    anywhere = pl.BlockSpec(memory_space=pl.ANY)
    whole_out = jax.ShapeDtypeStruct((rows, cols), jnp.bfloat16)
    mine = at(2 * heads)
    result = pl.pallas_call(
        lambda *refs: near_kernel(rows, *refs[:8], None, *refs[8:]),
        grid=(near,),
        out_shape=whole_out,
        in_specs=[smem, mine, mine, mine, block, at(near), block, at(near)],
        out_specs=mine,
        scratch_shapes=[pltpu.VMEM((rows, rows), jnp.float32)] * 3,
        compiler_params=pltpu.CompilerParams(vmem_limit_bytes=32 * 2**20),
        cost_estimate=pl.CostEstimate(
            flops=near * 3 * rows * rows * HD * 4 * 2,
            bytes_accessed=4 * 2**20,
            transcendentals=near * 3 * rows * rows,
        ),
        name="near",
    )(scalars, attn_query, attn_key, attn_value, kv1, kv1, kv2, kv2)
    for c in range(2):
        own, lse, ra, rb = outs[c]
        result = pl.pallas_call(
            lambda *refs: merge_kernel(rows, *refs),
            grid=(heads,),
            out_shape=whole_out,
            in_specs=[smem, block, packed, tall, tall, anywhere],
            out_specs=at(c * heads),
            input_output_aliases={5: 0},
            cost_estimate=pl.CostEstimate(
                flops=rows * width * 16, bytes_accessed=4 * 2**20, transcendentals=0
            ),
            name="merge",
        )(scalars, own, lse, ra, rb, result)
    return hyena_out, result


MESH_ID = pl.DeviceIdType.MESH
FAR = 1 << 20
CHUNK = 256
AHEAD = 4
BEHIND = 3


def start_at(pos, lens_ref):
    start = jnp.int32(0)
    end = jnp.int32(0)
    for doc in range(lens_ref.shape[0] - 1):
        end = end + lens_ref[doc]
        start = jnp.where(pos >= end, end, start)
    return start


def fused_kernel(
    rows, cols, lens_hbm, feat_hbm, q_hbm, k_hbm, v_hbm, short_hbm, med_hbm, skip_hbm, fwd_hbm, inv_hbm,
    hy_hbm, at_hbm,
    lens_ref, short_ref, med_ref, skip_ref, fwd_ref, inv_ref,
    feat, qv, kv, vv, ext, halo, up_rx, st_rx, q_near, q_far, up_tx, st_tx,
    b_own, b_own_l, b_near, b_near_l, b_far, spec, fix, hy_v, at_v,
    load_sem, hy_sem, at_sem, halo_sem, near_tx, near_rx, far_tx, far_rx, up_tx_sem, up_rx_sem,
    st_tx_sem, st_rx_sem,
):
    f32, bf16 = jnp.float32, jnp.bfloat16
    heads = cols // HD
    part = rows // 3
    span = lax.axis_index("seq")
    base = span * rows
    has_left, has_right = span > 0, span < 3
    has_far, sends_far = span < 2, span > 1

    def load(index, src, dst):
        return pltpu.make_async_copy(src, dst, load_sem.at[index])

    tail_load = load(0, feat_hbm.at[1:3, 2 * part :, :], feat.at[1:3, 2 * part :, :])
    front_load = load(1, feat_hbm.at[1:3, : 2 * part, :], feat.at[1:3, : 2 * part, :])
    mix_load = load(2, feat_hbm.at[0], feat.at[0])
    k_load = load(3, k_hbm, kv)
    v_load = load(4, v_hbm, vv)
    q_load = load(5, q_hbm, qv)
    lens_load = load(6, lens_hbm, lens_ref)
    filter_loads = [
        load(7, short_hbm, short_ref),
        load(8, med_hbm, med_ref),
        load(9, skip_hbm, skip_ref),
        load(10, fwd_hbm, fwd_ref),
        load(11, inv_hbm, inv_ref),
    ]

    def start_all(copies):
        for copy in copies:
            copy.start()

    start_all([lens_load, tail_load])
    head_loads = [k_load, v_load, q_load]
    mix_loads = filter_loads + [front_load, mix_load]
    pl.when(has_left)(lambda: start_all(mix_loads + head_loads))
    pl.when(jnp.logical_not(has_left))(lambda: start_all(head_loads + mix_loads))

    def lanes(h):
        return pl.ds(pl.multiple_of(h * HD, HD), HD)

    def remote(src, dst, tx, rx, to):
        return pltpu.make_async_remote_copy(
            src_ref=src, dst_ref=dst, send_sem=tx, recv_sem=rx, device_id={"seq": to},
            device_id_type=MESH_ID,
        )

    up_to = jnp.minimum(span + 1, 3)

    def near_copy(h):
        return remote(q_hbm.at[:, lanes(h)], q_near.at[h], near_tx.at[h], near_rx.at[h],
                      jnp.maximum(span - 1, 0))

    def far_copy(h):
        return remote(q_hbm.at[:part, lanes(h)], q_far.at[h], far_tx.at[h], far_rx.at[h],
                      jnp.maximum(span - 2, 0))

    def up_copy(h):
        return remote(up_tx.at[h], up_rx.at[h], up_tx_sem.at[h], up_rx_sem.at[h], up_to)

    def st_copy(h):
        return remote(st_tx.at[h], st_rx.at[h], st_tx_sem.at[h], st_rx_sem.at[h], up_to)

    def pass_copy(h):
        return remote(q_near.at[h, :part, :], q_far.at[h], far_tx.at[h], far_rx.at[h],
                      jnp.maximum(span - 1, 0))

    def pass_on(h):
        near_copy(h).wait_recv()
        pass_copy(h).start()
        pl.when(h + 2 < heads)(lambda: near_copy(h + 2).start())

    halo_copies = [
        remote(
            ext.at[rows : rows + part, i * cols // 2 : (i + 1) * cols // 2],
            halo.at[:, i * cols // 2 : (i + 1) * cols // 2],
            halo_sem.at[i], halo_sem.at[2 + i], up_to,
        )
        for i in range(2)
    ]

    barrier = pltpu.get_barrier_semaphore()
    for away in (-2, -1, 1, 2):

        @pl.when((span + away >= 0) & (span + away < 4))
        def _(away=away):
            pl.semaphore_signal(barrier, inc=1, device_id={"seq": span + away}, device_id_type=MESH_ID)

    pl.semaphore_wait(barrier, jnp.where(has_left & has_right, 3, 2))

    @pl.when(sends_far)
    def _():
        def send_queries(h, carry):
            pl.when(h < heads)(lambda: near_copy(h).start())
            pl.when((span == 3) & (h >= BEHIND))(lambda: far_copy(h - BEHIND).start())
            return carry

        lax.fori_loop(0, heads + BEHIND, send_queries, 0)

    @pl.when(span == 1)
    def _():
        near_copy(0).start()
        near_copy(1).start()

    chunks = cols // CHUNK

    def chunk_cols(c):
        return pl.ds(pl.multiple_of(c * CHUNK, CHUNK), CHUNK)

    def gate(lo, hi, at):
        return (feat[1, lo:hi, at].astype(f32) * feat[2, lo:hi, at].astype(f32)).astype(bf16)

    tail_load.wait()

    def gate_tail(c, carry):
        at = chunk_cols(c)
        ext[rows : rows + part, at] = gate(2 * part, rows, at)
        ext[:part, at] = jnp.zeros((part, CHUNK), bf16)
        return carry

    lax.fori_loop(0, chunks, gate_tail, 0)
    pl.when(has_right)(lambda: halo_copies[0].start())
    pl.when(has_left & has_right)(lambda: halo_copies[1].start())

    @pl.when(jnp.logical_not(has_left))
    def _():
        def clear(h, carry):
            up_rx[h] = jnp.zeros((rows + part, HD), bf16)
            st_rx[h] = jnp.zeros((8, HD), f32)
            return carry

        lax.fori_loop(0, heads, clear, 0)

    @pl.when(span == 2)
    def _():
        def clear(h, carry):
            q_far[h] = jnp.zeros((part, HD), bf16)
            return carry

        lax.fori_loop(0, heads, clear, 0)

    lens_load.wait()
    left_q = has_left & (base - start_at(base, lens_ref) > 2 * part)
    right_q = has_right & (base + rows - start_at(base + rows, lens_ref) > 2 * part)
    fresh = has_far & right_q & (start_at(base + 2 * rows, lens_ref) < base + rows)
    slot_mine = (span > 1) & (base - rows - start_at(base, lens_ref) > 2 * part)

    def column_iota(first, count):
        return first + lax.broadcasted_iota(jnp.int32, (count, 1), 0)

    own_pos = column_iota(base, rows)
    near_pos = column_iota(base + rows, rows)
    far_pos = column_iota(base + 2 * rows, part)
    key_pos = base + lax.broadcasted_iota(jnp.int32, (1, rows), 1)
    left_pos = base - 2 * part + lax.broadcasted_iota(jnp.int32, (1, 2 * part), 1)
    no_keys = jnp.where(has_left & jnp.logical_not(left_q), 0, FAR)
    no_near = jnp.where(right_q, 0, FAR)
    no_far = jnp.where(fresh, 0, FAR)
    own_start = doc_start(own_pos, lens_ref)
    near_start = doc_start(near_pos, lens_ref) + no_near
    far_start = doc_start(far_pos, lens_ref) + no_far

    def bias(ok):
        return jnp.where(ok, 0.0, NEG).astype(f32)

    b_own[...] = bias((key_pos <= own_pos) & (key_pos >= own_start))
    b_own_l[...] = bias(left_pos >= own_start + no_keys)
    b_near[...] = bias(key_pos >= near_start)
    b_near_l[...] = bias(left_pos >= near_start + no_keys)
    b_far[...] = bias(key_pos >= far_start)

    def dot(x, y):
        return jnp.dot(x, y, preferred_element_type=f32)

    first_cut = jnp.int32(FAR)
    last_cut = jnp.int32(-1)
    end = jnp.int32(0)
    for doc in range(lens_ref.shape[0] - 1):
        end = end + lens_ref[doc]
        first_cut = jnp.where((end > base) & (end < first_cut), end, first_cut)
        last_cut = jnp.where((end < base + rows) & (end > last_cut), end, last_cut)
    cuts = []
    for cut in (first_cut, last_cut):
        valid = (cut > base) & (cut < base + rows)
        block = jnp.where(valid, lax.div(jnp.where(valid, cut - base, 0), part), 0)
        cuts.append((jnp.where(valid, cut, FAR), block))
    win_iota = lax.broadcasted_iota(jnp.int32, (2 * part, 1), 0)
    out_iota = lax.broadcasted_iota(jnp.int32, (part, 1), 0)

    def transform(window, first_pos, from_pos, spec_r, spec_i):
        window = jnp.where(win_iota + first_pos >= from_pos, window, jnp.zeros_like(window))
        return spread(window, spec_r, spec_i)

    def spread(window, spec_r, spec_i):
        wave = dot(fwd_ref[0], window)
        wave_r, wave_i = wave[:part], wave[part:]
        prod = jnp.concatenate(
            (
                (wave_r * spec_r - wave_i * spec_i).astype(bf16),
                (wave_r * spec_i + wave_i * spec_r).astype(bf16),
            ),
            axis=0,
        )
        return dot(inv_ref[0], prod)

    def finish(block, at, sums, fixes):
        for (cut, cut_block), fixed in zip(cuts, fixes):
            cut_from = jnp.where(cut_block == block, cut, FAR)
            sums = jnp.where(out_iota + (base + block * part) >= cut_from, fixed, sums)
        r0 = block * part
        hy_v[r0 : r0 + part, at] = (feat[0, r0 : r0 + part, at].astype(f32) * sums).astype(bf16)

    def hyena_loads():
        front_load.wait()
        mix_load.wait()
        for copy in filter_loads:
            copy.wait()

    def hyena_main(c, carry):
        at = chunk_cols(c)
        ext[part:rows, at] = gate(0, 2 * part, at)
        short = short_ref[:, at]
        head = jnp.concatenate(
            (short[:1] + skip_ref[:, at], short[1:], jnp.zeros((8 - short.shape[0], CHUNK), f32)), axis=0
        )
        filt = jnp.concatenate((med_ref[:8, at] + head, med_ref[8:, at]), axis=0)
        filt_hi = filt.astype(bf16)
        filt_lo = (filt - filt_hi.astype(f32)).astype(bf16)
        both = (
            dot(fwd_ref[0, :, :part], filt_hi)
            + dot(fwd_ref[1, :, :part], filt_hi)
            + dot(fwd_ref[0, :, :part], filt_lo)
        )
        spec[:, at] = both
        spec_r, spec_i = both[:part], both[part:]
        fixes = []
        for index, (cut, cut_block) in enumerate(cuts):
            window = jnp.zeros((2 * part, CHUNK), bf16)
            for block in range(3):
                r0 = block * part
                cut_from = jnp.where(cut_block == block, cut, FAR)
                window = jnp.where(
                    win_iota + (base + r0 - part) >= cut_from, ext[r0 : r0 + 2 * part, at], window
                )
            sums = spread(window, spec_r, spec_i)
            fix[index, :, at] = sums
            fixes.append(sums)
        for block in (1, 2):
            r0 = block * part
            sums = transform(
                ext[r0 : r0 + 2 * part, at], base + r0 - part, start_at(base + r0, lens_ref), spec_r, spec_i
            )
            finish(block, at, sums, fixes)
        return carry

    hy_late = pltpu.make_async_copy(hy_v.at[part:, :], hy_hbm.at[part:, :], hy_sem.at[0])
    hy_first = pltpu.make_async_copy(hy_v.at[:part, :], hy_hbm.at[:part, :], hy_sem.at[1])

    def hyena_first():
        @pl.when(has_left)
        def _():
            for copy in halo_copies:
                copy.wait_recv()

        def one(c, carry):
            at = chunk_cols(c)
            window = jnp.concatenate((halo[:, at], ext[part : 2 * part, at]), axis=0)
            sums = transform(
                window, base - part, start_at(base, lens_ref), spec[:part, at], spec[part:, at]
            )
            finish(0, at, sums, [fix[i, :, at] for i in range(2)])
            return carry

        lax.fori_loop(0, chunks, one, 0)
        hy_first.start()

    @pl.when(has_left)
    def _():
        pl.when(span == 1)(lambda: pass_on(0))
        hyena_loads()

        def step(c, carry):
            for h, when in ((1, 1), (2, 3), (3, 5), (4, 7), (5, 7))[: AHEAD - 1]:

                @pl.when((span == 1) & (c == min(when, chunks - 1)))
                def _(h=h):
                    pass_on(h)

            return hyena_main(c, carry)

        lax.fori_loop(0, chunks, step, 0)
        hy_late.start()
        pl.when(sends_far)(hyena_first)

    k_load.wait()
    v_load.wait()
    q_load.wait()
    ones = jnp.ones((rows, HD), bf16)
    eye = lax.broadcasted_iota(jnp.int32, (part, HD), 0) == lax.broadcasted_iota(jnp.int32, (part, HD), 1)
    stat_iota = lax.broadcasted_iota(jnp.int32, (8, HD), 0)
    left_off = jnp.where(left_q, 0.0, NEG)
    slot_off = jnp.where(slot_mine, 0.0, NEG)

    def attend_to(q, keys, values, biases):
        scores = [
            lax.dot_general(q, k, (((1,), (1,)), ((), ())), preferred_element_type=f32) + b
            for k, b in zip(keys, biases)
        ]
        top = jnp.max(scores[0], axis=1, keepdims=True)
        for s in scores[1:]:
            top = jnp.maximum(top, jnp.max(s, axis=1, keepdims=True))
        acc = None
        for s, v in zip(scores, values):
            w = jnp.exp2((s - top) * SCALE2).astype(bf16)
            term = dot(w, v)
            acc = term if acc is None else acc + term
        return acc[:, :HD], acc[:, HD:], top * SCALE2

    spread_from = min(4, heads - chunks - 1)

    def head_step(h, carry):
        at = lanes(h)

        @pl.when(jnp.logical_not(has_left))
        def _():
            pl.when(h == spread_from)(hyena_loads)

            @pl.when((h >= spread_from) & (h < spread_from + chunks))
            def _():
                hyena_main(h - spread_from, 0)

            @pl.when(h == spread_from + chunks)
            def _():
                hy_late.start()
                hyena_first()

        @pl.when(has_left)
        def _():
            up_copy(h).wait_recv()
            st_copy(h).wait_recv()

        k = kv[:, at]
        v = vv[:, at]
        k_left = up_rx[h, : 2 * part, :]
        v_ones = jnp.concatenate((v, ones), axis=1)
        v_left = jnp.concatenate((up_rx[h, 2 * part :, :], ones[: 2 * part]), axis=1)

        @pl.when(has_right)
        def _():
            pl.when(span != 1)(lambda: near_copy(h).wait_recv())
            pl.when(has_far)(lambda: far_copy(h).wait_recv())
            tails = (k[part : 2 * part], k[2 * part :], v[part : 2 * part], v[2 * part :])
            stats = jnp.zeros((8, HD), f32)

            def give(i, out):
                up_tx[h, i * part : (i + 1) * part, :] = jnp.where(
                    right_q, out, tails[i].astype(f32)
                ).astype(bf16)

            def to_row(lse):
                return jnp.sum(jnp.where(eye, lse, 0.0), axis=0, keepdims=True)

            for i in range(3):
                r0 = i * part
                acc, total, top = attend_to(
                    q_near[h, r0 : r0 + part, :],
                    (k, k_left),
                    (v_ones, v_left),
                    (b_near[r0 : r0 + part, :], b_near_l[r0 : r0 + part, :]),
                )
                give(i, acc / total)
                stats = jnp.where(stat_iota == i, to_row(top + jnp.log2(total)), stats)
            passed = up_rx[h, rows:, :].astype(f32)
            passed_stat = st_rx[h]

            acc, total, top = attend_to(q_far[h], (k,), (v_ones,), (b_far[...],))
            give(3, jnp.where(fresh, acc / total, passed))
            lse = to_row(top + jnp.log2(total))
            st_tx[h] = jnp.where(stat_iota == 3, jnp.where(fresh, lse, passed_stat[3:4]), stats)
            up_copy(h).start()
            st_copy(h).start()
            pl.when((span == 1) & (h + AHEAD < heads))(lambda: pass_on(h + AHEAD))

        stats_in = st_rx[h]

        def column(i):
            return jnp.sum(jnp.where(eye, stats_in[i : i + 1], 0.0), axis=1, keepdims=True)

        for i in range(3):
            r0 = i * part
            r1 = r0 + part
            acc, total, top = attend_to(
                qv[r0:r1, at],
                (k[:r1], k_left),
                (v_ones[:r1], v_left),
                (b_own[r0:r1, :r1], b_own_l[r0:r1, :]),
            )
            lse = column(i) + left_off
            best = jnp.maximum(top, lse)
            if i == 0:
                slot_lse = column(3) + slot_off
                best = jnp.maximum(best, slot_lse)
            w0 = jnp.exp2(top - best)
            w1 = jnp.exp2(lse - best)
            mixed = acc * w0 + up_rx[h, r0:r1, :].astype(f32) * w1
            norm = total * w0 + w1
            if i == 0:
                w2 = jnp.exp2(slot_lse - best)
                mixed = mixed + up_rx[h, rows:, :].astype(f32) * w2
                norm = norm + w2
            at_v[r0:r1, at] = (mixed / norm).astype(bf16)
        pltpu.make_async_copy(at_v.at[:, at], at_hbm.at[:, at], at_sem.at[h]).start()
        return carry

    lax.fori_loop(0, heads, head_step, 0)
    pl.when(jnp.logical_not(has_left))(lambda: halo_copies[1].start())
    pl.when(span == 1)(hyena_first)

    def drain(h, carry):
        at = lanes(h)
        pltpu.make_async_copy(at_v.at[:, at], at_hbm.at[:, at], at_sem.at[h]).wait()

        @pl.when(has_right)
        def _():
            up_copy(h).wait_send()
            st_copy(h).wait_send()

        pl.when(has_left)(lambda: near_copy(h).wait_send())
        pl.when(span == 3)(lambda: far_copy(h).wait_send())
        pl.when(span == 1)(lambda: pass_copy(h).wait_send())
        return carry

    lax.fori_loop(0, heads, drain, 0)

    @pl.when(has_right)
    def _():
        for copy in halo_copies:
            copy.wait_send()

    hy_late.wait()
    hy_first.wait()


def land_kernel(pieces, hy_src, at_src, hy_dst, at_dst, held, in_sem, out_sem):
    step = hy_src.shape[0] // pieces
    moves = []
    for array, (src, dst) in enumerate(((hy_src, hy_dst), (at_src, at_dst))):
        for i in range(pieces):
            rows = pl.ds(i * step, step)
            here = held.at[array, rows, :]
            index = array * pieces + i
            inward = pltpu.make_async_copy(src.at[rows, :], here, in_sem.at[index])
            moves.append((inward, pltpu.make_async_copy(here, dst.at[rows, :], out_sem.at[index])))
            inward.start()
    for inward, outward in moves:
        inward.wait()
        outward.start()
    for inward, outward in moves:
        outward.wait()


def fused(features, short_filter, medium_filter, skip_gain, attn_query, attn_key, attn_value, lengths):
    rows, cols = attn_query.shape
    part = rows // 3
    heads = cols // HD
    angle = np.pi / (2 * part) * np.outer(2 * np.arange(part) + 1, np.arange(2 * part))
    wave = np.concatenate((np.cos(angle), -np.sin(angle)), axis=0)
    fwd = split_two(wave)
    inv = split_two(wave.T[part:] / part)
    anywhere = pl.BlockSpec(memory_space=pl.ANY)
    out = jax.ShapeDtypeStruct((rows, cols), jnp.bfloat16)

    def buf(*shape):
        return pltpu.VMEM(shape, jnp.bfloat16)

    def wide(*shape):
        return pltpu.VMEM(shape, jnp.float32)

    each = pltpu.SemaphoreType.DMA((heads,))
    made = pl.pallas_call(
        lambda *refs: fused_kernel(rows, cols, *refs),
        out_shape=(out, out),
        in_specs=[pl.BlockSpec(memory_space=pltpu.HBM)] * 10,
        out_specs=(anywhere, anywhere),
        scratch_shapes=[
            pltpu.SMEM(lengths.shape, jnp.int32), wide(*short_filter.shape), wide(part, cols), wide(1, cols),
            buf(*fwd.shape), buf(*inv.shape),
            buf(3, rows, cols), buf(rows, cols), buf(rows, cols), buf(rows, cols),
            buf(rows + part, cols), buf(part, cols),
            buf(heads, rows + part, HD), wide(heads, 8, HD),
            buf(heads, rows, HD), buf(heads, part, HD),
            buf(heads, rows + part, HD), wide(heads, 8, HD),
            wide(rows, rows), wide(rows, 2 * part), wide(rows, rows), wide(rows, 2 * part),
            wide(part, rows),
            wide(2 * part, cols), wide(2, part, cols),
            buf(rows, cols), buf(rows, cols),
            pltpu.SemaphoreType.DMA((12,)), pltpu.SemaphoreType.DMA((2,)), each,
            pltpu.SemaphoreType.DMA((4,)),
        ] + [each] * 8,
        compiler_params=pltpu.CompilerParams(
            collective_id=0, has_side_effects=True, vmem_limit_bytes=60 * 2**20
        ),
        cost_estimate=pl.CostEstimate(
            flops=heads * 32 * part * part * HD * 4, bytes_accessed=16 * 2**20,
            transcendentals=heads * 32 * part * part,
        ),
        name="fused",
    )(
        lengths, features.transpose(1, 0, 2), attn_query, attn_key, attn_value,
        short_filter, medium_filter, skip_gain[None, :], fwd, inv,
    )
    pieces = 4
    return pl.pallas_call(
        lambda *refs: land_kernel(pieces, *refs),
        out_shape=(out, out),
        in_specs=[anywhere] * 2,
        out_specs=(anywhere, anywhere),
        scratch_shapes=[
            buf(2, rows, cols), pltpu.SemaphoreType.DMA((2 * pieces,)), pltpu.SemaphoreType.DMA((2 * pieces,))
        ],
        compiler_params=pltpu.CompilerParams(vmem_limit_bytes=60 * 2**20),
        cost_estimate=pl.CostEstimate(flops=0, bytes_accessed=8 * rows * cols, transcendentals=0),
        name="land",
    )(*made)


def local(
    features, short_filter, medium_filter, skip_gain, attn_query, attn_key, attn_value, lengths
):
    rows, cols = attn_query.shape
    spans = lax.axis_size("seq")
    taps = medium_filter.shape[0]
    if spans == 4 and rows == 3 * taps and taps == HD and cols % CHUNK == 0 and short_filter.shape[0] < 8:
        return fused(
            features, short_filter, medium_filter, skip_gain, attn_query, attn_key, attn_value, lengths
        )
    if cols % 128 == 0 and taps % 128 == 0 and rows % taps == 0:
        hyena = hyena_fast
    else:
        hyena = hyena_mix
    hyena_out = hyena(features, short_filter, medium_filter, skip_gain, lengths)
    if spans == 4 and rows % 128 == 0 and rows <= 640 and cols % (8 * HD) == 0:
        return attention_fast(attn_query, attn_key, attn_value, lengths, hyena_out)
    return (hyena_out, attention_mix(attn_query, attn_key, attn_value, lengths))


def solution(mesh):
    in_specs = (
        P(("groups", "seq"), None, ("tensor", "sub")),
        P(None, ("tensor", "sub")),
        P(None, ("tensor", "sub")),
        P(("tensor", "sub")),
        P(("groups", "seq"), ("tensor", "sub")),
        P(("groups", "seq"), ("tensor", "sub")),
        P(("groups", "seq"), ("tensor", "sub")),
        P("groups"),
    )
    out_specs = (P(("groups", "seq"), ("tensor", "sub")), P(("groups", "seq"), ("tensor", "sub")))
    return jax.shard_map(local, mesh=mesh, in_specs=in_specs, out_specs=out_specs, check_vma=False)
```

```python
import math

import jax
import jax.numpy as jnp
import numpy as np
from jax import lax
from jax.experimental import pallas as pl
from jax.experimental.pallas import tpu as pltpu
from jax.sharding import PartitionSpec as P

HD = 128


def passed_along(value, axis, by):
    length = lax.axis_size(axis)
    pairs = [(i, i + by) for i in range(length) if 0 <= i + by < length]
    return lax.ppermute(value, axis, pairs)


def doc_of(positions, lengths):
    doc_ends = jnp.cumsum(lengths, dtype=jnp.int32)
    return jnp.sum(
        (positions[:, None] >= doc_ends[None, :]).astype(jnp.int32), axis=1, dtype=jnp.int32
    )


def hyena_mix(features, short_filter, medium_filter, skip_gain, lengths):
    row_count = features.shape[0]
    medium_taps = medium_filter.shape[0]
    rim_rows = medium_taps - 1
    span_index = lax.axis_index("seq")
    queries = features[:, 0].astype(jnp.float32)
    gated = (features[:, 1].astype(jnp.float32) * features[:, 2].astype(jnp.float32)).astype(
        jnp.bfloat16
    )
    gated = lax.optimization_barrier(gated)
    carried = passed_along(gated[row_count - rim_rows :], "seq", 1)
    extended = jnp.concatenate((carried, gated), axis=0)
    ext_positions = (
        span_index * row_count - rim_rows + jnp.arange(row_count + rim_rows, dtype=jnp.int32)
    )
    ext_docs = doc_of(ext_positions, lengths)
    ext_live = ext_positions >= 0
    own_docs = ext_docs[rim_rows:]

    def tap_term(tap_index, filter_bank):
        first_row = rim_rows - tap_index
        window = lax.dynamic_slice_in_dim(extended, first_row, row_count, 0).astype(jnp.float32)
        same_doc = lax.dynamic_slice_in_dim(ext_docs, first_row, row_count, 0) == own_docs
        live_mask = lax.dynamic_slice_in_dim(ext_live, first_row, row_count, 0)
        keep_mask = (same_doc & live_mask).astype(jnp.float32)[:, None]
        taps = lax.dynamic_index_in_dim(filter_bank, tap_index, 0, keepdims=False)
        return taps[None, :] * window * keep_mask

    short_sum = jnp.zeros(gated.shape, jnp.float32)
    for tap_index in range(short_filter.shape[0]):
        short_sum = short_sum + tap_term(tap_index, short_filter)

    def tap_block(block_index, partial_value):
        for offset in range(8):
            partial_value = partial_value + tap_term(block_index * 8 + offset, medium_filter)
        return partial_value

    medium_sum = lax.fori_loop(0, medium_taps // 8, tap_block, jnp.zeros(gated.shape, jnp.float32))
    mixed = queries * (short_sum + medium_sum + skip_gain[None, :] * gated.astype(jnp.float32))
    return mixed.astype(jnp.bfloat16)


def attention_mix(attn_query, attn_key, attn_value, lengths):
    row_count, col_count = attn_query.shape
    heads_here = col_count // HD
    span_index = lax.axis_index("seq")
    query_positions = span_index * row_count + jnp.arange(row_count, dtype=jnp.int32)
    query_docs = doc_of(query_positions, lengths)
    query_heads = attn_query.reshape(row_count, heads_here, HD)
    score_scale = HD ** (-0.5)
    last_query = query_positions[row_count - 1]
    first_query_doc = query_docs[0]

    def absorb(state_now, key_block, value_block, first_row):
        key_count = key_block.shape[0]
        last_key = first_row + key_count - 1
        last_key_doc = doc_of(jnp.reshape(last_key, (1,)), lengths)[0]
        masked_out = (first_row > last_query) | (last_key < 0) | (last_key_doc < first_query_doc)

        def compute(state_in):
            running_max, running_total, running_sum = state_in
            key_heads = key_block.reshape(key_count, heads_here, HD)
            value_heads = value_block.reshape(key_count, heads_here, HD)
            scores = (
                jnp.einsum(
                    "rhd,nhd->hrn", query_heads, key_heads, preferred_element_type=jnp.float32
                )
                * score_scale
            )
            key_positions = first_row + jnp.arange(key_count, dtype=jnp.int32)
            key_docs = doc_of(key_positions, lengths)
            allowed = (
                (key_positions[None, :] <= query_positions[:, None])
                & (key_docs[None, :] == query_docs[:, None])
                & (key_positions >= 0)[None, :]
            )
            masked = jnp.where(allowed[None], scores, -1e30)
            new_max = jnp.maximum(running_max, jnp.max(masked, axis=2))
            rescale = jnp.exp(running_max - new_max)
            weights = jnp.where(allowed[None], jnp.exp(scores - new_max[:, :, None]), 0.0)
            new_total = running_total * rescale + jnp.sum(weights, axis=2)
            product = jnp.einsum(
                "hrn,nhd->hrd",
                weights.astype(jnp.bfloat16),
                value_heads,
                preferred_element_type=jnp.float32,
            )
            new_sum = running_sum * rescale[:, :, None] + product
            return (new_max, new_total, new_sum)

        def keep_state(state_in):
            return state_in

        return lax.cond(masked_out, keep_state, compute, state_now)

    def fold_keys(state_now, pieces, first_row):
        key_all, value_all = pieces
        key_count = key_all.shape[0]
        block_rows = math.gcd(key_count, 1536)
        if block_rows == key_count:
            return absorb(state_now, key_all, value_all, first_row)
        block_total = key_count // block_rows
        key_blocks = key_all.reshape(block_total, block_rows, col_count)
        value_blocks = value_all.reshape(block_total, block_rows, col_count)

        def scan_step(state_inner, block_items):
            key_block, value_block, block_index = block_items
            return (
                absorb(state_inner, key_block, value_block, first_row + block_index * block_rows),
                None,
            )

        state_now, unused = lax.scan(
            scan_step,
            state_now,
            (key_blocks, value_blocks, jnp.arange(block_total, dtype=jnp.int32)),
        )
        return state_now

    initial = (
        jnp.full((heads_here, row_count), -1e30, jnp.float32),
        jnp.zeros((heads_here, row_count), jnp.float32),
        jnp.zeros((heads_here, row_count, HD), jnp.float32),
    )
    state_now = fold_keys(
        initial,
        (
            lax.all_gather(attn_key, "seq", axis=0, tiled=True),
            lax.all_gather(attn_value, "seq", axis=0, tiled=True),
        ),
        jnp.int32(0),
    )
    running_max, running_total, running_sum = state_now
    result = running_sum / running_total[:, :, None]
    return result.transpose(1, 0, 2).reshape(row_count, col_count).astype(jnp.bfloat16)


LOG2E = 1.4426950408889634
LN2 = 0.6931471805599453
SCALE2 = HD**-0.5 * LOG2E
NEG = -1e30
STAT_ROWS = 16


def hyena_kernel(row_count, taps, lens_ref, feat_ref, rim_ref, filt_ref, fwd_ref, inv_ref, out_ref,
                 ext_ref, sum_ref):
    base = lens_ref[lens_ref.shape[0] - 1]
    ext_ref[:taps, :] = rim_ref[...]
    ext_ref[taps:, :] = (
        feat_ref[1].astype(jnp.float32) * feat_ref[2].astype(jnp.float32)
    ).astype(jnp.bfloat16)

    def dot(x, y):
        return jnp.dot(x, y, preferred_element_type=jnp.float32)

    filt = filt_ref[...]
    filt_hi = filt.astype(jnp.bfloat16)
    filt_lo = (filt - filt_hi.astype(jnp.float32)).astype(jnp.bfloat16)
    spec = (
        dot(fwd_ref[0, :, :taps], filt_hi)
        + dot(fwd_ref[1, :, :taps], filt_hi)
        + dot(fwd_ref[0, :, :taps], filt_lo)
    )
    spec_r, spec_i = spec[:taps], spec[taps:]
    win_iota = lax.broadcasted_iota(jnp.int32, (2 * taps, 1), 0)
    out_iota = lax.broadcasted_iota(jnp.int32, (taps, 1), 0)
    for block in range(row_count // taps):
        r0 = block * taps
        start = jnp.int32(0)
        for doc in range(lens_ref.shape[0] - 1):
            end = start + lens_ref[doc]
            first, last = start - base, end - base

            @pl.when((last > r0) & (first < r0 + taps) & (first < last))
            def _(first=first):
                window = ext_ref[r0 : r0 + 2 * taps, :]
                window = jnp.where(win_iota + (r0 - taps) >= first, window, jnp.zeros_like(window))
                wave = dot(fwd_ref[0], window) + dot(fwd_ref[1], window)
                wave_r, wave_i = wave[:taps], wave[taps:]
                prod = jnp.concatenate(
                    (
                        (wave_r * spec_r - wave_i * spec_i).astype(jnp.bfloat16),
                        (wave_r * spec_i + wave_i * spec_r).astype(jnp.bfloat16),
                    ),
                    axis=0,
                )
                sums = dot(inv_ref[0], prod) + dot(inv_ref[1], prod)
                sum_ref[...] = jnp.where(out_iota + r0 >= first, sums, sum_ref[...])

            start = end
        out_ref[r0 : r0 + taps, :] = (
            feat_ref[0, r0 : r0 + taps, :].astype(jnp.float32) * sum_ref[...]
        ).astype(out_ref.dtype)


def split_two(matrix):
    high = matrix.astype(jnp.bfloat16)
    low = (matrix - high.astype(np.float64)).astype(jnp.bfloat16)
    return np.stack((high, low))


def hyena_fast(features, short_filter, medium_filter, skip_gain, lengths):
    row_count, _, cols = features.shape
    taps = medium_filter.shape[0]
    span_index = lax.axis_index("seq")
    streams = features.transpose(1, 0, 2)
    tail = streams[:, row_count - taps :]
    gated_tail = (tail[1].astype(jnp.float32) * tail[2].astype(jnp.float32)).astype(jnp.bfloat16)
    carried = passed_along(gated_tail, "seq", 1)
    head = jnp.concatenate((short_filter[:1] + skip_gain[None, :], short_filter[1:]), axis=0)
    filt = medium_filter + jnp.pad(head, ((0, taps - head.shape[0]), (0, 0)))
    angle = np.pi / (2 * taps) * np.outer(2 * np.arange(taps) + 1, np.arange(2 * taps))
    fwd = split_two(np.concatenate((np.cos(angle), -np.sin(angle)), axis=0))
    inv = split_two(
        np.concatenate((np.cos(angle), -np.sin(angle)), axis=0).T[taps:] / taps
    )
    scalars = jnp.concatenate((lengths, jnp.reshape(span_index * row_count, (1,)).astype(jnp.int32)))
    width = math.gcd(cols, 512)
    return pl.pallas_call(
        lambda *refs: hyena_kernel(row_count, taps, *refs),
        grid=(cols // width,),
        out_shape=jax.ShapeDtypeStruct((row_count, cols), jnp.bfloat16),
        in_specs=[
            pl.BlockSpec(memory_space=pltpu.SMEM),
            pl.BlockSpec((3, row_count, width), lambda i: (0, 0, i)),
            pl.BlockSpec((taps, width), lambda i: (0, i)),
            pl.BlockSpec((taps, width), lambda i: (0, i)),
            pl.BlockSpec(fwd.shape, lambda i: (0, 0, 0)),
            pl.BlockSpec(inv.shape, lambda i: (0, 0, 0)),
        ],
        out_specs=pl.BlockSpec((row_count, width), lambda i: (0, i)),
        scratch_shapes=[
            pltpu.VMEM((row_count + taps, width), jnp.bfloat16),
            pltpu.VMEM((taps, width), jnp.float32),
        ],
        compiler_params=pltpu.CompilerParams(vmem_limit_bytes=32 * 2**20),
        cost_estimate=pl.CostEstimate(
            flops=2 * 9 * 2 * taps * taps * 3 * cols, bytes_accessed=8 * 2**20, transcendentals=0
        ),
        name="hyena",
    )(scalars, streams, carried, filt, fwd, inv)


def doc_start(pos, lens_ref):
    start = jnp.zeros_like(pos)
    end = jnp.int32(0)
    for doc in range(lens_ref.shape[0] - 1):
        end = end + lens_ref[doc]
        start = jnp.where(pos >= end, end, start)
    return start


def attend(query_ref, keys, values, biases, emit):
    rows = query_ref.shape[0]
    step = 128
    ones = jnp.ones((rows, 128), jnp.bfloat16)
    vals = [jnp.concatenate((v[...], ones), axis=1) for v in values]
    for r in range(0, rows, step):
        q = query_ref[r : r + step, :]
        scores = [
            lax.dot_general(q, k[...], (((1,), (1,)), ((), ())),
                            preferred_element_type=jnp.float32) + b[r : r + step, :]
            for k, b in zip(keys, biases)
        ]
        top = jnp.max(scores[0], axis=1, keepdims=True)
        for s in scores[1:]:
            top = jnp.maximum(top, jnp.max(s, axis=1, keepdims=True))
        acc = None
        for s, v in zip(scores, vals):
            w = jnp.exp2((s - top) * SCALE2).astype(jnp.bfloat16)
            part = jnp.dot(w, v, preferred_element_type=jnp.float32)
            acc = part if acc is None else acc + part
        total = acc[:, 128:]
        emit(r, acc[:, :128] / total, top * SCALE2 + jnp.log2(total))


def needs(lens_ref, base, rows, ahead, back):
    q_first = base + ahead * rows
    start = jnp.int32(0)
    end = jnp.int32(0)
    for doc in range(lens_ref.shape[0] - 1):
        end = end + lens_ref[doc]
        start = jnp.where(q_first >= end, end, start)
    return start < base + (1 - back) * rows


def fill_bias(lens_ref, base, rows, ref, ahead, back):
    qpos = base + ahead * rows + lax.broadcasted_iota(jnp.int32, (rows, 1), 0)
    starts = doc_start(qpos, lens_ref)
    kpos = base - back * rows + lax.broadcasted_iota(jnp.int32, (1, rows), 1)
    ref[...] = jnp.where((kpos <= qpos) & (kpos >= starts), 0.0, NEG).astype(jnp.float32)


def near_kernel(rows, lens_ref, q_ref, k_ref, v_ref, k1_ref, v1_ref, k2_ref, v2_ref, all_ref, o_ref,
                b0, b1, b2):
    span = lens_ref[lens_ref.shape[0] - 1]
    base = span * rows
    one = (span >= 1) & needs(lens_ref, base, rows, 0, 1)
    two = (span >= 2) & needs(lens_ref, base, rows, 0, 2)

    @pl.when(pl.program_id(0) == 0)
    def _():
        fill_bias(lens_ref, base, rows, b0, 0, 0)
        pl.when(one)(lambda: fill_bias(lens_ref, base, rows, b1, 0, 1))
        pl.when(two)(lambda: fill_bias(lens_ref, base, rows, b2, 0, 2))

    def emit(r, out, lse):
        o_ref[r : r + 128, :] = out.astype(jnp.bfloat16)

    pl.when(two)(
        lambda: attend(q_ref, (k_ref, k1_ref, k2_ref), (v_ref, v1_ref, v2_ref), (b0, b1, b2), emit)
    )
    pl.when(one & jnp.logical_not(two))(
        lambda: attend(q_ref, (k_ref, k1_ref), (v_ref, v1_ref), (b0, b1), emit)
    )
    pl.when(jnp.logical_not(one))(lambda: attend(q_ref, (k_ref,), (v_ref,), (b0,), emit))


def attn_kernel(rows, lens_ref, q_ref, qa_ref, qb_ref, kp_ref, vp_ref, k_ref, v_ref,
                o_ref, lse_ref, oa_ref, ob_ref, b00, b10, b01, b11, b02):
    span = lens_ref[lens_ref.shape[0] - 1]
    base = span * rows

    def reads(ahead, back):
        return needs(lens_ref, base, rows, ahead, back)

    own_prev = (span == 1) & reads(0, 1)
    a_here = ((span == 1) | (span == 2)) & reads(1, 0)
    a_prev = (span == 1) & reads(1, 1)
    b_here = (span == 1) & reads(2, 0)

    @pl.when(pl.program_id(0) == 0)
    def _():
        lse_ref[...] = jnp.zeros_like(lse_ref)

        def fill(ref, ahead, back):
            fill_bias(lens_ref, base, rows, ref, ahead, back)

        fill(b00, 0, 0)
        pl.when(own_prev)(lambda: fill(b01, 0, 1))
        pl.when(a_here)(lambda: fill(b10, 1, 0))
        pl.when(a_prev)(lambda: fill(b11, 1, 1))
        pl.when(b_here)(lambda: fill(b02, 2, 0))

    step = 128
    head_lane = lax.broadcasted_iota(jnp.int32, (step, 128), 1) == pl.program_id(0)

    def emit_own(r, out, lse):
        o_ref[r : r + step, :] = out.astype(jnp.bfloat16)
        lse_ref[r : r + step, :] = jnp.where(head_lane, lse, lse_ref[r : r + step, :])

    eye = lax.broadcasted_iota(jnp.int32, (128, 128), 0) == lax.broadcasted_iota(
        jnp.int32, (128, 128), 1
    )
    stat_iota = lax.broadcasted_iota(jnp.int32, (STAT_ROWS, 128), 0)

    def emit_to(ref):
        stats = [jnp.zeros((STAT_ROWS, 128), jnp.float32)]

        def emit(r, out, lse):
            ref[r : r + step, :] = out.astype(jnp.bfloat16)
            rest = jnp.sum(jnp.where(eye, lse, 0.0), axis=0, keepdims=True)
            for piece in range(3):
                high = rest.astype(jnp.bfloat16).astype(jnp.float32)
                stats[0] = jnp.where(stat_iota == piece * (rows // step) + r // step, high, stats[0])
                rest = rest - high
            if r + step == rows:
                ref[rows:, :] = stats[0].astype(jnp.bfloat16)

        return emit

    def empty(ref):
        ref[:rows, :] = jnp.zeros((rows, 128), jnp.bfloat16)
        ref[rows:, :] = jnp.where(stat_iota < rows // step, NEG, 0.0).astype(jnp.bfloat16)

    pl.when(own_prev)(lambda: attend(q_ref, (kp_ref, k_ref), (vp_ref, v_ref), (b01, b00), emit_own))
    pl.when(jnp.logical_not(own_prev))(lambda: attend(q_ref, (k_ref,), (v_ref,), (b00,), emit_own))
    pl.when(a_prev)(
        lambda: attend(qa_ref, (kp_ref, k_ref), (vp_ref, v_ref), (b11, b10), emit_to(oa_ref))
    )
    pl.when(a_here & jnp.logical_not(a_prev))(
        lambda: attend(qa_ref, (k_ref,), (v_ref,), (b10,), emit_to(oa_ref))
    )
    pl.when(jnp.logical_not(a_here))(lambda: empty(oa_ref))
    pl.when(b_here)(lambda: attend(qb_ref, (k_ref,), (v_ref,), (b02,), emit_to(ob_ref)))
    pl.when(jnp.logical_not(b_here))(lambda: empty(ob_ref))


def merge_kernel(rows, lens_ref, o_ref, lse_ref, ra_ref, rb_ref, all_ref, out_ref):
    span = lens_ref[lens_ref.shape[0] - 1]
    step = 128
    eye = lax.broadcasted_iota(jnp.int32, (128, 128), 0) == lax.broadcasted_iota(
        jnp.int32, (128, 128), 1
    )

    @pl.when(span < 2)
    def _():
        out_ref[...] = o_ref[...]

    @pl.when(span >= 2)
    def _():
        blocks = rows // step
        head_lane = lax.broadcasted_iota(jnp.int32, (step, 128), 1) == pl.program_id(0)
        stat_a = ra_ref[rows:, :].astype(jnp.float32)
        stat_b = rb_ref[rows:, :].astype(jnp.float32)

        def column(stats, i):
            row = (stats[i : i + 1] + stats[blocks + i : blocks + i + 1]) + stats[
                2 * blocks + i : 2 * blocks + i + 1
            ]
            return jnp.sum(jnp.where(eye, row, 0.0), axis=1, keepdims=True)

        for i in range(blocks):
            r = i * step
            own = jnp.sum(jnp.where(head_lane, lse_ref[r : r + step, :], 0.0), axis=1, keepdims=True)
            lse_a = column(stat_a, i)
            lse_b = jnp.where(span == 3, column(stat_b, i), NEG)
            top = jnp.maximum(own, jnp.maximum(lse_a, lse_b))
            w0 = jnp.exp2(own - top)
            w1 = jnp.exp2(lse_a - top)
            w2 = jnp.exp2(lse_b - top)
            total = (
                o_ref[r : r + step, :].astype(jnp.float32) * w0
                + ra_ref[r : r + step, :].astype(jnp.float32) * w1
                + rb_ref[r : r + step, :].astype(jnp.float32) * w2
            )
            out_ref[r : r + step, :] = (total / (w0 + w1 + w2)).astype(jnp.bfloat16)


def attention_fast(attn_query, attn_key, attn_value, lengths, hyena_out):
    rows, cols = attn_query.shape
    span_index = lax.axis_index("seq")
    scalars = jnp.concatenate((lengths, jnp.reshape(span_index, (1,)).astype(jnp.int32)))
    all_heads = cols // HD
    heads = all_heads * 3 // 8
    near = all_heads - 2 * heads
    width = heads * HD
    smem = pl.BlockSpec(memory_space=pltpu.SMEM)
    block = pl.BlockSpec((rows, HD), lambda h: (0, h))
    tall = pl.BlockSpec((rows + STAT_ROWS, HD), lambda h: (0, h))
    packed = pl.BlockSpec((rows, 128), lambda h: (0, 0))

    def at(offset):
        return pl.BlockSpec((rows, HD), lambda h: (0, offset + h))

    def pair(lo, hi):
        return jnp.concatenate((attn_key[:, lo:hi], attn_value[:, lo:hi]), axis=1)

    sent = []
    for c in range(2):
        qc = attn_query[:, c * width : (c + 1) * width]
        qa = lax.ppermute(qc, "seq", [(2, 1), (3, 2)])
        qb = lax.ppermute(qc, "seq", [(3, 1)])
        kv = pair(c * width, (c + 1) * width)
        sent.append((qa, qb, lax.ppermute(kv, "seq", [(0, 1)])))
    kv = pair(2 * width, cols)
    kv1 = lax.ppermute(kv, "seq", [(0, 1), (1, 2), (2, 3)])
    kv2 = lax.ppermute(kv, "seq", [(0, 2), (1, 3)])
    scalars, hyena_out = lax.optimization_barrier((scalars, hyena_out))
    outs = []
    for c in range(2):
        qa, qb, kvp = sent[c]
        whole = at(c * heads)
        own, lse, oa, ob = pl.pallas_call(
            lambda *refs: attn_kernel(rows, *refs),
            grid=(heads,),
            out_shape=(
                jax.ShapeDtypeStruct((rows, width), jnp.bfloat16),
                jax.ShapeDtypeStruct((rows, 128), jnp.float32),
                jax.ShapeDtypeStruct((rows + STAT_ROWS, width), jnp.bfloat16),
                jax.ShapeDtypeStruct((rows + STAT_ROWS, width), jnp.bfloat16),
            ),
            in_specs=[smem, whole, block, block, block, at(heads), whole, whole],
            out_specs=(block, packed, tall, tall),
            scratch_shapes=[pltpu.VMEM((rows, rows), jnp.float32)] * 5,
            compiler_params=pltpu.CompilerParams(vmem_limit_bytes=32 * 2**20),
            cost_estimate=pl.CostEstimate(
                flops=heads * 5 * rows * rows * HD * 4 * 2,
                bytes_accessed=8 * 2**20,
                transcendentals=heads * 5 * rows * rows,
            ),
            name="attend",
        )(scalars, attn_query, qa, qb, kvp, kvp, attn_key, attn_value)
        ra = lax.ppermute(oa, "seq", [(1, 2), (2, 3)])
        rb = lax.ppermute(ob, "seq", [(1, 3)])
        outs.append((own, lse, ra, rb))
        scalars, _ = lax.optimization_barrier((scalars, own))
    anywhere = pl.BlockSpec(memory_space=pl.ANY)
    whole_out = jax.ShapeDtypeStruct((rows, cols), jnp.bfloat16)
    mine = at(2 * heads)
    result = pl.pallas_call(
        lambda *refs: near_kernel(rows, *refs[:8], None, *refs[8:]),
        grid=(near,),
        out_shape=whole_out,
        in_specs=[smem, mine, mine, mine, block, at(near), block, at(near)],
        out_specs=mine,
        scratch_shapes=[pltpu.VMEM((rows, rows), jnp.float32)] * 3,
        compiler_params=pltpu.CompilerParams(vmem_limit_bytes=32 * 2**20),
        cost_estimate=pl.CostEstimate(
            flops=near * 3 * rows * rows * HD * 4 * 2,
            bytes_accessed=4 * 2**20,
            transcendentals=near * 3 * rows * rows,
        ),
        name="near",
    )(scalars, attn_query, attn_key, attn_value, kv1, kv1, kv2, kv2)
    for c in range(2):
        own, lse, ra, rb = outs[c]
        result = pl.pallas_call(
            lambda *refs: merge_kernel(rows, *refs),
            grid=(heads,),
            out_shape=whole_out,
            in_specs=[smem, block, packed, tall, tall, anywhere],
            out_specs=at(c * heads),
            input_output_aliases={5: 0},
            cost_estimate=pl.CostEstimate(
                flops=rows * width * 16, bytes_accessed=4 * 2**20, transcendentals=0
            ),
            name="merge",
        )(scalars, own, lse, ra, rb, result)
    return hyena_out, result


MESH_ID = pl.DeviceIdType.MESH
FAR = 1 << 20
CHUNK = 256
AHEAD = 4
BEHIND = 3


def start_at(pos, lens_ref):
    start = jnp.int32(0)
    end = jnp.int32(0)
    for doc in range(lens_ref.shape[0] - 1):
        end = end + lens_ref[doc]
        start = jnp.where(pos >= end, end, start)
    return start


def fused_kernel(
    rows, cols, lens_hbm, feat_hbm, q_hbm, k_hbm, v_hbm, short_hbm, med_hbm, skip_hbm, fwd_hbm, inv_hbm,
    hy_hbm, at_hbm,
    lens_ref, short_ref, med_ref, skip_ref, fwd_ref, inv_ref,
    feat, qv, kv, vv, ext, halo, up_rx, st_rx, q_near, q_far, up_tx, st_tx,
    b_own, b_own_l, b_near, b_near_l, b_far, spec, fix, hy_v, at_v,
    load_sem, hy_sem, at_sem, halo_sem, near_tx, near_rx, far_tx, far_rx, up_tx_sem, up_rx_sem,
    st_tx_sem, st_rx_sem,
):
    f32, bf16 = jnp.float32, jnp.bfloat16
    heads = cols // HD
    part = rows // 3
    span = lax.axis_index("seq")
    base = span * rows
    has_left, has_right = span > 0, span < 3
    has_far, sends_far = span < 2, span > 1

    def load(index, src, dst):
        return pltpu.make_async_copy(src, dst, load_sem.at[index])

    tail_load = load(0, feat_hbm.at[1:3, 2 * part :, :], feat.at[1:3, 2 * part :, :])
    front_load = load(1, feat_hbm.at[1:3, : 2 * part, :], feat.at[1:3, : 2 * part, :])
    mix_load = load(2, feat_hbm.at[0], feat.at[0])
    k_load = load(3, k_hbm, kv)
    v_load = load(4, v_hbm, vv)
    q_load = load(5, q_hbm, qv)
    lens_load = load(6, lens_hbm, lens_ref)
    filter_loads = [
        load(7, short_hbm, short_ref),
        load(8, med_hbm, med_ref),
        load(9, skip_hbm, skip_ref),
        load(10, fwd_hbm, fwd_ref),
        load(11, inv_hbm, inv_ref),
    ]

    def start_all(copies):
        for copy in copies:
            copy.start()

    start_all([lens_load, tail_load])
    head_loads = [k_load, v_load, q_load]
    mix_loads = filter_loads + [front_load, mix_load]
    pl.when(has_left)(lambda: start_all(mix_loads + head_loads))
    pl.when(jnp.logical_not(has_left))(lambda: start_all(head_loads + mix_loads))

    def lanes(h):
        return pl.ds(pl.multiple_of(h * HD, HD), HD)

    def remote(src, dst, tx, rx, to):
        return pltpu.make_async_remote_copy(
            src_ref=src, dst_ref=dst, send_sem=tx, recv_sem=rx, device_id={"seq": to},
            device_id_type=MESH_ID,
        )

    up_to = jnp.minimum(span + 1, 3)

    def near_copy(h):
        return remote(q_hbm.at[:, lanes(h)], q_near.at[h], near_tx.at[h], near_rx.at[h],
                      jnp.maximum(span - 1, 0))

    def far_copy(h):
        return remote(q_hbm.at[:part, lanes(h)], q_far.at[h], far_tx.at[h], far_rx.at[h],
                      jnp.maximum(span - 2, 0))

    def up_copy(h):
        return remote(up_tx.at[h], up_rx.at[h], up_tx_sem.at[h], up_rx_sem.at[h], up_to)

    def st_copy(h):
        return remote(st_tx.at[h], st_rx.at[h], st_tx_sem.at[h], st_rx_sem.at[h], up_to)

    def pass_copy(h):
        return remote(q_near.at[h, :part, :], q_far.at[h], far_tx.at[h], far_rx.at[h],
                      jnp.maximum(span - 1, 0))

    def pass_on(h):
        near_copy(h).wait_recv()
        pass_copy(h).start()
        pl.when(h + 2 < heads)(lambda: near_copy(h + 2).start())

    halo_copies = [
        remote(
            ext.at[rows : rows + part, lo:hi],
            halo.at[:, lo:hi],
            halo_sem.at[i], halo_sem.at[2 + i], up_to,
        )
        for i, (lo, hi) in enumerate(((0, cols // 4), (cols // 4, cols)))
    ]

    barrier = pltpu.get_barrier_semaphore()
    for away in (-2, -1, 1, 2):

        @pl.when((span + away >= 0) & (span + away < 4))
        def _(away=away):
            pl.semaphore_signal(barrier, inc=1, device_id={"seq": span + away}, device_id_type=MESH_ID)

    pl.semaphore_wait(barrier, jnp.where(has_left & has_right, 3, 2))

    @pl.when(sends_far)
    def _():
        def send_queries(h, carry):
            pl.when(h < heads)(lambda: near_copy(h).start())
            pl.when((span == 3) & (h >= BEHIND))(lambda: far_copy(h - BEHIND).start())
            return carry

        lax.fori_loop(0, heads + BEHIND, send_queries, 0)

    @pl.when(span == 1)
    def _():
        near_copy(0).start()
        near_copy(1).start()

    chunks = cols // CHUNK

    def chunk_cols(c):
        return pl.ds(pl.multiple_of(c * CHUNK, CHUNK), CHUNK)

    def gate(lo, hi, at):
        return (feat[1, lo:hi, at].astype(f32) * feat[2, lo:hi, at].astype(f32)).astype(bf16)

    tail_load.wait()

    def gate_tail(c, carry):
        at = chunk_cols(c)
        ext[rows : rows + part, at] = gate(2 * part, rows, at)
        ext[:part, at] = jnp.zeros((part, CHUNK), bf16)
        return carry

    lax.fori_loop(0, chunks, gate_tail, 0)
    pl.when(has_right)(lambda: halo_copies[0].start())
    pl.when(has_left & has_right)(lambda: halo_copies[1].start())

    @pl.when(jnp.logical_not(has_left))
    def _():
        def clear(h, carry):
            up_rx[h] = jnp.zeros((rows + part, HD), bf16)
            st_rx[h] = jnp.zeros((8, HD), f32)
            return carry

        lax.fori_loop(0, heads, clear, 0)

    @pl.when(span == 2)
    def _():
        def clear(h, carry):
            q_far[h] = jnp.zeros((part, HD), bf16)
            return carry

        lax.fori_loop(0, heads, clear, 0)

    lens_load.wait()
    left_q = has_left & (base - start_at(base, lens_ref) > 2 * part)
    right_q = has_right & (base + rows - start_at(base + rows, lens_ref) > 2 * part)
    fresh = has_far & right_q & (start_at(base + 2 * rows, lens_ref) < base + rows)
    slot_mine = (span > 1) & (base - rows - start_at(base, lens_ref) > 2 * part)

    def column_iota(first, count):
        return first + lax.broadcasted_iota(jnp.int32, (count, 1), 0)

    own_pos = column_iota(base, rows)
    near_pos = column_iota(base + rows, rows)
    far_pos = column_iota(base + 2 * rows, part)
    key_pos = base + lax.broadcasted_iota(jnp.int32, (1, rows), 1)
    left_pos = base - 2 * part + lax.broadcasted_iota(jnp.int32, (1, 2 * part), 1)
    no_keys = jnp.where(has_left & jnp.logical_not(left_q), 0, FAR)
    no_near = jnp.where(right_q, 0, FAR)
    no_far = jnp.where(fresh, 0, FAR)
    own_start = doc_start(own_pos, lens_ref)
    near_start = doc_start(near_pos, lens_ref) + no_near
    far_start = doc_start(far_pos, lens_ref) + no_far

    def bias(ok):
        return jnp.where(ok, 0.0, NEG).astype(f32)

    b_own[...] = bias((key_pos <= own_pos) & (key_pos >= own_start))
    b_own_l[...] = bias(left_pos >= own_start + no_keys)
    b_near[...] = bias(key_pos >= near_start)
    b_near_l[...] = bias(left_pos >= near_start + no_keys)
    b_far[...] = bias(key_pos >= far_start)

    def dot(x, y):
        return jnp.dot(x, y, preferred_element_type=f32)

    first_cut = jnp.int32(FAR)
    last_cut = jnp.int32(-1)
    end = jnp.int32(0)
    for doc in range(lens_ref.shape[0] - 1):
        end = end + lens_ref[doc]
        first_cut = jnp.where((end > base) & (end < first_cut), end, first_cut)
        last_cut = jnp.where((end < base + rows) & (end > last_cut), end, last_cut)
    cuts = []
    for cut in (first_cut, last_cut):
        valid = (cut > base) & (cut < base + rows)
        block = jnp.where(valid, lax.div(jnp.where(valid, cut - base, 0), part), 0)
        cuts.append((jnp.where(valid, cut, FAR), block))
    win_iota = lax.broadcasted_iota(jnp.int32, (2 * part, 1), 0)
    out_iota = lax.broadcasted_iota(jnp.int32, (part, 1), 0)

    def transform(window, first_pos, from_pos, spec_r, spec_i):
        window = jnp.where(win_iota + first_pos >= from_pos, window, jnp.zeros_like(window))
        return spread(window, spec_r, spec_i)

    def spread(window, spec_r, spec_i):
        wave = dot(fwd_ref[0], window)
        wave_r, wave_i = wave[:part], wave[part:]
        prod = jnp.concatenate(
            (
                (wave_r * spec_r - wave_i * spec_i).astype(bf16),
                (wave_r * spec_i + wave_i * spec_r).astype(bf16),
            ),
            axis=0,
        )
        return dot(inv_ref[0], prod)

    def finish(block, at, sums, fixes):
        for (cut, cut_block), fixed in zip(cuts, fixes):
            cut_from = jnp.where(cut_block == block, cut, FAR)
            sums = jnp.where(out_iota + (base + block * part) >= cut_from, fixed, sums)
        r0 = block * part
        hy_v[r0 : r0 + part, at] = (feat[0, r0 : r0 + part, at].astype(f32) * sums).astype(bf16)

    def hyena_loads():
        front_load.wait()
        mix_load.wait()
        for copy in filter_loads:
            copy.wait()

    def hyena_main(c, carry):
        at = chunk_cols(c)
        ext[part:rows, at] = gate(0, 2 * part, at)
        short = short_ref[:, at]
        head = jnp.concatenate(
            (short[:1] + skip_ref[:, at], short[1:], jnp.zeros((8 - short.shape[0], CHUNK), f32)), axis=0
        )
        filt = jnp.concatenate((med_ref[:8, at] + head, med_ref[8:, at]), axis=0)
        filt_hi = filt.astype(bf16)
        filt_lo = (filt - filt_hi.astype(f32)).astype(bf16)
        both = (
            dot(fwd_ref[0, :, :part], filt_hi)
            + dot(fwd_ref[1, :, :part], filt_hi)
            + dot(fwd_ref[0, :, :part], filt_lo)
        )
        spec[:, at] = both
        spec_r, spec_i = both[:part], both[part:]
        fixes = []
        for index, (cut, cut_block) in enumerate(cuts):
            window = jnp.zeros((2 * part, CHUNK), bf16)
            for block in range(3):
                r0 = block * part
                cut_from = jnp.where(cut_block == block, cut, FAR)
                window = jnp.where(
                    win_iota + (base + r0 - part) >= cut_from, ext[r0 : r0 + 2 * part, at], window
                )
            sums = spread(window, spec_r, spec_i)
            fix[index, :, at] = sums
            fixes.append(sums)
        for block in (1, 2):
            r0 = block * part
            sums = transform(
                ext[r0 : r0 + 2 * part, at], base + r0 - part, start_at(base + r0, lens_ref), spec_r, spec_i
            )
            finish(block, at, sums, fixes)
        return carry

    hy_late = pltpu.make_async_copy(hy_v.at[part:, :], hy_hbm.at[part:, :], hy_sem.at[0])
    hy_first = pltpu.make_async_copy(hy_v.at[:part, :], hy_hbm.at[:part, :], hy_sem.at[1])

    def hyena_first():
        @pl.when(has_left)
        def _():
            for copy in halo_copies:
                copy.wait_recv()

        def one(c, carry):
            at = chunk_cols(c)
            window = jnp.concatenate((halo[:, at], ext[part : 2 * part, at]), axis=0)
            sums = transform(
                window, base - part, start_at(base, lens_ref), spec[:part, at], spec[part:, at]
            )
            finish(0, at, sums, [fix[i, :, at] for i in range(2)])
            return carry

        lax.fori_loop(0, chunks, one, 0, unroll=2)
        hy_first.start()

    @pl.when(has_left)
    def _():
        pl.when(span == 1)(lambda: pass_on(0))
        hyena_loads()

        def step(c, carry):
            for h, when in ((1, 1), (2, 3), (3, 5), (4, 7), (5, 7))[: AHEAD - 1]:

                @pl.when((span == 1) & (c == min(when, chunks - 1)))
                def _(h=h):
                    pass_on(h)

            return hyena_main(c, carry)

        lax.fori_loop(0, chunks, step, 0)
        hy_late.start()
        pl.when(sends_far)(hyena_first)

    k_load.wait()
    v_load.wait()
    q_load.wait()
    ones = jnp.ones((rows, HD), bf16)
    eye = lax.broadcasted_iota(jnp.int32, (part, HD), 0) == lax.broadcasted_iota(jnp.int32, (part, HD), 1)
    stat_iota = lax.broadcasted_iota(jnp.int32, (8, HD), 0)
    left_off = jnp.where(left_q, 0.0, NEG)
    slot_off = jnp.where(slot_mine, 0.0, NEG)

    def attend_to(q, keys, values, biases):
        scores = [
            lax.dot_general(q, k, (((1,), (1,)), ((), ())), preferred_element_type=f32) + b
            for k, b in zip(keys, biases)
        ]
        top = jnp.max(scores[0], axis=1, keepdims=True)
        for s in scores[1:]:
            top = jnp.maximum(top, jnp.max(s, axis=1, keepdims=True))
        acc = None
        for s, v in zip(scores, values):
            w = jnp.exp2((s - top) * SCALE2).astype(bf16)
            term = dot(w, v)
            acc = term if acc is None else acc + term
        return acc[:, :HD], acc[:, HD:], top * SCALE2

    spread_from = min(4, heads - chunks - 1)

    def head_step(h, carry):
        at = lanes(h)

        @pl.when(jnp.logical_not(has_left))
        def _():
            pl.when(h == spread_from)(hyena_loads)

            @pl.when((h >= spread_from) & (h < spread_from + chunks))
            def _():
                hyena_main(h - spread_from, 0)

            @pl.when(h == spread_from + chunks)
            def _():
                hy_late.start()
                hyena_first()

        @pl.when(has_left)
        def _():
            up_copy(h).wait_recv()
            st_copy(h).wait_recv()

        k = kv[:, at]
        v = vv[:, at]
        k_left = up_rx[h, : 2 * part, :]
        v_ones = jnp.concatenate((v, ones), axis=1)
        v_left = jnp.concatenate((up_rx[h, 2 * part :, :], ones[: 2 * part]), axis=1)

        @pl.when(has_right)
        def _():
            pl.when(span != 1)(lambda: near_copy(h).wait_recv())
            pl.when(has_far)(lambda: far_copy(h).wait_recv())
            tails = (k[part : 2 * part], k[2 * part :], v[part : 2 * part], v[2 * part :])
            stats = jnp.zeros((8, HD), f32)

            def give(i, out):
                up_tx[h, i * part : (i + 1) * part, :] = jnp.where(
                    right_q, out, tails[i].astype(f32)
                ).astype(bf16)

            def to_row(lse):
                return jnp.sum(jnp.where(eye, lse, 0.0), axis=0, keepdims=True)

            for i in range(3):
                r0 = i * part
                acc, total, top = attend_to(
                    q_near[h, r0 : r0 + part, :],
                    (k, k_left),
                    (v_ones, v_left),
                    (b_near[r0 : r0 + part, :], b_near_l[r0 : r0 + part, :]),
                )
                give(i, acc / total)
                stats = jnp.where(stat_iota == i, to_row(top + jnp.log2(total)), stats)
            passed = up_rx[h, rows:, :].astype(f32)
            passed_stat = st_rx[h]

            acc, total, top = attend_to(q_far[h], (k,), (v_ones,), (b_far[...],))
            give(3, jnp.where(fresh, acc / total, passed))
            lse = to_row(top + jnp.log2(total))
            st_tx[h] = jnp.where(stat_iota == 3, jnp.where(fresh, lse, passed_stat[3:4]), stats)
            up_copy(h).start()
            st_copy(h).start()
            pl.when((span == 1) & (h + AHEAD < heads))(lambda: pass_on(h + AHEAD))

        stats_in = st_rx[h]

        def column(i):
            return jnp.sum(jnp.where(eye, stats_in[i : i + 1], 0.0), axis=1, keepdims=True)

        for i in range(3):
            r0 = i * part
            r1 = r0 + part
            acc, total, top = attend_to(
                qv[r0:r1, at],
                (k[:r1], k_left),
                (v_ones[:r1], v_left),
                (b_own[r0:r1, :r1], b_own_l[r0:r1, :]),
            )
            lse = column(i) + left_off
            best = jnp.maximum(top, lse)
            if i == 0:
                slot_lse = column(3) + slot_off
                best = jnp.maximum(best, slot_lse)
            w0 = jnp.exp2(top - best)
            w1 = jnp.exp2(lse - best)
            mixed = acc * w0 + up_rx[h, r0:r1, :].astype(f32) * w1
            norm = total * w0 + w1
            if i == 0:
                w2 = jnp.exp2(slot_lse - best)
                mixed = mixed + up_rx[h, rows:, :].astype(f32) * w2
                norm = norm + w2
            at_v[r0:r1, at] = (mixed / norm).astype(bf16)
        pltpu.make_async_copy(at_v.at[:, at], at_hbm.at[:, at], at_sem.at[h]).start()
        return carry

    lax.fori_loop(0, heads, head_step, 0)
    pl.when(jnp.logical_not(has_left))(lambda: halo_copies[1].start())
    pl.when(span == 1)(hyena_first)

    def drain(h, carry):
        at = lanes(h)
        pltpu.make_async_copy(at_v.at[:, at], at_hbm.at[:, at], at_sem.at[h]).wait()

        @pl.when(has_right)
        def _():
            up_copy(h).wait_send()
            st_copy(h).wait_send()

        pl.when(has_left)(lambda: near_copy(h).wait_send())
        pl.when(span == 3)(lambda: far_copy(h).wait_send())
        pl.when(span == 1)(lambda: pass_copy(h).wait_send())
        return carry

    lax.fori_loop(0, heads, drain, 0)

    @pl.when(has_right)
    def _():
        for copy in halo_copies:
            copy.wait_send()

    hy_late.wait()
    hy_first.wait()


def land_kernel(pieces, hy_src, at_src, hy_dst, at_dst, held, in_sem, out_sem):
    step = hy_src.shape[0] // pieces
    moves = []
    for array, (src, dst) in enumerate(((hy_src, hy_dst), (at_src, at_dst))):
        for i in range(pieces):
            rows = pl.ds(i * step, step)
            here = held.at[array, rows, :]
            index = array * pieces + i
            inward = pltpu.make_async_copy(src.at[rows, :], here, in_sem.at[index])
            moves.append((inward, pltpu.make_async_copy(here, dst.at[rows, :], out_sem.at[index])))
            inward.start()
    for inward, outward in moves:
        inward.wait()
        outward.start()
    for inward, outward in moves:
        outward.wait()


def fused(features, short_filter, medium_filter, skip_gain, attn_query, attn_key, attn_value, lengths):
    rows, cols = attn_query.shape
    part = rows // 3
    heads = cols // HD
    angle = np.pi / (2 * part) * np.outer(2 * np.arange(part) + 1, np.arange(2 * part))
    wave = np.concatenate((np.cos(angle), -np.sin(angle)), axis=0)
    fwd = split_two(wave)
    inv = split_two(wave.T[part:] / part)
    anywhere = pl.BlockSpec(memory_space=pl.ANY)
    out = jax.ShapeDtypeStruct((rows, cols), jnp.bfloat16)

    def buf(*shape):
        return pltpu.VMEM(shape, jnp.bfloat16)

    def wide(*shape):
        return pltpu.VMEM(shape, jnp.float32)

    each = pltpu.SemaphoreType.DMA((heads,))
    made = pl.pallas_call(
        lambda *refs: fused_kernel(rows, cols, *refs),
        out_shape=(out, out),
        in_specs=[pl.BlockSpec(memory_space=pltpu.HBM)] * 10,
        out_specs=(anywhere, anywhere),
        scratch_shapes=[
            pltpu.SMEM(lengths.shape, jnp.int32), wide(*short_filter.shape), wide(part, cols), wide(1, cols),
            buf(*fwd.shape), buf(*inv.shape),
            buf(3, rows, cols), buf(rows, cols), buf(rows, cols), buf(rows, cols),
            buf(rows + part, cols), buf(part, cols),
            buf(heads, rows + part, HD), wide(heads, 8, HD),
            buf(heads, rows, HD), buf(heads, part, HD),
            buf(heads, rows + part, HD), wide(heads, 8, HD),
            wide(rows, rows), wide(rows, 2 * part), wide(rows, rows), wide(rows, 2 * part),
            wide(part, rows),
            wide(2 * part, cols), wide(2, part, cols),
            buf(rows, cols), buf(rows, cols),
            pltpu.SemaphoreType.DMA((12,)), pltpu.SemaphoreType.DMA((2,)), each,
            pltpu.SemaphoreType.DMA((4,)),
        ] + [each] * 8,
        compiler_params=pltpu.CompilerParams(
            collective_id=0, has_side_effects=True, vmem_limit_bytes=60 * 2**20
        ),
        cost_estimate=pl.CostEstimate(
            flops=heads * 32 * part * part * HD * 4, bytes_accessed=16 * 2**20,
            transcendentals=heads * 32 * part * part,
        ),
        name="fused",
    )(
        lengths, features.transpose(1, 0, 2), attn_query, attn_key, attn_value,
        short_filter, medium_filter, skip_gain[None, :], fwd, inv,
    )
    pieces = 4
    return pl.pallas_call(
        lambda *refs: land_kernel(pieces, *refs),
        out_shape=(out, out),
        in_specs=[anywhere] * 2,
        out_specs=(anywhere, anywhere),
        scratch_shapes=[
            buf(2, rows, cols), pltpu.SemaphoreType.DMA((2 * pieces,)), pltpu.SemaphoreType.DMA((2 * pieces,))
        ],
        compiler_params=pltpu.CompilerParams(vmem_limit_bytes=60 * 2**20),
        cost_estimate=pl.CostEstimate(flops=0, bytes_accessed=8 * rows * cols, transcendentals=0),
        name="land",
    )(*made)


def local(
    features, short_filter, medium_filter, skip_gain, attn_query, attn_key, attn_value, lengths
):
    rows, cols = attn_query.shape
    spans = lax.axis_size("seq")
    taps = medium_filter.shape[0]
    if spans == 4 and rows == 3 * taps and taps == HD and cols % CHUNK == 0 and short_filter.shape[0] < 8:
        return fused(
            features, short_filter, medium_filter, skip_gain, attn_query, attn_key, attn_value, lengths
        )
    if cols % 128 == 0 and taps % 128 == 0 and rows % taps == 0:
        hyena = hyena_fast
    else:
        hyena = hyena_mix
    hyena_out = hyena(features, short_filter, medium_filter, skip_gain, lengths)
    if spans == 4 and rows % 128 == 0 and rows <= 640 and cols % (8 * HD) == 0:
        return attention_fast(attn_query, attn_key, attn_value, lengths, hyena_out)
    return (hyena_out, attention_mix(attn_query, attn_key, attn_value, lengths))


def solution(mesh):
    in_specs = (
        P(("groups", "seq"), None, ("tensor", "sub")),
        P(None, ("tensor", "sub")),
        P(None, ("tensor", "sub")),
        P(("tensor", "sub")),
        P(("groups", "seq"), ("tensor", "sub")),
        P(("groups", "seq"), ("tensor", "sub")),
        P(("groups", "seq"), ("tensor", "sub")),
        P("groups"),
    )
    out_specs = (P(("groups", "seq"), ("tensor", "sub")), P(("groups", "seq"), ("tensor", "sub")))
    return jax.shard_map(local, mesh=mesh, in_specs=in_specs, out_specs=out_specs, check_vma=False)
```

```python
import math

import jax
import jax.numpy as jnp
import numpy as np
from jax import lax
from jax.experimental import pallas as pl
from jax.experimental.pallas import tpu as pltpu
from jax.sharding import PartitionSpec as P

HD = 128


def passed_along(value, axis, by):
    length = lax.axis_size(axis)
    pairs = [(i, i + by) for i in range(length) if 0 <= i + by < length]
    return lax.ppermute(value, axis, pairs)


def doc_of(positions, lengths):
    doc_ends = jnp.cumsum(lengths, dtype=jnp.int32)
    return jnp.sum(
        (positions[:, None] >= doc_ends[None, :]).astype(jnp.int32), axis=1, dtype=jnp.int32
    )


def hyena_mix(features, short_filter, medium_filter, skip_gain, lengths):
    row_count = features.shape[0]
    medium_taps = medium_filter.shape[0]
    rim_rows = medium_taps - 1
    span_index = lax.axis_index("seq")
    queries = features[:, 0].astype(jnp.float32)
    gated = (features[:, 1].astype(jnp.float32) * features[:, 2].astype(jnp.float32)).astype(
        jnp.bfloat16
    )
    gated = lax.optimization_barrier(gated)
    carried = passed_along(gated[row_count - rim_rows :], "seq", 1)
    extended = jnp.concatenate((carried, gated), axis=0)
    ext_positions = (
        span_index * row_count - rim_rows + jnp.arange(row_count + rim_rows, dtype=jnp.int32)
    )
    ext_docs = doc_of(ext_positions, lengths)
    ext_live = ext_positions >= 0
    own_docs = ext_docs[rim_rows:]

    def tap_term(tap_index, filter_bank):
        first_row = rim_rows - tap_index
        window = lax.dynamic_slice_in_dim(extended, first_row, row_count, 0).astype(jnp.float32)
        same_doc = lax.dynamic_slice_in_dim(ext_docs, first_row, row_count, 0) == own_docs
        live_mask = lax.dynamic_slice_in_dim(ext_live, first_row, row_count, 0)
        keep_mask = (same_doc & live_mask).astype(jnp.float32)[:, None]
        taps = lax.dynamic_index_in_dim(filter_bank, tap_index, 0, keepdims=False)
        return taps[None, :] * window * keep_mask

    short_sum = jnp.zeros(gated.shape, jnp.float32)
    for tap_index in range(short_filter.shape[0]):
        short_sum = short_sum + tap_term(tap_index, short_filter)

    def tap_block(block_index, partial_value):
        for offset in range(8):
            partial_value = partial_value + tap_term(block_index * 8 + offset, medium_filter)
        return partial_value

    medium_sum = lax.fori_loop(0, medium_taps // 8, tap_block, jnp.zeros(gated.shape, jnp.float32))
    mixed = queries * (short_sum + medium_sum + skip_gain[None, :] * gated.astype(jnp.float32))
    return mixed.astype(jnp.bfloat16)


def attention_mix(attn_query, attn_key, attn_value, lengths):
    row_count, col_count = attn_query.shape
    heads_here = col_count // HD
    span_index = lax.axis_index("seq")
    query_positions = span_index * row_count + jnp.arange(row_count, dtype=jnp.int32)
    query_docs = doc_of(query_positions, lengths)
    query_heads = attn_query.reshape(row_count, heads_here, HD)
    score_scale = HD ** (-0.5)
    last_query = query_positions[row_count - 1]
    first_query_doc = query_docs[0]

    def absorb(state_now, key_block, value_block, first_row):
        key_count = key_block.shape[0]
        last_key = first_row + key_count - 1
        last_key_doc = doc_of(jnp.reshape(last_key, (1,)), lengths)[0]
        masked_out = (first_row > last_query) | (last_key < 0) | (last_key_doc < first_query_doc)

        def compute(state_in):
            running_max, running_total, running_sum = state_in
            key_heads = key_block.reshape(key_count, heads_here, HD)
            value_heads = value_block.reshape(key_count, heads_here, HD)
            scores = (
                jnp.einsum(
                    "rhd,nhd->hrn", query_heads, key_heads, preferred_element_type=jnp.float32
                )
                * score_scale
            )
            key_positions = first_row + jnp.arange(key_count, dtype=jnp.int32)
            key_docs = doc_of(key_positions, lengths)
            allowed = (
                (key_positions[None, :] <= query_positions[:, None])
                & (key_docs[None, :] == query_docs[:, None])
                & (key_positions >= 0)[None, :]
            )
            masked = jnp.where(allowed[None], scores, -1e30)
            new_max = jnp.maximum(running_max, jnp.max(masked, axis=2))
            rescale = jnp.exp(running_max - new_max)
            weights = jnp.where(allowed[None], jnp.exp(scores - new_max[:, :, None]), 0.0)
            new_total = running_total * rescale + jnp.sum(weights, axis=2)
            product = jnp.einsum(
                "hrn,nhd->hrd",
                weights.astype(jnp.bfloat16),
                value_heads,
                preferred_element_type=jnp.float32,
            )
            new_sum = running_sum * rescale[:, :, None] + product
            return (new_max, new_total, new_sum)

        def keep_state(state_in):
            return state_in

        return lax.cond(masked_out, keep_state, compute, state_now)

    def fold_keys(state_now, pieces, first_row):
        key_all, value_all = pieces
        key_count = key_all.shape[0]
        block_rows = math.gcd(key_count, 1536)
        if block_rows == key_count:
            return absorb(state_now, key_all, value_all, first_row)
        block_total = key_count // block_rows
        key_blocks = key_all.reshape(block_total, block_rows, col_count)
        value_blocks = value_all.reshape(block_total, block_rows, col_count)

        def scan_step(state_inner, block_items):
            key_block, value_block, block_index = block_items
            return (
                absorb(state_inner, key_block, value_block, first_row + block_index * block_rows),
                None,
            )

        state_now, unused = lax.scan(
            scan_step,
            state_now,
            (key_blocks, value_blocks, jnp.arange(block_total, dtype=jnp.int32)),
        )
        return state_now

    initial = (
        jnp.full((heads_here, row_count), -1e30, jnp.float32),
        jnp.zeros((heads_here, row_count), jnp.float32),
        jnp.zeros((heads_here, row_count, HD), jnp.float32),
    )
    state_now = fold_keys(
        initial,
        (
            lax.all_gather(attn_key, "seq", axis=0, tiled=True),
            lax.all_gather(attn_value, "seq", axis=0, tiled=True),
        ),
        jnp.int32(0),
    )
    running_max, running_total, running_sum = state_now
    result = running_sum / running_total[:, :, None]
    return result.transpose(1, 0, 2).reshape(row_count, col_count).astype(jnp.bfloat16)


LOG2E = 1.4426950408889634
LN2 = 0.6931471805599453
SCALE2 = HD**-0.5 * LOG2E
NEG = -1e30
STAT_ROWS = 16


def hyena_kernel(row_count, taps, lens_ref, feat_ref, rim_ref, filt_ref, fwd_ref, inv_ref, out_ref,
                 ext_ref, sum_ref):
    base = lens_ref[lens_ref.shape[0] - 1]
    ext_ref[:taps, :] = rim_ref[...]
    ext_ref[taps:, :] = (
        feat_ref[1].astype(jnp.float32) * feat_ref[2].astype(jnp.float32)
    ).astype(jnp.bfloat16)

    def dot(x, y):
        return jnp.dot(x, y, preferred_element_type=jnp.float32)

    filt = filt_ref[...]
    filt_hi = filt.astype(jnp.bfloat16)
    filt_lo = (filt - filt_hi.astype(jnp.float32)).astype(jnp.bfloat16)
    spec = (
        dot(fwd_ref[0, :, :taps], filt_hi)
        + dot(fwd_ref[1, :, :taps], filt_hi)
        + dot(fwd_ref[0, :, :taps], filt_lo)
    )
    spec_r, spec_i = spec[:taps], spec[taps:]
    win_iota = lax.broadcasted_iota(jnp.int32, (2 * taps, 1), 0)
    out_iota = lax.broadcasted_iota(jnp.int32, (taps, 1), 0)
    for block in range(row_count // taps):
        r0 = block * taps
        start = jnp.int32(0)
        for doc in range(lens_ref.shape[0] - 1):
            end = start + lens_ref[doc]
            first, last = start - base, end - base

            @pl.when((last > r0) & (first < r0 + taps) & (first < last))
            def _(first=first):
                window = ext_ref[r0 : r0 + 2 * taps, :]
                window = jnp.where(win_iota + (r0 - taps) >= first, window, jnp.zeros_like(window))
                wave = dot(fwd_ref[0], window) + dot(fwd_ref[1], window)
                wave_r, wave_i = wave[:taps], wave[taps:]
                prod = jnp.concatenate(
                    (
                        (wave_r * spec_r - wave_i * spec_i).astype(jnp.bfloat16),
                        (wave_r * spec_i + wave_i * spec_r).astype(jnp.bfloat16),
                    ),
                    axis=0,
                )
                sums = dot(inv_ref[0], prod) + dot(inv_ref[1], prod)
                sum_ref[...] = jnp.where(out_iota + r0 >= first, sums, sum_ref[...])

            start = end
        out_ref[r0 : r0 + taps, :] = (
            feat_ref[0, r0 : r0 + taps, :].astype(jnp.float32) * sum_ref[...]
        ).astype(out_ref.dtype)


def split_two(matrix):
    high = matrix.astype(jnp.bfloat16)
    low = (matrix - high.astype(np.float64)).astype(jnp.bfloat16)
    return np.stack((high, low))


def hyena_fast(features, short_filter, medium_filter, skip_gain, lengths):
    row_count, _, cols = features.shape
    taps = medium_filter.shape[0]
    span_index = lax.axis_index("seq")
    streams = features.transpose(1, 0, 2)
    tail = streams[:, row_count - taps :]
    gated_tail = (tail[1].astype(jnp.float32) * tail[2].astype(jnp.float32)).astype(jnp.bfloat16)
    carried = passed_along(gated_tail, "seq", 1)
    head = jnp.concatenate((short_filter[:1] + skip_gain[None, :], short_filter[1:]), axis=0)
    filt = medium_filter + jnp.pad(head, ((0, taps - head.shape[0]), (0, 0)))
    angle = np.pi / (2 * taps) * np.outer(2 * np.arange(taps) + 1, np.arange(2 * taps))
    fwd = split_two(np.concatenate((np.cos(angle), -np.sin(angle)), axis=0))
    inv = split_two(
        np.concatenate((np.cos(angle), -np.sin(angle)), axis=0).T[taps:] / taps
    )
    scalars = jnp.concatenate((lengths, jnp.reshape(span_index * row_count, (1,)).astype(jnp.int32)))
    width = math.gcd(cols, 512)
    return pl.pallas_call(
        lambda *refs: hyena_kernel(row_count, taps, *refs),
        grid=(cols // width,),
        out_shape=jax.ShapeDtypeStruct((row_count, cols), jnp.bfloat16),
        in_specs=[
            pl.BlockSpec(memory_space=pltpu.SMEM),
            pl.BlockSpec((3, row_count, width), lambda i: (0, 0, i)),
            pl.BlockSpec((taps, width), lambda i: (0, i)),
            pl.BlockSpec((taps, width), lambda i: (0, i)),
            pl.BlockSpec(fwd.shape, lambda i: (0, 0, 0)),
            pl.BlockSpec(inv.shape, lambda i: (0, 0, 0)),
        ],
        out_specs=pl.BlockSpec((row_count, width), lambda i: (0, i)),
        scratch_shapes=[
            pltpu.VMEM((row_count + taps, width), jnp.bfloat16),
            pltpu.VMEM((taps, width), jnp.float32),
        ],
        compiler_params=pltpu.CompilerParams(vmem_limit_bytes=32 * 2**20),
        cost_estimate=pl.CostEstimate(
            flops=2 * 9 * 2 * taps * taps * 3 * cols, bytes_accessed=8 * 2**20, transcendentals=0
        ),
        name="hyena",
    )(scalars, streams, carried, filt, fwd, inv)


def doc_start(pos, lens_ref):
    start = jnp.zeros_like(pos)
    end = jnp.int32(0)
    for doc in range(lens_ref.shape[0] - 1):
        end = end + lens_ref[doc]
        start = jnp.where(pos >= end, end, start)
    return start


def attend(query_ref, keys, values, biases, emit):
    rows = query_ref.shape[0]
    step = 128
    ones = jnp.ones((rows, 128), jnp.bfloat16)
    vals = [jnp.concatenate((v[...], ones), axis=1) for v in values]
    for r in range(0, rows, step):
        q = query_ref[r : r + step, :]
        scores = [
            lax.dot_general(q, k[...], (((1,), (1,)), ((), ())),
                            preferred_element_type=jnp.float32) + b[r : r + step, :]
            for k, b in zip(keys, biases)
        ]
        top = jnp.max(scores[0], axis=1, keepdims=True)
        for s in scores[1:]:
            top = jnp.maximum(top, jnp.max(s, axis=1, keepdims=True))
        acc = None
        for s, v in zip(scores, vals):
            w = jnp.exp2((s - top) * SCALE2).astype(jnp.bfloat16)
            part = jnp.dot(w, v, preferred_element_type=jnp.float32)
            acc = part if acc is None else acc + part
        total = acc[:, 128:]
        emit(r, acc[:, :128] / total, top * SCALE2 + jnp.log2(total))


def needs(lens_ref, base, rows, ahead, back):
    q_first = base + ahead * rows
    start = jnp.int32(0)
    end = jnp.int32(0)
    for doc in range(lens_ref.shape[0] - 1):
        end = end + lens_ref[doc]
        start = jnp.where(q_first >= end, end, start)
    return start < base + (1 - back) * rows


def fill_bias(lens_ref, base, rows, ref, ahead, back):
    qpos = base + ahead * rows + lax.broadcasted_iota(jnp.int32, (rows, 1), 0)
    starts = doc_start(qpos, lens_ref)
    kpos = base - back * rows + lax.broadcasted_iota(jnp.int32, (1, rows), 1)
    ref[...] = jnp.where((kpos <= qpos) & (kpos >= starts), 0.0, NEG).astype(jnp.float32)


def near_kernel(rows, lens_ref, q_ref, k_ref, v_ref, k1_ref, v1_ref, k2_ref, v2_ref, all_ref, o_ref,
                b0, b1, b2):
    span = lens_ref[lens_ref.shape[0] - 1]
    base = span * rows
    one = (span >= 1) & needs(lens_ref, base, rows, 0, 1)
    two = (span >= 2) & needs(lens_ref, base, rows, 0, 2)

    @pl.when(pl.program_id(0) == 0)
    def _():
        fill_bias(lens_ref, base, rows, b0, 0, 0)
        pl.when(one)(lambda: fill_bias(lens_ref, base, rows, b1, 0, 1))
        pl.when(two)(lambda: fill_bias(lens_ref, base, rows, b2, 0, 2))

    def emit(r, out, lse):
        o_ref[r : r + 128, :] = out.astype(jnp.bfloat16)

    pl.when(two)(
        lambda: attend(q_ref, (k_ref, k1_ref, k2_ref), (v_ref, v1_ref, v2_ref), (b0, b1, b2), emit)
    )
    pl.when(one & jnp.logical_not(two))(
        lambda: attend(q_ref, (k_ref, k1_ref), (v_ref, v1_ref), (b0, b1), emit)
    )
    pl.when(jnp.logical_not(one))(lambda: attend(q_ref, (k_ref,), (v_ref,), (b0,), emit))


def attn_kernel(rows, lens_ref, q_ref, qa_ref, qb_ref, kp_ref, vp_ref, k_ref, v_ref,
                o_ref, lse_ref, oa_ref, ob_ref, b00, b10, b01, b11, b02):
    span = lens_ref[lens_ref.shape[0] - 1]
    base = span * rows

    def reads(ahead, back):
        return needs(lens_ref, base, rows, ahead, back)

    own_prev = (span == 1) & reads(0, 1)
    a_here = ((span == 1) | (span == 2)) & reads(1, 0)
    a_prev = (span == 1) & reads(1, 1)
    b_here = (span == 1) & reads(2, 0)

    @pl.when(pl.program_id(0) == 0)
    def _():
        lse_ref[...] = jnp.zeros_like(lse_ref)

        def fill(ref, ahead, back):
            fill_bias(lens_ref, base, rows, ref, ahead, back)

        fill(b00, 0, 0)
        pl.when(own_prev)(lambda: fill(b01, 0, 1))
        pl.when(a_here)(lambda: fill(b10, 1, 0))
        pl.when(a_prev)(lambda: fill(b11, 1, 1))
        pl.when(b_here)(lambda: fill(b02, 2, 0))

    step = 128
    head_lane = lax.broadcasted_iota(jnp.int32, (step, 128), 1) == pl.program_id(0)

    def emit_own(r, out, lse):
        o_ref[r : r + step, :] = out.astype(jnp.bfloat16)
        lse_ref[r : r + step, :] = jnp.where(head_lane, lse, lse_ref[r : r + step, :])

    eye = lax.broadcasted_iota(jnp.int32, (128, 128), 0) == lax.broadcasted_iota(
        jnp.int32, (128, 128), 1
    )
    stat_iota = lax.broadcasted_iota(jnp.int32, (STAT_ROWS, 128), 0)

    def emit_to(ref):
        stats = [jnp.zeros((STAT_ROWS, 128), jnp.float32)]

        def emit(r, out, lse):
            ref[r : r + step, :] = out.astype(jnp.bfloat16)
            rest = jnp.sum(jnp.where(eye, lse, 0.0), axis=0, keepdims=True)
            for piece in range(3):
                high = rest.astype(jnp.bfloat16).astype(jnp.float32)
                stats[0] = jnp.where(stat_iota == piece * (rows // step) + r // step, high, stats[0])
                rest = rest - high
            if r + step == rows:
                ref[rows:, :] = stats[0].astype(jnp.bfloat16)

        return emit

    def empty(ref):
        ref[:rows, :] = jnp.zeros((rows, 128), jnp.bfloat16)
        ref[rows:, :] = jnp.where(stat_iota < rows // step, NEG, 0.0).astype(jnp.bfloat16)

    pl.when(own_prev)(lambda: attend(q_ref, (kp_ref, k_ref), (vp_ref, v_ref), (b01, b00), emit_own))
    pl.when(jnp.logical_not(own_prev))(lambda: attend(q_ref, (k_ref,), (v_ref,), (b00,), emit_own))
    pl.when(a_prev)(
        lambda: attend(qa_ref, (kp_ref, k_ref), (vp_ref, v_ref), (b11, b10), emit_to(oa_ref))
    )
    pl.when(a_here & jnp.logical_not(a_prev))(
        lambda: attend(qa_ref, (k_ref,), (v_ref,), (b10,), emit_to(oa_ref))
    )
    pl.when(jnp.logical_not(a_here))(lambda: empty(oa_ref))
    pl.when(b_here)(lambda: attend(qb_ref, (k_ref,), (v_ref,), (b02,), emit_to(ob_ref)))
    pl.when(jnp.logical_not(b_here))(lambda: empty(ob_ref))


def merge_kernel(rows, lens_ref, o_ref, lse_ref, ra_ref, rb_ref, all_ref, out_ref):
    span = lens_ref[lens_ref.shape[0] - 1]
    step = 128
    eye = lax.broadcasted_iota(jnp.int32, (128, 128), 0) == lax.broadcasted_iota(
        jnp.int32, (128, 128), 1
    )

    @pl.when(span < 2)
    def _():
        out_ref[...] = o_ref[...]

    @pl.when(span >= 2)
    def _():
        blocks = rows // step
        head_lane = lax.broadcasted_iota(jnp.int32, (step, 128), 1) == pl.program_id(0)
        stat_a = ra_ref[rows:, :].astype(jnp.float32)
        stat_b = rb_ref[rows:, :].astype(jnp.float32)

        def column(stats, i):
            row = (stats[i : i + 1] + stats[blocks + i : blocks + i + 1]) + stats[
                2 * blocks + i : 2 * blocks + i + 1
            ]
            return jnp.sum(jnp.where(eye, row, 0.0), axis=1, keepdims=True)

        for i in range(blocks):
            r = i * step
            own = jnp.sum(jnp.where(head_lane, lse_ref[r : r + step, :], 0.0), axis=1, keepdims=True)
            lse_a = column(stat_a, i)
            lse_b = jnp.where(span == 3, column(stat_b, i), NEG)
            top = jnp.maximum(own, jnp.maximum(lse_a, lse_b))
            w0 = jnp.exp2(own - top)
            w1 = jnp.exp2(lse_a - top)
            w2 = jnp.exp2(lse_b - top)
            total = (
                o_ref[r : r + step, :].astype(jnp.float32) * w0
                + ra_ref[r : r + step, :].astype(jnp.float32) * w1
                + rb_ref[r : r + step, :].astype(jnp.float32) * w2
            )
            out_ref[r : r + step, :] = (total / (w0 + w1 + w2)).astype(jnp.bfloat16)


def attention_fast(attn_query, attn_key, attn_value, lengths, hyena_out):
    rows, cols = attn_query.shape
    span_index = lax.axis_index("seq")
    scalars = jnp.concatenate((lengths, jnp.reshape(span_index, (1,)).astype(jnp.int32)))
    all_heads = cols // HD
    heads = all_heads * 3 // 8
    near = all_heads - 2 * heads
    width = heads * HD
    smem = pl.BlockSpec(memory_space=pltpu.SMEM)
    block = pl.BlockSpec((rows, HD), lambda h: (0, h))
    tall = pl.BlockSpec((rows + STAT_ROWS, HD), lambda h: (0, h))
    packed = pl.BlockSpec((rows, 128), lambda h: (0, 0))

    def at(offset):
        return pl.BlockSpec((rows, HD), lambda h: (0, offset + h))

    def pair(lo, hi):
        return jnp.concatenate((attn_key[:, lo:hi], attn_value[:, lo:hi]), axis=1)

    sent = []
    for c in range(2):
        qc = attn_query[:, c * width : (c + 1) * width]
        qa = lax.ppermute(qc, "seq", [(2, 1), (3, 2)])
        qb = lax.ppermute(qc, "seq", [(3, 1)])
        kv = pair(c * width, (c + 1) * width)
        sent.append((qa, qb, lax.ppermute(kv, "seq", [(0, 1)])))
    kv = pair(2 * width, cols)
    kv1 = lax.ppermute(kv, "seq", [(0, 1), (1, 2), (2, 3)])
    kv2 = lax.ppermute(kv, "seq", [(0, 2), (1, 3)])
    scalars, hyena_out = lax.optimization_barrier((scalars, hyena_out))
    outs = []
    for c in range(2):
        qa, qb, kvp = sent[c]
        whole = at(c * heads)
        own, lse, oa, ob = pl.pallas_call(
            lambda *refs: attn_kernel(rows, *refs),
            grid=(heads,),
            out_shape=(
                jax.ShapeDtypeStruct((rows, width), jnp.bfloat16),
                jax.ShapeDtypeStruct((rows, 128), jnp.float32),
                jax.ShapeDtypeStruct((rows + STAT_ROWS, width), jnp.bfloat16),
                jax.ShapeDtypeStruct((rows + STAT_ROWS, width), jnp.bfloat16),
            ),
            in_specs=[smem, whole, block, block, block, at(heads), whole, whole],
            out_specs=(block, packed, tall, tall),
            scratch_shapes=[pltpu.VMEM((rows, rows), jnp.float32)] * 5,
            compiler_params=pltpu.CompilerParams(vmem_limit_bytes=32 * 2**20),
            cost_estimate=pl.CostEstimate(
                flops=heads * 5 * rows * rows * HD * 4 * 2,
                bytes_accessed=8 * 2**20,
                transcendentals=heads * 5 * rows * rows,
            ),
            name="attend",
        )(scalars, attn_query, qa, qb, kvp, kvp, attn_key, attn_value)
        ra = lax.ppermute(oa, "seq", [(1, 2), (2, 3)])
        rb = lax.ppermute(ob, "seq", [(1, 3)])
        outs.append((own, lse, ra, rb))
        scalars, _ = lax.optimization_barrier((scalars, own))
    anywhere = pl.BlockSpec(memory_space=pl.ANY)
    whole_out = jax.ShapeDtypeStruct((rows, cols), jnp.bfloat16)
    mine = at(2 * heads)
    result = pl.pallas_call(
        lambda *refs: near_kernel(rows, *refs[:8], None, *refs[8:]),
        grid=(near,),
        out_shape=whole_out,
        in_specs=[smem, mine, mine, mine, block, at(near), block, at(near)],
        out_specs=mine,
        scratch_shapes=[pltpu.VMEM((rows, rows), jnp.float32)] * 3,
        compiler_params=pltpu.CompilerParams(vmem_limit_bytes=32 * 2**20),
        cost_estimate=pl.CostEstimate(
            flops=near * 3 * rows * rows * HD * 4 * 2,
            bytes_accessed=4 * 2**20,
            transcendentals=near * 3 * rows * rows,
        ),
        name="near",
    )(scalars, attn_query, attn_key, attn_value, kv1, kv1, kv2, kv2)
    for c in range(2):
        own, lse, ra, rb = outs[c]
        result = pl.pallas_call(
            lambda *refs: merge_kernel(rows, *refs),
            grid=(heads,),
            out_shape=whole_out,
            in_specs=[smem, block, packed, tall, tall, anywhere],
            out_specs=at(c * heads),
            input_output_aliases={5: 0},
            cost_estimate=pl.CostEstimate(
                flops=rows * width * 16, bytes_accessed=4 * 2**20, transcendentals=0
            ),
            name="merge",
        )(scalars, own, lse, ra, rb, result)
    return hyena_out, result


MESH_ID = pl.DeviceIdType.MESH
FAR = 1 << 20
CHUNK = 256
AHEAD = 5
BEHIND = 4


def start_at(pos, lens_ref):
    start = jnp.int32(0)
    end = jnp.int32(0)
    for doc in range(lens_ref.shape[0] - 1):
        end = end + lens_ref[doc]
        start = jnp.where(pos >= end, end, start)
    return start


def fused_kernel(
    rows, cols, lens_hbm, feat_hbm, q_hbm, k_hbm, v_hbm, short_hbm, med_hbm, skip_hbm, fwd_hbm, inv_hbm,
    hy_hbm, at_hbm,
    lens_ref, short_ref, med_ref, skip_ref, fwd_ref, inv_ref,
    feat, qv, kv, vv, ext, halo, up_rx, st_rx, q_near, q_far, up_tx, st_tx,
    b_own, b_own_l, b_near, b_near_l, b_far, spec, fix, hy_v, at_v,
    load_sem, hy_sem, at_sem, halo_sem, near_tx, near_rx, far_tx, far_rx, up_tx_sem, up_rx_sem,
    st_tx_sem, st_rx_sem,
):
    f32, bf16 = jnp.float32, jnp.bfloat16
    heads = cols // HD
    part = rows // 3
    span = lax.axis_index("seq")
    base = span * rows
    has_left, has_right = span > 0, span < 3
    has_far, sends_far = span < 2, span > 1

    def load(index, src, dst):
        return pltpu.make_async_copy(src, dst, load_sem.at[index])

    tail_load = load(0, feat_hbm.at[1:3, 2 * part :, :], feat.at[1:3, 2 * part :, :])
    front_load = load(1, feat_hbm.at[1:3, : 2 * part, :], feat.at[1:3, : 2 * part, :])
    mix_load = load(2, feat_hbm.at[0], feat.at[0])
    k_load = load(3, k_hbm, kv)
    v_load = load(4, v_hbm, vv)
    q_load = load(5, q_hbm, qv)
    lens_load = load(6, lens_hbm, lens_ref)
    filter_loads = [
        load(7, short_hbm, short_ref),
        load(8, med_hbm, med_ref),
        load(9, skip_hbm, skip_ref),
        load(10, fwd_hbm, fwd_ref),
        load(11, inv_hbm, inv_ref),
    ]

    def start_all(copies):
        for copy in copies:
            copy.start()

    start_all([lens_load, tail_load])
    head_loads = [k_load, v_load, q_load]
    mix_loads = filter_loads + [front_load, mix_load]
    pl.when(has_left)(lambda: start_all(mix_loads + head_loads))
    pl.when(jnp.logical_not(has_left))(lambda: start_all(head_loads + mix_loads))

    def lanes(h):
        return pl.ds(pl.multiple_of(h * HD, HD), HD)

    def remote(src, dst, tx, rx, to):
        return pltpu.make_async_remote_copy(
            src_ref=src, dst_ref=dst, send_sem=tx, recv_sem=rx, device_id={"seq": to},
            device_id_type=MESH_ID,
        )

    up_to = jnp.minimum(span + 1, 3)

    def near_copy(h):
        return remote(q_hbm.at[:, lanes(h)], q_near.at[h], near_tx.at[h], near_rx.at[h],
                      jnp.maximum(span - 1, 0))

    def far_copy(h):
        return remote(q_hbm.at[:part, lanes(h)], q_far.at[h], far_tx.at[h], far_rx.at[h],
                      jnp.maximum(span - 2, 0))

    def up_copy(h):
        return remote(up_tx.at[h], up_rx.at[h], up_tx_sem.at[h], up_rx_sem.at[h], up_to)

    def st_copy(h):
        return remote(st_tx.at[h], st_rx.at[h], st_tx_sem.at[h], st_rx_sem.at[h], up_to)

    def pass_copy(h):
        return remote(q_near.at[h, :part, :], q_far.at[h], far_tx.at[h], far_rx.at[h],
                      jnp.maximum(span - 1, 0))

    def pass_on(h):
        near_copy(h).wait_recv()
        pass_copy(h).start()
        pl.when(h + 2 < heads)(lambda: near_copy(h + 2).start())

    halo_copies = [
        remote(
            ext.at[rows : rows + part, lo:hi],
            halo.at[:, lo:hi],
            halo_sem.at[i], halo_sem.at[2 + i], up_to,
        )
        for i, (lo, hi) in enumerate(((0, cols // 4), (cols // 4, cols)))
    ]

    barrier = pltpu.get_barrier_semaphore()
    for away in (-2, -1, 1, 2):

        @pl.when((span + away >= 0) & (span + away < 4))
        def _(away=away):
            pl.semaphore_signal(barrier, inc=1, device_id={"seq": span + away}, device_id_type=MESH_ID)

    pl.semaphore_wait(barrier, jnp.where(has_left & has_right, 3, 2))

    @pl.when(sends_far)
    def _():
        def send_queries(h, carry):
            pl.when(h < heads)(lambda: near_copy(h).start())
            pl.when((span == 3) & (h >= BEHIND))(lambda: far_copy(h - BEHIND).start())
            return carry

        lax.fori_loop(0, heads + BEHIND, send_queries, 0)

    @pl.when(span == 1)
    def _():
        near_copy(0).start()
        near_copy(1).start()

    chunks = cols // CHUNK

    def chunk_cols(c):
        return pl.ds(pl.multiple_of(c * CHUNK, CHUNK), CHUNK)

    def gate(lo, hi, at):
        return (feat[1, lo:hi, at].astype(f32) * feat[2, lo:hi, at].astype(f32)).astype(bf16)

    tail_load.wait()

    def gate_tail(c, carry):
        at = chunk_cols(c)
        ext[rows : rows + part, at] = gate(2 * part, rows, at)
        ext[:part, at] = jnp.zeros((part, CHUNK), bf16)
        return carry

    lax.fori_loop(0, chunks, gate_tail, 0)
    pl.when(has_right)(lambda: halo_copies[0].start())
    pl.when(has_left & has_right)(lambda: halo_copies[1].start())

    @pl.when(jnp.logical_not(has_left))
    def _():
        def clear(h, carry):
            up_rx[h] = jnp.zeros((rows + part, HD), bf16)
            st_rx[h] = jnp.zeros((8, HD), f32)
            return carry

        lax.fori_loop(0, heads, clear, 0)

    @pl.when(span == 2)
    def _():
        def clear(h, carry):
            q_far[h] = jnp.zeros((part, HD), bf16)
            return carry

        lax.fori_loop(0, heads, clear, 0)

    lens_load.wait()
    left_q = has_left & (base - start_at(base, lens_ref) > 2 * part)
    right_q = has_right & (base + rows - start_at(base + rows, lens_ref) > 2 * part)
    fresh = has_far & right_q & (start_at(base + 2 * rows, lens_ref) < base + rows)
    slot_mine = (span > 1) & (base - rows - start_at(base, lens_ref) > 2 * part)

    def column_iota(first, count):
        return first + lax.broadcasted_iota(jnp.int32, (count, 1), 0)

    own_pos = column_iota(base, rows)
    near_pos = column_iota(base + rows, rows)
    far_pos = column_iota(base + 2 * rows, part)
    key_pos = base + lax.broadcasted_iota(jnp.int32, (1, rows), 1)
    left_pos = base - 2 * part + lax.broadcasted_iota(jnp.int32, (1, 2 * part), 1)
    no_keys = jnp.where(has_left & jnp.logical_not(left_q), 0, FAR)
    no_near = jnp.where(right_q, 0, FAR)
    no_far = jnp.where(fresh, 0, FAR)
    own_start = doc_start(own_pos, lens_ref)
    near_start = doc_start(near_pos, lens_ref) + no_near
    far_start = doc_start(far_pos, lens_ref) + no_far

    def bias(ok):
        return jnp.where(ok, 0.0, NEG).astype(f32)

    b_own[...] = bias((key_pos <= own_pos) & (key_pos >= own_start))
    b_own_l[...] = bias(left_pos >= own_start + no_keys)
    b_near[...] = bias(key_pos >= near_start)
    b_near_l[...] = bias(left_pos >= near_start + no_keys)
    b_far[...] = bias(key_pos >= far_start)

    def dot(x, y):
        return jnp.dot(x, y, preferred_element_type=f32)

    first_cut = jnp.int32(FAR)
    last_cut = jnp.int32(-1)
    end = jnp.int32(0)
    for doc in range(lens_ref.shape[0] - 1):
        end = end + lens_ref[doc]
        first_cut = jnp.where((end > base) & (end < first_cut), end, first_cut)
        last_cut = jnp.where((end < base + rows) & (end > last_cut), end, last_cut)
    cuts = []
    for cut in (first_cut, last_cut):
        valid = (cut > base) & (cut < base + rows)
        block = jnp.where(valid, lax.div(jnp.where(valid, cut - base, 0), part), 0)
        cuts.append((jnp.where(valid, cut, FAR), block))
    win_iota = lax.broadcasted_iota(jnp.int32, (2 * part, 1), 0)
    out_iota = lax.broadcasted_iota(jnp.int32, (part, 1), 0)

    def transform(window, first_pos, from_pos, spec_r, spec_i):
        window = jnp.where(win_iota + first_pos >= from_pos, window, jnp.zeros_like(window))
        return spread(window, spec_r, spec_i)

    def spread(window, spec_r, spec_i):
        wave = dot(fwd_ref[0], window)
        wave_r, wave_i = wave[:part], wave[part:]
        prod = jnp.concatenate(
            (
                (wave_r * spec_r - wave_i * spec_i).astype(bf16),
                (wave_r * spec_i + wave_i * spec_r).astype(bf16),
            ),
            axis=0,
        )
        return dot(inv_ref[0], prod)

    def finish(block, at, sums, fixes):
        for (cut, cut_block), fixed in zip(cuts, fixes):
            cut_from = jnp.where(cut_block == block, cut, FAR)
            sums = jnp.where(out_iota + (base + block * part) >= cut_from, fixed, sums)
        r0 = block * part
        hy_v[r0 : r0 + part, at] = (feat[0, r0 : r0 + part, at].astype(f32) * sums).astype(bf16)

    def hyena_loads():
        front_load.wait()
        mix_load.wait()
        for copy in filter_loads:
            copy.wait()

    def hyena_main(c, carry):
        at = chunk_cols(c)
        ext[part:rows, at] = gate(0, 2 * part, at)
        short = short_ref[:, at]
        head = jnp.concatenate(
            (short[:1] + skip_ref[:, at], short[1:], jnp.zeros((8 - short.shape[0], CHUNK), f32)), axis=0
        )
        filt = jnp.concatenate((med_ref[:8, at] + head, med_ref[8:, at]), axis=0)
        filt_hi = filt.astype(bf16)
        filt_lo = (filt - filt_hi.astype(f32)).astype(bf16)
        both = (
            dot(fwd_ref[0, :, :part], filt_hi)
            + dot(fwd_ref[1, :, :part], filt_hi)
            + dot(fwd_ref[0, :, :part], filt_lo)
        )
        spec[:, at] = both
        spec_r, spec_i = both[:part], both[part:]
        fixes = []
        for index, (cut, cut_block) in enumerate(cuts):
            window = jnp.zeros((2 * part, CHUNK), bf16)
            for block in range(3):
                r0 = block * part
                cut_from = jnp.where(cut_block == block, cut, FAR)
                window = jnp.where(
                    win_iota + (base + r0 - part) >= cut_from, ext[r0 : r0 + 2 * part, at], window
                )
            sums = spread(window, spec_r, spec_i)
            fix[index, :, at] = sums
            fixes.append(sums)
        for block in (1, 2):
            r0 = block * part
            sums = transform(
                ext[r0 : r0 + 2 * part, at], base + r0 - part, start_at(base + r0, lens_ref), spec_r, spec_i
            )
            finish(block, at, sums, fixes)
        return carry

    hy_late = pltpu.make_async_copy(hy_v.at[part:, :], hy_hbm.at[part:, :], hy_sem.at[0])
    hy_first = pltpu.make_async_copy(hy_v.at[:part, :], hy_hbm.at[:part, :], hy_sem.at[1])

    def hyena_first():
        @pl.when(has_left)
        def _():
            for copy in halo_copies:
                copy.wait_recv()

        def one(c, carry):
            at = chunk_cols(c)
            window = jnp.concatenate((halo[:, at], ext[part : 2 * part, at]), axis=0)
            sums = transform(
                window, base - part, start_at(base, lens_ref), spec[:part, at], spec[part:, at]
            )
            finish(0, at, sums, [fix[i, :, at] for i in range(2)])
            return carry

        lax.fori_loop(0, chunks, one, 0, unroll=2)
        hy_first.start()

    @pl.when(has_left)
    def _():
        pl.when(span == 1)(lambda: pass_on(0))
        hyena_loads()

        def step(c, carry):
            for h, when in ((1, 1), (2, 3), (3, 5), (4, 7), (5, 7))[: AHEAD - 1]:

                @pl.when((span == 1) & (c == min(when, chunks - 1)))
                def _(h=h):
                    pass_on(h)

            return hyena_main(c, carry)

        lax.fori_loop(0, chunks, step, 0)
        hy_late.start()
        pl.when(sends_far)(hyena_first)

    k_load.wait()
    v_load.wait()
    q_load.wait()
    ones = jnp.ones((rows, HD), bf16)
    eye = lax.broadcasted_iota(jnp.int32, (part, HD), 0) == lax.broadcasted_iota(jnp.int32, (part, HD), 1)
    stat_iota = lax.broadcasted_iota(jnp.int32, (8, HD), 0)
    left_off = jnp.where(left_q, 0.0, NEG)
    slot_off = jnp.where(slot_mine, 0.0, NEG)

    def attend_to(q, keys, values, biases):
        scores = [
            lax.dot_general(q, k, (((1,), (1,)), ((), ())), preferred_element_type=f32) + b
            for k, b in zip(keys, biases)
        ]
        top = jnp.max(scores[0], axis=1, keepdims=True)
        for s in scores[1:]:
            top = jnp.maximum(top, jnp.max(s, axis=1, keepdims=True))
        acc = None
        for s, v in zip(scores, values):
            w = jnp.exp2((s - top) * SCALE2).astype(bf16)
            term = dot(w, v)
            acc = term if acc is None else acc + term
        return acc[:, :HD], acc[:, HD:], top * SCALE2

    spread_from = min(4, heads - chunks - 1)

    def head_step(h, carry):
        at = lanes(h)

        @pl.when(jnp.logical_not(has_left))
        def _():
            pl.when(h == spread_from)(hyena_loads)

            @pl.when((h >= spread_from) & (h < spread_from + chunks))
            def _():
                hyena_main(h - spread_from, 0)

            @pl.when(h == spread_from + chunks)
            def _():
                hy_late.start()
                hyena_first()

        @pl.when(has_left)
        def _():
            up_copy(h).wait_recv()
            st_copy(h).wait_recv()

        k = kv[:, at]
        v = vv[:, at]
        k_left = up_rx[h, : 2 * part, :]
        v_ones = jnp.concatenate((v, ones), axis=1)
        v_left = jnp.concatenate((up_rx[h, 2 * part :, :], ones[: 2 * part]), axis=1)

        @pl.when(has_right)
        def _():
            pl.when(span != 1)(lambda: near_copy(h).wait_recv())
            pl.when(has_far)(lambda: far_copy(h).wait_recv())
            tails = (k[part : 2 * part], k[2 * part :], v[part : 2 * part], v[2 * part :])
            stats = jnp.zeros((8, HD), f32)

            def give(i, out):
                up_tx[h, i * part : (i + 1) * part, :] = jnp.where(
                    right_q, out, tails[i].astype(f32)
                ).astype(bf16)

            def to_row(lse):
                return jnp.sum(jnp.where(eye, lse, 0.0), axis=0, keepdims=True)

            for i in range(3):
                r0 = i * part
                acc, total, top = attend_to(
                    q_near[h, r0 : r0 + part, :],
                    (k, k_left),
                    (v_ones, v_left),
                    (b_near[r0 : r0 + part, :], b_near_l[r0 : r0 + part, :]),
                )
                give(i, acc / total)
                stats = jnp.where(stat_iota == i, to_row(top + jnp.log2(total)), stats)
            passed = up_rx[h, rows:, :].astype(f32)
            passed_stat = st_rx[h]

            acc, total, top = attend_to(q_far[h], (k,), (v_ones,), (b_far[...],))
            give(3, jnp.where(fresh, acc / total, passed))
            lse = to_row(top + jnp.log2(total))
            st_tx[h] = jnp.where(stat_iota == 3, jnp.where(fresh, lse, passed_stat[3:4]), stats)
            up_copy(h).start()
            st_copy(h).start()
            pl.when((span == 1) & (h + AHEAD < heads))(lambda: pass_on(h + AHEAD))

        stats_in = st_rx[h]

        def column(i):
            return jnp.sum(jnp.where(eye, stats_in[i : i + 1], 0.0), axis=1, keepdims=True)

        for i in range(3):
            r0 = i * part
            r1 = r0 + part
            acc, total, top = attend_to(
                qv[r0:r1, at],
                (k[:r1], k_left),
                (v_ones[:r1], v_left),
                (b_own[r0:r1, :r1], b_own_l[r0:r1, :]),
            )
            lse = column(i) + left_off
            best = jnp.maximum(top, lse)
            if i == 0:
                slot_lse = column(3) + slot_off
                best = jnp.maximum(best, slot_lse)
            w0 = jnp.exp2(top - best)
            w1 = jnp.exp2(lse - best)
            mixed = acc * w0 + up_rx[h, r0:r1, :].astype(f32) * w1
            norm = total * w0 + w1
            if i == 0:
                w2 = jnp.exp2(slot_lse - best)
                mixed = mixed + up_rx[h, rows:, :].astype(f32) * w2
                norm = norm + w2
            at_v[r0:r1, at] = (mixed / norm).astype(bf16)
        pltpu.make_async_copy(at_v.at[:, at], at_hbm.at[:, at], at_sem.at[h]).start()
        return carry

    lax.fori_loop(0, heads, head_step, 0)
    pl.when(jnp.logical_not(has_left))(lambda: halo_copies[1].start())
    pl.when(span == 1)(hyena_first)

    def drain(h, carry):
        at = lanes(h)
        pltpu.make_async_copy(at_v.at[:, at], at_hbm.at[:, at], at_sem.at[h]).wait()

        @pl.when(has_right)
        def _():
            up_copy(h).wait_send()
            st_copy(h).wait_send()

        pl.when(has_left)(lambda: near_copy(h).wait_send())
        pl.when(span == 3)(lambda: far_copy(h).wait_send())
        pl.when(span == 1)(lambda: pass_copy(h).wait_send())
        return carry

    lax.fori_loop(0, heads, drain, 0)

    @pl.when(has_right)
    def _():
        for copy in halo_copies:
            copy.wait_send()

    hy_late.wait()
    hy_first.wait()


def land_kernel(pieces, hy_src, at_src, hy_dst, at_dst, held, in_sem, out_sem):
    step = hy_src.shape[0] // pieces
    moves = []
    for array, (src, dst) in enumerate(((hy_src, hy_dst), (at_src, at_dst))):
        for i in range(pieces):
            rows = pl.ds(i * step, step)
            here = held.at[array, rows, :]
            index = array * pieces + i
            inward = pltpu.make_async_copy(src.at[rows, :], here, in_sem.at[index])
            moves.append((inward, pltpu.make_async_copy(here, dst.at[rows, :], out_sem.at[index])))
            inward.start()
    for inward, outward in moves:
        inward.wait()
        outward.start()
    for inward, outward in moves:
        outward.wait()


def fused(features, short_filter, medium_filter, skip_gain, attn_query, attn_key, attn_value, lengths):
    rows, cols = attn_query.shape
    part = rows // 3
    heads = cols // HD
    angle = np.pi / (2 * part) * np.outer(2 * np.arange(part) + 1, np.arange(2 * part))
    wave = np.concatenate((np.cos(angle), -np.sin(angle)), axis=0)
    fwd = split_two(wave)
    inv = split_two(wave.T[part:] / part)
    anywhere = pl.BlockSpec(memory_space=pl.ANY)
    out = jax.ShapeDtypeStruct((rows, cols), jnp.bfloat16)

    def buf(*shape):
        return pltpu.VMEM(shape, jnp.bfloat16)

    def wide(*shape):
        return pltpu.VMEM(shape, jnp.float32)

    each = pltpu.SemaphoreType.DMA((heads,))
    made = pl.pallas_call(
        lambda *refs: fused_kernel(rows, cols, *refs),
        out_shape=(out, out),
        in_specs=[pl.BlockSpec(memory_space=pltpu.HBM)] * 10,
        out_specs=(anywhere, anywhere),
        scratch_shapes=[
            pltpu.SMEM(lengths.shape, jnp.int32), wide(*short_filter.shape), wide(part, cols), wide(1, cols),
            buf(*fwd.shape), buf(*inv.shape),
            buf(3, rows, cols), buf(rows, cols), buf(rows, cols), buf(rows, cols),
            buf(rows + part, cols), buf(part, cols),
            buf(heads, rows + part, HD), wide(heads, 8, HD),
            buf(heads, rows, HD), buf(heads, part, HD),
            buf(heads, rows + part, HD), wide(heads, 8, HD),
            wide(rows, rows), wide(rows, 2 * part), wide(rows, rows), wide(rows, 2 * part),
            wide(part, rows),
            wide(2 * part, cols), wide(2, part, cols),
            buf(rows, cols), buf(rows, cols),
            pltpu.SemaphoreType.DMA((12,)), pltpu.SemaphoreType.DMA((2,)), each,
            pltpu.SemaphoreType.DMA((4,)),
        ] + [each] * 8,
        compiler_params=pltpu.CompilerParams(
            collective_id=0, has_side_effects=True, vmem_limit_bytes=60 * 2**20
        ),
        cost_estimate=pl.CostEstimate(
            flops=heads * 32 * part * part * HD * 4, bytes_accessed=16 * 2**20,
            transcendentals=heads * 32 * part * part,
        ),
        name="fused",
    )(
        lengths, features.transpose(1, 0, 2), attn_query, attn_key, attn_value,
        short_filter, medium_filter, skip_gain[None, :], fwd, inv,
    )
    pieces = 4
    return pl.pallas_call(
        lambda *refs: land_kernel(pieces, *refs),
        out_shape=(out, out),
        in_specs=[anywhere] * 2,
        out_specs=(anywhere, anywhere),
        scratch_shapes=[
            buf(2, rows, cols), pltpu.SemaphoreType.DMA((2 * pieces,)), pltpu.SemaphoreType.DMA((2 * pieces,))
        ],
        compiler_params=pltpu.CompilerParams(vmem_limit_bytes=60 * 2**20),
        cost_estimate=pl.CostEstimate(flops=0, bytes_accessed=8 * rows * cols, transcendentals=0),
        name="land",
    )(*made)


def local(
    features, short_filter, medium_filter, skip_gain, attn_query, attn_key, attn_value, lengths
):
    rows, cols = attn_query.shape
    spans = lax.axis_size("seq")
    taps = medium_filter.shape[0]
    if spans == 4 and rows == 3 * taps and taps == HD and cols % CHUNK == 0 and short_filter.shape[0] < 8:
        return fused(
            features, short_filter, medium_filter, skip_gain, attn_query, attn_key, attn_value, lengths
        )
    if cols % 128 == 0 and taps % 128 == 0 and rows % taps == 0:
        hyena = hyena_fast
    else:
        hyena = hyena_mix
    hyena_out = hyena(features, short_filter, medium_filter, skip_gain, lengths)
    if spans == 4 and rows % 128 == 0 and rows <= 640 and cols % (8 * HD) == 0:
        return attention_fast(attn_query, attn_key, attn_value, lengths, hyena_out)
    return (hyena_out, attention_mix(attn_query, attn_key, attn_value, lengths))


def solution(mesh):
    in_specs = (
        P(("groups", "seq"), None, ("tensor", "sub")),
        P(None, ("tensor", "sub")),
        P(None, ("tensor", "sub")),
        P(("tensor", "sub")),
        P(("groups", "seq"), ("tensor", "sub")),
        P(("groups", "seq"), ("tensor", "sub")),
        P(("groups", "seq"), ("tensor", "sub")),
        P("groups"),
    )
    out_specs = (P(("groups", "seq"), ("tensor", "sub")), P(("groups", "seq"), ("tensor", "sub")))
    return jax.shard_map(local, mesh=mesh, in_specs=in_specs, out_specs=out_specs, check_vma=False)
```

```python
import math

import jax
import jax.numpy as jnp
import numpy as np
from jax import lax
from jax.experimental import pallas as pl
from jax.experimental.pallas import tpu as pltpu
from jax.sharding import PartitionSpec as P

HD = 128


def passed_along(value, axis, by):
    length = lax.axis_size(axis)
    pairs = [(i, i + by) for i in range(length) if 0 <= i + by < length]
    return lax.ppermute(value, axis, pairs)


def doc_of(positions, lengths):
    doc_ends = jnp.cumsum(lengths, dtype=jnp.int32)
    return jnp.sum(
        (positions[:, None] >= doc_ends[None, :]).astype(jnp.int32), axis=1, dtype=jnp.int32
    )


def hyena_mix(features, short_filter, medium_filter, skip_gain, lengths):
    row_count = features.shape[0]
    medium_taps = medium_filter.shape[0]
    rim_rows = medium_taps - 1
    span_index = lax.axis_index("seq")
    queries = features[:, 0].astype(jnp.float32)
    gated = (features[:, 1].astype(jnp.float32) * features[:, 2].astype(jnp.float32)).astype(
        jnp.bfloat16
    )
    gated = lax.optimization_barrier(gated)
    carried = passed_along(gated[row_count - rim_rows :], "seq", 1)
    extended = jnp.concatenate((carried, gated), axis=0)
    ext_positions = (
        span_index * row_count - rim_rows + jnp.arange(row_count + rim_rows, dtype=jnp.int32)
    )
    ext_docs = doc_of(ext_positions, lengths)
    ext_live = ext_positions >= 0
    own_docs = ext_docs[rim_rows:]

    def tap_term(tap_index, filter_bank):
        first_row = rim_rows - tap_index
        window = lax.dynamic_slice_in_dim(extended, first_row, row_count, 0).astype(jnp.float32)
        same_doc = lax.dynamic_slice_in_dim(ext_docs, first_row, row_count, 0) == own_docs
        live_mask = lax.dynamic_slice_in_dim(ext_live, first_row, row_count, 0)
        keep_mask = (same_doc & live_mask).astype(jnp.float32)[:, None]
        taps = lax.dynamic_index_in_dim(filter_bank, tap_index, 0, keepdims=False)
        return taps[None, :] * window * keep_mask

    short_sum = jnp.zeros(gated.shape, jnp.float32)
    for tap_index in range(short_filter.shape[0]):
        short_sum = short_sum + tap_term(tap_index, short_filter)

    def tap_block(block_index, partial_value):
        for offset in range(8):
            partial_value = partial_value + tap_term(block_index * 8 + offset, medium_filter)
        return partial_value

    medium_sum = lax.fori_loop(0, medium_taps // 8, tap_block, jnp.zeros(gated.shape, jnp.float32))
    mixed = queries * (short_sum + medium_sum + skip_gain[None, :] * gated.astype(jnp.float32))
    return mixed.astype(jnp.bfloat16)


def attention_mix(attn_query, attn_key, attn_value, lengths):
    row_count, col_count = attn_query.shape
    heads_here = col_count // HD
    span_index = lax.axis_index("seq")
    query_positions = span_index * row_count + jnp.arange(row_count, dtype=jnp.int32)
    query_docs = doc_of(query_positions, lengths)
    query_heads = attn_query.reshape(row_count, heads_here, HD)
    score_scale = HD ** (-0.5)
    last_query = query_positions[row_count - 1]
    first_query_doc = query_docs[0]

    def absorb(state_now, key_block, value_block, first_row):
        key_count = key_block.shape[0]
        last_key = first_row + key_count - 1
        last_key_doc = doc_of(jnp.reshape(last_key, (1,)), lengths)[0]
        masked_out = (first_row > last_query) | (last_key < 0) | (last_key_doc < first_query_doc)

        def compute(state_in):
            running_max, running_total, running_sum = state_in
            key_heads = key_block.reshape(key_count, heads_here, HD)
            value_heads = value_block.reshape(key_count, heads_here, HD)
            scores = (
                jnp.einsum(
                    "rhd,nhd->hrn", query_heads, key_heads, preferred_element_type=jnp.float32
                )
                * score_scale
            )
            key_positions = first_row + jnp.arange(key_count, dtype=jnp.int32)
            key_docs = doc_of(key_positions, lengths)
            allowed = (
                (key_positions[None, :] <= query_positions[:, None])
                & (key_docs[None, :] == query_docs[:, None])
                & (key_positions >= 0)[None, :]
            )
            masked = jnp.where(allowed[None], scores, -1e30)
            new_max = jnp.maximum(running_max, jnp.max(masked, axis=2))
            rescale = jnp.exp(running_max - new_max)
            weights = jnp.where(allowed[None], jnp.exp(scores - new_max[:, :, None]), 0.0)
            new_total = running_total * rescale + jnp.sum(weights, axis=2)
            product = jnp.einsum(
                "hrn,nhd->hrd",
                weights.astype(jnp.bfloat16),
                value_heads,
                preferred_element_type=jnp.float32,
            )
            new_sum = running_sum * rescale[:, :, None] + product
            return (new_max, new_total, new_sum)

        def keep_state(state_in):
            return state_in

        return lax.cond(masked_out, keep_state, compute, state_now)

    def fold_keys(state_now, pieces, first_row):
        key_all, value_all = pieces
        key_count = key_all.shape[0]
        block_rows = math.gcd(key_count, 1536)
        if block_rows == key_count:
            return absorb(state_now, key_all, value_all, first_row)
        block_total = key_count // block_rows
        key_blocks = key_all.reshape(block_total, block_rows, col_count)
        value_blocks = value_all.reshape(block_total, block_rows, col_count)

        def scan_step(state_inner, block_items):
            key_block, value_block, block_index = block_items
            return (
                absorb(state_inner, key_block, value_block, first_row + block_index * block_rows),
                None,
            )

        state_now, unused = lax.scan(
            scan_step,
            state_now,
            (key_blocks, value_blocks, jnp.arange(block_total, dtype=jnp.int32)),
        )
        return state_now

    initial = (
        jnp.full((heads_here, row_count), -1e30, jnp.float32),
        jnp.zeros((heads_here, row_count), jnp.float32),
        jnp.zeros((heads_here, row_count, HD), jnp.float32),
    )
    state_now = fold_keys(
        initial,
        (
            lax.all_gather(attn_key, "seq", axis=0, tiled=True),
            lax.all_gather(attn_value, "seq", axis=0, tiled=True),
        ),
        jnp.int32(0),
    )
    running_max, running_total, running_sum = state_now
    result = running_sum / running_total[:, :, None]
    return result.transpose(1, 0, 2).reshape(row_count, col_count).astype(jnp.bfloat16)


LOG2E = 1.4426950408889634
LN2 = 0.6931471805599453
SCALE2 = HD**-0.5 * LOG2E
NEG = -1e30
STAT_ROWS = 16


def hyena_kernel(row_count, taps, lens_ref, feat_ref, rim_ref, filt_ref, fwd_ref, inv_ref, out_ref,
                 ext_ref, sum_ref):
    base = lens_ref[lens_ref.shape[0] - 1]
    ext_ref[:taps, :] = rim_ref[...]
    ext_ref[taps:, :] = (
        feat_ref[1].astype(jnp.float32) * feat_ref[2].astype(jnp.float32)
    ).astype(jnp.bfloat16)

    def dot(x, y):
        return jnp.dot(x, y, preferred_element_type=jnp.float32)

    filt = filt_ref[...]
    filt_hi = filt.astype(jnp.bfloat16)
    filt_lo = (filt - filt_hi.astype(jnp.float32)).astype(jnp.bfloat16)
    spec = (
        dot(fwd_ref[0, :, :taps], filt_hi)
        + dot(fwd_ref[1, :, :taps], filt_hi)
        + dot(fwd_ref[0, :, :taps], filt_lo)
    )
    spec_r, spec_i = spec[:taps], spec[taps:]
    win_iota = lax.broadcasted_iota(jnp.int32, (2 * taps, 1), 0)
    out_iota = lax.broadcasted_iota(jnp.int32, (taps, 1), 0)
    for block in range(row_count // taps):
        r0 = block * taps
        start = jnp.int32(0)
        for doc in range(lens_ref.shape[0] - 1):
            end = start + lens_ref[doc]
            first, last = start - base, end - base

            @pl.when((last > r0) & (first < r0 + taps) & (first < last))
            def _(first=first):
                window = ext_ref[r0 : r0 + 2 * taps, :]
                window = jnp.where(win_iota + (r0 - taps) >= first, window, jnp.zeros_like(window))
                wave = dot(fwd_ref[0], window) + dot(fwd_ref[1], window)
                wave_r, wave_i = wave[:taps], wave[taps:]
                prod = jnp.concatenate(
                    (
                        (wave_r * spec_r - wave_i * spec_i).astype(jnp.bfloat16),
                        (wave_r * spec_i + wave_i * spec_r).astype(jnp.bfloat16),
                    ),
                    axis=0,
                )
                sums = dot(inv_ref[0], prod) + dot(inv_ref[1], prod)
                sum_ref[...] = jnp.where(out_iota + r0 >= first, sums, sum_ref[...])

            start = end
        out_ref[r0 : r0 + taps, :] = (
            feat_ref[0, r0 : r0 + taps, :].astype(jnp.float32) * sum_ref[...]
        ).astype(out_ref.dtype)


def split_two(matrix):
    high = matrix.astype(jnp.bfloat16)
    low = (matrix - high.astype(np.float64)).astype(jnp.bfloat16)
    return np.stack((high, low))


def hyena_fast(features, short_filter, medium_filter, skip_gain, lengths):
    row_count, _, cols = features.shape
    taps = medium_filter.shape[0]
    span_index = lax.axis_index("seq")
    streams = features.transpose(1, 0, 2)
    tail = streams[:, row_count - taps :]
    gated_tail = (tail[1].astype(jnp.float32) * tail[2].astype(jnp.float32)).astype(jnp.bfloat16)
    carried = passed_along(gated_tail, "seq", 1)
    head = jnp.concatenate((short_filter[:1] + skip_gain[None, :], short_filter[1:]), axis=0)
    filt = medium_filter + jnp.pad(head, ((0, taps - head.shape[0]), (0, 0)))
    angle = np.pi / (2 * taps) * np.outer(2 * np.arange(taps) + 1, np.arange(2 * taps))
    fwd = split_two(np.concatenate((np.cos(angle), -np.sin(angle)), axis=0))
    inv = split_two(
        np.concatenate((np.cos(angle), -np.sin(angle)), axis=0).T[taps:] / taps
    )
    scalars = jnp.concatenate((lengths, jnp.reshape(span_index * row_count, (1,)).astype(jnp.int32)))
    width = math.gcd(cols, 512)
    return pl.pallas_call(
        lambda *refs: hyena_kernel(row_count, taps, *refs),
        grid=(cols // width,),
        out_shape=jax.ShapeDtypeStruct((row_count, cols), jnp.bfloat16),
        in_specs=[
            pl.BlockSpec(memory_space=pltpu.SMEM),
            pl.BlockSpec((3, row_count, width), lambda i: (0, 0, i)),
            pl.BlockSpec((taps, width), lambda i: (0, i)),
            pl.BlockSpec((taps, width), lambda i: (0, i)),
            pl.BlockSpec(fwd.shape, lambda i: (0, 0, 0)),
            pl.BlockSpec(inv.shape, lambda i: (0, 0, 0)),
        ],
        out_specs=pl.BlockSpec((row_count, width), lambda i: (0, i)),
        scratch_shapes=[
            pltpu.VMEM((row_count + taps, width), jnp.bfloat16),
            pltpu.VMEM((taps, width), jnp.float32),
        ],
        compiler_params=pltpu.CompilerParams(vmem_limit_bytes=32 * 2**20),
        cost_estimate=pl.CostEstimate(
            flops=2 * 9 * 2 * taps * taps * 3 * cols, bytes_accessed=8 * 2**20, transcendentals=0
        ),
        name="hyena",
    )(scalars, streams, carried, filt, fwd, inv)


def doc_start(pos, lens_ref):
    start = jnp.zeros_like(pos)
    end = jnp.int32(0)
    for doc in range(lens_ref.shape[0] - 1):
        end = end + lens_ref[doc]
        start = jnp.where(pos >= end, end, start)
    return start


def attend(query_ref, keys, values, biases, emit):
    rows = query_ref.shape[0]
    step = 128
    ones = jnp.ones((rows, 128), jnp.bfloat16)
    vals = [jnp.concatenate((v[...], ones), axis=1) for v in values]
    for r in range(0, rows, step):
        q = query_ref[r : r + step, :]
        scores = [
            lax.dot_general(q, k[...], (((1,), (1,)), ((), ())),
                            preferred_element_type=jnp.float32) + b[r : r + step, :]
            for k, b in zip(keys, biases)
        ]
        top = jnp.max(scores[0], axis=1, keepdims=True)
        for s in scores[1:]:
            top = jnp.maximum(top, jnp.max(s, axis=1, keepdims=True))
        acc = None
        for s, v in zip(scores, vals):
            w = jnp.exp2((s - top) * SCALE2).astype(jnp.bfloat16)
            part = jnp.dot(w, v, preferred_element_type=jnp.float32)
            acc = part if acc is None else acc + part
        total = acc[:, 128:]
        emit(r, acc[:, :128] / total, top * SCALE2 + jnp.log2(total))


def needs(lens_ref, base, rows, ahead, back):
    q_first = base + ahead * rows
    start = jnp.int32(0)
    end = jnp.int32(0)
    for doc in range(lens_ref.shape[0] - 1):
        end = end + lens_ref[doc]
        start = jnp.where(q_first >= end, end, start)
    return start < base + (1 - back) * rows


def fill_bias(lens_ref, base, rows, ref, ahead, back):
    qpos = base + ahead * rows + lax.broadcasted_iota(jnp.int32, (rows, 1), 0)
    starts = doc_start(qpos, lens_ref)
    kpos = base - back * rows + lax.broadcasted_iota(jnp.int32, (1, rows), 1)
    ref[...] = jnp.where((kpos <= qpos) & (kpos >= starts), 0.0, NEG).astype(jnp.float32)


def near_kernel(rows, lens_ref, q_ref, k_ref, v_ref, k1_ref, v1_ref, k2_ref, v2_ref, all_ref, o_ref,
                b0, b1, b2):
    span = lens_ref[lens_ref.shape[0] - 1]
    base = span * rows
    one = (span >= 1) & needs(lens_ref, base, rows, 0, 1)
    two = (span >= 2) & needs(lens_ref, base, rows, 0, 2)

    @pl.when(pl.program_id(0) == 0)
    def _():
        fill_bias(lens_ref, base, rows, b0, 0, 0)
        pl.when(one)(lambda: fill_bias(lens_ref, base, rows, b1, 0, 1))
        pl.when(two)(lambda: fill_bias(lens_ref, base, rows, b2, 0, 2))

    def emit(r, out, lse):
        o_ref[r : r + 128, :] = out.astype(jnp.bfloat16)

    pl.when(two)(
        lambda: attend(q_ref, (k_ref, k1_ref, k2_ref), (v_ref, v1_ref, v2_ref), (b0, b1, b2), emit)
    )
    pl.when(one & jnp.logical_not(two))(
        lambda: attend(q_ref, (k_ref, k1_ref), (v_ref, v1_ref), (b0, b1), emit)
    )
    pl.when(jnp.logical_not(one))(lambda: attend(q_ref, (k_ref,), (v_ref,), (b0,), emit))


def attn_kernel(rows, lens_ref, q_ref, qa_ref, qb_ref, kp_ref, vp_ref, k_ref, v_ref,
                o_ref, lse_ref, oa_ref, ob_ref, b00, b10, b01, b11, b02):
    span = lens_ref[lens_ref.shape[0] - 1]
    base = span * rows

    def reads(ahead, back):
        return needs(lens_ref, base, rows, ahead, back)

    own_prev = (span == 1) & reads(0, 1)
    a_here = ((span == 1) | (span == 2)) & reads(1, 0)
    a_prev = (span == 1) & reads(1, 1)
    b_here = (span == 1) & reads(2, 0)

    @pl.when(pl.program_id(0) == 0)
    def _():
        lse_ref[...] = jnp.zeros_like(lse_ref)

        def fill(ref, ahead, back):
            fill_bias(lens_ref, base, rows, ref, ahead, back)

        fill(b00, 0, 0)
        pl.when(own_prev)(lambda: fill(b01, 0, 1))
        pl.when(a_here)(lambda: fill(b10, 1, 0))
        pl.when(a_prev)(lambda: fill(b11, 1, 1))
        pl.when(b_here)(lambda: fill(b02, 2, 0))

    step = 128
    head_lane = lax.broadcasted_iota(jnp.int32, (step, 128), 1) == pl.program_id(0)

    def emit_own(r, out, lse):
        o_ref[r : r + step, :] = out.astype(jnp.bfloat16)
        lse_ref[r : r + step, :] = jnp.where(head_lane, lse, lse_ref[r : r + step, :])

    eye = lax.broadcasted_iota(jnp.int32, (128, 128), 0) == lax.broadcasted_iota(
        jnp.int32, (128, 128), 1
    )
    stat_iota = lax.broadcasted_iota(jnp.int32, (STAT_ROWS, 128), 0)

    def emit_to(ref):
        stats = [jnp.zeros((STAT_ROWS, 128), jnp.float32)]

        def emit(r, out, lse):
            ref[r : r + step, :] = out.astype(jnp.bfloat16)
            rest = jnp.sum(jnp.where(eye, lse, 0.0), axis=0, keepdims=True)
            for piece in range(3):
                high = rest.astype(jnp.bfloat16).astype(jnp.float32)
                stats[0] = jnp.where(stat_iota == piece * (rows // step) + r // step, high, stats[0])
                rest = rest - high
            if r + step == rows:
                ref[rows:, :] = stats[0].astype(jnp.bfloat16)

        return emit

    def empty(ref):
        ref[:rows, :] = jnp.zeros((rows, 128), jnp.bfloat16)
        ref[rows:, :] = jnp.where(stat_iota < rows // step, NEG, 0.0).astype(jnp.bfloat16)

    pl.when(own_prev)(lambda: attend(q_ref, (kp_ref, k_ref), (vp_ref, v_ref), (b01, b00), emit_own))
    pl.when(jnp.logical_not(own_prev))(lambda: attend(q_ref, (k_ref,), (v_ref,), (b00,), emit_own))
    pl.when(a_prev)(
        lambda: attend(qa_ref, (kp_ref, k_ref), (vp_ref, v_ref), (b11, b10), emit_to(oa_ref))
    )
    pl.when(a_here & jnp.logical_not(a_prev))(
        lambda: attend(qa_ref, (k_ref,), (v_ref,), (b10,), emit_to(oa_ref))
    )
    pl.when(jnp.logical_not(a_here))(lambda: empty(oa_ref))
    pl.when(b_here)(lambda: attend(qb_ref, (k_ref,), (v_ref,), (b02,), emit_to(ob_ref)))
    pl.when(jnp.logical_not(b_here))(lambda: empty(ob_ref))


def merge_kernel(rows, lens_ref, o_ref, lse_ref, ra_ref, rb_ref, all_ref, out_ref):
    span = lens_ref[lens_ref.shape[0] - 1]
    step = 128
    eye = lax.broadcasted_iota(jnp.int32, (128, 128), 0) == lax.broadcasted_iota(
        jnp.int32, (128, 128), 1
    )

    @pl.when(span < 2)
    def _():
        out_ref[...] = o_ref[...]

    @pl.when(span >= 2)
    def _():
        blocks = rows // step
        head_lane = lax.broadcasted_iota(jnp.int32, (step, 128), 1) == pl.program_id(0)
        stat_a = ra_ref[rows:, :].astype(jnp.float32)
        stat_b = rb_ref[rows:, :].astype(jnp.float32)

        def column(stats, i):
            row = (stats[i : i + 1] + stats[blocks + i : blocks + i + 1]) + stats[
                2 * blocks + i : 2 * blocks + i + 1
            ]
            return jnp.sum(jnp.where(eye, row, 0.0), axis=1, keepdims=True)

        for i in range(blocks):
            r = i * step
            own = jnp.sum(jnp.where(head_lane, lse_ref[r : r + step, :], 0.0), axis=1, keepdims=True)
            lse_a = column(stat_a, i)
            lse_b = jnp.where(span == 3, column(stat_b, i), NEG)
            top = jnp.maximum(own, jnp.maximum(lse_a, lse_b))
            w0 = jnp.exp2(own - top)
            w1 = jnp.exp2(lse_a - top)
            w2 = jnp.exp2(lse_b - top)
            total = (
                o_ref[r : r + step, :].astype(jnp.float32) * w0
                + ra_ref[r : r + step, :].astype(jnp.float32) * w1
                + rb_ref[r : r + step, :].astype(jnp.float32) * w2
            )
            out_ref[r : r + step, :] = (total / (w0 + w1 + w2)).astype(jnp.bfloat16)


def attention_fast(attn_query, attn_key, attn_value, lengths, hyena_out):
    rows, cols = attn_query.shape
    span_index = lax.axis_index("seq")
    scalars = jnp.concatenate((lengths, jnp.reshape(span_index, (1,)).astype(jnp.int32)))
    all_heads = cols // HD
    heads = all_heads * 3 // 8
    near = all_heads - 2 * heads
    width = heads * HD
    smem = pl.BlockSpec(memory_space=pltpu.SMEM)
    block = pl.BlockSpec((rows, HD), lambda h: (0, h))
    tall = pl.BlockSpec((rows + STAT_ROWS, HD), lambda h: (0, h))
    packed = pl.BlockSpec((rows, 128), lambda h: (0, 0))

    def at(offset):
        return pl.BlockSpec((rows, HD), lambda h: (0, offset + h))

    def pair(lo, hi):
        return jnp.concatenate((attn_key[:, lo:hi], attn_value[:, lo:hi]), axis=1)

    sent = []
    for c in range(2):
        qc = attn_query[:, c * width : (c + 1) * width]
        qa = lax.ppermute(qc, "seq", [(2, 1), (3, 2)])
        qb = lax.ppermute(qc, "seq", [(3, 1)])
        kv = pair(c * width, (c + 1) * width)
        sent.append((qa, qb, lax.ppermute(kv, "seq", [(0, 1)])))
    kv = pair(2 * width, cols)
    kv1 = lax.ppermute(kv, "seq", [(0, 1), (1, 2), (2, 3)])
    kv2 = lax.ppermute(kv, "seq", [(0, 2), (1, 3)])
    scalars, hyena_out = lax.optimization_barrier((scalars, hyena_out))
    outs = []
    for c in range(2):
        qa, qb, kvp = sent[c]
        whole = at(c * heads)
        own, lse, oa, ob = pl.pallas_call(
            lambda *refs: attn_kernel(rows, *refs),
            grid=(heads,),
            out_shape=(
                jax.ShapeDtypeStruct((rows, width), jnp.bfloat16),
                jax.ShapeDtypeStruct((rows, 128), jnp.float32),
                jax.ShapeDtypeStruct((rows + STAT_ROWS, width), jnp.bfloat16),
                jax.ShapeDtypeStruct((rows + STAT_ROWS, width), jnp.bfloat16),
            ),
            in_specs=[smem, whole, block, block, block, at(heads), whole, whole],
            out_specs=(block, packed, tall, tall),
            scratch_shapes=[pltpu.VMEM((rows, rows), jnp.float32)] * 5,
            compiler_params=pltpu.CompilerParams(vmem_limit_bytes=32 * 2**20),
            cost_estimate=pl.CostEstimate(
                flops=heads * 5 * rows * rows * HD * 4 * 2,
                bytes_accessed=8 * 2**20,
                transcendentals=heads * 5 * rows * rows,
            ),
            name="attend",
        )(scalars, attn_query, qa, qb, kvp, kvp, attn_key, attn_value)
        ra = lax.ppermute(oa, "seq", [(1, 2), (2, 3)])
        rb = lax.ppermute(ob, "seq", [(1, 3)])
        outs.append((own, lse, ra, rb))
        scalars, _ = lax.optimization_barrier((scalars, own))
    anywhere = pl.BlockSpec(memory_space=pl.ANY)
    whole_out = jax.ShapeDtypeStruct((rows, cols), jnp.bfloat16)
    mine = at(2 * heads)
    result = pl.pallas_call(
        lambda *refs: near_kernel(rows, *refs[:8], None, *refs[8:]),
        grid=(near,),
        out_shape=whole_out,
        in_specs=[smem, mine, mine, mine, block, at(near), block, at(near)],
        out_specs=mine,
        scratch_shapes=[pltpu.VMEM((rows, rows), jnp.float32)] * 3,
        compiler_params=pltpu.CompilerParams(vmem_limit_bytes=32 * 2**20),
        cost_estimate=pl.CostEstimate(
            flops=near * 3 * rows * rows * HD * 4 * 2,
            bytes_accessed=4 * 2**20,
            transcendentals=near * 3 * rows * rows,
        ),
        name="near",
    )(scalars, attn_query, attn_key, attn_value, kv1, kv1, kv2, kv2)
    for c in range(2):
        own, lse, ra, rb = outs[c]
        result = pl.pallas_call(
            lambda *refs: merge_kernel(rows, *refs),
            grid=(heads,),
            out_shape=whole_out,
            in_specs=[smem, block, packed, tall, tall, anywhere],
            out_specs=at(c * heads),
            input_output_aliases={5: 0},
            cost_estimate=pl.CostEstimate(
                flops=rows * width * 16, bytes_accessed=4 * 2**20, transcendentals=0
            ),
            name="merge",
        )(scalars, own, lse, ra, rb, result)
    return hyena_out, result


MESH_ID = pl.DeviceIdType.MESH
FAR = 1 << 20
CHUNK = 256
AHEAD = 5
BEHIND = 4


def start_at(pos, lens_ref):
    start = jnp.int32(0)
    end = jnp.int32(0)
    for doc in range(lens_ref.shape[0] - 1):
        end = end + lens_ref[doc]
        start = jnp.where(pos >= end, end, start)
    return start


def fused_kernel(
    rows, cols, lens_hbm, feat_hbm, q_hbm, k_hbm, v_hbm, short_hbm, med_hbm, skip_hbm, fwd_hbm, inv_hbm,
    hy_hbm, at_hbm,
    lens_ref, short_ref, med_ref, skip_ref, fwd_ref, inv_ref,
    feat, qv, kv, vv, ext, halo, up_rx, st_rx, q_near, q_far, up_tx, st_tx,
    b_own, b_own_l, b_near, b_near_l, b_far, spec, fix, hy_v, at_v,
    load_sem, hy_sem, at_sem, halo_sem, near_tx, near_rx, far_tx, far_rx, up_tx_sem, up_rx_sem,
    st_tx_sem, st_rx_sem,
):
    f32, bf16 = jnp.float32, jnp.bfloat16
    heads = cols // HD
    part = rows // 3
    span = lax.axis_index("seq")
    base = span * rows
    has_left, has_right = span > 0, span < 3
    has_far, sends_far = span < 2, span > 1

    def load(index, src, dst):
        return pltpu.make_async_copy(src, dst, load_sem.at[index])

    tail_load = load(0, feat_hbm.at[1:3, 2 * part :, :], feat.at[1:3, 2 * part :, :])
    front_load = load(1, feat_hbm.at[1:3, : 2 * part, :], feat.at[1:3, : 2 * part, :])
    mix_load = load(2, feat_hbm.at[0], feat.at[0])
    k_load = load(3, k_hbm, kv)
    v_load = load(4, v_hbm, vv)
    q_load = load(5, q_hbm, qv)
    lens_load = load(6, lens_hbm, lens_ref)
    filter_loads = [
        load(7, short_hbm, short_ref),
        load(8, med_hbm, med_ref),
        load(9, skip_hbm, skip_ref),
        load(10, fwd_hbm, fwd_ref),
        load(11, inv_hbm, inv_ref),
    ]

    def start_all(copies):
        for copy in copies:
            copy.start()

    start_all([lens_load, tail_load])
    head_loads = [k_load, v_load, q_load]
    mix_loads = filter_loads + [front_load, mix_load]
    pl.when(has_left)(lambda: start_all(mix_loads + head_loads))
    pl.when(jnp.logical_not(has_left))(lambda: start_all(head_loads + mix_loads))

    def lanes(h):
        return pl.ds(pl.multiple_of(h * HD, HD), HD)

    def remote(src, dst, tx, rx, to):
        return pltpu.make_async_remote_copy(
            src_ref=src, dst_ref=dst, send_sem=tx, recv_sem=rx, device_id={"seq": to},
            device_id_type=MESH_ID,
        )

    up_to = jnp.minimum(span + 1, 3)

    def near_copy(h):
        return remote(q_hbm.at[:, lanes(h)], q_near.at[h], near_tx.at[h], near_rx.at[h],
                      jnp.maximum(span - 1, 0))

    def far_copy(h):
        return remote(q_hbm.at[:part, lanes(h)], q_far.at[h], far_tx.at[h], far_rx.at[h],
                      jnp.maximum(span - 2, 0))

    def up_copy(h):
        return remote(up_tx.at[h], up_rx.at[h], up_tx_sem.at[h], up_rx_sem.at[h], up_to)

    def st_copy(h):
        return remote(st_tx.at[h], st_rx.at[h], st_tx_sem.at[h], st_rx_sem.at[h], up_to)

    def pass_copy(h):
        return remote(q_near.at[h, :part, :], q_far.at[h], far_tx.at[h], far_rx.at[h],
                      jnp.maximum(span - 1, 0))

    def pass_on(h):
        near_copy(h).wait_recv()
        pass_copy(h).start()
        pl.when(h + 2 < heads)(lambda: near_copy(h + 2).start())

    halo_copies = [
        remote(
            ext.at[rows : rows + part, lo:hi],
            halo.at[:, lo:hi],
            halo_sem.at[i], halo_sem.at[2 + i], up_to,
        )
        for i, (lo, hi) in enumerate(((0, cols // 4), (cols // 4, cols)))
    ]

    barrier = pltpu.get_barrier_semaphore()
    for away in (-2, -1, 1, 2):

        @pl.when((span + away >= 0) & (span + away < 4) & ((abs(away) == 1) | (lax.rem(span, 2) == 1)))
        def _(away=away):
            pl.semaphore_signal(barrier, inc=1, device_id={"seq": span + away}, device_id_type=MESH_ID)

    pl.semaphore_wait(barrier, jnp.where(has_left, jnp.where(span == 1, 3, 2), 1))

    @pl.when(sends_far)
    def _():
        def send_queries(h, carry):
            pl.when(h < heads)(lambda: near_copy(h).start())
            pl.when((span == 3) & (h >= BEHIND))(lambda: far_copy(h - BEHIND).start())
            return carry

        lax.fori_loop(0, heads + BEHIND, send_queries, 0)

    @pl.when(span == 1)
    def _():
        near_copy(0).start()
        near_copy(1).start()

    chunks = cols // CHUNK

    def chunk_cols(c):
        return pl.ds(pl.multiple_of(c * CHUNK, CHUNK), CHUNK)

    def gate(lo, hi, at):
        return (feat[1, lo:hi, at].astype(f32) * feat[2, lo:hi, at].astype(f32)).astype(bf16)

    tail_load.wait()

    def gate_tail(c, carry):
        at = chunk_cols(c)
        ext[rows : rows + part, at] = gate(2 * part, rows, at)
        ext[:part, at] = jnp.zeros((part, CHUNK), bf16)
        return carry

    lax.fori_loop(0, chunks, gate_tail, 0)
    pl.when(has_right)(lambda: halo_copies[0].start())
    pl.when(has_left & has_right)(lambda: halo_copies[1].start())

    @pl.when(jnp.logical_not(has_left))
    def _():
        def clear(h, carry):
            up_rx[h] = jnp.zeros((rows + part, HD), bf16)
            st_rx[h] = jnp.zeros((8, HD), f32)
            return carry

        lax.fori_loop(0, heads, clear, 0)

    @pl.when(span == 2)
    def _():
        def clear(h, carry):
            q_far[h] = jnp.zeros((part, HD), bf16)
            return carry

        lax.fori_loop(0, heads, clear, 0)

    lens_load.wait()
    left_q = has_left & (base - start_at(base, lens_ref) > 2 * part)
    right_q = has_right & (base + rows - start_at(base + rows, lens_ref) > 2 * part)
    fresh = has_far & right_q & (start_at(base + 2 * rows, lens_ref) < base + rows)
    slot_mine = (span > 1) & (base - rows - start_at(base, lens_ref) > 2 * part)

    def column_iota(first, count):
        return first + lax.broadcasted_iota(jnp.int32, (count, 1), 0)

    own_pos = column_iota(base, rows)
    near_pos = column_iota(base + rows, rows)
    far_pos = column_iota(base + 2 * rows, part)
    key_pos = base + lax.broadcasted_iota(jnp.int32, (1, rows), 1)
    left_pos = base - 2 * part + lax.broadcasted_iota(jnp.int32, (1, 2 * part), 1)
    no_keys = jnp.where(has_left & jnp.logical_not(left_q), 0, FAR)
    no_near = jnp.where(right_q, 0, FAR)
    no_far = jnp.where(fresh, 0, FAR)
    own_start = doc_start(own_pos, lens_ref)
    near_start = doc_start(near_pos, lens_ref) + no_near
    far_start = doc_start(far_pos, lens_ref) + no_far

    def bias(ok):
        return jnp.where(ok, 0.0, NEG).astype(f32)

    b_own[...] = bias((key_pos <= own_pos) & (key_pos >= own_start))
    b_own_l[...] = bias(left_pos >= own_start + no_keys)
    b_near[...] = bias(key_pos >= near_start)
    b_near_l[...] = bias(left_pos >= near_start + no_keys)
    b_far[...] = bias(key_pos >= far_start)

    def dot(x, y):
        return jnp.dot(x, y, preferred_element_type=f32)

    first_cut = jnp.int32(FAR)
    last_cut = jnp.int32(-1)
    end = jnp.int32(0)
    for doc in range(lens_ref.shape[0] - 1):
        end = end + lens_ref[doc]
        first_cut = jnp.where((end > base) & (end < first_cut), end, first_cut)
        last_cut = jnp.where((end < base + rows) & (end > last_cut), end, last_cut)
    cuts = []
    for cut in (first_cut, last_cut):
        valid = (cut > base) & (cut < base + rows)
        block = jnp.where(valid, lax.div(jnp.where(valid, cut - base, 0), part), 0)
        cuts.append((jnp.where(valid, cut, FAR), block))
    win_iota = lax.broadcasted_iota(jnp.int32, (2 * part, 1), 0)
    out_iota = lax.broadcasted_iota(jnp.int32, (part, 1), 0)

    def transform(window, first_pos, from_pos, spec_r, spec_i):
        window = jnp.where(win_iota + first_pos >= from_pos, window, jnp.zeros_like(window))
        return spread(window, spec_r, spec_i)

    def spread(window, spec_r, spec_i):
        wave = dot(fwd_ref[0], window)
        wave_r, wave_i = wave[:part], wave[part:]
        prod = jnp.concatenate(
            (
                (wave_r * spec_r - wave_i * spec_i).astype(bf16),
                (wave_r * spec_i + wave_i * spec_r).astype(bf16),
            ),
            axis=0,
        )
        return dot(inv_ref[0], prod)

    def finish(block, at, sums, fixes):
        for (cut, cut_block), fixed in zip(cuts, fixes):
            cut_from = jnp.where(cut_block == block, cut, FAR)
            sums = jnp.where(out_iota + (base + block * part) >= cut_from, fixed, sums)
        r0 = block * part
        hy_v[r0 : r0 + part, at] = (feat[0, r0 : r0 + part, at].astype(f32) * sums).astype(bf16)

    def hyena_loads():
        front_load.wait()
        mix_load.wait()
        for copy in filter_loads:
            copy.wait()

    def hyena_main(c, carry):
        at = chunk_cols(c)
        ext[part:rows, at] = gate(0, 2 * part, at)
        short = short_ref[:, at]
        head = jnp.concatenate(
            (short[:1] + skip_ref[:, at], short[1:], jnp.zeros((8 - short.shape[0], CHUNK), f32)), axis=0
        )
        filt = jnp.concatenate((med_ref[:8, at] + head, med_ref[8:, at]), axis=0)
        filt_hi = filt.astype(bf16)
        filt_lo = (filt - filt_hi.astype(f32)).astype(bf16)
        both = (
            dot(fwd_ref[0, :, :part], filt_hi)
            + dot(fwd_ref[1, :, :part], filt_hi)
            + dot(fwd_ref[0, :, :part], filt_lo)
        )
        spec[:, at] = both
        spec_r, spec_i = both[:part], both[part:]
        fixes = []
        for index, (cut, cut_block) in enumerate(cuts):
            window = jnp.zeros((2 * part, CHUNK), bf16)
            for block in range(3):
                r0 = block * part
                cut_from = jnp.where(cut_block == block, cut, FAR)
                window = jnp.where(
                    win_iota + (base + r0 - part) >= cut_from, ext[r0 : r0 + 2 * part, at], window
                )
            sums = spread(window, spec_r, spec_i)
            fix[index, :, at] = sums
            fixes.append(sums)
        for block in (1, 2):
            r0 = block * part
            sums = transform(
                ext[r0 : r0 + 2 * part, at], base + r0 - part, start_at(base + r0, lens_ref), spec_r, spec_i
            )
            finish(block, at, sums, fixes)
        return carry

    hy_late = pltpu.make_async_copy(hy_v.at[part:, :], hy_hbm.at[part:, :], hy_sem.at[0])
    hy_first = pltpu.make_async_copy(hy_v.at[:part, :], hy_hbm.at[:part, :], hy_sem.at[1])

    def hyena_first():
        @pl.when(has_left)
        def _():
            for copy in halo_copies:
                copy.wait_recv()

        def one(c, carry):
            at = chunk_cols(c)
            window = jnp.concatenate((halo[:, at], ext[part : 2 * part, at]), axis=0)
            sums = transform(
                window, base - part, start_at(base, lens_ref), spec[:part, at], spec[part:, at]
            )
            finish(0, at, sums, [fix[i, :, at] for i in range(2)])
            return carry

        lax.fori_loop(0, chunks, one, 0, unroll=2)
        hy_first.start()

    @pl.when(has_left)
    def _():
        pl.when(span == 1)(lambda: pass_on(0))
        hyena_loads()

        def step(c, carry):
            for h, when in ((1, 1), (2, 3), (3, 5), (4, 7), (5, 7))[: AHEAD - 1]:

                @pl.when((span == 1) & (c == min(when, chunks - 1)))
                def _(h=h):
                    pass_on(h)

            return hyena_main(c, carry)

        lax.fori_loop(0, chunks, step, 0)
        hy_late.start()
        pl.when(sends_far)(hyena_first)

    k_load.wait()
    v_load.wait()
    q_load.wait()
    ones = jnp.ones((rows, HD), bf16)
    eye = lax.broadcasted_iota(jnp.int32, (part, HD), 0) == lax.broadcasted_iota(jnp.int32, (part, HD), 1)
    stat_iota = lax.broadcasted_iota(jnp.int32, (8, HD), 0)
    left_off = jnp.where(left_q, 0.0, NEG)
    slot_off = jnp.where(slot_mine, 0.0, NEG)

    def attend_to(q, keys, values, biases):
        scores = [
            lax.dot_general(q, k, (((1,), (1,)), ((), ())), preferred_element_type=f32) + b
            for k, b in zip(keys, biases)
        ]
        top = jnp.max(scores[0], axis=1, keepdims=True)
        for s in scores[1:]:
            top = jnp.maximum(top, jnp.max(s, axis=1, keepdims=True))
        acc = None
        for s, v in zip(scores, values):
            w = jnp.exp2((s - top) * SCALE2).astype(bf16)
            term = dot(w, v)
            acc = term if acc is None else acc + term
        return acc[:, :HD], acc[:, HD:], top * SCALE2

    spread_from = min(4, heads - chunks - 1)

    def head_step(h, carry):
        at = lanes(h)

        @pl.when(jnp.logical_not(has_left))
        def _():
            pl.when(h == spread_from)(hyena_loads)

            @pl.when((h >= spread_from) & (h < spread_from + chunks))
            def _():
                hyena_main(h - spread_from, 0)

            @pl.when(h == spread_from + chunks)
            def _():
                hy_late.start()
                hyena_first()

        @pl.when(has_left)
        def _():
            up_copy(h).wait_recv()
            st_copy(h).wait_recv()

        k = kv[:, at]
        v = vv[:, at]
        k_left = up_rx[h, : 2 * part, :]
        v_ones = jnp.concatenate((v, ones), axis=1)
        v_left = jnp.concatenate((up_rx[h, 2 * part :, :], ones[: 2 * part]), axis=1)

        @pl.when(has_right)
        def _():
            pl.when(span != 1)(lambda: near_copy(h).wait_recv())
            pl.when(has_far)(lambda: far_copy(h).wait_recv())
            tails = (k[part : 2 * part], k[2 * part :], v[part : 2 * part], v[2 * part :])
            stats = jnp.zeros((8, HD), f32)

            def give(i, out):
                up_tx[h, i * part : (i + 1) * part, :] = jnp.where(
                    right_q, out, tails[i].astype(f32)
                ).astype(bf16)

            def to_row(lse):
                return jnp.sum(jnp.where(eye, lse, 0.0), axis=0, keepdims=True)

            for i in range(3):
                r0 = i * part
                acc, total, top = attend_to(
                    q_near[h, r0 : r0 + part, :],
                    (k, k_left),
                    (v_ones, v_left),
                    (b_near[r0 : r0 + part, :], b_near_l[r0 : r0 + part, :]),
                )
                give(i, acc / total)
                stats = jnp.where(stat_iota == i, to_row(top + jnp.log2(total)), stats)
            passed = up_rx[h, rows:, :].astype(f32)
            passed_stat = st_rx[h]

            acc, total, top = attend_to(q_far[h], (k,), (v_ones,), (b_far[...],))
            give(3, jnp.where(fresh, acc / total, passed))
            lse = to_row(top + jnp.log2(total))
            st_tx[h] = jnp.where(stat_iota == 3, jnp.where(fresh, lse, passed_stat[3:4]), stats)
            up_copy(h).start()
            st_copy(h).start()
            pl.when((span == 1) & (h + AHEAD < heads))(lambda: pass_on(h + AHEAD))

        stats_in = st_rx[h]

        def column(i):
            return jnp.sum(jnp.where(eye, stats_in[i : i + 1], 0.0), axis=1, keepdims=True)

        for i in range(3):
            r0 = i * part
            r1 = r0 + part
            acc, total, top = attend_to(
                qv[r0:r1, at],
                (k[:r1], k_left),
                (v_ones[:r1], v_left),
                (b_own[r0:r1, :r1], b_own_l[r0:r1, :]),
            )
            lse = column(i) + left_off
            best = jnp.maximum(top, lse)
            if i == 0:
                slot_lse = column(3) + slot_off
                best = jnp.maximum(best, slot_lse)
            w0 = jnp.exp2(top - best)
            w1 = jnp.exp2(lse - best)
            mixed = acc * w0 + up_rx[h, r0:r1, :].astype(f32) * w1
            norm = total * w0 + w1
            if i == 0:
                w2 = jnp.exp2(slot_lse - best)
                mixed = mixed + up_rx[h, rows:, :].astype(f32) * w2
                norm = norm + w2
            at_v[r0:r1, at] = (mixed / norm).astype(bf16)
        pltpu.make_async_copy(at_v.at[:, at], at_hbm.at[:, at], at_sem.at[h]).start()
        return carry

    lax.fori_loop(0, heads, head_step, 0)
    pl.when(jnp.logical_not(has_left))(lambda: halo_copies[1].start())
    pl.when(span == 1)(hyena_first)

    def drain(h, carry):
        at = lanes(h)
        pltpu.make_async_copy(at_v.at[:, at], at_hbm.at[:, at], at_sem.at[h]).wait()

        @pl.when(has_right)
        def _():
            up_copy(h).wait_send()
            st_copy(h).wait_send()

        pl.when(has_left)(lambda: near_copy(h).wait_send())
        pl.when(span == 3)(lambda: far_copy(h).wait_send())
        pl.when(span == 1)(lambda: pass_copy(h).wait_send())
        return carry

    lax.fori_loop(0, heads, drain, 0)

    @pl.when(has_right)
    def _():
        for copy in halo_copies:
            copy.wait_send()

    hy_late.wait()
    hy_first.wait()


def land_kernel(pieces, hy_src, at_src, hy_dst, at_dst, held, in_sem, out_sem):
    step = hy_src.shape[0] // pieces
    moves = []
    for array, (src, dst) in enumerate(((hy_src, hy_dst), (at_src, at_dst))):
        for i in range(pieces):
            rows = pl.ds(i * step, step)
            here = held.at[array, rows, :]
            index = array * pieces + i
            inward = pltpu.make_async_copy(src.at[rows, :], here, in_sem.at[index])
            moves.append((inward, pltpu.make_async_copy(here, dst.at[rows, :], out_sem.at[index])))
            inward.start()
    for inward, outward in moves:
        inward.wait()
        outward.start()
    for inward, outward in moves:
        outward.wait()


def fused(features, short_filter, medium_filter, skip_gain, attn_query, attn_key, attn_value, lengths):
    rows, cols = attn_query.shape
    part = rows // 3
    heads = cols // HD
    angle = np.pi / (2 * part) * np.outer(2 * np.arange(part) + 1, np.arange(2 * part))
    wave = np.concatenate((np.cos(angle), -np.sin(angle)), axis=0)
    fwd = split_two(wave)
    inv = split_two(wave.T[part:] / part)
    anywhere = pl.BlockSpec(memory_space=pl.ANY)
    out = jax.ShapeDtypeStruct((rows, cols), jnp.bfloat16)

    def buf(*shape):
        return pltpu.VMEM(shape, jnp.bfloat16)

    def wide(*shape):
        return pltpu.VMEM(shape, jnp.float32)

    each = pltpu.SemaphoreType.DMA((heads,))
    made = pl.pallas_call(
        lambda *refs: fused_kernel(rows, cols, *refs),
        out_shape=(out, out),
        in_specs=[pl.BlockSpec(memory_space=pltpu.HBM)] * 10,
        out_specs=(anywhere, anywhere),
        scratch_shapes=[
            pltpu.SMEM(lengths.shape, jnp.int32), wide(*short_filter.shape), wide(part, cols), wide(1, cols),
            buf(*fwd.shape), buf(*inv.shape),
            buf(3, rows, cols), buf(rows, cols), buf(rows, cols), buf(rows, cols),
            buf(rows + part, cols), buf(part, cols),
            buf(heads, rows + part, HD), wide(heads, 8, HD),
            buf(heads, rows, HD), buf(heads, part, HD),
            buf(heads, rows + part, HD), wide(heads, 8, HD),
            wide(rows, rows), wide(rows, 2 * part), wide(rows, rows), wide(rows, 2 * part),
            wide(part, rows),
            wide(2 * part, cols), wide(2, part, cols),
            buf(rows, cols), buf(rows, cols),
            pltpu.SemaphoreType.DMA((12,)), pltpu.SemaphoreType.DMA((2,)), each,
            pltpu.SemaphoreType.DMA((4,)),
        ] + [each] * 8,
        compiler_params=pltpu.CompilerParams(
            collective_id=0, has_side_effects=True, vmem_limit_bytes=60 * 2**20
        ),
        cost_estimate=pl.CostEstimate(
            flops=heads * 32 * part * part * HD * 4, bytes_accessed=16 * 2**20,
            transcendentals=heads * 32 * part * part,
        ),
        name="fused",
    )(
        lengths, features.transpose(1, 0, 2), attn_query, attn_key, attn_value,
        short_filter, medium_filter, skip_gain[None, :], fwd, inv,
    )
    pieces = 4
    return pl.pallas_call(
        lambda *refs: land_kernel(pieces, *refs),
        out_shape=(out, out),
        in_specs=[anywhere] * 2,
        out_specs=(anywhere, anywhere),
        scratch_shapes=[
            buf(2, rows, cols), pltpu.SemaphoreType.DMA((2 * pieces,)), pltpu.SemaphoreType.DMA((2 * pieces,))
        ],
        compiler_params=pltpu.CompilerParams(vmem_limit_bytes=60 * 2**20),
        cost_estimate=pl.CostEstimate(flops=0, bytes_accessed=8 * rows * cols, transcendentals=0),
        name="land",
    )(*made)


def local(
    features, short_filter, medium_filter, skip_gain, attn_query, attn_key, attn_value, lengths
):
    rows, cols = attn_query.shape
    spans = lax.axis_size("seq")
    taps = medium_filter.shape[0]
    if spans == 4 and rows == 3 * taps and taps == HD and cols % CHUNK == 0 and short_filter.shape[0] < 8:
        return fused(
            features, short_filter, medium_filter, skip_gain, attn_query, attn_key, attn_value, lengths
        )
    if cols % 128 == 0 and taps % 128 == 0 and rows % taps == 0:
        hyena = hyena_fast
    else:
        hyena = hyena_mix
    hyena_out = hyena(features, short_filter, medium_filter, skip_gain, lengths)
    if spans == 4 and rows % 128 == 0 and rows <= 640 and cols % (8 * HD) == 0:
        return attention_fast(attn_query, attn_key, attn_value, lengths, hyena_out)
    return (hyena_out, attention_mix(attn_query, attn_key, attn_value, lengths))


def solution(mesh):
    in_specs = (
        P(("groups", "seq"), None, ("tensor", "sub")),
        P(None, ("tensor", "sub")),
        P(None, ("tensor", "sub")),
        P(("tensor", "sub")),
        P(("groups", "seq"), ("tensor", "sub")),
        P(("groups", "seq"), ("tensor", "sub")),
        P(("groups", "seq"), ("tensor", "sub")),
        P("groups"),
    )
    out_specs = (P(("groups", "seq"), ("tensor", "sub")), P(("groups", "seq"), ("tensor", "sub")))
    return jax.shard_map(local, mesh=mesh, in_specs=in_specs, out_specs=out_specs, check_vma=False)
```
